32 devices in a mesh: branch: 2 (over core), dp: 16 (over z, y, x).
Axes of the slice: x: 2, y: 2, z: 4, core: 2. Of those that a mesh axis runs over, the one named last changes fastest.
Arguments:
- small_tokens: bfloat16 [2, 128, 145, 192], P('branch', 'dp'), may hold values from -6 to 6
- large_tokens: bfloat16 [2, 128, 197, 384], P('branch', 'dp'), may hold values from -6 to 6
- small_cot: bfloat16 [2, 128, 145, 192], P('branch', 'dp'), may hold values from -6 to 6
- large_cot: bfloat16 [2, 128, 197, 384], P('branch', 'dp'), may hold values from -6 to 6
- live_counts: int32 [2, 16], P(None, 'dp'), may hold values from 1 to 8, as said below
- master: float32 [3257856], P(('branch', 'dp'))
- first_moment: float32 [3257856], P(('branch', 'dp')), may hold values from -0.0034179688 to 0.0034179688
- second_moment: float32 [3257856], P(('branch', 'dp')), may hold values from 3.0695034e-07 to 1.2278014e-06
Outputs:
- small_out: bfloat16 [2, 128, 145, 192], P('branch', 'dp')
- large_out: bfloat16 [2, 128, 197, 384], P('branch', 'dp')
- small_grad: bfloat16 [2, 128, 145, 192], P('branch', 'dp')
- large_grad: bfloat16 [2, 128, 197, 384], P('branch', 'dp')
- grad_norm: float32 [], replicated
- new_first: float32 [3257856], P(('branch', 'dp'))
- new_second: float32 [3257856], P(('branch', 'dp'))
- new_master: float32 [3257856], P(('branch', 'dp'))
- new_master16: bfloat16 [3257856], P(('branch', 'dp'))
The draws below stay inside these ranges and needn't reach their ends.
Inputs may be any that keep to these rules, and one draw needn't show every extreme that they name: `live_counts`: 8 is reached in every draw.
All inputs are finite; a program needn't handle non-finite values.
Results may differ from the reference program's by a relative error of at most 0.014.
The reference program's roundings to bfloat16 on the way count: a program that leaves them out, or rounds other values in their place, can miss the bound.
Values may be sent and summed in bfloat16 or wider, within the bound.
No kernel may reach another device: no remote copies, remote signals or barrier semaphores. Data moves between devices by JAX's collectives and lax.ppermute only.
A program may use at most 192 MiB of HBM per device.

```python
import math
import jax
import jax.numpy as jnp
from jax import lax

DS = 192
DL = 384
MS = 768
ML = 1536
HEADS = 6
SLOTS = 8
TOK_S = 145
TOK_L = 197
CROPS = 128
PARAMS = 3257856
N_DP = 16


def layout_drawn():
    shapes = []
    for label, width, hidden in (('s', DS, MS), ('l', DL, ML)):
        shapes += [(label + '_ln1', (2, width)), (label + '_qkv_w', (width, 3 * width)), (label + '_qkv_b', (3 * width,)), (label + '_proj_w', (width, width)), (label + '_proj_b', (width,)), (label + '_ln2', (2, width)), (label + '_fc1_w', (width, hidden)), (label + '_fc1_b', (hidden,)), (label + '_fc2_w', (hidden, width)), (label + '_fc2_b', (width,))]
    for label, owner, other in (('s', DS, DL), ('l', DL, DS)):
        shapes += [(label + '_to_ln', (2, owner)), (label + '_to_w', (owner, other)), (label + '_to_b', (other,)), (label + '_ca_ln', (2, other)), (label + '_ca_q_w', (other, other)), (label + '_ca_q_b', (other,)), (label + '_ca_k_w', (other, other)), (label + '_ca_v_w', (other, other)), (label + '_ca_v_b', (other,)), (label + '_ca_o_w', (other, other)), (label + '_ca_o_b', (other,)), (label + '_back_ln', (2, other)), (label + '_back_w', (other, owner)), (label + '_back_b', (owner,))]
    return shapes


def ends_with(label, tail):
    return label[len(label) - len(tail):] == tail


def unit_noise(key, shape):
    return jax.random.normal(key, shape, jnp.float32)


def matrix_factor(label):
    if ends_with(label, '_proj_w') or ends_with(label, '_ca_o_w'):
        return 4.0
    if ends_with(label, '_qkv_w') or ends_with(label, '_ca_q_w') or ends_with(label, '_ca_k_w'):
        return 1.3
    if ends_with(label, '_fc2_w'):
        return 1.5
    return 1.0


def draw_master(key, part):
    pieces = []
    for number, (label, shape) in enumerate(layout_drawn()):
        piece_key = jax.random.fold_in(key, number)
        if len(shape) == 1:
            piece = 0.1 * unit_noise(piece_key, shape)
        elif ends_with(label, '_ln') or ends_with(label, '_ln1') or ends_with(label, '_ln2'):
            gain_key, shift_key = jax.random.split(piece_key)
            gains = 1.0 + 0.3 * jax.random.uniform(gain_key, (1, shape[1]), jnp.float32, -1.0, 1.0)
            shifts = 0.1 * unit_noise(shift_key, (1, shape[1]))
            piece = jnp.concatenate([gains, shifts], 0)
        else:
            piece = unit_noise(piece_key, shape) * (matrix_factor(label) / math.sqrt(shape[0]))
        pieces.append(piece.reshape(-1))
    return jnp.concatenate(pieces).astype(jnp.float32)


def draw_live_counts(key, part):
    first_key, second_key = jax.random.split(jax.random.fold_in(key, 7))
    counts = jax.random.randint(first_key, (2 * N_DP,), 1, SLOTS + 1)
    place = jax.random.randint(second_key, (), 0, 2 * N_DP)
    counts = jnp.where(jnp.arange(2 * N_DP) == place, SLOTS, counts)
    return counts.reshape(2, N_DP).astype(jnp.int32)


def level_of(key, extent, shards, low, high):
    factor_of, own = 1.0, jax.random.fold_in(key, 6)
    for dim, blocks in shards:
        draws = jnp.exp(jax.random.uniform(jax.random.fold_in(own, dim), (blocks,), jnp.float32, low / len(shards), high / len(shards)))
        factor_of = factor_of * jnp.repeat(draws, extent[dim] // blocks).reshape([-1 if axis == dim else 1 for axis in range(len(extent))])
    return factor_of


def bell_draw(stream_key, shape, scale, reach, cuts=(), kind=jnp.bfloat16):
    gain = level_of(stream_key, shape, cuts, -0.22, 0.18) if cuts else 1.0
    entries = jax.random.normal(stream_key, shape, jnp.float32) * scale * gain
    return jnp.minimum(jnp.maximum(entries, -reach), reach).astype(kind)


def setup_inputs(seed: int = 0) -> dict:
    arg_keys = jax.random.split(jax.random.key(seed), 9)
    return {
        "small_tokens": bell_draw(arg_keys[0], (2, CROPS, TOK_S, DS), 1.0, 6.0, ((0, 2), (1, 16))),
        "large_tokens": bell_draw(arg_keys[1], (2, CROPS, TOK_L, DL), 1.0, 6.0, ((0, 2), (1, 16))),
        "small_cot": bell_draw(arg_keys[2], (2, CROPS, TOK_S, DS), 1.0, 6.0, ((0, 2), (1, 16))),
        "large_cot": bell_draw(arg_keys[3], (2, CROPS, TOK_L, DL), 1.0, 6.0, ((0, 2), (1, 16))),
        "live_counts": draw_live_counts(jax.random.fold_in(arg_keys[8], 71), 0),
        "master": draw_master(jax.random.fold_in(arg_keys[8], 71), 0),
        "first_moment": bell_draw(arg_keys[6], (PARAMS,), (1.0 / PARAMS ** 0.5), 0.0034179688, ((0, 32),), jnp.float32),
        "second_moment": jnp.clip(jnp.exp(math.log(1.2278013628019835e-06) - 1.3862944 * jax.random.uniform(arg_keys[7], (PARAMS,), jnp.float32) ** level_of(arg_keys[7], (PARAMS,), ((0, 32),), -0.2, 0.2)), 3.0695034070049587e-07, 1.2278013628019835e-06),
    }


@jax.custom_vjp
def low(v):
    return lax.optimization_barrier(v.astype(jnp.bfloat16)).astype(jnp.float32)

@jax.custom_vjp
def low_back(v):
    return v

def low_keep(v):
    return (low(v), None)

def low_pass(kept, grad):
    return (grad,)

def back_keep(v):
    return (v, None)

def back_low(kept, grad):
    return (low(grad),)
low.defvjp(low_keep, low_pass)
low_back.defvjp(back_keep, back_low)
highest = lax.Precision.HIGHEST
norm_eps = 1e-06
clip_norm = 1.0
beta_one = 0.5
beta_two = 0.5
adam_eps = 1e-08
rate = 0.05
decay = 0.05
bias_one = 1.0 - 0.5 ** 5
bias_two = 1.0 - 0.5 ** 5

def layout():
    shapes = []
    for label, width, hidden in (('s', DS, MS), ('l', DL, ML)):
        shapes += [(label + '_ln1', (2, width)), (label + '_qkv_w', (width, 3 * width)), (label + '_qkv_b', (3 * width,)), (label + '_proj_w', (width, width)), (label + '_proj_b', (width,)), (label + '_ln2', (2, width)), (label + '_fc1_w', (width, hidden)), (label + '_fc1_b', (hidden,)), (label + '_fc2_w', (hidden, width)), (label + '_fc2_b', (width,))]
    for label, owner, other in (('s', DS, DL), ('l', DL, DS)):
        shapes += [(label + '_to_ln', (2, owner)), (label + '_to_w', (owner, other)), (label + '_to_b', (other,)), (label + '_ca_ln', (2, other)), (label + '_ca_q_w', (other, other)), (label + '_ca_q_b', (other,)), (label + '_ca_k_w', (other, other)), (label + '_ca_v_w', (other, other)), (label + '_ca_v_b', (other,)), (label + '_ca_o_w', (other, other)), (label + '_ca_o_b', (other,)), (label + '_back_ln', (2, other)), (label + '_back_w', (other, owner)), (label + '_back_b', (owner,))]
    return shapes

def unflatten(flat):
    params = {}
    offset = 0
    for label, shape in layout():
        count = math.prod(shape)
        params[label] = flat[offset:offset + count].reshape(shape)
        offset = offset + count
    return params

def round_both(value):
    return low(low_back(value))

def norm_rows(value, pair):
    mean = lax.optimization_barrier(jnp.mean(value, -1, keepdims=True))
    centred = value - mean
    variance = lax.optimization_barrier(jnp.mean(centred * centred, -1, keepdims=True))
    return centred * lax.rsqrt(variance + norm_eps) * pair[0] + pair[1]

def gelu_exact(value):
    return jax.nn.gelu(value, approximate=False)

def project(value, weight):
    return jnp.einsum('...i,ij->...j', value, weight, precision=highest)

def encoder_block(tokens, params, label):
    crops, length, width = tokens.shape
    size = width // HEADS
    normed = low(norm_rows(tokens, params[label + '_ln1']))
    mixed = round_both(project(normed, params[label + '_qkv_w']) + params[label + '_qkv_b'])
    shaped = mixed.reshape(crops, length, 3, HEADS, size)
    scores = low_back(jnp.einsum('bqhd,bkhd->bhqk', shaped[:, :, 0], shaped[:, :, 1], precision=highest) * size ** (-0.5))
    probs = low(jax.nn.softmax(scores, -1))
    attended = round_both(jnp.einsum('bhqk,bkhd->bqhd', probs, shaped[:, :, 2], precision=highest).reshape(crops, length, width))
    middle = tokens + low_back(project(attended, params[label + '_proj_w']) + params[label + '_proj_b'])
    normed_two = low(norm_rows(middle, params[label + '_ln2']))
    hidden = low(gelu_exact(low_back(project(normed_two, params[label + '_fc1_w']) + params[label + '_fc1_b'])))
    return middle + low_back(project(hidden, params[label + '_fc2_w']) + params[label + '_fc2_b'])

def carry_over(value, params, prefix):
    hidden = low(gelu_exact(norm_rows(value, params[prefix + '_ln'])))
    return round_both(project(hidden, params[prefix + '_w']) + params[prefix + '_b'])

def cross_block(sent, patches, params, label):
    crops, rows, width = patches.shape
    size = width // HEADS
    joined = jnp.concatenate([sent[:, None], patches], 1)
    normed = low(norm_rows(joined, params[label + '_ca_ln']))
    query = round_both(project(normed[:, 0], params[label + '_ca_q_w']) + params[label + '_ca_q_b']).reshape(crops, HEADS, size)
    key = round_both(project(normed, params[label + '_ca_k_w'])).reshape(crops, rows + 1, HEADS, size)
    value = round_both(project(normed, params[label + '_ca_v_w']) + params[label + '_ca_v_b']).reshape(crops, rows + 1, HEADS, size)
    scores = low_back(jnp.einsum('bhd,bkhd->bhk', query, key, precision=highest) * size ** (-0.5))
    probs = low(jax.nn.softmax(scores, -1))
    attended = round_both(jnp.einsum('bhk,bkhd->bhd', probs, value, precision=highest).reshape(crops, width))
    return sent + low_back(project(attended, params[label + '_ca_o_w']) + params[label + '_ca_o_b'])

def layer(weights, small, large):
    params = unflatten(weights)
    small_block = encoder_block(small, params, 's')
    large_block = encoder_block(large, params, 'l')
    sent_small = carry_over(small_block[:, 0], params, 's_to')
    sent_large = carry_over(large_block[:, 0], params, 'l_to')
    merged_small = cross_block(sent_small, large_block[:, 1:], params, 's')
    merged_large = cross_block(sent_large, small_block[:, 1:], params, 'l')
    back_small = carry_over(merged_small, params, 's_back')
    back_large = carry_over(merged_large, params, 'l_back')
    return (jnp.concatenate([back_small[:, None], small_block[:, 1:]], 1), jnp.concatenate([back_large[:, None], large_block[:, 1:]], 1))

def reference(small_tokens, large_tokens, small_cot, large_cot, live_counts, master, first_moment, second_moment):
    weights = master.astype(jnp.bfloat16).astype(jnp.float32)
    groups = 2 * N_DP
    slots = jnp.arange(SLOTS, dtype=jnp.int32)
    live = (slots[None, None, :] < live_counts[:, :, None]).astype(jnp.float32).reshape(groups, SLOTS, 1, 1)
    small = small_tokens.astype(jnp.float32).reshape(groups, SLOTS, TOK_S, DS)
    large = jnp.flip(large_tokens, 0).astype(jnp.float32).reshape(groups, SLOTS, TOK_L, DL)
    small_back = small_cot.astype(jnp.float32).reshape(groups, SLOTS, TOK_S, DS) * live
    large_back = jnp.flip(large_cot, 0).astype(jnp.float32).reshape(groups, SLOTS, TOK_L, DL) * live

    def advance(total, item):
        small_item, large_item, small_seed, large_seed = item
        outputs, pullback = jax.vjp(layer, weights, small_item, large_item)
        weight_grads, small_input, large_input = pullback((small_seed, large_seed))
        return (total + weight_grads, (outputs[0].astype(jnp.bfloat16), outputs[1].astype(jnp.bfloat16), small_input.astype(jnp.bfloat16), large_input.astype(jnp.bfloat16)))
    total, (small_out, large_out, small_in, large_in) = lax.scan(advance, jnp.zeros((PARAMS,), jnp.float32), (small, large, small_back, large_back))
    small_out = small_out.reshape(2, CROPS, TOK_S, DS)
    large_out = jnp.flip(large_out.reshape(2, CROPS, TOK_L, DL), 0)
    small_in = small_in.reshape(2, CROPS, TOK_S, DS)
    large_in = jnp.flip(large_in.reshape(2, CROPS, TOK_L, DL), 0)
    grad_norm = jnp.sqrt(jnp.sum(total * total))
    clipped = total * jnp.minimum(1.0, clip_norm / grad_norm)
    new_first = beta_one * first_moment + (1.0 - beta_one) * clipped
    new_second = beta_two * second_moment + (1.0 - beta_two) * clipped * clipped
    new_master = master - rate * (new_first / bias_one / (jnp.sqrt(new_second / bias_two) + adam_eps) + decay * master)
    return (small_out, large_out, small_in, large_in, grad_norm, new_first, new_second, new_master, new_master.astype(jnp.bfloat16))
```

```python
import functools
import math

import jax
import jax.numpy as jnp
import numpy as np
from jax import lax
from jax.experimental import pallas as pl
from jax.experimental.pallas import tpu as pltpu
from jax.sharding import PartitionSpec as P

DS = 192
DL = 384
MS = 768
ML = 1536
HEADS = 6

norm_eps = 1e-06
clip_norm = 1.0
beta_one = 0.5
beta_two = 0.5
adam_eps = 1e-08
rate = 0.05
decay = 0.05
bias_one = 1.0 - 0.5**5
bias_two = 1.0 - 0.5**5

f32 = jnp.float32
bf16 = jnp.bfloat16
LANES = 128


def layout():
    shapes = []
    for label, width, hidden in (("s", DS, MS), ("l", DL, ML)):
        shapes += [
            (label + "_ln1", (2, width)),
            (label + "_qkv_w", (width, 3 * width)),
            (label + "_qkv_b", (3 * width,)),
            (label + "_proj_w", (width, width)),
            (label + "_proj_b", (width,)),
            (label + "_ln2", (2, width)),
            (label + "_fc1_w", (width, hidden)),
            (label + "_fc1_b", (hidden,)),
            (label + "_fc2_w", (hidden, width)),
            (label + "_fc2_b", (width,)),
        ]
    for label, owner, other in (("s", DS, DL), ("l", DL, DS)):
        shapes += [
            (label + "_to_ln", (2, owner)),
            (label + "_to_w", (owner, other)),
            (label + "_to_b", (other,)),
            (label + "_ca_ln", (2, other)),
            (label + "_ca_q_w", (other, other)),
            (label + "_ca_q_b", (other,)),
            (label + "_ca_k_w", (other, other)),
            (label + "_ca_v_w", (other, other)),
            (label + "_ca_v_b", (other,)),
            (label + "_ca_o_w", (other, other)),
            (label + "_ca_o_b", (other,)),
            (label + "_back_ln", (2, other)),
            (label + "_back_w", (other, owner)),
            (label + "_back_b", (owner,)),
        ]
    return shapes


def round_up(value, unit):
    return -(-value // unit) * unit


def grid_plan(shards):
    names = []
    regions = []
    offset = 0
    for label, shape in layout():
        count = math.prod(shape)
        phase = offset % LANES
        if not regions or regions[-1][2] != phase:
            regions.append([offset, offset, phase])
        names.append((label, shape, offset, len(regions) - 1))
        offset += count
        regions[-1][1] = offset
    total = offset
    starts = []
    row = 0
    for first, last, phase in regions:
        starts.append(row)
        row += -(-(last - first) // LANES)
    rows = row
    places = {}
    for label, shape, place, region in names:
        places[label] = (starts[region] + (place - regions[region][0]) // LANES, shape)
    size = total // shards
    bases = []
    pieces = []
    for device in range(shards):
        low, high = device * size, (device + 1) * size
        own = []
        base = None
        for (first, last, phase), start in zip(regions, starts):
            left, right = max(low, first), min(high, last)
            if left >= right:
                continue
            if base is None:
                base = (start + (left - first) // LANES) // 16 * 16
            delta = start * LANES - first + low - base * LANES
            own.append((left - low, right - low, delta))
        bases.append(base)
        pieces.append(own)
    most = max(len(own) for own in pieces)
    table = np.zeros((shards, most * 3), np.int32)
    need = 0
    for device, own in enumerate(pieces):
        for number, (left, right, delta) in enumerate(own):
            table[device, 3 * number : 3 * number + 3] = (left, right, delta)
            need = max(need, right + delta)
    span = round_up(-(-need // LANES), 16)
    overlap = 16
    for device in range(1, shards):
        overlap = max(overlap, bases[device - 1] + span - bases[device])
    return dict(
        places=places,
        rows=rows,
        size=size,
        bases=bases,
        table=table,
        most=most,
        span=span,
        overlap=overlap,
        height=round_up(max(bases) + span + overlap, 16),
        shard_rows=round_up(-(-size // LANES), 16),
    )


def mm(left, right):
    return lax.dot_general(left, right, (((1,), (0,)), ((), ())), preferred_element_type=f32)


def mm_t(left, right):
    return lax.dot_general(left, right, (((1,), (1,)), ((), ())), preferred_element_type=f32)


def t_mm(left, right):
    return lax.dot_general(left, right, (((0,), (0,)), ((), ())), preferred_element_type=f32)


def vmem_spec(shape, index):
    return pl.BlockSpec(shape, index)


def whole(shape):
    rank = len(shape)
    return pl.BlockSpec(shape, lambda *_: (0,) * rank, pipeline_mode=pl.Buffered(1))


def estimate(flops, moved):
    return pl.CostEstimate(flops=int(flops), bytes_accessed=int(moved), transcendentals=0)


def shift_rows(ref, amount, rows, margin):
    down = amount // LANES
    across = amount - down * LANES
    here = ref[pl.ds(margin - down, rows), :]
    above = ref[pl.ds(margin - down - 1, rows), :]
    here = pltpu.roll(here, across, 1)
    above = pltpu.roll(above, across, 1)
    lane = lax.broadcasted_iota(jnp.int32, here.shape, 1)
    return jnp.where(lane < across, above, here)


def align_kernel(most, rows, span, margin, table_ref, shard_ref, out_ref, padded):
    padded[...] = jnp.zeros_like(padded)
    padded[margin : margin + rows, :] = shard_ref[...]
    place = lax.broadcasted_iota(jnp.int32, (span, LANES), 0) * LANES
    place = place + lax.broadcasted_iota(jnp.int32, (span, LANES), 1)
    total = jnp.zeros((span, LANES), f32)
    for number in range(most):
        left = table_ref[3 * number]
        right = table_ref[3 * number + 1]
        delta = table_ref[3 * number + 2]
        moved = shift_rows(padded, delta, span, margin)
        total = jnp.where((place >= left + delta) & (place < right + delta), moved, total)
    out_ref[...] = total.astype(bf16)


def unalign_kernel(most, rows, span, margin, table_ref, grid_ref, out_ref, norm_ref, padded):
    padded[...] = jnp.zeros_like(padded)
    padded[0:span, :] = grid_ref[...]
    place = lax.broadcasted_iota(jnp.int32, (rows, LANES), 0) * LANES
    place = place + lax.broadcasted_iota(jnp.int32, (rows, LANES), 1)
    total = jnp.zeros((rows, LANES), f32)
    lane = lax.broadcasted_iota(jnp.int32, (rows, LANES), 1)
    for number in range(most):
        left = table_ref[3 * number]
        right = table_ref[3 * number + 1]
        delta = table_ref[3 * number + 2]
        down = delta // LANES
        across = delta - down * LANES
        back = lax.rem(LANES - across, LANES)
        here = pltpu.roll(padded[pl.ds(down, rows), :], back, 1)
        below = pltpu.roll(padded[pl.ds(down + 1, rows), :], back, 1)
        moved = jnp.where(lane < LANES - across, here, below)
        total = jnp.where((place >= left) & (place < right), moved, total)
    out_ref[...] = total
    norm_ref[...] = jnp.broadcast_to(jnp.sum(total * total).reshape(1, 1), (8, LANES))


def align(shard, table, plan):
    rows, span, most = plan["shard_rows"], plan["span"], plan["most"]
    margin = 8 + round_up(int(plan["table"].max(initial=0, where=pick_delta(plan))) // LANES + 1, 8)
    tall = margin + max(rows, span) + 8
    return pl.pallas_call(
        functools.partial(align_kernel, most, rows, span, margin),
        out_shape=jax.ShapeDtypeStruct((span, LANES), bf16),
        in_specs=[
            pl.BlockSpec(memory_space=pltpu.SMEM),
            pl.BlockSpec(memory_space=pltpu.VMEM),
        ],
        out_specs=pl.BlockSpec(memory_space=pltpu.VMEM),
        scratch_shapes=[pltpu.VMEM((tall, LANES), f32)],
        name="align",
    )(table, shard)


def unalign(grid, table, plan):
    rows, span, most = plan["shard_rows"], plan["span"], plan["most"]
    margin = 16 + round_up(int(plan["table"].max(initial=0, where=pick_delta(plan))) // LANES + 1, 8)
    tall = max(rows, span) + margin
    return pl.pallas_call(
        functools.partial(unalign_kernel, most, rows, span, margin),
        out_shape=(
            jax.ShapeDtypeStruct((rows, LANES), f32),
            jax.ShapeDtypeStruct((8, LANES), f32),
        ),
        in_specs=[
            pl.BlockSpec(memory_space=pltpu.SMEM),
            pl.BlockSpec(memory_space=pltpu.VMEM),
        ],
        out_specs=(
            pl.BlockSpec(memory_space=pltpu.VMEM),
            pl.BlockSpec(memory_space=pltpu.VMEM),
        ),
        scratch_shapes=[pltpu.VMEM((tall, LANES), f32)],
        name="unalign",
    )(table, grid)


def pick_delta(plan):
    mask = np.zeros(plan["table"].shape, bool)
    mask[:, 2::3] = True
    return mask


def two_dim(shape):
    return shape if len(shape) == 2 else (1, shape[0])


def is_matrix(label):
    return label[-2:] == "_w"


def strided(start, count, step):
    return pl.ds(start, count) if step == 1 or count == 1 else pl.ds(start, count, stride=step)


def half_swap(value):
    return pltpu.roll(value, LANES // 2, 1)


def read_param(flat, row, shape, out_ref, pair_ref):
    depth, width = two_dim(shape)
    dtype = out_ref.dtype
    if width % LANES == 0:
        step = width // LANES
        for col in range(step):
            out_ref[:, col * LANES : (col + 1) * LANES] = flat[
                strided(row + col, depth, step), :
            ].astype(dtype)
        return
    half = LANES // 2
    lead = width // LANES
    if depth == 1:
        for col in range(lead):
            out_ref[:, col * LANES : (col + 1) * LANES] = flat[row + col : row + col + 1, :].astype(
                dtype
            )
        out_ref[:, lead * LANES :] = flat[row + lead : row + lead + 1, 0:half].astype(dtype)
        return
    step = 2 * width // LANES
    pairs = depth // 2
    lane = lax.broadcasted_iota(jnp.int32, (pairs, LANES), 1)
    blocks = [flat[strided(row + col, pairs, step), :] for col in range(step)]
    turned = [half_swap(block) for block in blocks[lead:]]
    for col in range(lead):
        pair_ref[col, strided(0, pairs, 2), :] = blocks[col]
        pair_ref[col, strided(1, pairs, 2), :] = jnp.where(lane < half, turned[col], turned[col + 1])
    pair_ref[lead, strided(0, pairs, 2), :] = blocks[lead]
    pair_ref[lead, strided(1, pairs, 2), :] = turned[lead]
    for col in range(lead):
        out_ref[:, col * LANES : (col + 1) * LANES] = pair_ref[col, 0:depth, :].astype(dtype)
    out_ref[:, lead * LANES :] = pair_ref[lead, 0:depth, 0:half].astype(dtype)


def write_param(flat, row, shape, in_ref, pair_ref):
    depth, width = two_dim(shape)
    if width % LANES == 0:
        step = width // LANES
        for col in range(step):
            flat[strided(row + col, depth, step), :] = in_ref[:, col * LANES : (col + 1) * LANES]
        return
    half = LANES // 2
    lead = width // LANES
    if depth == 1:
        for col in range(lead):
            flat[row + col : row + col + 1, :] = in_ref[:, col * LANES : (col + 1) * LANES]
        tail = jnp.concatenate([in_ref[:, lead * LANES :], jnp.zeros((1, half), f32)], 1)
        flat[row + lead : row + lead + 1, :] = tail
        return
    step = 2 * width // LANES
    pairs = depth // 2
    lane = lax.broadcasted_iota(jnp.int32, (pairs, LANES), 1)
    for col in range(lead):
        pair_ref[col, 0:depth, :] = in_ref[:, col * LANES : (col + 1) * LANES]
    pair_ref[lead, 0:depth, 0:half] = in_ref[:, lead * LANES :]
    even = [pair_ref[col, strided(0, pairs, 2), :] for col in range(lead + 1)]
    odd = [half_swap(pair_ref[col, strided(1, pairs, 2), :]) for col in range(lead + 1)]
    for col in range(lead):
        flat[strided(row + col, pairs, step), :] = even[col]
    flat[strided(row + lead, pairs, step), :] = jnp.where(lane < half, even[lead], odd[0])
    for col in range(lead):
        flat[strided(row + lead + 1 + col, pairs, step), :] = jnp.where(
            lane < half, odd[col], odd[col + 1]
        )


def unflatten_kernel(plan, shards, base_ref, grid_ref, *refs):
    outs, (flat, pair_ref) = refs[:-2], refs[-2:]
    span, overlap = plan["span"], plan["overlap"]
    flat[0:overlap, :] = jnp.zeros((overlap, LANES), f32)

    def place(device, carry):
        base = pl.multiple_of(base_ref[device], 16)
        head = flat[pl.ds(base, overlap), :]
        flat[pl.ds(base, span), :] = grid_ref[device].astype(f32)
        flat[pl.ds(base, overlap), :] += head
        flat[pl.ds(base + span, overlap), :] = jnp.zeros((overlap, LANES), f32)
        return carry

    lax.fori_loop(0, shards, place, 0)
    for (label, shape), out_ref in zip(layout(), outs):
        read_param(flat, plan["places"][label][0], shape, out_ref, pair_ref)


def unflatten(grid, plan, shards):
    outs = []
    for label, shape in layout():
        outs.append(jax.ShapeDtypeStruct(two_dim(shape), bf16 if is_matrix(label) else f32))
    vmem = pl.BlockSpec(memory_space=pltpu.VMEM)
    values = pl.pallas_call(
        functools.partial(unflatten_kernel, plan, shards),
        out_shape=outs,
        in_specs=[pl.BlockSpec(memory_space=pltpu.SMEM), vmem],
        out_specs=[vmem] * len(outs),
        scratch_shapes=[
            pltpu.VMEM((plan["height"], LANES), f32),
            pltpu.VMEM((5, MS, LANES), f32),
        ],
        name="unflatten",
    )(jnp.asarray(plan["bases"], jnp.int32), grid)
    return {label: value for (label, shape), value in zip(layout(), values)}


def flatten_kernel(plan, shards, base_ref, *refs):
    count = len(layout())
    grads, out_ref, flat, pair_ref = refs[:count], refs[count], refs[count + 1], refs[count + 2]
    span, rows = plan["span"], plan["rows"]
    tail = rows // 8 * 8
    flat[tail:, :] = jnp.zeros((plan["height"] - tail, LANES), f32)
    for (label, shape), ref in zip(layout(), grads):
        write_param(flat, plan["places"][label][0], shape, ref, pair_ref)

    def place(device, carry):
        base = pl.multiple_of(base_ref[device], 16)
        out_ref[device] = flat[pl.ds(base, span), :].astype(bf16)
        return carry

    lax.fori_loop(0, shards, place, 0)


def flatten(grads, plan, shards):
    vmem = pl.BlockSpec(memory_space=pltpu.VMEM)
    return pl.pallas_call(
        functools.partial(flatten_kernel, plan, shards),
        out_shape=jax.ShapeDtypeStruct((shards, plan["span"], LANES), bf16),
        in_specs=[pl.BlockSpec(memory_space=pltpu.SMEM)] + [vmem] * len(layout()),
        out_specs=vmem,
        scratch_shapes=[
            pltpu.VMEM((plan["height"], LANES), f32),
            pltpu.VMEM((5, MS, LANES), f32),
        ],
        name="flatten",
    )(jnp.asarray(plan["bases"], jnp.int32), *[grads[label] for label, shape in layout()])


def ln_parts(value):
    mean = jnp.mean(value, -1, keepdims=True)
    centred = value - mean
    variance = jnp.mean(centred * centred, -1, keepdims=True)
    inverse = lax.rsqrt(variance + norm_eps)
    return centred * inverse, inverse


def ln_back(grad, hat, inverse, gain):
    scaled = grad * gain
    first = jnp.mean(scaled, -1, keepdims=True)
    second = jnp.mean(scaled * hat, -1, keepdims=True)
    return inverse * (scaled - first - hat * second)


def gelu_parts(value):
    cdf = 0.5 + 0.5 * lax.erf(value * (2.0**-0.5))
    density = jnp.exp(value * value * -0.5) * (1.0 / math.sqrt(2.0 * math.pi))
    return value * cdf, cdf + value * density


def col_sum(value):
    return jnp.sum(value, 0, keepdims=True)


def groups(width):
    size = width // HEADS
    found = []
    for start in range(0, width, LANES):
        stop = min(start + LANES, width)
        found.append((start, stop, (stop - start) // size))
    return found, size


def stack_heads(value, count, size):
    lane = lax.broadcasted_iota(jnp.int32, value.shape, 1)
    zero = jnp.zeros_like(value)
    return jnp.concatenate(
        [
            jnp.where((lane >= head * size) & (lane < (head + 1) * size), value, zero)
            for head in range(count)
        ],
        0,
    )


def merge_heads(value, count, size):
    rows = value.shape[0] // count
    lane = lax.broadcasted_iota(jnp.int32, (rows, value.shape[1]), 1)
    merged = value[0:rows]
    for head in range(1, count):
        merged = jnp.where(lane >= head * size, value[head * rows : (head + 1) * rows], merged)
    return merged


def forward_kernel(
    pair,
    length,
    tall,
    chunk,
    tok_ref,
    ln1_ref,
    qkv_w,
    qkv_b,
    proj_w,
    proj_b,
    ln2_ref,
    fc1_w,
    fc1_b,
    fc2_w,
    fc2_b,
    to_ln,
    to_w,
    to_b,
    a1_ref,
    qkv_ref,
    probs_ref,
    att_ref,
    mid_ref,
    n2_ref,
    z_ref,
    slope_ref,
    y_ref,
    sent_ref,
    head_ref,
):
    step = pl.program_id(0)
    rows = pair * tall
    width = tok_ref.shape[-1]
    hidden = fc1_w.shape[1]
    found, size = groups(width)
    scale = size ** (-0.5)
    tokens = tok_ref[...].reshape(rows, width).astype(f32)
    hat, _ = ln_parts(tokens)
    a1 = (hat * ln1_ref[0:1, :] + ln1_ref[1:2, :]).astype(bf16)
    a1_ref[...] = a1
    qkv_ref[...] = (mm(a1, qkv_w[...]) + qkv_b[...]).astype(bf16)
    key_lane = lax.broadcasted_iota(jnp.int32, (1, tall), 1)
    bias = jnp.where(key_lane < length, 0.0, -1e30).astype(f32)
    for crop in range(pair):
        here = slice(crop * tall, (crop + 1) * tall)
        for start, stop, count in found:
            query = stack_heads(qkv_ref[here, start:stop], count, size)
            key = qkv_ref[here, width + start : width + stop]
            value = qkv_ref[here, 2 * width + start : 2 * width + stop]
            scores = mm_t(query, key) * scale + bias
            summit = jnp.max(scores, -1, keepdims=True)
            weights = jnp.exp(scores - summit)
            probs = (weights / jnp.sum(weights, -1, keepdims=True)).astype(bf16)
            first = start // size
            for head in range(count):
                probs_ref[crop, first + head] = probs[head * tall : (head + 1) * tall]
            att_ref[here, start:stop] = merge_heads(mm(probs, value), count, size).astype(bf16)
    mid = tokens + mm(att_ref[...], proj_w[...]) + proj_b[...]
    mid_ref[...] = mid
    hat, _ = ln_parts(mid)
    n2_ref[...] = (hat * ln2_ref[0:1, :] + ln2_ref[1:2, :]).astype(bf16)
    y_ref[...] = mid + fc2_b[...]
    for number in range(hidden // chunk):
        cols = slice(number * chunk, (number + 1) * chunk)
        inner = mm(n2_ref[...], fc1_w[:, cols]) + fc1_b[:, cols]
        active, slope = gelu_parts(inner)
        z_ref[:, cols] = active.astype(bf16)
        slope_ref[:, cols] = slope.astype(bf16)
        y_ref[...] += mm(z_ref[:, cols], fc2_w[cols, :])
    for crop in range(pair):
        head_ref[pl.ds(step * pair + crop, 1), :] = y_ref[crop * tall : crop * tall + 1, :]

    @pl.when(step == pl.num_programs(0) - 1)
    def _():
        hat, _ = ln_parts(head_ref[...])
        active, _ = gelu_parts(hat * to_ln[0:1, :] + to_ln[1:2, :])
        sent_ref[...] = (mm(active.astype(bf16), to_w[...]) + to_b[...]).astype(bf16)


def block_forward(tokens, params, label, length, pair):
    crops, tall, width = tokens.shape
    hidden = params[label + "_fc1_w"].shape[1]
    other = params[label + "_to_w"].shape[1]
    rows = pair * tall
    names = ("ln1", "qkv_w", "qkv_b", "proj_w", "proj_b", "ln2", "fc1_w", "fc1_b", "fc2_w", "fc2_b")
    names = names + ("to_ln", "to_w", "to_b")
    weights = [params[label + "_" + name] for name in names]
    flat = crops * tall

    def by_rows(cols):
        return pl.BlockSpec((rows, cols), lambda i: (i, 0))

    outs = [
        (by_rows(width), jax.ShapeDtypeStruct((flat, width), bf16)),
        (by_rows(3 * width), jax.ShapeDtypeStruct((flat, 3 * width), bf16)),
        (
            pl.BlockSpec((pair, HEADS, tall, tall), lambda i: (i, 0, 0, 0)),
            jax.ShapeDtypeStruct((crops, HEADS, tall, tall), bf16),
        ),
        (by_rows(width), jax.ShapeDtypeStruct((flat, width), bf16)),
        (by_rows(width), jax.ShapeDtypeStruct((flat, width), f32)),
        (by_rows(width), jax.ShapeDtypeStruct((flat, width), bf16)),
        (by_rows(hidden), jax.ShapeDtypeStruct((flat, hidden), bf16)),
        (by_rows(hidden), jax.ShapeDtypeStruct((flat, hidden), bf16)),
        (by_rows(width), jax.ShapeDtypeStruct((flat, width), f32)),
        (
            pl.BlockSpec((crops, other), lambda i: (0, 0)),
            jax.ShapeDtypeStruct((crops, other), bf16),
        ),
        (
            pl.BlockSpec((crops, width), lambda i: (0, 0)),
            jax.ShapeDtypeStruct((crops, width), f32),
        ),
    ]
    flops = 2 * flat * (4 * width * width + 2 * width * hidden)
    return pl.pallas_call(
        functools.partial(forward_kernel, pair, length, tall, 384),
        grid=(crops // pair,),
        out_shape=[shape for spec, shape in outs],
        in_specs=[pl.BlockSpec((pair, tall, width), lambda i: (i, 0, 0))]
        + [whole(value.shape) for value in weights],
        out_specs=[spec for spec, shape in outs],
        cost_estimate=estimate(flops, 20_000_000),
        name="forward_" + label,
    )(tokens, *weights)


def cross_kernel(
    length,
    tall,
    crops,
    sent_ref,
    y_ref,
    gret_ref,
    ca_ln,
    q_w,
    q_b,
    k_w,
    v_w,
    v_b,
    o_w,
    o_b,
    back_ln,
    back_w,
    back_b,
    returned_ref,
    gsent_ref,
    gj_ref,
    d_ca_ln,
    d_q_w,
    d_q_b,
    d_k_w,
    d_v_w,
    d_v_b,
    d_o_w,
    d_o_b,
    d_back_ln,
    d_back_w,
    d_back_b,
    sent_f,
    n_all,
    k_all,
    v_all,
    gk_all,
    gv_all,
    query_all,
    probs_all,
    att_all,
    gatt_all,
    gq_all,
    gn_head,
    gj_head,
):
    width = y_ref.shape[1]
    size = width // HEADS
    scale = size ** (-0.5)
    lane = lax.broadcasted_iota(jnp.int32, (8, width), 1)
    head = lax.broadcasted_iota(jnp.int32, (8, width), 0)
    own_head = (lane >= head * size) & (lane < (head + 1) * size)
    row = lax.broadcasted_iota(jnp.int32, (tall, 1), 0)
    key_lane = lax.broadcasted_iota(jnp.int32, (1, tall), 1)
    bias = jnp.where(key_lane < length, 0.0, -1e30).astype(f32)
    gain, shift = ca_ln[0:1, :], ca_ln[1:2, :]
    sent_f[...] = sent_ref[...].astype(f32)
    hat, _ = ln_parts(sent_f[...])
    n_head = (hat * gain + shift).astype(bf16)
    query_all[...] = (mm(n_head, q_w[...]) + q_b[...]).astype(bf16).astype(f32)

    def joined(crop):
        here = pl.ds(pl.multiple_of(crop * tall, 16), tall)
        return here, jnp.where(row == 0, sent_f[pl.ds(crop, 1), :], y_ref[here, :])

    def spread(ref, crop):
        return jnp.where(own_head, ref[pl.ds(crop, 1), :], 0.0).astype(bf16)

    def ahead(crop, carry):
        here, value = joined(crop)
        hat, _ = ln_parts(value)
        normed = (hat * gain + shift).astype(bf16)
        n_all[here, :] = normed
        key = mm(normed, k_w[...]).astype(bf16)
        k_all[here, :] = key
        vals = (mm(normed, v_w[...]) + v_b[...]).astype(bf16)
        v_all[here, :] = vals
        scores = mm_t(spread(query_all, crop), key) * scale + bias
        summit = jnp.max(scores, -1, keepdims=True)
        weights = jnp.exp(scores - summit)
        probs = weights / jnp.sum(weights, -1, keepdims=True)
        probs_all[crop] = probs
        mixed = jnp.where(own_head, mm(probs.astype(bf16), vals), 0.0)
        att_all[pl.ds(crop, 1), :] = col_sum(mixed)
        return carry

    lax.fori_loop(0, crops, ahead, 0)
    attended = att_all[...].astype(bf16)
    merged = sent_f[...] + mm(attended, o_w[...]) + o_b[...]
    hat, inverse = ln_parts(merged)
    active, slope = gelu_parts(hat * back_ln[0:1, :] + back_ln[1:2, :])
    active = active.astype(bf16)
    returned_ref[...] = (mm(active, back_w[...]) + back_b[...]).astype(bf16)
    gret = gret_ref[...]
    d_back_w[...] = t_mm(active, gret)
    d_back_b[...] = col_sum(gret.astype(f32))
    gact = mm_t(gret, back_w[...]) * slope
    d_back_ln[0:1, :] = col_sum(gact * hat)
    d_back_ln[1:2, :] = col_sum(gact)
    gfused = ln_back(gact, hat, inverse, back_ln[0:1, :])
    gfo = gfused.astype(bf16)
    d_o_w[...] = t_mm(attended, gfo)
    d_o_b[...] = col_sum(gfo.astype(f32))
    gatt_all[...] = mm_t(gfo, o_w[...]).astype(bf16).astype(f32)

    def behind(crop, carry):
        here = pl.ds(pl.multiple_of(crop * tall, 16), tall)
        probs = probs_all[crop]
        gatt = spread(gatt_all, crop)
        gprobs = mm_t(gatt, v_all[here, :])
        gv_all[here, :] = t_mm(probs.astype(bf16), gatt).astype(bf16)
        inner = gprobs - jnp.sum(gprobs * probs, -1, keepdims=True)
        gscores = (probs * inner).astype(bf16)
        gq = jnp.where(own_head, mm(gscores, k_all[here, :]), 0.0)
        gq_all[pl.ds(crop, 1), :] = col_sum(gq) * scale
        gk_all[here, :] = (t_mm(gscores, spread(query_all, crop)) * scale).astype(bf16)
        return carry

    lax.fori_loop(0, crops, behind, 0)
    gq = gq_all[...].astype(bf16)
    d_q_w[...] = t_mm(n_head, gq)
    d_q_b[...] = col_sum(gq.astype(f32))
    gn_head[...] = mm_t(gq, q_w[...])
    d_ca_ln[...] = jnp.zeros_like(d_ca_ln)
    d_v_b[...] = jnp.zeros_like(d_v_b)
    d_k_w[...] = jnp.zeros_like(d_k_w)
    d_v_w[...] = jnp.zeros_like(d_v_w)

    def finish(crop, carry):
        here, value = joined(crop)
        hat, inverse = ln_parts(value)
        gk, gv = gk_all[here, :], gv_all[here, :]
        gn = mm_t(gk, k_w[...]) + mm_t(gv, v_w[...])
        gn = gn + jnp.where(row == 0, gn_head[pl.ds(crop, 1), :], 0.0)
        d_ca_ln[0:1, :] += col_sum(gn * hat)
        d_ca_ln[1:2, :] += col_sum(gn)
        gj = ln_back(gn, hat, inverse, gain)
        gj_ref[here, :] = gj
        gj_head[pl.ds(crop, 1), :] = gj[0:1, :]
        d_v_b[...] += col_sum(gv.astype(f32))
        return carry

    lax.fori_loop(0, crops, finish, 0)
    gsent_ref[...] = (gj_head[...] + gfused).astype(bf16)

    def weights_of(pair, carry):
        here = pl.ds(pl.multiple_of(pair * 2 * tall, 32), 2 * tall)
        normed = n_all[here, :]
        d_k_w[...] += t_mm(normed, gk_all[here, :])
        d_v_w[...] += t_mm(normed, gv_all[here, :])
        return carry

    lax.fori_loop(0, crops // 2, weights_of, 0)


def cross(sent, hosted, gret, params, label, length, tall):
    crops, width = sent.shape
    own = gret.shape[1]
    flat = crops * tall
    names = ("ca_ln", "ca_q_w", "ca_q_b", "ca_k_w", "ca_v_w", "ca_v_b", "ca_o_w", "ca_o_b")
    names = names + ("back_ln", "back_w", "back_b")
    weights = [params[label + "_" + name] for name in names]
    outs = [
        jax.ShapeDtypeStruct((crops, own), bf16),
        jax.ShapeDtypeStruct((crops, width), bf16),
        jax.ShapeDtypeStruct((flat, width), f32),
    ] + [jax.ShapeDtypeStruct(value.shape, f32) for value in weights]
    vmem = pl.BlockSpec(memory_space=pltpu.VMEM)
    small = pltpu.VMEM((crops, width), f32)
    big = pltpu.VMEM((flat, width), bf16)
    values = pl.pallas_call(
        functools.partial(cross_kernel, length, tall, crops),
        out_shape=outs,
        in_specs=[vmem] * (3 + len(weights)),
        out_specs=[vmem] * len(outs),
        scratch_shapes=[small]
        + [big] * 5
        + [small, pltpu.VMEM((crops, 8, tall), f32)]
        + [small] * 5,
        cost_estimate=estimate(2 * flat * width * width * 6, 8_000_000),
        name="cross_" + label,
    )(sent, hosted, gret, *weights)
    grads = {label + "_" + name: value for name, value in zip(names, values[3:])}
    return values[0], values[1], values[2], grads


def backward_kernel(
    pair,
    length,
    tall,
    chunk,
    live_ref,
    tok_ref,
    cot_ref,
    y_ref,
    gj_ref,
    a1_ref,
    qkv_ref,
    probs_ref,
    att_ref,
    mid_ref,
    n2_ref,
    z_ref,
    slope_ref,
    headrow_ref,
    gsent_ref,
    returned_ref,
    ln1_ref,
    qkv_w,
    proj_w,
    ln2_ref,
    fc1_w,
    fc2_w,
    to_ln,
    to_w,
    out_ref,
    gtok_ref,
    d_ln1,
    d_qkv_w,
    d_qkv_b,
    d_proj_w,
    d_proj_b,
    d_ln2,
    d_fc1_w,
    d_fc1_b,
    d_fc2_w,
    d_fc2_b,
    d_to_ln,
    d_to_w,
    d_to_b,
    ghead,
    gy,
    gnormed,
    gqkv,
    gatt_ref,
):
    step = pl.program_id(0)
    rows = pair * tall
    width = tok_ref.shape[-1]
    hidden = fc1_w.shape[1]
    found, size = groups(width)
    scale = size ** (-0.5)

    @pl.when(step == 0)
    def _():
        hat, inverse = ln_parts(headrow_ref[...])
        active, slope = gelu_parts(hat * to_ln[0:1, :] + to_ln[1:2, :])
        gsent = gsent_ref[...]
        d_to_w[...] = t_mm(active.astype(bf16), gsent)
        d_to_b[...] = col_sum(gsent.astype(f32))
        gact = mm_t(gsent, to_w[...]) * slope
        d_to_ln[0:1, :] = col_sum(gact * hat)
        d_to_ln[1:2, :] = col_sum(gact)
        ghead[...] = ln_back(gact, hat, inverse, to_ln[0:1, :])
        for ref in (d_ln1, d_qkv_w, d_qkv_b, d_proj_w, d_proj_b, d_ln2):
            ref[...] = jnp.zeros_like(ref)
        for ref in (d_fc1_w, d_fc1_b, d_fc2_w, d_fc2_b):
            ref[...] = jnp.zeros_like(ref)

    row = lax.broadcasted_iota(jnp.int32, (tall, 1), 0)
    for crop in range(pair):
        here = slice(crop * tall, (crop + 1) * tall)
        slot = step * pair + crop
        live = jnp.where(slot < live_ref[0], 1.0, 0.0).astype(f32)
        seed = cot_ref[crop].astype(f32) * live + gj_ref[here, :]
        gy[here, :] = jnp.where(row == 0, ghead[pl.ds(slot, 1), :], seed)
        home = returned_ref[pl.ds(slot, 1), :]
        final = jnp.where(row == 0, home, y_ref[here, :])
        out_ref[0, crop] = final[0:length].astype(bf16)
    gm = gy[...].astype(bf16)
    d_fc2_b[...] += col_sum(gm.astype(f32))
    for number in range(hidden // chunk):
        cols = slice(number * chunk, (number + 1) * chunk)
        d_fc2_w[cols, :] += t_mm(z_ref[:, cols], gm)
        gu = slope_ref[:, cols].astype(f32) * mm_t(gm, fc2_w[cols, :])
        gu = gu.astype(bf16)
        d_fc1_w[:, cols] += t_mm(n2_ref[...], gu)
        d_fc1_b[:, cols] += col_sum(gu.astype(f32))
        part = mm_t(gu, fc1_w[:, cols])
        gnormed[...] = part if number == 0 else gnormed[...] + part
    hat, inverse = ln_parts(mid_ref[...])
    gn = gnormed[...]
    d_ln2[0:1, :] += col_sum(gn * hat)
    d_ln2[1:2, :] += col_sum(gn)
    gmid = gy[...] + ln_back(gn, hat, inverse, ln2_ref[0:1, :])
    gy[...] = gmid
    gp = gmid.astype(bf16)
    d_proj_w[...] += t_mm(att_ref[...], gp)
    d_proj_b[...] += col_sum(gp.astype(f32))
    gatt_ref[...] = mm_t(gp, proj_w[...]).astype(bf16)
    for crop in range(pair):
        here = slice(crop * tall, (crop + 1) * tall)
        for start, stop, count in found:
            first = start // size
            query = stack_heads(qkv_ref[here, start:stop], count, size)
            key = qkv_ref[here, width + start : width + stop]
            value = qkv_ref[here, 2 * width + start : 2 * width + stop]
            gatt = stack_heads(gatt_ref[here, start:stop], count, size)
            probs_low = jnp.concatenate([probs_ref[crop, first + head] for head in range(count)], 0)
            probs = probs_low.astype(f32)
            gprobs = mm_t(gatt, value)
            inner = gprobs - jnp.sum(gprobs * probs, -1, keepdims=True)
            gscores = (probs * inner).astype(bf16)
            gq = merge_heads(mm(gscores, key), count, size) * scale
            gk = t_mm(gscores, query) * scale
            gv = t_mm(probs_low, gatt)
            gqkv[here, start:stop] = gq.astype(bf16)
            gqkv[here, width + start : width + stop] = gk.astype(bf16)
            gqkv[here, 2 * width + start : 2 * width + stop] = gv.astype(bf16)
    grad = gqkv[...]
    d_qkv_w[...] += t_mm(a1_ref[...], grad)
    d_qkv_b[...] += col_sum(grad.astype(f32))
    gn = mm_t(grad, qkv_w[...])
    hat, inverse = ln_parts(tok_ref[...].reshape(rows, width).astype(f32))
    d_ln1[0:1, :] += col_sum(gn * hat)
    d_ln1[1:2, :] += col_sum(gn)
    gtok = gy[...] + ln_back(gn, hat, inverse, ln1_ref[0:1, :])
    for crop in range(pair):
        gtok_ref[0, crop] = gtok[crop * tall : crop * tall + length].astype(bf16)


def block_backward(tokens, cot, live, kept, gj, gsent, returned, params, label, length, pair):
    crops, tall, width = tokens.shape
    a1, qkv, probs, att, mid, n2, z, slope, y, headrow = kept
    hidden = params[label + "_fc1_w"].shape[1]
    rows = pair * tall
    flat = crops * tall
    names = ("ln1", "qkv_w", "proj_w", "ln2", "fc1_w", "fc2_w", "to_ln", "to_w")
    weights = [params[label + "_" + name] for name in names]

    def by_rows(cols):
        return pl.BlockSpec((rows, cols), lambda i: (i, 0))

    token_spec = pl.BlockSpec((pair, tall, width), lambda i: (i, 0, 0))
    out_spec = pl.BlockSpec((1, pair, length, width), lambda i: (0, i, 0, 0))
    grad_names = (
        "ln1",
        "qkv_w",
        "qkv_b",
        "proj_w",
        "proj_b",
        "ln2",
        "fc1_w",
        "fc1_b",
        "fc2_w",
        "fc2_b",
        "to_ln",
        "to_w",
        "to_b",
    )
    grad_shapes = [params[label + "_" + name].shape for name in grad_names]
    out_shape = jax.ShapeDtypeStruct((1, crops, length, width), bf16)
    returned = returned.astype(f32)
    values = pl.pallas_call(
        functools.partial(backward_kernel, pair, length, tall, 384),
        grid=(crops // pair,),
        out_shape=[out_shape, out_shape] + [jax.ShapeDtypeStruct(s, f32) for s in grad_shapes],
        in_specs=[
            pl.BlockSpec(memory_space=pltpu.SMEM),
            token_spec,
            token_spec,
            by_rows(width),
            by_rows(width),
            by_rows(width),
            by_rows(3 * width),
            pl.BlockSpec((pair, HEADS, tall, tall), lambda i: (i, 0, 0, 0)),
            by_rows(width),
            by_rows(width),
            by_rows(width),
            by_rows(hidden),
            by_rows(hidden),
            whole(headrow.shape),
            whole(gsent.shape),
            whole(returned.shape),
        ]
        + [whole(value.shape) for value in weights],
        out_specs=[out_spec, out_spec] + [pl.BlockSpec(s, lambda i: (0, 0)) for s in grad_shapes],
        scratch_shapes=[
            pltpu.VMEM((crops, width), f32),
            pltpu.VMEM((rows, width), f32),
            pltpu.VMEM((rows, width), f32),
            pltpu.VMEM((rows, 3 * width), bf16),
            pltpu.VMEM((rows, width), bf16),
        ],
        cost_estimate=estimate(4 * flat * (4 * width * width + 2 * width * hidden), 30_000_000),
        name="backward_" + label,
    )(
        live,
        tokens,
        cot,
        y,
        gj,
        a1,
        qkv,
        probs,
        att,
        mid,
        n2,
        z,
        slope,
        headrow,
        gsent,
        returned,
        *weights,
    )
    grads = {label + "_" + name: value for name, value in zip(grad_names, values[2:])}
    return values[0], values[1], grads


def swap(value):
    return lax.ppermute(value, "branch", [(0, 1), (1, 0)])


def partner(value, bit):
    count = lax.axis_size("dp")
    return lax.ppermute(value, "dp", [(i, i ^ bit) for i in range(count)])


def shards(
    small_tokens,
    large_tokens,
    small_cot,
    large_cot,
    live_counts,
    master,
    first_moment,
    second_moment,
):
    count = lax.axis_size("branch") * lax.axis_size("dp")
    plan = grid_plan(count)
    index = lax.axis_index(("branch", "dp"))
    size = master.shape[0]
    rows = plan["shard_rows"]
    table = lax.dynamic_index_in_dim(jnp.asarray(plan["table"]), index, 0, False)
    padded = jnp.pad(master, (0, rows * LANES - size)).reshape(rows, LANES)
    own = align(padded, table, plan)
    grid = lax.all_gather(own, ("branch", "dp"), axis=0, tiled=False)
    params = unflatten(grid, plan, count)

    half = lax.axis_index("branch")
    counts = live_counts[:, 0]
    own_count = lax.dynamic_slice_in_dim(counts, half, 1)
    far_count = lax.dynamic_slice_in_dim(counts, 1 - half, 1)
    crops, length_s = small_tokens.shape[1], small_tokens.shape[2]
    length_l = large_tokens.shape[2]
    tall_s, tall_l = round_up(length_s, 16), round_up(length_l, 16)
    pair = 2

    def taller(value, length, tall):
        return jnp.pad(value[0], ((0, 0), (0, tall - length), (0, 0)))

    small = taller(small_tokens, length_s, tall_s)
    large = taller(large_tokens, length_l, tall_l)
    small_seed = taller(small_cot, length_s, tall_s)
    large_seed = taller(large_cot, length_l, tall_l)
    slots = jnp.arange(crops, dtype=jnp.int32)[:, None]
    ret_small = jnp.where(slots < own_count, small_cot[0, :, 0], 0)
    ret_large = jnp.where(slots < far_count, large_cot[0, :, 0], 0)
    ret_small, ret_large = swap(ret_small), swap(ret_large)

    *kept_s, sent_s, head_s = block_forward(small, params, "s", length_s, pair)
    got_s = swap(sent_s)
    *kept_l, sent_l, head_l = block_forward(large, params, "l", length_l, pair)
    got_l = swap(sent_l)
    grads = {}
    back_s, gsent_s, gj_l, part = cross(got_s, kept_l[-1], ret_small, params, "s", length_l, tall_l)
    grads.update(part)
    home_s, own_s = swap(back_s), swap(gsent_s)
    back_l, gsent_l, gj_s, part = cross(got_l, kept_s[-1], ret_large, params, "l", length_s, tall_s)
    grads.update(part)
    home_l, own_l = swap(back_l), swap(gsent_l)
    small_out, small_grad, part = block_backward(
        small, small_seed, own_count, (*kept_s, head_s), gj_s, own_s, home_s, params, "s", length_s, pair
    )
    grads.update(part)
    large_out, large_grad, part = block_backward(
        large, large_seed, far_count, (*kept_l, head_l), gj_l, own_l, home_l, params, "l", length_l, pair
    )
    grads.update(part)

    flat = flatten(grads, plan, count)
    mine = lax.psum_scatter(flat, ("branch", "dp"), scatter_dimension=0, tiled=False)
    summed, square = unalign(mine.astype(f32), table, plan)
    square = square + swap(square)
    bit = 1
    while bit < lax.axis_size("dp"):
        square = square + partner(square, bit)
        bit *= 2
    grad_norm = jnp.sqrt(square[0, 0])
    own_grad = summed.reshape(-1)[:size]
    clipped = own_grad * jnp.minimum(1.0, clip_norm / grad_norm)
    new_first = beta_one * first_moment + (1.0 - beta_one) * clipped
    new_second = beta_two * second_moment + (1.0 - beta_two) * clipped * clipped
    new_master = master - rate * (
        new_first / bias_one / (jnp.sqrt(new_second / bias_two) + adam_eps) + decay * master
    )
    return (
        small_out,
        large_out,
        small_grad,
        large_grad,
        grad_norm,
        new_first,
        new_second,
        new_master,
        new_master.astype(bf16),
    )


def solution(mesh):
    return jax.shard_map(
        shards,
        mesh=mesh,
        in_specs=(
            P("branch", "dp", None, None),
            P("branch", "dp", None, None),
            P("branch", "dp", None, None),
            P("branch", "dp", None, None),
            P(None, "dp"),
            P(("branch", "dp")),
            P(("branch", "dp")),
            P(("branch", "dp")),
        ),
        out_specs=(
            P("branch", "dp", None, None),
            P("branch", "dp", None, None),
            P("branch", "dp", None, None),
            P("branch", "dp", None, None),
            P(),
            P(("branch", "dp")),
            P(("branch", "dp")),
            P(("branch", "dp")),
            P(("branch", "dp")),
        ),
        check_vma=False,
    )
```

```python
import functools
import math

import jax
import jax.numpy as jnp
import numpy as np
from jax import lax
from jax.experimental import pallas as pl
from jax.experimental.pallas import tpu as pltpu
from jax.sharding import PartitionSpec as P

DS = 192
DL = 384
MS = 768
ML = 1536
HEADS = 6

norm_eps = 1e-06
clip_norm = 1.0
beta_one = 0.5
beta_two = 0.5
adam_eps = 1e-08
rate = 0.05
decay = 0.05
bias_one = 1.0 - 0.5**5
bias_two = 1.0 - 0.5**5

f32 = jnp.float32
bf16 = jnp.bfloat16
LANES = 128


def layout():
    shapes = []
    for label, width, hidden in (("s", DS, MS), ("l", DL, ML)):
        shapes += [
            (label + "_ln1", (2, width)),
            (label + "_qkv_w", (width, 3 * width)),
            (label + "_qkv_b", (3 * width,)),
            (label + "_proj_w", (width, width)),
            (label + "_proj_b", (width,)),
            (label + "_ln2", (2, width)),
            (label + "_fc1_w", (width, hidden)),
            (label + "_fc1_b", (hidden,)),
            (label + "_fc2_w", (hidden, width)),
            (label + "_fc2_b", (width,)),
        ]
    for label, owner, other in (("s", DS, DL), ("l", DL, DS)):
        shapes += [
            (label + "_to_ln", (2, owner)),
            (label + "_to_w", (owner, other)),
            (label + "_to_b", (other,)),
            (label + "_ca_ln", (2, other)),
            (label + "_ca_q_w", (other, other)),
            (label + "_ca_q_b", (other,)),
            (label + "_ca_k_w", (other, other)),
            (label + "_ca_v_w", (other, other)),
            (label + "_ca_v_b", (other,)),
            (label + "_ca_o_w", (other, other)),
            (label + "_ca_o_b", (other,)),
            (label + "_back_ln", (2, other)),
            (label + "_back_w", (other, owner)),
            (label + "_back_b", (owner,)),
        ]
    return shapes


def round_up(value, unit):
    return -(-value // unit) * unit


def grid_plan(shards):
    names = []
    regions = []
    offset = 0
    for label, shape in layout():
        count = math.prod(shape)
        phase = offset % LANES
        if not regions or regions[-1][2] != phase:
            regions.append([offset, offset, phase])
        names.append((label, shape, offset, len(regions) - 1))
        offset += count
        regions[-1][1] = offset
    total = offset
    starts = []
    row = 0
    for first, last, phase in regions:
        starts.append(row)
        row += -(-(last - first) // LANES)
    rows = row
    places = {}
    for label, shape, place, region in names:
        places[label] = (starts[region] + (place - regions[region][0]) // LANES, shape)
    size = total // shards
    bases = []
    pieces = []
    for device in range(shards):
        low, high = device * size, (device + 1) * size
        own = []
        base = None
        for (first, last, phase), start in zip(regions, starts):
            left, right = max(low, first), min(high, last)
            if left >= right:
                continue
            if base is None:
                base = (start + (left - first) // LANES) // 16 * 16
            delta = start * LANES - first + low - base * LANES
            own.append((left - low, right - low, delta))
        bases.append(base)
        pieces.append(own)
    most = max(len(own) for own in pieces)
    table = np.zeros((shards, most * 3), np.int32)
    need = 0
    for device, own in enumerate(pieces):
        for number, (left, right, delta) in enumerate(own):
            table[device, 3 * number : 3 * number + 3] = (left, right, delta)
            need = max(need, right + delta)
    span = round_up(-(-need // LANES), 32)
    overlap = 16
    for device in range(1, shards):
        overlap = max(overlap, bases[device - 1] + span - bases[device])
    half = shards // 2
    edge = half * size
    sides = [[], []]
    for label, shape, place, region in names:
        if place < edge:
            sides[0].append((label, shape))
        if place + math.prod(shape) > edge:
            sides[1].append((label, shape))
    origins = [0, min(bases[half], places[sides[1][0][0]][0]) // 16 * 16]
    heights = []
    for side in range(2):
        last = bases[half * (side + 1) - 1] + span
        for label, shape in sides[side]:
            last = max(last, places[label][0] + -(-math.prod(shape) // LANES))
        heights.append(round_up(last - origins[side] + overlap, 16))
    return dict(
        places=places,
        rows=rows,
        half=half,
        sides=sides,
        origins=origins,
        heights=heights,
        size=size,
        bases=bases,
        table=table,
        most=most,
        span=span,
        overlap=overlap,
        shard_rows=round_up(-(-size // LANES), 16),
    )


def mm(left, right):
    return lax.dot_general(left, right, (((1,), (0,)), ((), ())), preferred_element_type=f32)


def mm_t(left, right):
    return lax.dot_general(left, right, (((1,), (1,)), ((), ())), preferred_element_type=f32)


def t_mm(left, right):
    return lax.dot_general(left, right, (((0,), (0,)), ((), ())), preferred_element_type=f32)


def vmem_spec(shape, index):
    return pl.BlockSpec(shape, index)


def whole(shape):
    rank = len(shape)
    return pl.BlockSpec(shape, lambda *_: (0,) * rank, pipeline_mode=pl.Buffered(1))


def estimate(flops, moved):
    return pl.CostEstimate(flops=int(flops), bytes_accessed=int(moved), transcendentals=0)


def shift_rows(ref, amount, rows, margin):
    down = amount // LANES
    across = amount - down * LANES
    here = ref[pl.ds(margin - down, rows), :]
    above = ref[pl.ds(margin - down - 1, rows), :]
    here = pltpu.roll(here, across, 1)
    above = pltpu.roll(above, across, 1)
    lane = lax.broadcasted_iota(jnp.int32, here.shape, 1)
    return jnp.where(lane < across, above, here)


def align_kernel(most, rows, span, margin, core_ref, table_ref, shard_ref, keep_ref, send_ref, padded):
    padded[...] = jnp.zeros_like(padded)
    padded[margin : margin + rows, :] = shard_ref[...]
    place = lax.broadcasted_iota(jnp.int32, (span, LANES), 0) * LANES
    place = place + lax.broadcasted_iota(jnp.int32, (span, LANES), 1)
    total = jnp.zeros((span, LANES), f32)
    for number in range(most):
        left = table_ref[3 * number]
        right = table_ref[3 * number + 1]
        delta = table_ref[3 * number + 2]
        moved = shift_rows(padded, delta, span, margin)
        total = jnp.where((place >= left + delta) & (place < right + delta), moved, total)
    total = total.astype(bf16)
    first = core_ref[0] == 0
    upper, lower = total[: span // 2], total[span // 2 :]
    keep_ref[...] = jnp.where(first, upper, lower)
    send_ref[...] = jnp.where(first, lower, upper)


def unalign_kernel(
    most, rows, span, margin, core_ref, table_ref, own_ref, got_ref, out_ref, norm_ref, padded
):
    first = core_ref[0] == 0
    padded[span:, :] = jnp.zeros((padded.shape[0] - span, LANES), f32)
    padded[0 : span // 2, :] = jnp.where(first, own_ref[...], got_ref[...])
    padded[span // 2 : span, :] = jnp.where(first, got_ref[...], own_ref[...])
    place = lax.broadcasted_iota(jnp.int32, (rows, LANES), 0) * LANES
    place = place + lax.broadcasted_iota(jnp.int32, (rows, LANES), 1)
    total = jnp.zeros((rows, LANES), f32)
    lane = lax.broadcasted_iota(jnp.int32, (rows, LANES), 1)
    for number in range(most):
        left = table_ref[3 * number]
        right = table_ref[3 * number + 1]
        delta = table_ref[3 * number + 2]
        down = delta // LANES
        across = delta - down * LANES
        back = lax.rem(LANES - across, LANES)
        here = pltpu.roll(padded[pl.ds(down, rows), :], back, 1)
        below = pltpu.roll(padded[pl.ds(down + 1, rows), :], back, 1)
        moved = jnp.where(lane < LANES - across, here, below)
        total = jnp.where((place >= left) & (place < right), moved, total)
    out_ref[...] = total
    norm_ref[...] = jnp.broadcast_to(jnp.sum(total * total).reshape(1, 1), (8, LANES))


def align(core, table, shard, plan):
    rows, span, most = plan["shard_rows"], plan["span"], plan["most"]
    margin = 8 + round_up(int(plan["table"].max(initial=0, where=pick_delta(plan))) // LANES + 1, 8)
    tall = margin + max(rows, span) + 8
    vmem = pl.BlockSpec(memory_space=pltpu.VMEM)
    smem = pl.BlockSpec(memory_space=pltpu.SMEM)
    part = jax.ShapeDtypeStruct((span // 2, LANES), bf16)
    return pl.pallas_call(
        functools.partial(align_kernel, most, rows, span, margin),
        out_shape=(part, part),
        in_specs=[smem, smem, vmem],
        out_specs=(vmem, vmem),
        scratch_shapes=[pltpu.VMEM((tall, LANES), f32)],
        cost_estimate=estimate(1_000_000, 1_000_000),
        name="align",
    )(core, table, shard)


def unalign(core, table, own, got, plan):
    rows, span, most = plan["shard_rows"], plan["span"], plan["most"]
    margin = 16 + round_up(int(plan["table"].max(initial=0, where=pick_delta(plan))) // LANES + 1, 8)
    tall = max(rows, span) + margin
    vmem = pl.BlockSpec(memory_space=pltpu.VMEM)
    smem = pl.BlockSpec(memory_space=pltpu.SMEM)
    return pl.pallas_call(
        functools.partial(unalign_kernel, most, rows, span, margin),
        out_shape=(
            jax.ShapeDtypeStruct((rows, LANES), f32),
            jax.ShapeDtypeStruct((8, LANES), f32),
        ),
        in_specs=[smem, smem, vmem, vmem],
        out_specs=(vmem, vmem),
        scratch_shapes=[pltpu.VMEM((tall, LANES), f32)],
        cost_estimate=estimate(1_000_000, 1_000_000),
        name="unalign",
    )(core, table, own, got)


def pick_delta(plan):
    mask = np.zeros(plan["table"].shape, bool)
    mask[:, 2::3] = True
    return mask


def two_dim(shape):
    return shape if len(shape) == 2 else (1, shape[0])


def is_matrix(label):
    return label[-2:] == "_w"


def strided(start, count, step):
    return pl.ds(start, count) if step == 1 or count == 1 else pl.ds(start, count, stride=step)


def half_swap(value):
    return pltpu.roll(value, LANES // 2, 1)


def read_param(flat, row, shape, out_ref, pair_ref):
    depth, width = two_dim(shape)
    dtype = out_ref.dtype
    if width % LANES == 0:
        step = width // LANES
        for col in range(step):
            out_ref[:, col * LANES : (col + 1) * LANES] = flat[
                strided(row + col, depth, step), :
            ].astype(dtype)
        return
    half = LANES // 2
    lead = width // LANES
    if depth == 1:
        for col in range(lead):
            out_ref[:, col * LANES : (col + 1) * LANES] = flat[row + col : row + col + 1, :].astype(
                dtype
            )
        out_ref[:, lead * LANES :] = flat[row + lead : row + lead + 1, 0:half].astype(dtype)
        return
    step = 2 * width // LANES
    pairs = depth // 2
    lane = lax.broadcasted_iota(jnp.int32, (pairs, LANES), 1)
    blocks = [flat[strided(row + col, pairs, step), :] for col in range(step)]
    turned = [half_swap(block) for block in blocks[lead:]]
    for col in range(lead):
        pair_ref[col, strided(0, pairs, 2), :] = blocks[col]
        pair_ref[col, strided(1, pairs, 2), :] = jnp.where(lane < half, turned[col], turned[col + 1])
    pair_ref[lead, strided(0, pairs, 2), :] = blocks[lead]
    pair_ref[lead, strided(1, pairs, 2), :] = turned[lead]
    for col in range(lead):
        out_ref[:, col * LANES : (col + 1) * LANES] = pair_ref[col, 0:depth, :].astype(dtype)
    out_ref[:, lead * LANES :] = pair_ref[lead, 0:depth, 0:half].astype(dtype)


def write_param(flat, row, shape, in_ref, pair_ref):
    depth, width = two_dim(shape)
    if width % LANES == 0:
        step = width // LANES
        for col in range(step):
            flat[strided(row + col, depth, step), :] = in_ref[:, col * LANES : (col + 1) * LANES]
        return
    half = LANES // 2
    lead = width // LANES
    if depth == 1:
        for col in range(lead):
            flat[row + col : row + col + 1, :] = in_ref[:, col * LANES : (col + 1) * LANES]
        tail = jnp.concatenate([in_ref[:, lead * LANES :], jnp.zeros((1, half), f32)], 1)
        flat[row + lead : row + lead + 1, :] = tail
        return
    step = 2 * width // LANES
    pairs = depth // 2
    lane = lax.broadcasted_iota(jnp.int32, (pairs, LANES), 1)
    for col in range(lead):
        pair_ref[col, 0:depth, :] = in_ref[:, col * LANES : (col + 1) * LANES]
    pair_ref[lead, 0:depth, 0:half] = in_ref[:, lead * LANES :]
    even = [pair_ref[col, strided(0, pairs, 2), :] for col in range(lead + 1)]
    odd = [half_swap(pair_ref[col, strided(1, pairs, 2), :]) for col in range(lead + 1)]
    for col in range(lead):
        flat[strided(row + col, pairs, step), :] = even[col]
    flat[strided(row + lead, pairs, step), :] = jnp.where(lane < half, even[lead], odd[0])
    for col in range(lead):
        flat[strided(row + lead + 1 + col, pairs, step), :] = jnp.where(
            lane < half, odd[col], odd[col + 1]
        )


def decode(number, core, bits):
    first = (number >> (bits - 1)) & 1
    second = (number >> (bits - 2)) & 1
    found = (first << core) | (second << (1 - core))
    for place in range(2, bits):
        found = found | (((number >> (bits - 1 - place)) & 1) << place)
    return found


def unflatten_kernel(plan, side, bits, where_ref, base_ref, *refs):
    pieces, refs = refs[:4], refs[4:]
    carried, refs = (refs[:1], refs[1:]) if side else ((), refs)
    outs, (flat, pair_ref) = refs[:-2], refs[-2:]
    span, overlap, half = plan["span"], plan["overlap"], plan["half"]
    origin = plan["origins"][side]
    core, mine = where_ref[0], where_ref[1]
    lead = plan["bases"][side * half] - origin
    if lead:
        flat[0:lead, :] = jnp.zeros((lead, LANES), f32)
    last = plan["bases"][side * half + half - 1] - origin + span
    if flat.shape[0] > last:
        flat[last:, :] = jnp.zeros((flat.shape[0] - last, LANES), f32)

    def base_of(owner):
        return pl.multiple_of(base_ref[side * half + owner] - origin, 16)

    def clear(owner, carry):
        base = base_of(owner)
        flat[pl.ds(base, overlap), :] = jnp.zeros((overlap, LANES), f32)
        flat[pl.ds(base + span - overlap, overlap), :] = jnp.zeros((overlap, LANES), f32)
        return carry

    lax.fori_loop(0, half, clear, 0)
    middle = span // 2
    for number, piece in enumerate(pieces):
        theirs = number // 2
        owner_core = core if theirs == 0 else 1 - core
        upper = number % 2 * (half // 2)
        for part in range(2):

            @pl.when(owner_core == part)
            def _(part=part, piece=piece, upper=upper):
                def place(entry, carry):
                    base = base_of(decode(entry + upper, part, bits) ^ mine)
                    value = piece[entry].astype(f32)
                    if part == 0:
                        flat[pl.ds(base, overlap), :] += value[:overlap]
                        flat[pl.ds(base + overlap, middle - overlap), :] = value[overlap:]
                    else:
                        flat[pl.ds(base + middle, middle - overlap), :] = value[: middle - overlap]
                        flat[pl.ds(base + span - overlap, overlap), :] += value[middle - overlap :]
                    return carry

                lax.fori_loop(0, half // 2, place, 0)

    for number, ((label, shape), out_ref) in enumerate(zip(plan["sides"][side], outs)):
        read_param(flat, plan["places"][label][0] - origin, shape, out_ref, pair_ref)
        if side and number == 0:
            out_ref[...] += carried[0][...]


def unflatten(where, pieces, plan, side, bits, carried=()):
    outs = []
    for label, shape in plan["sides"][side]:
        outs.append(jax.ShapeDtypeStruct(two_dim(shape), bf16 if is_matrix(label) else f32))
    vmem = pl.BlockSpec(memory_space=pltpu.VMEM)
    smem = pl.BlockSpec(memory_space=pltpu.SMEM)
    values = pl.pallas_call(
        functools.partial(unflatten_kernel, plan, side, bits),
        out_shape=outs,
        in_specs=[smem, smem] + [vmem] * (len(pieces) + len(carried)),
        out_specs=[vmem] * len(outs),
        scratch_shapes=[
            pltpu.VMEM((plan["heights"][side], LANES), f32),
            pltpu.VMEM((5, MS, LANES), f32),
        ],
        cost_estimate=estimate(1_000_000, 8_000_000),
        name="unflatten" + str(side),
    )(where, jnp.asarray(plan["bases"], jnp.int32), *pieces, *carried)
    return {label: value for (label, shape), value in zip(plan["sides"][side], values)}


def flatten_kernel(plan, side, bits, where_ref, base_ref, *refs):
    count = len(plan["sides"][side])
    grads, (low_ref, high_ref, send_ref, flat, pair_ref) = refs[:count], refs[count:]
    span, half, origin = plan["span"], plan["half"], plan["origins"][side]
    core, mine = where_ref[0], where_ref[1]
    first, last = None, 0
    for (label, shape), ref in zip(plan["sides"][side], grads):
        row = plan["places"][label][0] - origin
        first = row if first is None else first
        last = row + -(-math.prod(shape) // LANES)
    if first:
        flat[0:first, :] = jnp.zeros((first, LANES), f32)
    flat[last // 8 * 8 :, :] = jnp.zeros((flat.shape[0] - last // 8 * 8, LANES), f32)
    for (label, shape), ref in zip(plan["sides"][side], grads):
        write_param(flat, plan["places"][label][0] - origin, shape, ref, pair_ref)

    def rows_of(entry, part):
        owner = decode(entry, part, bits) ^ mine
        base = base_ref[side * half + owner] - origin + part * (span // 2)
        return flat[pl.ds(pl.multiple_of(base, 16), span // 2), :].astype(bf16)

    def place(entry, carry):
        low_ref[entry] = rows_of(entry, core)
        high_ref[entry] = rows_of(entry + half // 2, core)
        send_ref[entry] = rows_of(entry, 1 - core)
        send_ref[entry + half // 2] = rows_of(entry + half // 2, 1 - core)
        return carry

    lax.fori_loop(0, half // 2, place, 0)


def flatten(where, grads, plan, side, bits):
    vmem = pl.BlockSpec(memory_space=pltpu.VMEM)
    smem = pl.BlockSpec(memory_space=pltpu.SMEM)
    half, rows = plan["half"], plan["span"] // 2
    values = [grads[label] for label, shape in plan["sides"][side]]
    return pl.pallas_call(
        functools.partial(flatten_kernel, plan, side, bits),
        out_shape=(
            jax.ShapeDtypeStruct((half // 2, rows, LANES), bf16),
            jax.ShapeDtypeStruct((half // 2, rows, LANES), bf16),
            jax.ShapeDtypeStruct((half, rows, LANES), bf16),
        ),
        in_specs=[smem, smem] + [vmem] * len(values),
        out_specs=(vmem, vmem, vmem),
        scratch_shapes=[
            pltpu.VMEM((plan["heights"][side], LANES), f32),
            pltpu.VMEM((5, MS, LANES), f32),
        ],
        cost_estimate=estimate(1_000_000, 10_000_000),
        name="flatten" + str(side),
    )(where, jnp.asarray(plan["bases"], jnp.int32), *values)


def ln_parts(value):
    mean = jnp.mean(value, -1, keepdims=True)
    centred = value - mean
    variance = jnp.mean(centred * centred, -1, keepdims=True)
    inverse = lax.rsqrt(variance + norm_eps)
    return centred * inverse, inverse


def ln_back(grad, hat, inverse, gain):
    scaled = grad * gain
    first = jnp.mean(scaled, -1, keepdims=True)
    second = jnp.mean(scaled * hat, -1, keepdims=True)
    return inverse * (scaled - first - hat * second)


def gelu_parts(value):
    cdf = 0.5 + 0.5 * lax.erf(value * (2.0**-0.5))
    density = jnp.exp(value * value * -0.5) * (1.0 / math.sqrt(2.0 * math.pi))
    return value * cdf, cdf + value * density


def col_sum(value):
    return jnp.sum(value, 0, keepdims=True)


def groups(width):
    size = width // HEADS
    found = []
    for start in range(0, width, LANES):
        stop = min(start + LANES, width)
        found.append((start, stop, (stop - start) // size))
    return found, size


def stack_heads(value, count, size):
    lane = lax.broadcasted_iota(jnp.int32, value.shape, 1)
    zero = jnp.zeros_like(value)
    return jnp.concatenate(
        [
            jnp.where((lane >= head * size) & (lane < (head + 1) * size), value, zero)
            for head in range(count)
        ],
        0,
    )


def merge_heads(value, count, size):
    rows = value.shape[0] // count
    lane = lax.broadcasted_iota(jnp.int32, (rows, value.shape[1]), 1)
    merged = value[0:rows]
    for head in range(1, count):
        merged = jnp.where(lane >= head * size, value[head * rows : (head + 1) * rows], merged)
    return merged


def attention_forward(pair, length, tall, tokens, weights, keeps):
    ln1_ref, qkv_w, qkv_b, proj_w, proj_b, ln2_ref = weights
    a1_ref, qkv_ref, probs_ref, att_ref, mid_ref, n2_ref = keeps
    width = tokens.shape[-1]
    found, size = groups(width)
    scale = size ** (-0.5)
    hat, _ = ln_parts(tokens)
    a1 = (hat * ln1_ref[0:1, :] + ln1_ref[1:2, :]).astype(bf16)
    a1_ref[...] = a1
    qkv_ref[...] = (mm(a1, qkv_w[...]) + qkv_b[...]).astype(bf16)
    key_lane = lax.broadcasted_iota(jnp.int32, (1, tall), 1)
    bias = jnp.where(key_lane < length, 0.0, -1e30).astype(f32)
    for crop in range(pair):
        here = slice(crop * tall, (crop + 1) * tall)
        for start, stop, count in found:
            query = stack_heads(qkv_ref[here, start:stop], count, size)
            key = qkv_ref[here, width + start : width + stop]
            value = qkv_ref[here, 2 * width + start : 2 * width + stop]
            scores = mm_t(query, key) * scale + bias
            summit = jnp.max(scores, -1, keepdims=True)
            weights = jnp.exp(scores - summit)
            probs = (weights / jnp.sum(weights, -1, keepdims=True)).astype(bf16)
            first = start // size
            for head in range(count):
                probs_ref[crop, first + head] = probs[head * tall : (head + 1) * tall]
            att_ref[here, start:stop] = merge_heads(mm(probs, value), count, size).astype(bf16)
    mid = tokens + mm(att_ref[...], proj_w[...]) + proj_b[...]
    mid_ref[...] = mid
    hat, _ = ln_parts(mid)
    n2_ref[...] = (hat * ln2_ref[0:1, :] + ln2_ref[1:2, :]).astype(bf16)


def mlp_forward(chunk, mid_ref, n2_ref, weights, keeps):
    fc1_w, fc1_b, fc2_w, fc2_b = weights
    z_ref, slope_ref, y_ref = keeps
    y_ref[...] = mid_ref[...] + fc2_b[...]
    for number in range(fc1_w.shape[1] // chunk):
        cols = slice(number * chunk, (number + 1) * chunk)
        inner = mm(n2_ref[...], fc1_w[:, cols]) + fc1_b[:, cols]
        active, slope = gelu_parts(inner)
        z_ref[:, cols] = active.astype(bf16)
        slope_ref[:, cols] = slope.astype(bf16)
        y_ref[...] += mm(z_ref[:, cols], fc2_w[cols, :])


def keep_heads(pair, tall, y_ref, head_ref):
    for crop in range(pair):
        slot = pl.program_id(0) * pair + crop
        head_ref[pl.ds(slot, 1), :] = y_ref[crop * tall : crop * tall + 1, :]


def carry(value, norm, weight, bias):
    hat, _ = ln_parts(value)
    active, _ = gelu_parts(hat * norm[0:1, :] + norm[1:2, :])
    return (mm(active.astype(bf16), weight[...]) + bias[...]).astype(bf16)


def attention_kernel(pair, length, tall, tok_ref, *refs):
    tokens = tok_ref[...].reshape(pair * tall, tok_ref.shape[-1]).astype(f32)
    attention_forward(pair, length, tall, tokens, refs[:6], refs[6:])


def block_kernel(pair, length, tall, chunk, tok_ref, *refs):
    tokens = tok_ref[...].reshape(pair * tall, tok_ref.shape[-1]).astype(f32)
    attention_forward(pair, length, tall, tokens, refs[:6], refs[10:16])
    mlp_forward(chunk, refs[14], refs[15], refs[6:10], refs[16:19])
    keep_heads(pair, tall, refs[18], refs[19])


def mlp_kernel(pair, tall, chunk, mid_ref, n2_ref, *refs):
    weights, heads, (far_head, *far), near = refs[:4], None, refs[4:8], refs[8:11]
    z_ref, slope_ref, y_ref, head_ref, near_ref, far_ref = refs[11:]
    mlp_forward(chunk, mid_ref, n2_ref, weights, (z_ref, slope_ref, y_ref))
    keep_heads(pair, tall, y_ref, head_ref)

    @pl.when(pl.program_id(0) == pl.num_programs(0) - 1)
    def _():
        near_ref[...] = carry(head_ref[...], *near)
        far_ref[...] = carry(far_head[...], *far)


ATTENTION = ("ln1", "qkv_w", "qkv_b", "proj_w", "proj_b", "ln2")
MLP = ("fc1_w", "fc1_b", "fc2_w", "fc2_b")
TO = ("to_ln", "to_w", "to_b")


def pick(params, label, names):
    return [params[label + "_" + name] for name in names]


def row_spec(rows, cols):
    return pl.BlockSpec((rows, cols), lambda i: (i, 0))


def fixed_spec(shape):
    rank = len(shape)
    return pl.BlockSpec(shape, lambda i: (0,) * rank)


def kept_outs(crops, tall, width, hidden, pair):
    rows, flat = pair * tall, crops * tall

    def entry(cols, dtype):
        return row_spec(rows, cols), jax.ShapeDtypeStruct((flat, cols), dtype)

    attention = [
        entry(width, bf16),
        entry(3 * width, bf16),
        (
            pl.BlockSpec((pair, HEADS, tall, tall), lambda i: (i, 0, 0, 0)),
            jax.ShapeDtypeStruct((crops, HEADS, tall, tall), bf16),
        ),
        entry(width, bf16),
        entry(width, f32),
        entry(width, bf16),
    ]
    mlp = [
        entry(hidden, bf16),
        entry(hidden, bf16),
        entry(width, f32),
        (fixed_spec((crops, width)), jax.ShapeDtypeStruct((crops, width), f32)),
    ]
    return attention, mlp


def block_forward(tokens, params, label, length, pair):
    crops, tall, width = tokens.shape
    hidden = params[label + "_fc1_w"].shape[1]
    weights = pick(params, label, ATTENTION + MLP)
    attention, mlp = kept_outs(crops, tall, width, hidden, pair)
    outs = attention + mlp
    flops = 2 * crops * tall * (4 * width * width + 2 * width * hidden)
    return pl.pallas_call(
        functools.partial(block_kernel, pair, length, tall, 384),
        grid=(crops // pair,),
        out_shape=[shape for spec, shape in outs],
        in_specs=[pl.BlockSpec((pair, tall, width), lambda i: (i, 0, 0))]
        + [whole(value.shape) for value in weights],
        out_specs=[spec for spec, shape in outs],
        cost_estimate=estimate(8 * flops, 10_000_000),
        name="block_" + label,
    )(tokens, *weights)


def attention_only(tokens, params, label, length, pair):
    crops, tall, width = tokens.shape
    weights = pick(params, label, ATTENTION)
    outs, _ = kept_outs(crops, tall, width, width, pair)
    flops = 2 * crops * tall * 4 * width * width
    return pl.pallas_call(
        functools.partial(attention_kernel, pair, length, tall),
        grid=(crops // pair,),
        out_shape=[shape for spec, shape in outs],
        in_specs=[pl.BlockSpec((pair, tall, width), lambda i: (i, 0, 0))]
        + [whole(value.shape) for value in weights],
        out_specs=[spec for spec, shape in outs],
        cost_estimate=estimate(8 * flops, 20_000_000),
        name="attention_" + label,
    )(tokens, *weights)


def mlp_only(mid, n2, far_head, params, label, far, crops, pair):
    flat, width = mid.shape
    tall = flat // crops
    rows = pair * tall
    hidden = params[label + "_fc1_w"].shape[1]
    weights = pick(params, label, MLP)
    extra = [far_head] + pick(params, far, TO) + pick(params, label, TO)
    _, outs = kept_outs(crops, tall, width, hidden, pair)
    for name in (label, far):
        shape = (crops, params[name + "_to_w"].shape[1])
        outs.append((fixed_spec(shape), jax.ShapeDtypeStruct(shape, bf16)))
    flops = 2 * flat * 2 * width * hidden
    return pl.pallas_call(
        functools.partial(mlp_kernel, pair, tall, 384),
        grid=(crops // pair,),
        out_shape=[shape for spec, shape in outs],
        in_specs=[row_spec(rows, width), row_spec(rows, width)]
        + [whole(value.shape) for value in weights + extra],
        out_specs=[spec for spec, shape in outs],
        cost_estimate=estimate(8 * flops, 20_000_000),
        name="mlp_" + label,
    )(mid, n2, *weights, *extra)


def cross_kernel(
    length,
    tall,
    crops,
    sent_ref,
    y_ref,
    gret_ref,
    ca_ln,
    q_w,
    q_b,
    k_w,
    v_w,
    v_b,
    o_w,
    o_b,
    back_ln,
    back_w,
    back_b,
    returned_ref,
    gsent_ref,
    gj_ref,
    d_ca_ln,
    d_q_w,
    d_q_b,
    d_k_w,
    d_v_w,
    d_v_b,
    d_o_w,
    d_o_b,
    d_back_ln,
    d_back_w,
    d_back_b,
    sent_f,
    n_all,
    k_all,
    v_all,
    gk_all,
    gv_all,
    query_all,
    probs_all,
    att_all,
    gatt_all,
    gq_all,
    gn_head,
    gj_head,
):
    width = y_ref.shape[1]
    size = width // HEADS
    scale = size ** (-0.5)
    lane = lax.broadcasted_iota(jnp.int32, (8, width), 1)
    head = lax.broadcasted_iota(jnp.int32, (8, width), 0)
    own_head = (lane >= head * size) & (lane < (head + 1) * size)
    row = lax.broadcasted_iota(jnp.int32, (tall, 1), 0)
    key_lane = lax.broadcasted_iota(jnp.int32, (1, tall), 1)
    bias = jnp.where(key_lane < length, 0.0, -1e30).astype(f32)
    gain, shift = ca_ln[0:1, :], ca_ln[1:2, :]
    sent_f[...] = sent_ref[...].astype(f32)
    hat, _ = ln_parts(sent_f[...])
    n_head = (hat * gain + shift).astype(bf16)
    query_all[...] = (mm(n_head, q_w[...]) + q_b[...]).astype(bf16).astype(f32)

    def joined(crop):
        here = pl.ds(pl.multiple_of(crop * tall, 16), tall)
        return here, jnp.where(row == 0, sent_f[pl.ds(crop, 1), :], y_ref[here, :])

    def spread(ref, crop):
        return jnp.where(own_head, ref[pl.ds(crop, 1), :], 0.0).astype(bf16)

    def ahead(crop, carry):
        here, value = joined(crop)
        hat, _ = ln_parts(value)
        normed = (hat * gain + shift).astype(bf16)
        n_all[here, :] = normed
        key = mm(normed, k_w[...]).astype(bf16)
        k_all[here, :] = key
        vals = (mm(normed, v_w[...]) + v_b[...]).astype(bf16)
        v_all[here, :] = vals
        scores = mm_t(spread(query_all, crop), key) * scale + bias
        summit = jnp.max(scores, -1, keepdims=True)
        weights = jnp.exp(scores - summit)
        probs = weights / jnp.sum(weights, -1, keepdims=True)
        probs_all[crop] = probs
        mixed = jnp.where(own_head, mm(probs.astype(bf16), vals), 0.0)
        att_all[pl.ds(crop, 1), :] = col_sum(mixed)
        return carry

    lax.fori_loop(0, crops, ahead, 0)
    attended = att_all[...].astype(bf16)
    merged = sent_f[...] + mm(attended, o_w[...]) + o_b[...]
    hat, inverse = ln_parts(merged)
    active, slope = gelu_parts(hat * back_ln[0:1, :] + back_ln[1:2, :])
    active = active.astype(bf16)
    returned_ref[...] = (mm(active, back_w[...]) + back_b[...]).astype(bf16)
    gret = gret_ref[...]
    d_back_w[...] = t_mm(active, gret)
    d_back_b[...] = col_sum(gret.astype(f32))
    gact = mm_t(gret, back_w[...]) * slope
    d_back_ln[0:1, :] = col_sum(gact * hat)
    d_back_ln[1:2, :] = col_sum(gact)
    gfused = ln_back(gact, hat, inverse, back_ln[0:1, :])
    gfo = gfused.astype(bf16)
    d_o_w[...] = t_mm(attended, gfo)
    d_o_b[...] = col_sum(gfo.astype(f32))
    gatt_all[...] = mm_t(gfo, o_w[...]).astype(bf16).astype(f32)

    def behind(crop, carry):
        here = pl.ds(pl.multiple_of(crop * tall, 16), tall)
        probs = probs_all[crop]
        gatt = spread(gatt_all, crop)
        gprobs = mm_t(gatt, v_all[here, :])
        gv_all[here, :] = t_mm(probs.astype(bf16), gatt).astype(bf16)
        inner = gprobs - jnp.sum(gprobs * probs, -1, keepdims=True)
        gscores = (probs * inner).astype(bf16)
        gq = jnp.where(own_head, mm(gscores, k_all[here, :]), 0.0)
        gq_all[pl.ds(crop, 1), :] = col_sum(gq) * scale
        gk_all[here, :] = (t_mm(gscores, spread(query_all, crop)) * scale).astype(bf16)
        return carry

    lax.fori_loop(0, crops, behind, 0)
    gq = gq_all[...].astype(bf16)
    d_q_w[...] = t_mm(n_head, gq)
    d_q_b[...] = col_sum(gq.astype(f32))
    gn_head[...] = mm_t(gq, q_w[...])
    d_ca_ln[...] = jnp.zeros_like(d_ca_ln)
    d_v_b[...] = jnp.zeros_like(d_v_b)
    d_k_w[...] = jnp.zeros_like(d_k_w)
    d_v_w[...] = jnp.zeros_like(d_v_w)

    def finish(crop, carry):
        here, value = joined(crop)
        hat, inverse = ln_parts(value)
        gk, gv = gk_all[here, :], gv_all[here, :]
        gn = mm_t(gk, k_w[...]) + mm_t(gv, v_w[...])
        gn = gn + jnp.where(row == 0, gn_head[pl.ds(crop, 1), :], 0.0)
        d_ca_ln[0:1, :] += col_sum(gn * hat)
        d_ca_ln[1:2, :] += col_sum(gn)
        gj = ln_back(gn, hat, inverse, gain)
        gj_ref[here, :] = gj
        gj_head[pl.ds(crop, 1), :] = gj[0:1, :]
        d_v_b[...] += col_sum(gv.astype(f32))
        return carry

    lax.fori_loop(0, crops, finish, 0)
    gsent_ref[...] = (gj_head[...] + gfused).astype(bf16)

    def weights_of(pair, carry):
        here = pl.ds(pl.multiple_of(pair * 2 * tall, 32), 2 * tall)
        normed = n_all[here, :]
        d_k_w[...] += t_mm(normed, gk_all[here, :])
        d_v_w[...] += t_mm(normed, gv_all[here, :])
        return carry

    lax.fori_loop(0, crops // 2, weights_of, 0)


def cross(sent, hosted, gret, params, label, length, tall):
    crops, width = sent.shape
    own = gret.shape[1]
    flat = crops * tall
    names = ("ca_ln", "ca_q_w", "ca_q_b", "ca_k_w", "ca_v_w", "ca_v_b", "ca_o_w", "ca_o_b")
    names = names + ("back_ln", "back_w", "back_b")
    weights = [params[label + "_" + name] for name in names]
    outs = [
        jax.ShapeDtypeStruct((crops, own), bf16),
        jax.ShapeDtypeStruct((crops, width), bf16),
        jax.ShapeDtypeStruct((flat, width), f32),
    ] + [jax.ShapeDtypeStruct(value.shape, f32) for value in weights]
    vmem = pl.BlockSpec(memory_space=pltpu.VMEM)
    small = pltpu.VMEM((crops, width), f32)
    big = pltpu.VMEM((flat, width), bf16)
    values = pl.pallas_call(
        functools.partial(cross_kernel, length, tall, crops),
        out_shape=outs,
        in_specs=[vmem] * (3 + len(weights)),
        out_specs=[vmem] * len(outs),
        scratch_shapes=[small]
        + [big] * 5
        + [small, pltpu.VMEM((crops, 8, tall), f32)]
        + [small] * 5,
        cost_estimate=estimate(2 * flat * width * width * 6, 8_000_000),
        name="cross_" + label,
    )(sent, hosted, gret, *weights)
    grads = {label + "_" + name: value for name, value in zip(names, values[3:])}
    return values[0], values[1], values[2], grads


def head_backward(headrow_ref, gsent_ref, to_ln, to_w, d_to_ln, d_to_w, d_to_b, ghead_ref):
    hat, inverse = ln_parts(headrow_ref[...])
    active, slope = gelu_parts(hat * to_ln[0:1, :] + to_ln[1:2, :])
    gsent = gsent_ref[...]
    d_to_w[...] = t_mm(active.astype(bf16), gsent)
    d_to_b[...] = col_sum(gsent.astype(f32))
    gact = mm_t(gsent, to_w[...]) * slope
    d_to_ln[0:1, :] = col_sum(gact * hat)
    d_to_ln[1:2, :] = col_sum(gact)
    ghead_ref[...] = ln_back(gact, hat, inverse, to_ln[0:1, :])


def clear_all(refs):
    for ref in refs:
        ref[...] = jnp.zeros_like(ref)


def mlp_backward(pair, tall, chunk, live_ref, acts, weights, grads, out_ref, gy, gnormed):
    cot_ref, y_ref, gj_ref, mid_ref, n2_ref, z_ref, slope_ref, ghead, returned_ref = acts
    ln2_ref, fc1_w, fc2_w = weights
    d_ln2, d_fc1_w, d_fc1_b, d_fc2_w, d_fc2_b = grads
    length = out_ref.shape[2]
    row = lax.broadcasted_iota(jnp.int32, (tall, 1), 0)
    for crop in range(pair):
        here = slice(crop * tall, (crop + 1) * tall)
        slot = pl.program_id(0) * pair + crop
        live = jnp.where(slot < live_ref[0], 1.0, 0.0).astype(f32)
        seed = cot_ref[crop].astype(f32) * live + gj_ref[here, :]
        gy[here, :] = jnp.where(row == 0, ghead[pl.ds(slot, 1), :], seed)
        home = returned_ref[pl.ds(slot, 1), :]
        final = jnp.where(row == 0, home, y_ref[here, :])
        out_ref[0, crop] = final[0:length].astype(bf16)
    gm = gy[...].astype(bf16)
    d_fc2_b[...] += col_sum(gm.astype(f32))
    for number in range(fc1_w.shape[1] // chunk):
        cols = slice(number * chunk, (number + 1) * chunk)
        d_fc2_w[cols, :] += t_mm(z_ref[:, cols], gm)
        gu = slope_ref[:, cols].astype(f32) * mm_t(gm, fc2_w[cols, :])
        gu = gu.astype(bf16)
        d_fc1_w[:, cols] += t_mm(n2_ref[...], gu)
        d_fc1_b[:, cols] += col_sum(gu.astype(f32))
        part = mm_t(gu, fc1_w[:, cols])
        gnormed[...] = part if number == 0 else gnormed[...] + part
    hat, inverse = ln_parts(mid_ref[...])
    gn = gnormed[...]
    d_ln2[0:1, :] += col_sum(gn * hat)
    d_ln2[1:2, :] += col_sum(gn)
    gy[...] += ln_back(gn, hat, inverse, ln2_ref[0:1, :])


def attention_backward(pair, tall, acts, weights, grads, gtok_ref, gmid_ref, gqkv, gatt_ref):
    tok_ref, a1_ref, qkv_ref, probs_ref, att_ref = acts
    ln1_ref, qkv_w, proj_w = weights
    d_ln1, d_qkv_w, d_qkv_b, d_proj_w, d_proj_b = grads
    width = tok_ref.shape[-1]
    length = gtok_ref.shape[2]
    found, size = groups(width)
    scale = size ** (-0.5)
    gp = gmid_ref[...].astype(bf16)
    d_proj_w[...] += t_mm(att_ref[...], gp)
    d_proj_b[...] += col_sum(gp.astype(f32))
    gatt_ref[...] = mm_t(gp, proj_w[...]).astype(bf16)
    for crop in range(pair):
        here = slice(crop * tall, (crop + 1) * tall)
        for start, stop, count in found:
            first = start // size
            query = stack_heads(qkv_ref[here, start:stop], count, size)
            key = qkv_ref[here, width + start : width + stop]
            value = qkv_ref[here, 2 * width + start : 2 * width + stop]
            gatt = stack_heads(gatt_ref[here, start:stop], count, size)
            probs_low = jnp.concatenate([probs_ref[crop, first + head] for head in range(count)], 0)
            probs = probs_low.astype(f32)
            gprobs = mm_t(gatt, value)
            inner = gprobs - jnp.sum(gprobs * probs, -1, keepdims=True)
            gscores = (probs * inner).astype(bf16)
            gq = merge_heads(mm(gscores, key), count, size) * scale
            gk = t_mm(gscores, query) * scale
            gv = t_mm(probs_low, gatt)
            gqkv[here, start:stop] = gq.astype(bf16)
            gqkv[here, width + start : width + stop] = gk.astype(bf16)
            gqkv[here, 2 * width + start : 2 * width + stop] = gv.astype(bf16)
    grad = gqkv[...]
    d_qkv_w[...] += t_mm(a1_ref[...], grad)
    d_qkv_b[...] += col_sum(grad.astype(f32))
    gn = mm_t(grad, qkv_w[...])
    hat, inverse = ln_parts(tok_ref[...].reshape(pair * tall, width).astype(f32))
    d_ln1[0:1, :] += col_sum(gn * hat)
    d_ln1[1:2, :] += col_sum(gn)
    gtok = gmid_ref[...] + ln_back(gn, hat, inverse, ln1_ref[0:1, :])
    for crop in range(pair):
        gtok_ref[0, crop] = gtok[crop * tall : crop * tall + length].astype(bf16)


GRAD_MLP = ("ln2", "fc1_w", "fc1_b", "fc2_w", "fc2_b")
GRAD_ATTENTION = ("ln1", "qkv_w", "qkv_b", "proj_w", "proj_b")


def mlp_back_kernel(pair, tall, chunk, live_ref, *refs):
    cot_ref, y_ref, gj_ref, mid_ref, n2_ref, z_ref, slope_ref, returned_ref = refs[:8]
    weights = refs[8:11]
    near, far = refs[11:15], refs[15:19]
    out_ref, gmid_ref, ghead_far = refs[19:22]
    grads, near_grads, far_grads = refs[22:27], refs[27:30], refs[30:33]
    ghead, gnormed = refs[33:]

    @pl.when(pl.program_id(0) == 0)
    def _():
        head_backward(*near, *near_grads, ghead)
        head_backward(*far, *far_grads, ghead_far)
        clear_all(grads)

    acts = (cot_ref, y_ref, gj_ref, mid_ref, n2_ref, z_ref, slope_ref, ghead, returned_ref)
    mlp_backward(pair, tall, chunk, live_ref, acts, weights, grads, out_ref, gmid_ref, gnormed)


def attention_back_kernel(pair, tall, gmid_ref, *refs):
    acts, weights, gtok_ref, grads = refs[:5], refs[5:8], refs[8], refs[9:14]

    @pl.when(pl.program_id(0) == 0)
    def _():
        clear_all(grads)

    attention_backward(pair, tall, acts, weights, grads, gtok_ref, gmid_ref, *refs[14:])


def block_back_kernel(pair, tall, chunk, live_ref, *refs):
    mlp_acts, acts = refs[:9], refs[9:14]
    weights, mlp_weights = refs[14:17], refs[17:20]
    out_ref, gtok_ref = refs[20:22]
    mlp_grads, grads = refs[22:27], refs[27:32]
    gy, gnormed, gqkv, gatt_ref = refs[32:]

    @pl.when(pl.program_id(0) == 0)
    def _():
        clear_all(mlp_grads + grads)

    mlp_backward(
        pair, tall, chunk, live_ref, mlp_acts, mlp_weights, mlp_grads, out_ref, gy, gnormed
    )
    attention_backward(pair, tall, acts, weights, grads, gtok_ref, gy, gqkv, gatt_ref)


def named(label, names, values):
    return {label + "_" + name: value for name, value in zip(names, values)}


def grad_outs(params, label, names):
    return [
        (fixed_spec(value.shape), jax.ShapeDtypeStruct(value.shape, f32))
        for value in pick(params, label, names)
    ]


def token_out(crops, length, width, pair):
    return (
        pl.BlockSpec((1, pair, length, width), lambda i: (0, i, 0, 0)),
        jax.ShapeDtypeStruct((1, crops, length, width), bf16),
    )


def mlp_back(cot, live, kept, gj, near, far, returned, params, label, other, length, pair):
    crops, tall, width = cot.shape
    mid, n2, z, slope, y = kept
    hidden = z.shape[1]
    rows, flat = pair * tall, crops * tall
    weights = pick(params, label, ("ln2", "fc1_w", "fc2_w"))
    near = list(near) + pick(params, label, ("to_ln", "to_w"))
    far = list(far) + pick(params, other, ("to_ln", "to_w"))
    smem = pl.BlockSpec(memory_space=pltpu.SMEM)
    outs = [
        token_out(crops, length, width, pair),
        (row_spec(rows, width), jax.ShapeDtypeStruct((flat, width), f32)),
        (fixed_spec(far[0].shape), jax.ShapeDtypeStruct(far[0].shape, f32)),
    ]
    outs += grad_outs(params, label, GRAD_MLP)
    outs += grad_outs(params, label, TO) + grad_outs(params, other, TO)
    returned = returned.astype(f32)
    values = pl.pallas_call(
        functools.partial(mlp_back_kernel, pair, tall, 384),
        grid=(crops // pair,),
        out_shape=[shape for spec, shape in outs],
        in_specs=[smem, pl.BlockSpec((pair, tall, width), lambda i: (i, 0, 0))]
        + [row_spec(rows, width)] * 4
        + [row_spec(rows, hidden)] * 2
        + [whole(value.shape) for value in [returned] + weights + near + far],
        out_specs=[spec for spec, shape in outs],
        scratch_shapes=[pltpu.VMEM((crops, width), f32), pltpu.VMEM((rows, width), f32)],
        cost_estimate=estimate(8 * 8 * flat * width * hidden, 20_000_000),
        name="mlp_back_" + label,
    )(live, cot, y, gj, mid, n2, z, slope, returned, *weights, *near, *far)
    grads = named(label, GRAD_MLP, values[3:8])
    grads.update(named(label, TO, values[8:11]))
    grads.update(named(other, TO, values[11:14]))
    return values[0], values[1], values[2], grads


def attention_back(tokens, gmid, kept, params, label, length, pair):
    crops, tall, width = tokens.shape
    a1, qkv, probs, att = kept
    rows, flat = pair * tall, crops * tall
    weights = pick(params, label, ("ln1", "qkv_w", "proj_w"))
    outs = [token_out(crops, length, width, pair)] + grad_outs(params, label, GRAD_ATTENTION)
    values = pl.pallas_call(
        functools.partial(attention_back_kernel, pair, tall),
        grid=(crops // pair,),
        out_shape=[shape for spec, shape in outs],
        in_specs=[
            row_spec(rows, width),
            pl.BlockSpec((pair, tall, width), lambda i: (i, 0, 0)),
            row_spec(rows, width),
            row_spec(rows, 3 * width),
            pl.BlockSpec((pair, HEADS, tall, tall), lambda i: (i, 0, 0, 0)),
            row_spec(rows, width),
        ]
        + [whole(value.shape) for value in weights],
        out_specs=[spec for spec, shape in outs],
        scratch_shapes=[pltpu.VMEM((rows, 3 * width), bf16), pltpu.VMEM((rows, width), bf16)],
        cost_estimate=estimate(8 * 16 * flat * width * width, 20_000_000),
        name="attention_back_" + label,
    )(gmid, tokens, a1, qkv, probs, att, *weights)
    return values[0], named(label, GRAD_ATTENTION, values[1:])


def block_back(tokens, cot, live, kept, gj, ghead, returned, params, label, length, pair):
    crops, tall, width = tokens.shape
    a1, qkv, probs, att, mid, n2, z, slope, y = kept
    hidden = z.shape[1]
    rows, flat = pair * tall, crops * tall
    weights = pick(params, label, ("ln1", "qkv_w", "proj_w", "ln2", "fc1_w", "fc2_w"))
    smem = pl.BlockSpec(memory_space=pltpu.SMEM)
    token_spec = pl.BlockSpec((pair, tall, width), lambda i: (i, 0, 0))
    outs = [token_out(crops, length, width, pair)] * 2
    outs += grad_outs(params, label, GRAD_MLP) + grad_outs(params, label, GRAD_ATTENTION)
    returned = returned.astype(f32)
    values = pl.pallas_call(
        functools.partial(block_back_kernel, pair, tall, 384),
        grid=(crops // pair,),
        out_shape=[shape for spec, shape in outs],
        in_specs=[smem, token_spec]
        + [row_spec(rows, width)] * 4
        + [row_spec(rows, hidden)] * 2
        + [whole(ghead.shape), whole(returned.shape)]
        + [
            token_spec,
            row_spec(rows, width),
            row_spec(rows, 3 * width),
            pl.BlockSpec((pair, HEADS, tall, tall), lambda i: (i, 0, 0, 0)),
            row_spec(rows, width),
        ]
        + [whole(value.shape) for value in weights],
        out_specs=[spec for spec, shape in outs],
        scratch_shapes=[
            pltpu.VMEM((rows, width), f32),
            pltpu.VMEM((rows, width), f32),
            pltpu.VMEM((rows, 3 * width), bf16),
            pltpu.VMEM((rows, width), bf16),
        ],
        cost_estimate=estimate(8 * 4 * flat * (4 * width * width + 2 * width * hidden), 20_000_000),
        name="block_back_" + label,
    )(live, cot, y, gj, mid, n2, z, slope, ghead, returned, tokens, a1, qkv, probs, att, *weights)
    grads = named(label, GRAD_MLP, values[2:7])
    grads.update(named(label, GRAD_ATTENTION, values[7:12]))
    return values[0], values[1], grads


def swap(value):
    return lax.ppermute(value, "branch", [(0, 1), (1, 0)])


def partner(value, bit):
    count = lax.axis_size("dp")
    return lax.ppermute(value, "dp", [(i, i ^ bit) for i in range(count)])


def side_partner(value, place):
    count = lax.axis_size("dp")
    pairs = []
    for core in range(2):
        bit = 1 << (place ^ core)
        pairs += [(core * count + i, core * count + (i ^ bit)) for i in range(count)]
    return lax.ppermute(value, ("branch", "dp"), pairs)


def tie(value, *others):
    return lax.optimization_barrier((value, *others))[0]


def gather_lines(held, first, last):
    for place in range(first, last, -1):
        held = jnp.concatenate([held, partner(held, 1 << place)], 0)
    return held


def gather_middle(held):
    return jnp.concatenate([held, side_partner(held, 1)], 0)


def add_low(*values):
    total = values[0].astype(f32)
    for value in values[1:]:
        total = total + value.astype(f32)
    return total.astype(bf16)


def reduce_start(low, high, send):
    half = low.shape[0]
    got = swap(send)
    sent = add_low(high, got[half:])
    return sent, [low, got[:half], side_partner(sent, 0)]


def reduce_middle(parts):
    quarter = parts[0].shape[0] // 2
    sent = add_low(*[part[quarter:] for part in parts])
    return sent, [part[:quarter] for part in parts] + [side_partner(sent, 1)]


def reduce_lines(parts, bits):
    for place in range(2, bits):
        count = parts[0].shape[0] // 2
        sent = add_low(*[part[count:] for part in parts])
        parts = [part[:count] for part in parts] + [partner(sent, 1 << place)]
    total = parts[0][0].astype(f32)
    for part in parts[1:]:
        total = total + part[0].astype(f32)
    return total


def shards(
    small_tokens,
    large_tokens,
    small_cot,
    large_cot,
    live_counts,
    master,
    first_moment,
    second_moment,
):
    count = lax.axis_size("branch") * lax.axis_size("dp")
    bits = lax.axis_size("dp").bit_length() - 1
    plan = grid_plan(count)
    core, mine = lax.axis_index("branch"), lax.axis_index("dp")
    where = jnp.stack([core, mine]).astype(jnp.int32)
    index = lax.axis_index(("branch", "dp"))
    size = master.shape[0]
    rows = plan["shard_rows"]
    table = lax.dynamic_index_in_dim(jnp.asarray(plan["table"]), index, 0, False)
    padded = jnp.pad(master, (0, rows * LANES - size)).reshape(rows, LANES)
    keep, send = align(where, table, padded, plan)
    got = swap(send)
    near = gather_lines(jnp.where(core == 0, keep, got)[None], bits - 1, 1)
    far = tie(jnp.where(core == 0, got, keep)[None], near)
    middle = (bits + 1) // 2
    far = gather_lines(far, bits - 1, middle)
    near = tie(gather_middle(near), far)
    near_end = side_partner(near, 0)
    far = gather_lines(far, middle, 1)
    near_end = tie(near_end, far)
    near_pieces = (near, near_end, swap(near), swap(near_end))

    counts = live_counts[:, 0]
    own_count = lax.dynamic_slice_in_dim(counts, core, 1)
    far_count = lax.dynamic_slice_in_dim(counts, 1 - core, 1)
    crops, length_s = small_tokens.shape[1], small_tokens.shape[2]
    length_l = large_tokens.shape[2]
    tall_s, tall_l = round_up(length_s, 16), round_up(length_l, 16)
    pair = 2

    def taller(value, length, tall):
        return jnp.pad(value[0], ((0, 0), (0, tall - length), (0, 0)))

    small = taller(small_tokens, length_s, tall_s)
    large = taller(large_tokens, length_l, tall_l)
    small_seed = taller(small_cot, length_s, tall_s)
    large_seed = taller(large_cot, length_l, tall_l)
    slots = jnp.arange(crops, dtype=jnp.int32)[:, None]
    ret_small = jnp.where(slots < own_count, small_cot[0, :, 0], 0)
    ret_large = jnp.where(slots < far_count, large_cot[0, :, 0], 0)
    ret_small, ret_large = swap(ret_small), swap(ret_large)

    params = unflatten(where, near_pieces, plan, 0, bits)
    straddling = params.pop(plan["sides"][1][0][0])
    far = tie(far, near_end)
    far = jnp.concatenate([far, tie(side_partner(far, 1), params["s_ln1"])], 0)
    *kept_s, head_s = block_forward(tie(small, far), params, "s", length_s, pair)
    far_end = side_partner(far, 0)
    kept_l = attention_only(tie(large, far_end), params, "l", length_l, pair)
    far_pieces = (far, far_end, swap(far), swap(far_end))
    params.update(unflatten(where, far_pieces, plan, 1, bits, (straddling,)))
    z_l, slope_l, y_l, head_l, sent_l, sent_s = mlp_only(
        kept_l[4], kept_l[5], head_s, params, "l", "s", crops, pair
    )
    got_s, got_l = swap(sent_s), swap(sent_l)
    grads = {}
    back_s, gsent_s, gj_l, part = cross(got_s, y_l, ret_small, params, "s", length_l, tall_l)
    grads.update(part)
    home_s, own_s = swap(back_s), swap(gsent_s)
    back_l, gsent_l, gj_s, part = cross(got_l, kept_s[8], ret_large, params, "l", length_s, tall_s)
    grads.update(part)
    home_l, own_l = swap(back_l), swap(gsent_l)
    large_out, gmid, ghead_s, part = mlp_back(
        large_seed,
        far_count,
        (kept_l[4], kept_l[5], z_l, slope_l, y_l),
        gj_l,
        (head_l, own_l),
        (head_s, own_s),
        home_l,
        params,
        "l",
        "s",
        length_l,
        pair,
    )
    grads.update(part)
    sent, far_side = reduce_start(*flatten(where, grads, plan, 1, bits))
    gmid = tie(gmid, sent)
    large_grad, part = attention_back(large, gmid, kept_l[:4], params, "l", length_l, pair)
    grads.update(part)
    sent, far_side = reduce_middle(far_side)
    ghead_s = tie(ghead_s, sent, gmid)
    small_out, small_grad, part = block_back(
        small, small_seed, own_count, kept_s, gj_s, ghead_s, home_s, params, "s", length_s, pair
    )
    grads.update(part)
    grads["s_ln1"] = tie(grads["s_ln1"], far_side[-1])
    near_side = reduce_start(*flatten(where, grads, plan, 0, bits))[1]
    far_total = reduce_lines(far_side, bits)
    near_side = reduce_middle(near_side)[1]
    near_total = reduce_lines(near_side, bits)
    own = jnp.where(core == 0, near_total, far_total)
    got = swap(jnp.where(core == 0, far_total, near_total))
    summed, square = unalign(where, table, own, got, plan)
    square = square + swap(square)
    for place in range(bits):
        square = square + partner(square, 1 << place)
    grad_norm = jnp.sqrt(square[0, 0])
    own_grad = summed.reshape(-1)[:size]
    clipped = own_grad * jnp.minimum(1.0, clip_norm / grad_norm)
    new_first = beta_one * first_moment + (1.0 - beta_one) * clipped
    new_second = beta_two * second_moment + (1.0 - beta_two) * clipped * clipped
    new_master = master - rate * (
        new_first / bias_one / (jnp.sqrt(new_second / bias_two) + adam_eps) + decay * master
    )
    return (
        small_out,
        large_out,
        small_grad,
        large_grad,
        grad_norm,
        new_first,
        new_second,
        new_master,
        new_master.astype(bf16),
    )


def solution(mesh):
    return jax.shard_map(
        shards,
        mesh=mesh,
        in_specs=(
            P("branch", "dp", None, None),
            P("branch", "dp", None, None),
            P("branch", "dp", None, None),
            P("branch", "dp", None, None),
            P(None, "dp"),
            P(("branch", "dp")),
            P(("branch", "dp")),
            P(("branch", "dp")),
        ),
        out_specs=(
            P("branch", "dp", None, None),
            P("branch", "dp", None, None),
            P("branch", "dp", None, None),
            P("branch", "dp", None, None),
            P(),
            P(("branch", "dp")),
            P(("branch", "dp")),
            P(("branch", "dp")),
            P(("branch", "dp")),
        ),
        check_vma=False,
    )
```

```python
import functools
import math

import jax
import jax.numpy as jnp
import numpy as np
from jax import lax
from jax.experimental import pallas as pl
from jax.experimental.pallas import tpu as pltpu
from jax.sharding import PartitionSpec as P

DS = 192
DL = 384
MS = 768
ML = 1536
HEADS = 6

norm_eps = 1e-06
clip_norm = 1.0
beta_one = 0.5
beta_two = 0.5
adam_eps = 1e-08
rate = 0.05
decay = 0.05
bias_one = 1.0 - 0.5**5
bias_two = 1.0 - 0.5**5

f32 = jnp.float32
bf16 = jnp.bfloat16
LANES = 128


def layout():
    shapes = []
    for label, width, hidden in (("s", DS, MS), ("l", DL, ML)):
        shapes += [
            (label + "_ln1", (2, width)),
            (label + "_qkv_w", (width, 3 * width)),
            (label + "_qkv_b", (3 * width,)),
            (label + "_proj_w", (width, width)),
            (label + "_proj_b", (width,)),
            (label + "_ln2", (2, width)),
            (label + "_fc1_w", (width, hidden)),
            (label + "_fc1_b", (hidden,)),
            (label + "_fc2_w", (hidden, width)),
            (label + "_fc2_b", (width,)),
        ]
    for label, owner, other in (("s", DS, DL), ("l", DL, DS)):
        shapes += [
            (label + "_to_ln", (2, owner)),
            (label + "_to_w", (owner, other)),
            (label + "_to_b", (other,)),
            (label + "_ca_ln", (2, other)),
            (label + "_ca_q_w", (other, other)),
            (label + "_ca_q_b", (other,)),
            (label + "_ca_k_w", (other, other)),
            (label + "_ca_v_w", (other, other)),
            (label + "_ca_v_b", (other,)),
            (label + "_ca_o_w", (other, other)),
            (label + "_ca_o_b", (other,)),
            (label + "_back_ln", (2, other)),
            (label + "_back_w", (other, owner)),
            (label + "_back_b", (owner,)),
        ]
    return shapes


def round_up(value, unit):
    return -(-value // unit) * unit


def grid_plan(shards):
    names = []
    regions = []
    offset = 0
    for label, shape in layout():
        count = math.prod(shape)
        phase = offset % LANES
        if not regions or regions[-1][2] != phase:
            regions.append([offset, offset, phase])
        names.append((label, shape, offset, len(regions) - 1))
        offset += count
        regions[-1][1] = offset
    total = offset
    starts = []
    row = 0
    for first, last, phase in regions:
        starts.append(row)
        row += -(-(last - first) // LANES)
    rows = row
    places = {}
    for label, shape, place, region in names:
        places[label] = (starts[region] + (place - regions[region][0]) // LANES, shape)
    size = total // shards
    bases = []
    pieces = []
    for device in range(shards):
        low, high = device * size, (device + 1) * size
        own = []
        base = None
        for (first, last, phase), start in zip(regions, starts):
            left, right = max(low, first), min(high, last)
            if left >= right:
                continue
            if base is None:
                base = (start + (left - first) // LANES) // 16 * 16
            delta = start * LANES - first + low - base * LANES
            own.append((left - low, right - low, delta))
        bases.append(base)
        pieces.append(own)
    most = max(len(own) for own in pieces)
    table = np.zeros((shards, most * 3), np.int32)
    need = 0
    for device, own in enumerate(pieces):
        for number, (left, right, delta) in enumerate(own):
            table[device, 3 * number : 3 * number + 3] = (left, right, delta)
            need = max(need, right + delta)
    span = round_up(-(-need // LANES), 32)
    overlap = 16
    for device in range(1, shards):
        overlap = max(overlap, bases[device - 1] + span - bases[device])
    half = shards // 2
    edge = half * size
    sides = [[], []]
    for label, shape, place, region in names:
        if place < edge:
            sides[0].append((label, shape))
        if place + math.prod(shape) > edge:
            sides[1].append((label, shape))
    origins = [0, min(bases[half], places[sides[1][0][0]][0]) // 16 * 16]
    heights = []
    for side in range(2):
        last = bases[half * (side + 1) - 1] + span
        for label, shape in sides[side]:
            last = max(last, places[label][0] + -(-math.prod(shape) // LANES))
        heights.append(round_up(last - origins[side] + overlap, 16))
    return dict(
        places=places,
        rows=rows,
        half=half,
        sides=sides,
        origins=origins,
        heights=heights,
        size=size,
        bases=bases,
        table=table,
        most=most,
        span=span,
        overlap=overlap,
        shard_rows=round_up(-(-size // LANES), 16),
    )


def mm(left, right):
    return lax.dot_general(left, right, (((1,), (0,)), ((), ())), preferred_element_type=f32)


def mm_t(left, right):
    return lax.dot_general(left, right, (((1,), (1,)), ((), ())), preferred_element_type=f32)


def t_mm(left, right):
    return lax.dot_general(left, right, (((0,), (0,)), ((), ())), preferred_element_type=f32)


def vmem_spec(shape, index):
    return pl.BlockSpec(shape, index)


def whole(shape):
    rank = len(shape)
    return pl.BlockSpec(shape, lambda *_: (0,) * rank, pipeline_mode=pl.Buffered(1))


def estimate(flops, moved):
    return pl.CostEstimate(flops=int(flops), bytes_accessed=int(moved), transcendentals=0)


def shift_rows(ref, amount, rows, margin):
    down = amount // LANES
    across = amount - down * LANES
    here = ref[pl.ds(margin - down, rows), :]
    above = ref[pl.ds(margin - down - 1, rows), :]
    here = pltpu.roll(here, across, 1)
    above = pltpu.roll(above, across, 1)
    lane = lax.broadcasted_iota(jnp.int32, here.shape, 1)
    return jnp.where(lane < across, above, here)


def align_kernel(most, rows, span, margin, core_ref, table_ref, shard_ref, keep_ref, send_ref, padded):
    padded[...] = jnp.zeros_like(padded)
    padded[margin : margin + rows, :] = shard_ref[...]
    place = lax.broadcasted_iota(jnp.int32, (span, LANES), 0) * LANES
    place = place + lax.broadcasted_iota(jnp.int32, (span, LANES), 1)
    total = jnp.zeros((span, LANES), f32)
    for number in range(most):
        left = table_ref[3 * number]
        right = table_ref[3 * number + 1]
        delta = table_ref[3 * number + 2]
        moved = shift_rows(padded, delta, span, margin)
        total = jnp.where((place >= left + delta) & (place < right + delta), moved, total)
    total = total.astype(bf16)
    first = core_ref[0] == 0
    upper, lower = total[: span // 2], total[span // 2 :]
    keep_ref[...] = jnp.where(first, upper, lower)
    send_ref[...] = jnp.where(first, lower, upper)


def unalign_kernel(
    most, rows, span, margin, core_ref, table_ref, own_ref, got_ref, out_ref, norm_ref, padded
):
    first = core_ref[0] == 0
    padded[span:, :] = jnp.zeros((padded.shape[0] - span, LANES), f32)
    padded[0 : span // 2, :] = jnp.where(first, own_ref[...], got_ref[...])
    padded[span // 2 : span, :] = jnp.where(first, got_ref[...], own_ref[...])
    place = lax.broadcasted_iota(jnp.int32, (rows, LANES), 0) * LANES
    place = place + lax.broadcasted_iota(jnp.int32, (rows, LANES), 1)
    total = jnp.zeros((rows, LANES), f32)
    lane = lax.broadcasted_iota(jnp.int32, (rows, LANES), 1)
    for number in range(most):
        left = table_ref[3 * number]
        right = table_ref[3 * number + 1]
        delta = table_ref[3 * number + 2]
        down = delta // LANES
        across = delta - down * LANES
        back = lax.rem(LANES - across, LANES)
        here = pltpu.roll(padded[pl.ds(down, rows), :], back, 1)
        below = pltpu.roll(padded[pl.ds(down + 1, rows), :], back, 1)
        moved = jnp.where(lane < LANES - across, here, below)
        total = jnp.where((place >= left) & (place < right), moved, total)
    out_ref[...] = total
    norm_ref[...] = jnp.broadcast_to(jnp.sum(total * total).reshape(1, 1), (8, LANES))


def align(core, table, shard, plan):
    rows, span, most = plan["shard_rows"], plan["span"], plan["most"]
    margin = 8 + round_up(int(plan["table"].max(initial=0, where=pick_delta(plan))) // LANES + 1, 8)
    tall = margin + max(rows, span) + 8
    vmem = pl.BlockSpec(memory_space=pltpu.VMEM)
    smem = pl.BlockSpec(memory_space=pltpu.SMEM)
    part = jax.ShapeDtypeStruct((span // 2, LANES), bf16)
    return pl.pallas_call(
        functools.partial(align_kernel, most, rows, span, margin),
        out_shape=(part, part),
        in_specs=[smem, smem, vmem],
        out_specs=(vmem, vmem),
        scratch_shapes=[pltpu.VMEM((tall, LANES), f32)],
        cost_estimate=estimate(1_000_000, 1_000_000),
        name="align",
    )(core, table, shard)


def unalign(core, table, own, got, plan):
    rows, span, most = plan["shard_rows"], plan["span"], plan["most"]
    margin = 16 + round_up(int(plan["table"].max(initial=0, where=pick_delta(plan))) // LANES + 1, 8)
    tall = max(rows, span) + margin
    vmem = pl.BlockSpec(memory_space=pltpu.VMEM)
    smem = pl.BlockSpec(memory_space=pltpu.SMEM)
    return pl.pallas_call(
        functools.partial(unalign_kernel, most, rows, span, margin),
        out_shape=(
            jax.ShapeDtypeStruct((rows, LANES), f32),
            jax.ShapeDtypeStruct((8, LANES), f32),
        ),
        in_specs=[smem, smem, vmem, vmem],
        out_specs=(vmem, vmem),
        scratch_shapes=[pltpu.VMEM((tall, LANES), f32)],
        cost_estimate=estimate(1_000_000, 1_000_000),
        name="unalign",
    )(core, table, own, got)


def pick_delta(plan):
    mask = np.zeros(plan["table"].shape, bool)
    mask[:, 2::3] = True
    return mask


def two_dim(shape):
    return shape if len(shape) == 2 else (1, shape[0])


def is_matrix(label):
    return label[-2:] == "_w"


def strided(start, count, step):
    return pl.ds(start, count) if step == 1 or count == 1 else pl.ds(start, count, stride=step)


def half_swap(value):
    return pltpu.roll(value, LANES // 2, 1)


def read_param(flat, row, shape, out_ref, pair_ref):
    depth, width = two_dim(shape)
    dtype = out_ref.dtype
    if width % LANES == 0:
        step = width // LANES
        for col in range(step):
            out_ref[:, col * LANES : (col + 1) * LANES] = flat[
                strided(row + col, depth, step), :
            ].astype(dtype)
        return
    half = LANES // 2
    lead = width // LANES
    if depth == 1:
        for col in range(lead):
            out_ref[:, col * LANES : (col + 1) * LANES] = flat[row + col : row + col + 1, :].astype(
                dtype
            )
        out_ref[:, lead * LANES :] = flat[row + lead : row + lead + 1, 0:half].astype(dtype)
        return
    step = 2 * width // LANES
    pairs = depth // 2
    lane = lax.broadcasted_iota(jnp.int32, (pairs, LANES), 1)
    blocks = [flat[strided(row + col, pairs, step), :] for col in range(step)]
    turned = [half_swap(block) for block in blocks[lead:]]
    for col in range(lead):
        pair_ref[col, strided(0, pairs, 2), :] = blocks[col]
        pair_ref[col, strided(1, pairs, 2), :] = jnp.where(lane < half, turned[col], turned[col + 1])
    pair_ref[lead, strided(0, pairs, 2), :] = blocks[lead]
    pair_ref[lead, strided(1, pairs, 2), :] = turned[lead]
    for col in range(lead):
        out_ref[:, col * LANES : (col + 1) * LANES] = pair_ref[col, 0:depth, :].astype(dtype)
    out_ref[:, lead * LANES :] = pair_ref[lead, 0:depth, 0:half].astype(dtype)


def write_param(flat, row, shape, in_ref, pair_ref):
    depth, width = two_dim(shape)
    if width % LANES == 0:
        step = width // LANES
        for col in range(step):
            flat[strided(row + col, depth, step), :] = in_ref[:, col * LANES : (col + 1) * LANES]
        return
    half = LANES // 2
    lead = width // LANES
    if depth == 1:
        for col in range(lead):
            flat[row + col : row + col + 1, :] = in_ref[:, col * LANES : (col + 1) * LANES]
        tail = jnp.concatenate([in_ref[:, lead * LANES :], jnp.zeros((1, half), f32)], 1)
        flat[row + lead : row + lead + 1, :] = tail
        return
    step = 2 * width // LANES
    pairs = depth // 2
    lane = lax.broadcasted_iota(jnp.int32, (pairs, LANES), 1)
    for col in range(lead):
        pair_ref[col, 0:depth, :] = in_ref[:, col * LANES : (col + 1) * LANES]
    pair_ref[lead, 0:depth, 0:half] = in_ref[:, lead * LANES :]
    even = [pair_ref[col, strided(0, pairs, 2), :] for col in range(lead + 1)]
    odd = [half_swap(pair_ref[col, strided(1, pairs, 2), :]) for col in range(lead + 1)]
    for col in range(lead):
        flat[strided(row + col, pairs, step), :] = even[col]
    flat[strided(row + lead, pairs, step), :] = jnp.where(lane < half, even[lead], odd[0])
    for col in range(lead):
        flat[strided(row + lead + 1 + col, pairs, step), :] = jnp.where(
            lane < half, odd[col], odd[col + 1]
        )


def decode(number, core, bits):
    first = (number >> (bits - 1)) & 1
    second = (number >> (bits - 2)) & 1
    found = (first << core) | (second << (1 - core))
    for place in range(2, bits):
        found = found | (((number >> (bits - 1 - place)) & 1) << place)
    return found


def unflatten_kernel(plan, side, bits, where_ref, base_ref, *refs):
    pieces, refs = refs[:4], refs[4:]
    carried, refs = (refs[:1], refs[1:]) if side else ((), refs)
    outs, (flat, pair_ref) = refs[:-2], refs[-2:]
    span, overlap, half = plan["span"], plan["overlap"], plan["half"]
    origin = plan["origins"][side]
    core, mine = where_ref[0], where_ref[1]
    lead = plan["bases"][side * half] - origin
    if lead:
        flat[0:lead, :] = jnp.zeros((lead, LANES), f32)
    last = plan["bases"][side * half + half - 1] - origin + span
    if flat.shape[0] > last:
        flat[last:, :] = jnp.zeros((flat.shape[0] - last, LANES), f32)

    def base_of(owner):
        return pl.multiple_of(base_ref[side * half + owner] - origin, 16)

    def clear(owner, carry):
        base = base_of(owner)
        flat[pl.ds(base, overlap), :] = jnp.zeros((overlap, LANES), f32)
        flat[pl.ds(base + span - overlap, overlap), :] = jnp.zeros((overlap, LANES), f32)
        return carry

    lax.fori_loop(0, half, clear, 0)
    middle = span // 2
    for number, piece in enumerate(pieces):
        theirs = number // 2
        owner_core = core if theirs == 0 else 1 - core
        upper = number % 2 * (half // 2)
        for part in range(2):

            @pl.when(owner_core == part)
            def _(part=part, piece=piece, upper=upper):
                def place(entry, carry):
                    base = base_of(decode(entry + upper, part, bits) ^ mine)
                    value = piece[entry].astype(f32)
                    if part == 0:
                        flat[pl.ds(base, overlap), :] += value[:overlap]
                        flat[pl.ds(base + overlap, middle - overlap), :] = value[overlap:]
                    else:
                        flat[pl.ds(base + middle, middle - overlap), :] = value[: middle - overlap]
                        flat[pl.ds(base + span - overlap, overlap), :] += value[middle - overlap :]
                    return carry

                lax.fori_loop(0, half // 2, place, 0)

    for number, ((label, shape), out_ref) in enumerate(zip(plan["sides"][side], outs)):
        read_param(flat, plan["places"][label][0] - origin, shape, out_ref, pair_ref)
        if side and number == 0:
            out_ref[...] += carried[0][...]


def unflatten(where, pieces, plan, side, bits, carried=()):
    outs = []
    for label, shape in plan["sides"][side]:
        outs.append(jax.ShapeDtypeStruct(two_dim(shape), bf16 if is_matrix(label) else f32))
    vmem = pl.BlockSpec(memory_space=pltpu.VMEM)
    smem = pl.BlockSpec(memory_space=pltpu.SMEM)
    values = pl.pallas_call(
        functools.partial(unflatten_kernel, plan, side, bits),
        out_shape=outs,
        in_specs=[smem, smem] + [vmem] * (len(pieces) + len(carried)),
        out_specs=[vmem] * len(outs),
        scratch_shapes=[
            pltpu.VMEM((plan["heights"][side], LANES), f32),
            pltpu.VMEM((5, MS, LANES), f32),
        ],
        cost_estimate=estimate(1_000_000, 8_000_000),
        name="unflatten" + str(side),
    )(where, jnp.asarray(plan["bases"], jnp.int32), *pieces, *carried)
    return {label: value for (label, shape), value in zip(plan["sides"][side], values)}


def flatten_kernel(plan, side, bits, where_ref, base_ref, *refs):
    count = len(plan["sides"][side])
    grads, (low_ref, high_ref, send_ref, flat, pair_ref) = refs[:count], refs[count:]
    span, half, origin = plan["span"], plan["half"], plan["origins"][side]
    core, mine = where_ref[0], where_ref[1]
    first, last = None, 0
    for (label, shape), ref in zip(plan["sides"][side], grads):
        row = plan["places"][label][0] - origin
        first = row if first is None else first
        last = row + -(-math.prod(shape) // LANES)
    if first:
        flat[0:first, :] = jnp.zeros((first, LANES), f32)
    flat[last // 8 * 8 :, :] = jnp.zeros((flat.shape[0] - last // 8 * 8, LANES), f32)
    for (label, shape), ref in zip(plan["sides"][side], grads):
        write_param(flat, plan["places"][label][0] - origin, shape, ref, pair_ref)

    def rows_of(entry, part):
        owner = decode(entry, part, bits) ^ mine
        base = base_ref[side * half + owner] - origin + part * (span // 2)
        return flat[pl.ds(pl.multiple_of(base, 16), span // 2), :].astype(bf16)

    def place(entry, carry):
        low_ref[entry] = rows_of(entry, core)
        high_ref[entry] = rows_of(entry + half // 2, core)
        send_ref[entry] = rows_of(entry, 1 - core)
        send_ref[entry + half // 2] = rows_of(entry + half // 2, 1 - core)
        return carry

    lax.fori_loop(0, half // 2, place, 0)


def flatten(where, grads, plan, side, bits):
    vmem = pl.BlockSpec(memory_space=pltpu.VMEM)
    smem = pl.BlockSpec(memory_space=pltpu.SMEM)
    half, rows = plan["half"], plan["span"] // 2
    values = [grads[label] for label, shape in plan["sides"][side]]
    return pl.pallas_call(
        functools.partial(flatten_kernel, plan, side, bits),
        out_shape=(
            jax.ShapeDtypeStruct((half // 2, rows, LANES), bf16),
            jax.ShapeDtypeStruct((half // 2, rows, LANES), bf16),
            jax.ShapeDtypeStruct((half, rows, LANES), bf16),
        ),
        in_specs=[smem, smem] + [vmem] * len(values),
        out_specs=(vmem, vmem, vmem),
        scratch_shapes=[
            pltpu.VMEM((plan["heights"][side], LANES), f32),
            pltpu.VMEM((5, MS, LANES), f32),
        ],
        cost_estimate=estimate(1_000_000, 10_000_000),
        name="flatten" + str(side),
    )(where, jnp.asarray(plan["bases"], jnp.int32), *values)


def ln_parts(value):
    mean = jnp.mean(value, -1, keepdims=True)
    centred = value - mean
    variance = jnp.mean(centred * centred, -1, keepdims=True)
    inverse = lax.rsqrt(variance + norm_eps)
    return centred * inverse, inverse


def ln_back(grad, hat, inverse, gain):
    scaled = grad * gain
    first = jnp.mean(scaled, -1, keepdims=True)
    second = jnp.mean(scaled * hat, -1, keepdims=True)
    return inverse * (scaled - first - hat * second)


def gelu_parts(value):
    cdf = 0.5 + 0.5 * lax.erf(value * (2.0**-0.5))
    density = jnp.exp(value * value * -0.5) * (1.0 / math.sqrt(2.0 * math.pi))
    return value * cdf, cdf + value * density


def col_sum(value):
    return jnp.sum(value, 0, keepdims=True)


def groups(width):
    size = width // HEADS
    found = []
    for start in range(0, width, LANES):
        stop = min(start + LANES, width)
        found.append((start, stop, (stop - start) // size))
    return found, size


def stack_heads(value, count, size):
    lane = lax.broadcasted_iota(jnp.int32, value.shape, 1)
    zero = jnp.zeros_like(value)
    return jnp.concatenate(
        [
            jnp.where((lane >= head * size) & (lane < (head + 1) * size), value, zero)
            for head in range(count)
        ],
        0,
    )


def merge_heads(value, count, size):
    rows = value.shape[0] // count
    lane = lax.broadcasted_iota(jnp.int32, (rows, value.shape[1]), 1)
    merged = value[0:rows]
    for head in range(1, count):
        merged = jnp.where(lane >= head * size, value[head * rows : (head + 1) * rows], merged)
    return merged


def attention_forward(pair, length, tall, tokens, weights, keeps):
    ln1_ref, qkv_w, qkv_b, proj_w, proj_b, ln2_ref = weights
    a1_ref, qkv_ref, probs_ref, att_ref, mid_ref, n2_ref = keeps
    width = tokens.shape[-1]
    found, size = groups(width)
    scale = size ** (-0.5)
    hat, _ = ln_parts(tokens)
    a1 = (hat * ln1_ref[0:1, :] + ln1_ref[1:2, :]).astype(bf16)
    a1_ref[...] = a1
    qkv_ref[...] = (mm(a1, qkv_w[...]) + qkv_b[...]).astype(bf16)
    key_lane = lax.broadcasted_iota(jnp.int32, (1, tall), 1)
    bias = jnp.where(key_lane < length, 0.0, -1e30).astype(f32)
    for crop in range(pair):
        here = slice(crop * tall, (crop + 1) * tall)
        for start, stop, count in found:
            query = stack_heads(qkv_ref[here, start:stop], count, size)
            key = qkv_ref[here, width + start : width + stop]
            value = qkv_ref[here, 2 * width + start : 2 * width + stop]
            scores = mm_t(query, key) * scale + bias
            summit = jnp.max(scores, -1, keepdims=True)
            weights = jnp.exp(scores - summit)
            probs = (weights / jnp.sum(weights, -1, keepdims=True)).astype(bf16)
            first = start // size
            for head in range(count):
                probs_ref[crop, first + head] = probs[head * tall : (head + 1) * tall]
            att_ref[here, start:stop] = merge_heads(mm(probs, value), count, size).astype(bf16)
    mid = tokens + mm(att_ref[...], proj_w[...]) + proj_b[...]
    mid_ref[...] = mid
    hat, _ = ln_parts(mid)
    n2_ref[...] = (hat * ln2_ref[0:1, :] + ln2_ref[1:2, :]).astype(bf16)


def mlp_forward(chunk, mid_ref, n2_ref, weights, keeps):
    fc1_w, fc1_b, fc2_w, fc2_b = weights
    z_ref, slope_ref, y_ref = keeps
    y_ref[...] = mid_ref[...] + fc2_b[...]
    for number in range(fc1_w.shape[1] // chunk):
        cols = slice(number * chunk, (number + 1) * chunk)
        inner = mm(n2_ref[...], fc1_w[:, cols]) + fc1_b[:, cols]
        active, slope = gelu_parts(inner)
        z_ref[:, cols] = active.astype(bf16)
        slope_ref[:, cols] = slope.astype(bf16)
        y_ref[...] += mm(z_ref[:, cols], fc2_w[cols, :])


def keep_heads(pair, tall, y_ref, head_ref):
    for crop in range(pair):
        slot = pl.program_id(0) * pair + crop
        head_ref[pl.ds(slot, 1), :] = y_ref[crop * tall : crop * tall + 1, :]


def carry(value, norm, weight, bias):
    hat, _ = ln_parts(value)
    active, _ = gelu_parts(hat * norm[0:1, :] + norm[1:2, :])
    return (mm(active.astype(bf16), weight[...]) + bias[...]).astype(bf16)


def attention_kernel(pair, length, tall, tok_ref, *refs):
    tokens = tok_ref[...].reshape(pair * tall, tok_ref.shape[-1]).astype(f32)
    attention_forward(pair, length, tall, tokens, refs[:6], refs[6:])


def block_kernel(pair, length, tall, chunk, tok_ref, *refs):
    tokens = tok_ref[...].reshape(pair * tall, tok_ref.shape[-1]).astype(f32)
    attention_forward(pair, length, tall, tokens, refs[:6], refs[10:16])
    mlp_forward(chunk, refs[14], refs[15], refs[6:10], refs[16:19])
    keep_heads(pair, tall, refs[18], refs[19])


def mlp_kernel(pair, tall, chunk, mid_ref, n2_ref, *refs):
    weights, heads, (far_head, *far), near = refs[:4], None, refs[4:8], refs[8:11]
    z_ref, slope_ref, y_ref, head_ref, near_ref, far_ref = refs[11:]
    mlp_forward(chunk, mid_ref, n2_ref, weights, (z_ref, slope_ref, y_ref))
    keep_heads(pair, tall, y_ref, head_ref)

    @pl.when(pl.program_id(0) == pl.num_programs(0) - 1)
    def _():
        near_ref[...] = carry(head_ref[...], *near)
        far_ref[...] = carry(far_head[...], *far)


ATTENTION = ("ln1", "qkv_w", "qkv_b", "proj_w", "proj_b", "ln2")
MLP = ("fc1_w", "fc1_b", "fc2_w", "fc2_b")
TO = ("to_ln", "to_w", "to_b")


def pick(params, label, names):
    return [params[label + "_" + name] for name in names]


def row_spec(rows, cols):
    return pl.BlockSpec((rows, cols), lambda i: (i, 0))


def fixed_spec(shape):
    rank = len(shape)
    return pl.BlockSpec(shape, lambda i: (0,) * rank)


def kept_outs(crops, tall, width, hidden, pair):
    rows, flat = pair * tall, crops * tall

    def entry(cols, dtype):
        return row_spec(rows, cols), jax.ShapeDtypeStruct((flat, cols), dtype)

    attention = [
        entry(width, bf16),
        entry(3 * width, bf16),
        (
            pl.BlockSpec((pair, HEADS, tall, tall), lambda i: (i, 0, 0, 0)),
            jax.ShapeDtypeStruct((crops, HEADS, tall, tall), bf16),
        ),
        entry(width, bf16),
        entry(width, f32),
        entry(width, bf16),
    ]
    mlp = [
        entry(hidden, bf16),
        entry(hidden, bf16),
        entry(width, f32),
        (fixed_spec((crops, width)), jax.ShapeDtypeStruct((crops, width), f32)),
    ]
    return attention, mlp


def block_forward(tokens, params, label, length, pair):
    crops, tall, width = tokens.shape
    hidden = params[label + "_fc1_w"].shape[1]
    weights = pick(params, label, ATTENTION + MLP)
    attention, mlp = kept_outs(crops, tall, width, hidden, pair)
    outs = attention + mlp
    flops = 2 * crops * tall * (4 * width * width + 2 * width * hidden)
    return pl.pallas_call(
        functools.partial(block_kernel, pair, length, tall, 384),
        grid=(crops // pair,),
        out_shape=[shape for spec, shape in outs],
        in_specs=[pl.BlockSpec((pair, tall, width), lambda i: (i, 0, 0))]
        + [whole(value.shape) for value in weights],
        out_specs=[spec for spec, shape in outs],
        cost_estimate=estimate(8 * flops, 10_000_000),
        name="block_" + label,
    )(tokens, *weights)


def attention_only(tokens, params, label, length, pair):
    crops, tall, width = tokens.shape
    weights = pick(params, label, ATTENTION)
    outs, _ = kept_outs(crops, tall, width, width, pair)
    flops = 2 * crops * tall * 4 * width * width
    return pl.pallas_call(
        functools.partial(attention_kernel, pair, length, tall),
        grid=(crops // pair,),
        out_shape=[shape for spec, shape in outs],
        in_specs=[pl.BlockSpec((pair, tall, width), lambda i: (i, 0, 0))]
        + [whole(value.shape) for value in weights],
        out_specs=[spec for spec, shape in outs],
        cost_estimate=estimate(8 * flops, 20_000_000),
        name="attention_" + label,
    )(tokens, *weights)


def mlp_only(mid, n2, far_head, params, label, far, crops, pair):
    flat, width = mid.shape
    tall = flat // crops
    rows = pair * tall
    hidden = params[label + "_fc1_w"].shape[1]
    weights = pick(params, label, MLP)
    extra = [far_head] + pick(params, far, TO) + pick(params, label, TO)
    _, outs = kept_outs(crops, tall, width, hidden, pair)
    for name in (label, far):
        shape = (crops, params[name + "_to_w"].shape[1])
        outs.append((fixed_spec(shape), jax.ShapeDtypeStruct(shape, bf16)))
    flops = 2 * flat * 2 * width * hidden
    return pl.pallas_call(
        functools.partial(mlp_kernel, pair, tall, 384),
        grid=(crops // pair,),
        out_shape=[shape for spec, shape in outs],
        in_specs=[row_spec(rows, width), row_spec(rows, width)]
        + [whole(value.shape) for value in weights + extra],
        out_specs=[spec for spec, shape in outs],
        cost_estimate=estimate(8 * flops, 20_000_000),
        name="mlp_" + label,
    )(mid, n2, *weights, *extra)


def cross_kernel(
    length,
    tall,
    crops,
    sent_ref,
    y_ref,
    gret_ref,
    ca_ln,
    q_w,
    q_b,
    k_w,
    v_w,
    v_b,
    o_w,
    o_b,
    back_ln,
    back_w,
    back_b,
    returned_ref,
    gsent_ref,
    gj_ref,
    d_ca_ln,
    d_q_w,
    d_q_b,
    d_k_w,
    d_v_w,
    d_v_b,
    d_o_w,
    d_o_b,
    d_back_ln,
    d_back_w,
    d_back_b,
    sent_f,
    n_all,
    score_all,
    mates_all,
    pairs_all,
    gn_head,
    gj_head,
):
    width = y_ref.shape[1]
    size = width // HEADS
    scale = size ** (-0.5)
    stacked = crops * 8
    lane = lax.broadcasted_iota(jnp.int32, (8, width), 1)
    head = lax.broadcasted_iota(jnp.int32, (8, width), 0)
    own_head = (lane >= head * size) & (lane < (head + 1) * size)
    row = lax.broadcasted_iota(jnp.int32, (tall, 1), 0)
    key_lane = lax.broadcasted_iota(jnp.int32, (1, tall), 1)
    bias = jnp.where(key_lane < length, 0.0, -1e30).astype(f32)
    gain, shift = ca_ln[0:1, :], ca_ln[1:2, :]
    sent_f[...] = sent_ref[...].astype(f32)
    hat, _ = ln_parts(sent_f[...])
    n_head = (hat * gain + shift).astype(bf16)

    def spread(value):
        return jnp.concatenate(
            [jnp.where(own_head, value[crop : crop + 1], 0.0) for crop in range(crops)], 0
        )

    def gathered(value):
        return jnp.concatenate(
            [
                col_sum(jnp.where(own_head, value[crop * 8 : crop * 8 + 8], 0.0))
                for crop in range(crops)
            ],
            0,
        )

    def normed_of(crop):
        return n_all[crop * tall : (crop + 1) * tall, :]

    def against(value):
        return jnp.concatenate(
            [
                mm_t(value[crop * 8 : crop * 8 + 8].astype(bf16), normed_of(crop))
                for crop in range(crops)
            ],
            0,
        )

    def mixed(value):
        return jnp.concatenate(
            [
                mm(value[crop * 8 : crop * 8 + 8].astype(bf16), normed_of(crop))
                for crop in range(crops)
            ],
            0,
        )

    query = spread((mm(n_head, q_w[...]) + q_b[...]).astype(bf16).astype(f32)).astype(bf16)
    keyed = mm_t(query, k_w[...]) * scale
    blank = jnp.zeros((8, width), f32)
    for crop in range(crops):
        mates_all[crop] = jnp.concatenate([keyed[crop * 8 : crop * 8 + 8], blank], 0).astype(bf16)

    def joined(crop):
        here = pl.ds(pl.multiple_of(crop * tall, 16), tall)
        return here, jnp.where(row == 0, sent_f[pl.ds(crop, 1), :], y_ref[here, :])

    def ahead(crop, carry):
        here, value = joined(crop)
        hat, _ = ln_parts(value)
        normed = (hat * gain + shift).astype(bf16)
        n_all[here, :] = normed
        score_all[pl.ds(crop, 1)] = mm_t(mates_all[crop], normed)[None, 0:8]
        return carry

    lax.fori_loop(0, crops, ahead, 0)
    scores = score_all[...].reshape(stacked, tall) + bias
    summit = jnp.max(scores, -1, keepdims=True)
    weights = jnp.exp(scores - summit)
    probs = weights / jnp.sum(weights, -1, keepdims=True)
    rounded = probs.astype(bf16).astype(f32)
    total = jnp.sum(rounded, -1, keepdims=True)
    mean_n = mixed(rounded).astype(bf16)
    attended = gathered(mm(mean_n, v_w[...]) + total * v_b[...]).astype(bf16)
    merged = sent_f[...] + mm(attended, o_w[...]) + o_b[...]
    hat, inverse = ln_parts(merged)
    active, slope = gelu_parts(hat * back_ln[0:1, :] + back_ln[1:2, :])
    active = active.astype(bf16)
    returned_ref[...] = (mm(active, back_w[...]) + back_b[...]).astype(bf16)
    gret = gret_ref[...]
    d_back_w[...] = t_mm(active, gret)
    d_back_b[...] = col_sum(gret.astype(f32))
    gact = mm_t(gret, back_w[...]) * slope
    d_back_ln[0:1, :] = col_sum(gact * hat)
    d_back_ln[1:2, :] = col_sum(gact)
    gfused = ln_back(gact, hat, inverse, back_ln[0:1, :])
    gfo = gfused.astype(bf16)
    d_o_w[...] = t_mm(attended, gfo)
    d_o_b[...] = col_sum(gfo.astype(f32))
    gatt = spread(mm_t(gfo, o_w[...]).astype(bf16).astype(f32))
    d_v_b[...] = col_sum(total * gatt)
    gbias = jnp.sum(gatt * v_b[...], -1, keepdims=True)
    gatt = gatt.astype(bf16)
    d_v_w[...] = t_mm(mean_n, gatt)
    valued = mm_t(gatt, v_w[...])
    gprobs = against(valued) + gbias
    inner = gprobs - jnp.sum(gprobs * probs, -1, keepdims=True)
    gscores = (probs * inner).astype(bf16).astype(f32)
    for crop in range(crops):
        part = slice(crop * 8, crop * 8 + 8)
        mates_all[crop] = jnp.concatenate([keyed[part], valued[part]], 0).astype(bf16)
        pairs_all[crop] = jnp.concatenate([gscores[part], rounded[part]], 0).astype(bf16)
    slid = (mixed(gscores) * scale).astype(bf16)
    d_k_w[...] = t_mm(slid, query)
    gq = gathered(mm(slid, k_w[...])).astype(bf16)
    d_q_w[...] = t_mm(n_head, gq)
    d_q_b[...] = col_sum(gq.astype(f32))
    gn_head[...] = mm_t(gq, q_w[...])
    d_ca_ln[...] = jnp.zeros_like(d_ca_ln)

    def finish(crop, carry):
        here, value = joined(crop)
        hat, inverse = ln_parts(value)
        gn = t_mm(pairs_all[crop], mates_all[crop])
        gn = gn + jnp.where(row == 0, gn_head[pl.ds(crop, 1), :], 0.0)
        d_ca_ln[0:1, :] += col_sum(gn * hat)
        d_ca_ln[1:2, :] += col_sum(gn)
        gj = ln_back(gn, hat, inverse, gain)
        gj_ref[here, :] = gj
        gj_head[pl.ds(crop, 1), :] = gj[0:1, :]
        return carry

    lax.fori_loop(0, crops, finish, 0)
    gsent_ref[...] = (gj_head[...] + gfused).astype(bf16)


def cross(sent, hosted, gret, params, label, length, tall):
    crops, width = sent.shape
    own = gret.shape[1]
    flat = crops * tall
    names = ("ca_ln", "ca_q_w", "ca_q_b", "ca_k_w", "ca_v_w", "ca_v_b", "ca_o_w", "ca_o_b")
    names = names + ("back_ln", "back_w", "back_b")
    weights = [params[label + "_" + name] for name in names]
    outs = [
        jax.ShapeDtypeStruct((crops, own), bf16),
        jax.ShapeDtypeStruct((crops, width), bf16),
        jax.ShapeDtypeStruct((flat, width), f32),
    ] + [jax.ShapeDtypeStruct(value.shape, f32) for value in weights]
    vmem = pl.BlockSpec(memory_space=pltpu.VMEM)
    small = pltpu.VMEM((crops, width), f32)
    values = pl.pallas_call(
        functools.partial(cross_kernel, length, tall, crops),
        out_shape=outs,
        in_specs=[vmem] * (3 + len(weights)),
        out_specs=[vmem] * len(outs),
        scratch_shapes=[
            small,
            pltpu.VMEM((flat, width), bf16),
            pltpu.VMEM((crops, 8, tall), f32),
            pltpu.VMEM((crops, 16, width), bf16),
            pltpu.VMEM((crops, 16, tall), bf16),
            small,
            small,
        ],
        cost_estimate=estimate(2 * flat * width * width * 2, 8_000_000),
        name="cross_" + label,
    )(sent, hosted, gret, *weights)
    grads = {label + "_" + name: value for name, value in zip(names, values[3:])}
    return values[0], values[1], values[2], grads


def head_backward(headrow_ref, gsent_ref, to_ln, to_w, d_to_ln, d_to_w, d_to_b, ghead_ref):
    hat, inverse = ln_parts(headrow_ref[...])
    active, slope = gelu_parts(hat * to_ln[0:1, :] + to_ln[1:2, :])
    gsent = gsent_ref[...]
    d_to_w[...] = t_mm(active.astype(bf16), gsent)
    d_to_b[...] = col_sum(gsent.astype(f32))
    gact = mm_t(gsent, to_w[...]) * slope
    d_to_ln[0:1, :] = col_sum(gact * hat)
    d_to_ln[1:2, :] = col_sum(gact)
    ghead_ref[...] = ln_back(gact, hat, inverse, to_ln[0:1, :])


def clear_all(refs):
    for ref in refs:
        ref[...] = jnp.zeros_like(ref)


def mlp_backward(pair, tall, chunk, live_ref, acts, weights, grads, out_ref, gy, gnormed):
    cot_ref, y_ref, gj_ref, mid_ref, n2_ref, z_ref, slope_ref, ghead, returned_ref = acts
    ln2_ref, fc1_w, fc2_w = weights
    d_ln2, d_fc1_w, d_fc1_b, d_fc2_w, d_fc2_b = grads
    length = out_ref.shape[2]
    row = lax.broadcasted_iota(jnp.int32, (tall, 1), 0)
    for crop in range(pair):
        here = slice(crop * tall, (crop + 1) * tall)
        slot = pl.program_id(0) * pair + crop
        live = jnp.where(slot < live_ref[0], 1.0, 0.0).astype(f32)
        seed = cot_ref[crop].astype(f32) * live + gj_ref[here, :]
        gy[here, :] = jnp.where(row == 0, ghead[pl.ds(slot, 1), :], seed)
        home = returned_ref[pl.ds(slot, 1), :]
        final = jnp.where(row == 0, home, y_ref[here, :])
        out_ref[0, crop] = final[0:length].astype(bf16)
    gm = gy[...].astype(bf16)
    d_fc2_b[...] += col_sum(gm.astype(f32))
    for number in range(fc1_w.shape[1] // chunk):
        cols = slice(number * chunk, (number + 1) * chunk)
        d_fc2_w[cols, :] += t_mm(z_ref[:, cols], gm)
        gu = slope_ref[:, cols].astype(f32) * mm_t(gm, fc2_w[cols, :])
        gu = gu.astype(bf16)
        d_fc1_w[:, cols] += t_mm(n2_ref[...], gu)
        d_fc1_b[:, cols] += col_sum(gu.astype(f32))
        part = mm_t(gu, fc1_w[:, cols])
        gnormed[...] = part if number == 0 else gnormed[...] + part
    hat, inverse = ln_parts(mid_ref[...])
    gn = gnormed[...]
    d_ln2[0:1, :] += col_sum(gn * hat)
    d_ln2[1:2, :] += col_sum(gn)
    gy[...] += ln_back(gn, hat, inverse, ln2_ref[0:1, :])


def attention_backward(pair, tall, acts, weights, grads, gtok_ref, gmid_ref, gqkv, gatt_ref):
    tok_ref, a1_ref, qkv_ref, probs_ref, att_ref = acts
    ln1_ref, qkv_w, proj_w = weights
    d_ln1, d_qkv_w, d_qkv_b, d_proj_w, d_proj_b = grads
    width = tok_ref.shape[-1]
    length = gtok_ref.shape[2]
    found, size = groups(width)
    scale = size ** (-0.5)
    gp = gmid_ref[...].astype(bf16)
    d_proj_w[...] += t_mm(att_ref[...], gp)
    d_proj_b[...] += col_sum(gp.astype(f32))
    gatt_ref[...] = mm_t(gp, proj_w[...]).astype(bf16)
    for crop in range(pair):
        here = slice(crop * tall, (crop + 1) * tall)
        for start, stop, count in found:
            first = start // size
            query = stack_heads(qkv_ref[here, start:stop], count, size)
            key = qkv_ref[here, width + start : width + stop]
            value = qkv_ref[here, 2 * width + start : 2 * width + stop]
            gatt = stack_heads(gatt_ref[here, start:stop], count, size)
            probs_low = jnp.concatenate([probs_ref[crop, first + head] for head in range(count)], 0)
            probs = probs_low.astype(f32)
            gprobs = mm_t(gatt, value)
            inner = gprobs - jnp.sum(gprobs * probs, -1, keepdims=True)
            gscores = (probs * inner).astype(bf16)
            gq = merge_heads(mm(gscores, key), count, size) * scale
            gk = t_mm(gscores, query) * scale
            gv = t_mm(probs_low, gatt)
            gqkv[here, start:stop] = gq.astype(bf16)
            gqkv[here, width + start : width + stop] = gk.astype(bf16)
            gqkv[here, 2 * width + start : 2 * width + stop] = gv.astype(bf16)
    grad = gqkv[...]
    d_qkv_w[...] += t_mm(a1_ref[...], grad)
    d_qkv_b[...] += col_sum(grad.astype(f32))
    gn = mm_t(grad, qkv_w[...])
    hat, inverse = ln_parts(tok_ref[...].reshape(pair * tall, width).astype(f32))
    d_ln1[0:1, :] += col_sum(gn * hat)
    d_ln1[1:2, :] += col_sum(gn)
    gtok = gmid_ref[...] + ln_back(gn, hat, inverse, ln1_ref[0:1, :])
    for crop in range(pair):
        gtok_ref[0, crop] = gtok[crop * tall : crop * tall + length].astype(bf16)


GRAD_MLP = ("ln2", "fc1_w", "fc1_b", "fc2_w", "fc2_b")
GRAD_ATTENTION = ("ln1", "qkv_w", "qkv_b", "proj_w", "proj_b")


def mlp_back_kernel(pair, tall, chunk, live_ref, *refs):
    cot_ref, y_ref, gj_ref, mid_ref, n2_ref, z_ref, slope_ref, returned_ref = refs[:8]
    weights = refs[8:11]
    near, far = refs[11:15], refs[15:19]
    out_ref, gmid_ref, ghead_far = refs[19:22]
    grads, near_grads, far_grads = refs[22:27], refs[27:30], refs[30:33]
    ghead, gnormed = refs[33:]

    @pl.when(pl.program_id(0) == 0)
    def _():
        head_backward(*near, *near_grads, ghead)
        head_backward(*far, *far_grads, ghead_far)
        clear_all(grads)

    acts = (cot_ref, y_ref, gj_ref, mid_ref, n2_ref, z_ref, slope_ref, ghead, returned_ref)
    mlp_backward(pair, tall, chunk, live_ref, acts, weights, grads, out_ref, gmid_ref, gnormed)


def attention_back_kernel(pair, tall, gmid_ref, *refs):
    acts, weights, gtok_ref, grads = refs[:5], refs[5:8], refs[8], refs[9:14]

    @pl.when(pl.program_id(0) == 0)
    def _():
        clear_all(grads)

    attention_backward(pair, tall, acts, weights, grads, gtok_ref, gmid_ref, *refs[14:])


def block_back_kernel(pair, tall, chunk, live_ref, *refs):
    mlp_acts, acts = refs[:9], refs[9:14]
    weights, mlp_weights = refs[14:17], refs[17:20]
    out_ref, gtok_ref = refs[20:22]
    mlp_grads, grads = refs[22:27], refs[27:32]
    gy, gnormed, gqkv, gatt_ref = refs[32:]

    @pl.when(pl.program_id(0) == 0)
    def _():
        clear_all(mlp_grads + grads)

    mlp_backward(
        pair, tall, chunk, live_ref, mlp_acts, mlp_weights, mlp_grads, out_ref, gy, gnormed
    )
    attention_backward(pair, tall, acts, weights, grads, gtok_ref, gy, gqkv, gatt_ref)


def named(label, names, values):
    return {label + "_" + name: value for name, value in zip(names, values)}


def grad_outs(params, label, names):
    return [
        (fixed_spec(value.shape), jax.ShapeDtypeStruct(value.shape, f32))
        for value in pick(params, label, names)
    ]


def token_out(crops, length, width, pair):
    return (
        pl.BlockSpec((1, pair, length, width), lambda i: (0, i, 0, 0)),
        jax.ShapeDtypeStruct((1, crops, length, width), bf16),
    )


def mlp_back(cot, live, kept, gj, near, far, returned, params, label, other, length, pair):
    crops, tall, width = cot.shape
    mid, n2, z, slope, y = kept
    hidden = z.shape[1]
    rows, flat = pair * tall, crops * tall
    weights = pick(params, label, ("ln2", "fc1_w", "fc2_w"))
    near = list(near) + pick(params, label, ("to_ln", "to_w"))
    far = list(far) + pick(params, other, ("to_ln", "to_w"))
    smem = pl.BlockSpec(memory_space=pltpu.SMEM)
    outs = [
        token_out(crops, length, width, pair),
        (row_spec(rows, width), jax.ShapeDtypeStruct((flat, width), f32)),
        (fixed_spec(far[0].shape), jax.ShapeDtypeStruct(far[0].shape, f32)),
    ]
    outs += grad_outs(params, label, GRAD_MLP)
    outs += grad_outs(params, label, TO) + grad_outs(params, other, TO)
    returned = returned.astype(f32)
    values = pl.pallas_call(
        functools.partial(mlp_back_kernel, pair, tall, 384),
        grid=(crops // pair,),
        out_shape=[shape for spec, shape in outs],
        in_specs=[smem, pl.BlockSpec((pair, tall, width), lambda i: (i, 0, 0))]
        + [row_spec(rows, width)] * 4
        + [row_spec(rows, hidden)] * 2
        + [whole(value.shape) for value in [returned] + weights + near + far],
        out_specs=[spec for spec, shape in outs],
        scratch_shapes=[pltpu.VMEM((crops, width), f32), pltpu.VMEM((rows, width), f32)],
        cost_estimate=estimate(8 * 8 * flat * width * hidden, 20_000_000),
        name="mlp_back_" + label,
    )(live, cot, y, gj, mid, n2, z, slope, returned, *weights, *near, *far)
    grads = named(label, GRAD_MLP, values[3:8])
    grads.update(named(label, TO, values[8:11]))
    grads.update(named(other, TO, values[11:14]))
    return values[0], values[1], values[2], grads


def attention_back(tokens, gmid, kept, params, label, length, pair):
    crops, tall, width = tokens.shape
    a1, qkv, probs, att = kept
    rows, flat = pair * tall, crops * tall
    weights = pick(params, label, ("ln1", "qkv_w", "proj_w"))
    outs = [token_out(crops, length, width, pair)] + grad_outs(params, label, GRAD_ATTENTION)
    values = pl.pallas_call(
        functools.partial(attention_back_kernel, pair, tall),
        grid=(crops // pair,),
        out_shape=[shape for spec, shape in outs],
        in_specs=[
            row_spec(rows, width),
            pl.BlockSpec((pair, tall, width), lambda i: (i, 0, 0)),
            row_spec(rows, width),
            row_spec(rows, 3 * width),
            pl.BlockSpec((pair, HEADS, tall, tall), lambda i: (i, 0, 0, 0)),
            row_spec(rows, width),
        ]
        + [whole(value.shape) for value in weights],
        out_specs=[spec for spec, shape in outs],
        scratch_shapes=[pltpu.VMEM((rows, 3 * width), bf16), pltpu.VMEM((rows, width), bf16)],
        cost_estimate=estimate(8 * 16 * flat * width * width, 20_000_000),
        name="attention_back_" + label,
    )(gmid, tokens, a1, qkv, probs, att, *weights)
    return values[0], named(label, GRAD_ATTENTION, values[1:])


def block_back(tokens, cot, live, kept, gj, ghead, returned, params, label, length, pair):
    crops, tall, width = tokens.shape
    a1, qkv, probs, att, mid, n2, z, slope, y = kept
    hidden = z.shape[1]
    rows, flat = pair * tall, crops * tall
    weights = pick(params, label, ("ln1", "qkv_w", "proj_w", "ln2", "fc1_w", "fc2_w"))
    smem = pl.BlockSpec(memory_space=pltpu.SMEM)
    token_spec = pl.BlockSpec((pair, tall, width), lambda i: (i, 0, 0))
    outs = [token_out(crops, length, width, pair)] * 2
    outs += grad_outs(params, label, GRAD_MLP) + grad_outs(params, label, GRAD_ATTENTION)
    returned = returned.astype(f32)
    values = pl.pallas_call(
        functools.partial(block_back_kernel, pair, tall, 384),
        grid=(crops // pair,),
        out_shape=[shape for spec, shape in outs],
        in_specs=[smem, token_spec]
        + [row_spec(rows, width)] * 4
        + [row_spec(rows, hidden)] * 2
        + [whole(ghead.shape), whole(returned.shape)]
        + [
            token_spec,
            row_spec(rows, width),
            row_spec(rows, 3 * width),
            pl.BlockSpec((pair, HEADS, tall, tall), lambda i: (i, 0, 0, 0)),
            row_spec(rows, width),
        ]
        + [whole(value.shape) for value in weights],
        out_specs=[spec for spec, shape in outs],
        scratch_shapes=[
            pltpu.VMEM((rows, width), f32),
            pltpu.VMEM((rows, width), f32),
            pltpu.VMEM((rows, 3 * width), bf16),
            pltpu.VMEM((rows, width), bf16),
        ],
        cost_estimate=estimate(8 * 4 * flat * (4 * width * width + 2 * width * hidden), 20_000_000),
        name="block_back_" + label,
    )(live, cot, y, gj, mid, n2, z, slope, ghead, returned, tokens, a1, qkv, probs, att, *weights)
    grads = named(label, GRAD_MLP, values[2:7])
    grads.update(named(label, GRAD_ATTENTION, values[7:12]))
    return values[0], values[1], grads


def swap(value):
    return lax.ppermute(value, "branch", [(0, 1), (1, 0)])


def partner(value, bit):
    count = lax.axis_size("dp")
    return lax.ppermute(value, "dp", [(i, i ^ bit) for i in range(count)])


def side_partner(value, place):
    count = lax.axis_size("dp")
    pairs = []
    for core in range(2):
        bit = 1 << (place ^ core)
        pairs += [(core * count + i, core * count + (i ^ bit)) for i in range(count)]
    return lax.ppermute(value, ("branch", "dp"), pairs)


def tie(value, *others):
    return lax.optimization_barrier((value, *others))[0]


def gather_lines(held, first, last):
    for place in range(first, last, -1):
        held = jnp.concatenate([held, partner(held, 1 << place)], 0)
    return held


def gather_middle(held):
    return jnp.concatenate([held, side_partner(held, 1)], 0)


def add_low(*values):
    total = values[0].astype(f32)
    for value in values[1:]:
        total = total + value.astype(f32)
    return total.astype(bf16)


def reduce_start(low, high, send):
    half = low.shape[0]
    got = swap(send)
    sent = add_low(high, got[half:])
    return sent, [low, got[:half], side_partner(sent, 0)]


def reduce_middle(parts):
    quarter = parts[0].shape[0] // 2
    sent = add_low(*[part[quarter:] for part in parts])
    return sent, [part[:quarter] for part in parts] + [side_partner(sent, 1)]


def reduce_lines(parts, bits):
    for place in range(2, bits):
        count = parts[0].shape[0] // 2
        sent = add_low(*[part[count:] for part in parts])
        parts = [part[:count] for part in parts] + [partner(sent, 1 << place)]
    total = parts[0][0].astype(f32)
    for part in parts[1:]:
        total = total + part[0].astype(f32)
    return total


def shards(
    small_tokens,
    large_tokens,
    small_cot,
    large_cot,
    live_counts,
    master,
    first_moment,
    second_moment,
):
    count = lax.axis_size("branch") * lax.axis_size("dp")
    bits = lax.axis_size("dp").bit_length() - 1
    plan = grid_plan(count)
    core, mine = lax.axis_index("branch"), lax.axis_index("dp")
    where = jnp.stack([core, mine]).astype(jnp.int32)
    index = lax.axis_index(("branch", "dp"))
    size = master.shape[0]
    rows = plan["shard_rows"]
    table = lax.dynamic_index_in_dim(jnp.asarray(plan["table"]), index, 0, False)
    padded = jnp.pad(master, (0, rows * LANES - size)).reshape(rows, LANES)
    keep, send = align(where, table, padded, plan)
    got = swap(send)
    near = gather_lines(jnp.where(core == 0, keep, got)[None], bits - 1, 1)
    far = tie(jnp.where(core == 0, got, keep)[None], near)
    middle = (bits + 1) // 2
    far = gather_lines(far, bits - 1, middle)
    near = tie(gather_middle(near), far)
    near_end = side_partner(near, 0)
    far = gather_lines(far, middle, 1)
    near_end = tie(near_end, far)
    near_pieces = (near, near_end, swap(near), swap(near_end))

    counts = live_counts[:, 0]
    own_count = lax.dynamic_slice_in_dim(counts, core, 1)
    far_count = lax.dynamic_slice_in_dim(counts, 1 - core, 1)
    crops, length_s = small_tokens.shape[1], small_tokens.shape[2]
    length_l = large_tokens.shape[2]
    tall_s, tall_l = round_up(length_s, 16), round_up(length_l, 16)
    pair = 2

    def taller(value, length, tall):
        return jnp.pad(value[0], ((0, 0), (0, tall - length), (0, 0)))

    small = taller(small_tokens, length_s, tall_s)
    large = taller(large_tokens, length_l, tall_l)
    small_seed = taller(small_cot, length_s, tall_s)
    large_seed = taller(large_cot, length_l, tall_l)
    slots = jnp.arange(crops, dtype=jnp.int32)[:, None]
    ret_small = jnp.where(slots < own_count, small_cot[0, :, 0], 0)
    ret_large = jnp.where(slots < far_count, large_cot[0, :, 0], 0)
    ret_small, ret_large = swap(ret_small), swap(ret_large)

    params = unflatten(where, near_pieces, plan, 0, bits)
    straddling = params.pop(plan["sides"][1][0][0])
    far = tie(far, near_end)
    far = jnp.concatenate([far, tie(side_partner(far, 1), params["s_ln1"])], 0)
    *kept_s, head_s = block_forward(tie(small, far), params, "s", length_s, pair)
    far_end = side_partner(far, 0)
    kept_l = attention_only(tie(large, far_end), params, "l", length_l, pair)
    far_pieces = (far, far_end, swap(far), swap(far_end))
    params.update(unflatten(where, far_pieces, plan, 1, bits, (straddling,)))
    z_l, slope_l, y_l, head_l, sent_l, sent_s = mlp_only(
        kept_l[4], kept_l[5], head_s, params, "l", "s", crops, pair
    )
    got_s, got_l = swap(sent_s), swap(sent_l)
    grads = {}
    back_s, gsent_s, gj_l, part = cross(got_s, y_l, ret_small, params, "s", length_l, tall_l)
    grads.update(part)
    home_s, own_s = swap(back_s), swap(gsent_s)
    back_l, gsent_l, gj_s, part = cross(got_l, kept_s[8], ret_large, params, "l", length_s, tall_s)
    grads.update(part)
    home_l, own_l = swap(back_l), swap(gsent_l)
    large_out, gmid, ghead_s, part = mlp_back(
        large_seed,
        far_count,
        (kept_l[4], kept_l[5], z_l, slope_l, y_l),
        gj_l,
        (head_l, own_l),
        (head_s, own_s),
        home_l,
        params,
        "l",
        "s",
        length_l,
        pair,
    )
    grads.update(part)
    sent, far_side = reduce_start(*flatten(where, grads, plan, 1, bits))
    gmid = tie(gmid, sent)
    large_grad, part = attention_back(large, gmid, kept_l[:4], params, "l", length_l, pair)
    grads.update(part)
    sent, far_side = reduce_middle(far_side)
    ghead_s = tie(ghead_s, sent, gmid)
    small_out, small_grad, part = block_back(
        small, small_seed, own_count, kept_s, gj_s, ghead_s, home_s, params, "s", length_s, pair
    )
    grads.update(part)
    grads["s_ln1"] = tie(grads["s_ln1"], far_side[-1])
    near_side = reduce_start(*flatten(where, grads, plan, 0, bits))[1]
    far_total = reduce_lines(far_side, bits)
    near_side = reduce_middle(near_side)[1]
    near_total = reduce_lines(near_side, bits)
    own = jnp.where(core == 0, near_total, far_total)
    got = swap(jnp.where(core == 0, far_total, near_total))
    summed, square = unalign(where, table, own, got, plan)
    square = square + swap(square)
    for place in range(bits):
        square = square + partner(square, 1 << place)
    grad_norm = jnp.sqrt(square[0, 0])
    own_grad = summed.reshape(-1)[:size]
    clipped = own_grad * jnp.minimum(1.0, clip_norm / grad_norm)
    new_first = beta_one * first_moment + (1.0 - beta_one) * clipped
    new_second = beta_two * second_moment + (1.0 - beta_two) * clipped * clipped
    new_master = master - rate * (
        new_first / bias_one / (jnp.sqrt(new_second / bias_two) + adam_eps) + decay * master
    )
    return (
        small_out,
        large_out,
        small_grad,
        large_grad,
        grad_norm,
        new_first,
        new_second,
        new_master,
        new_master.astype(bf16),
    )


def solution(mesh):
    return jax.shard_map(
        shards,
        mesh=mesh,
        in_specs=(
            P("branch", "dp", None, None),
            P("branch", "dp", None, None),
            P("branch", "dp", None, None),
            P("branch", "dp", None, None),
            P(None, "dp"),
            P(("branch", "dp")),
            P(("branch", "dp")),
            P(("branch", "dp")),
        ),
        out_specs=(
            P("branch", "dp", None, None),
            P("branch", "dp", None, None),
            P("branch", "dp", None, None),
            P("branch", "dp", None, None),
            P(),
            P(("branch", "dp")),
            P(("branch", "dp")),
            P(("branch", "dp")),
            P(("branch", "dp")),
        ),
        check_vma=False,
    )
```

```python
import functools
import math

import jax
import jax.numpy as jnp
import numpy as np
from jax import lax
from jax.experimental import pallas as pl
from jax.experimental.pallas import tpu as pltpu
from jax.experimental.layout import Layout, with_layout_constraint
from jax.sharding import PartitionSpec as P

DS = 192
DL = 384
MS = 768
ML = 1536
HEADS = 6

norm_eps = 1e-06
clip_norm = 1.0
beta_one = 0.5
beta_two = 0.5
adam_eps = 1e-08
rate = 0.05
decay = 0.05
bias_one = 1.0 - 0.5**5
bias_two = 1.0 - 0.5**5

f32 = jnp.float32
bf16 = jnp.bfloat16
LANES = 128


def layout():
    shapes = []
    for label, width, hidden in (("s", DS, MS), ("l", DL, ML)):
        shapes += [
            (label + "_ln1", (2, width)),
            (label + "_qkv_w", (width, 3 * width)),
            (label + "_qkv_b", (3 * width,)),
            (label + "_proj_w", (width, width)),
            (label + "_proj_b", (width,)),
            (label + "_ln2", (2, width)),
            (label + "_fc1_w", (width, hidden)),
            (label + "_fc1_b", (hidden,)),
            (label + "_fc2_w", (hidden, width)),
            (label + "_fc2_b", (width,)),
        ]
    for label, owner, other in (("s", DS, DL), ("l", DL, DS)):
        shapes += [
            (label + "_to_ln", (2, owner)),
            (label + "_to_w", (owner, other)),
            (label + "_to_b", (other,)),
            (label + "_ca_ln", (2, other)),
            (label + "_ca_q_w", (other, other)),
            (label + "_ca_q_b", (other,)),
            (label + "_ca_k_w", (other, other)),
            (label + "_ca_v_w", (other, other)),
            (label + "_ca_v_b", (other,)),
            (label + "_ca_o_w", (other, other)),
            (label + "_ca_o_b", (other,)),
            (label + "_back_ln", (2, other)),
            (label + "_back_w", (other, owner)),
            (label + "_back_b", (owner,)),
        ]
    return shapes


def round_up(value, unit):
    return -(-value // unit) * unit


def grid_plan(shards):
    names = []
    regions = []
    offset = 0
    for label, shape in layout():
        count = math.prod(shape)
        phase = offset % LANES
        if not regions or regions[-1][2] != phase:
            regions.append([offset, offset, phase])
        names.append((label, shape, offset, len(regions) - 1))
        offset += count
        regions[-1][1] = offset
    total = offset
    starts = []
    row = 0
    for first, last, phase in regions:
        starts.append(row)
        row += -(-(last - first) // LANES)
    rows = row
    places = {}
    for label, shape, place, region in names:
        places[label] = (starts[region] + (place - regions[region][0]) // LANES, shape)
    size = total // shards
    bases = []
    pieces = []
    for device in range(shards):
        low, high = device * size, (device + 1) * size
        own = []
        base = None
        for (first, last, phase), start in zip(regions, starts):
            left, right = max(low, first), min(high, last)
            if left >= right:
                continue
            if base is None:
                base = (start + (left - first) // LANES) // 16 * 16
            delta = start * LANES - first + low - base * LANES
            own.append((left - low, right - low, delta))
        bases.append(base)
        pieces.append(own)
    most = max(len(own) for own in pieces)
    table = np.zeros((shards, most * 3), np.int32)
    need = 0
    for device, own in enumerate(pieces):
        for number, (left, right, delta) in enumerate(own):
            table[device, 3 * number : 3 * number + 3] = (left, right, delta)
            need = max(need, right + delta)
    span = round_up(-(-need // LANES), 32)
    overlap = 16
    for device in range(1, shards):
        overlap = max(overlap, bases[device - 1] + span - bases[device])
    half = shards // 2
    edge = half * size
    sides = [[], []]
    for label, shape, place, region in names:
        if place < edge:
            sides[0].append((label, shape))
        if place + math.prod(shape) > edge:
            sides[1].append((label, shape))
    origins = [0, min(bases[half], places[sides[1][0][0]][0]) // 16 * 16]
    heights = []
    for side in range(2):
        last = bases[half * (side + 1) - 1] + span
        for label, shape in sides[side]:
            last = max(last, places[label][0] + -(-math.prod(shape) // LANES))
        heights.append(round_up(last - origins[side] + overlap, 16))
    groups = []
    for first, last in ((0, half // 2), (half // 2, half), (half, shards)):
        held = [
            (label, shape)
            for label, shape, place, region in names
            if place < last * size and place + math.prod(shape) > first * size
        ]
        origin = min([bases[first]] + [places[label][0] for label, shape in held]) // 16 * 16
        stop = max(
            [bases[last - 1] + span]
            + [places[label][0] + -(-math.prod(shape) // LANES) for label, shape in held]
        )
        groups.append((first, last - first, held, origin, round_up(stop - origin + overlap, 16)))
    return dict(
        places=places,
        groups=groups,
        rows=rows,
        half=half,
        sides=sides,
        origins=origins,
        heights=heights,
        size=size,
        bases=bases,
        table=table,
        most=most,
        span=span,
        overlap=overlap,
        shard_rows=round_up(-(-size // LANES), 16),
    )


def mm(left, right):
    return lax.dot_general(left, right, (((1,), (0,)), ((), ())), preferred_element_type=f32)


def mm_t(left, right):
    return lax.dot_general(left, right, (((1,), (1,)), ((), ())), preferred_element_type=f32)


def t_mm(left, right):
    return lax.dot_general(left, right, (((0,), (0,)), ((), ())), preferred_element_type=f32)


def vmem_spec(shape, index):
    return pl.BlockSpec(shape, index)


def whole(shape):
    rank = len(shape)
    return pl.BlockSpec(shape, lambda *_: (0,) * rank, pipeline_mode=pl.Buffered(1))


def estimate(flops, moved):
    return pl.CostEstimate(flops=int(flops), bytes_accessed=int(moved), transcendentals=0)


def shift_rows(ref, amount, rows, margin):
    down = amount // LANES
    across = amount - down * LANES
    here = ref[pl.ds(margin - down, rows), :]
    above = ref[pl.ds(margin - down - 1, rows), :]
    here = pltpu.roll(here, across, 1)
    above = pltpu.roll(above, across, 1)
    lane = lax.broadcasted_iota(jnp.int32, here.shape, 1)
    return jnp.where(lane < across, above, here)


def align_kernel(most, rows, span, margin, core_ref, table_ref, shard_ref, keep_ref, send_ref, padded):
    padded[...] = jnp.zeros_like(padded)
    padded[margin : margin + rows, :] = shard_ref[...]
    place = lax.broadcasted_iota(jnp.int32, (span, LANES), 0) * LANES
    place = place + lax.broadcasted_iota(jnp.int32, (span, LANES), 1)
    total = jnp.zeros((span, LANES), f32)
    for number in range(most):
        left = table_ref[3 * number]
        right = table_ref[3 * number + 1]
        delta = table_ref[3 * number + 2]
        moved = shift_rows(padded, delta, span, margin)
        total = jnp.where((place >= left + delta) & (place < right + delta), moved, total)
    total = total.astype(bf16)
    first = core_ref[0] == 0
    upper, lower = total[: span // 2], total[span // 2 :]
    keep_ref[...] = jnp.where(first, upper, lower)
    send_ref[...] = jnp.where(first, lower, upper)


def unalign_kernel(
    most, rows, span, margin, core_ref, table_ref, own_ref, got_ref, out_ref, norm_ref, padded
):
    first = core_ref[0] == 0
    padded[span:, :] = jnp.zeros((padded.shape[0] - span, LANES), f32)
    padded[0 : span // 2, :] = jnp.where(first, own_ref[...], got_ref[...])
    padded[span // 2 : span, :] = jnp.where(first, got_ref[...], own_ref[...])
    place = lax.broadcasted_iota(jnp.int32, (rows, LANES), 0) * LANES
    place = place + lax.broadcasted_iota(jnp.int32, (rows, LANES), 1)
    total = jnp.zeros((rows, LANES), f32)
    lane = lax.broadcasted_iota(jnp.int32, (rows, LANES), 1)
    for number in range(most):
        left = table_ref[3 * number]
        right = table_ref[3 * number + 1]
        delta = table_ref[3 * number + 2]
        down = delta // LANES
        across = delta - down * LANES
        back = lax.rem(LANES - across, LANES)
        here = pltpu.roll(padded[pl.ds(down, rows), :], back, 1)
        below = pltpu.roll(padded[pl.ds(down + 1, rows), :], back, 1)
        moved = jnp.where(lane < LANES - across, here, below)
        total = jnp.where((place >= left) & (place < right), moved, total)
    out_ref[...] = total
    norm_ref[...] = jnp.broadcast_to(jnp.sum(total * total).reshape(1, 1), (8, LANES))


def align(core, table, shard, plan):
    rows, span, most = plan["shard_rows"], plan["span"], plan["most"]
    margin = 8 + round_up(int(plan["table"].max(initial=0, where=pick_delta(plan))) // LANES + 1, 8)
    tall = margin + max(rows, span) + 8
    vmem = pl.BlockSpec(memory_space=pltpu.VMEM)
    smem = pl.BlockSpec(memory_space=pltpu.SMEM)
    part = jax.ShapeDtypeStruct((span // 2, LANES), bf16)
    return pl.pallas_call(
        functools.partial(align_kernel, most, rows, span, margin),
        out_shape=(part, part),
        in_specs=[smem, smem, vmem],
        out_specs=(vmem, vmem),
        scratch_shapes=[pltpu.VMEM((tall, LANES), f32)],
        cost_estimate=estimate(1_000_000, 1_000_000),
        name="align",
    )(core, table, shard)


def unalign(core, table, own, got, plan):
    rows, span, most = plan["shard_rows"], plan["span"], plan["most"]
    margin = 16 + round_up(int(plan["table"].max(initial=0, where=pick_delta(plan))) // LANES + 1, 8)
    tall = max(rows, span) + margin
    vmem = pl.BlockSpec(memory_space=pltpu.VMEM)
    smem = pl.BlockSpec(memory_space=pltpu.SMEM)
    return pl.pallas_call(
        functools.partial(unalign_kernel, most, rows, span, margin),
        out_shape=(
            jax.ShapeDtypeStruct((rows, LANES), f32),
            jax.ShapeDtypeStruct((8, LANES), f32),
        ),
        in_specs=[smem, smem, vmem, vmem],
        out_specs=(vmem, vmem),
        scratch_shapes=[pltpu.VMEM((tall, LANES), f32)],
        cost_estimate=estimate(1_000_000, 1_000_000),
        name="unalign",
    )(core, table, own, got)


def pick_delta(plan):
    mask = np.zeros(plan["table"].shape, bool)
    mask[:, 2::3] = True
    return mask


def two_dim(shape):
    return shape if len(shape) == 2 else (1, shape[0])


def is_matrix(label):
    return label[-2:] == "_w"


def strided(start, count, step):
    return pl.ds(start, count) if step == 1 or count == 1 else pl.ds(start, count, stride=step)


def half_swap(value):
    return pltpu.roll(value, LANES // 2, 1)


def read_param(flat, row, shape, out_ref, pair_ref):
    depth, width = two_dim(shape)
    dtype = out_ref.dtype
    if width % LANES == 0:
        step = width // LANES
        for col in range(step):
            out_ref[:, col * LANES : (col + 1) * LANES] = flat[
                strided(row + col, depth, step), :
            ].astype(dtype)
        return
    half = LANES // 2
    lead = width // LANES
    if depth == 1:
        for col in range(lead):
            out_ref[:, col * LANES : (col + 1) * LANES] = flat[row + col : row + col + 1, :].astype(
                dtype
            )
        out_ref[:, lead * LANES :] = flat[row + lead : row + lead + 1, 0:half].astype(dtype)
        return
    step = 2 * width // LANES
    pairs = depth // 2
    lane = lax.broadcasted_iota(jnp.int32, (pairs, LANES), 1)
    blocks = [flat[strided(row + col, pairs, step), :] for col in range(step)]
    turned = [half_swap(block) for block in blocks[lead:]]
    for col in range(lead):
        pair_ref[col, strided(0, pairs, 2), :] = blocks[col]
        pair_ref[col, strided(1, pairs, 2), :] = jnp.where(lane < half, turned[col], turned[col + 1])
    pair_ref[lead, strided(0, pairs, 2), :] = blocks[lead]
    pair_ref[lead, strided(1, pairs, 2), :] = turned[lead]
    for col in range(lead):
        out_ref[:, col * LANES : (col + 1) * LANES] = pair_ref[col, 0:depth, :].astype(dtype)
    out_ref[:, lead * LANES :] = pair_ref[lead, 0:depth, 0:half].astype(dtype)


def write_param(flat, row, shape, in_ref, pair_ref, window):
    depth, width = two_dim(shape)
    if width % LANES == 0:
        step = width // LANES
        first = max(0, (window[0] - row) // step) // 8 * 8
        last = min(depth, round_up(max(0, -(-(window[1] - row) // step)), 8))
        for col in range(step):
            flat[strided(row + first * step + col, last - first, step), :] = in_ref[
                first:last, col * LANES : (col + 1) * LANES
            ]
        return
    half = LANES // 2
    lead = width // LANES
    if depth == 1:
        for col in range(lead):
            flat[row + col : row + col + 1, :] = in_ref[:, col * LANES : (col + 1) * LANES]
        tail = jnp.concatenate([in_ref[:, lead * LANES :], jnp.zeros((1, half), f32)], 1)
        flat[row + lead : row + lead + 1, :] = tail
        return
    step = 2 * width // LANES
    pairs = depth // 2
    lane = lax.broadcasted_iota(jnp.int32, (pairs, LANES), 1)
    for col in range(lead):
        pair_ref[col, 0:depth, :] = in_ref[:, col * LANES : (col + 1) * LANES]
    pair_ref[lead, 0:depth, 0:half] = in_ref[:, lead * LANES :]
    even = [pair_ref[col, strided(0, pairs, 2), :] for col in range(lead + 1)]
    odd = [half_swap(pair_ref[col, strided(1, pairs, 2), :]) for col in range(lead + 1)]
    for col in range(lead):
        flat[strided(row + col, pairs, step), :] = even[col]
    flat[strided(row + lead, pairs, step), :] = jnp.where(lane < half, even[lead], odd[0])
    for col in range(lead):
        flat[strided(row + lead + 1 + col, pairs, step), :] = jnp.where(
            lane < half, odd[col], odd[col + 1]
        )


def decode(number, core, bits):
    first = (number >> (bits - 1)) & 1
    second = (number >> (bits - 2)) & 1
    found = (first << core) | (second << (1 - core))
    for place in range(2, bits):
        found = found | (((number >> (bits - 1 - place)) & 1) << place)
    return found


def unflatten_kernel(plan, side, bits, where_ref, base_ref, *refs):
    pieces, refs = refs[:4], refs[4:]
    carried, refs = (refs[:1], refs[1:]) if side else ((), refs)
    outs, (flat, pair_ref) = refs[:-2], refs[-2:]
    span, overlap, half = plan["span"], plan["overlap"], plan["half"]
    origin = plan["origins"][side]
    core, mine = where_ref[0], where_ref[1]
    lead = plan["bases"][side * half] - origin
    if lead:
        flat[0:lead, :] = jnp.zeros((lead, LANES), f32)
    last = plan["bases"][side * half + half - 1] - origin + span
    if flat.shape[0] > last:
        flat[last:, :] = jnp.zeros((flat.shape[0] - last, LANES), f32)

    def base_of(owner):
        return pl.multiple_of(base_ref[side * half + owner] - origin, 16)

    def clear(owner, carry):
        base = base_of(owner)
        flat[pl.ds(base, overlap), :] = jnp.zeros((overlap, LANES), f32)
        flat[pl.ds(base + span - overlap, overlap), :] = jnp.zeros((overlap, LANES), f32)
        return carry

    lax.fori_loop(0, half, clear, 0)
    middle = span // 2
    for number, piece in enumerate(pieces):
        theirs = number // 2
        owner_core = core if theirs == 0 else 1 - core
        upper = number % 2 * (half // 2)
        for part in range(2):

            @pl.when(owner_core == part)
            def _(part=part, piece=piece, upper=upper):
                def place(entry, carry):
                    base = base_of(decode(entry + upper, part, bits) ^ mine)
                    value = piece[entry].astype(f32)
                    if part == 0:
                        flat[pl.ds(base, overlap), :] += value[:overlap]
                        flat[pl.ds(base + overlap, middle - overlap), :] = value[overlap:]
                    else:
                        flat[pl.ds(base + middle, middle - overlap), :] = value[: middle - overlap]
                        flat[pl.ds(base + span - overlap, overlap), :] += value[middle - overlap :]
                    return carry

                lax.fori_loop(0, half // 2, place, 0)

    for number, ((label, shape), out_ref) in enumerate(zip(plan["sides"][side], outs)):
        read_param(flat, plan["places"][label][0] - origin, shape, out_ref, pair_ref)
        if side and number == 0:
            out_ref[...] += carried[0][...]


def unflatten(where, pieces, plan, side, bits, carried=()):
    outs = []
    for label, shape in plan["sides"][side]:
        outs.append(jax.ShapeDtypeStruct(two_dim(shape), bf16 if is_matrix(label) else f32))
    vmem = pl.BlockSpec(memory_space=pltpu.VMEM)
    smem = pl.BlockSpec(memory_space=pltpu.SMEM)
    values = pl.pallas_call(
        functools.partial(unflatten_kernel, plan, side, bits),
        out_shape=outs,
        in_specs=[smem, smem] + [vmem] * (len(pieces) + len(carried)),
        out_specs=[vmem] * len(outs),
        scratch_shapes=[
            pltpu.VMEM((plan["heights"][side], LANES), f32),
            pltpu.VMEM((5, MS, LANES), f32),
        ],
        cost_estimate=estimate(1_000_000, 8_000_000),
        name="unflatten" + str(side),
    )(where, jnp.asarray(plan["bases"], jnp.int32), *pieces, *carried)
    return {label: value for (label, shape), value in zip(plan["sides"][side], values)}


def flatten_kernel(plan, group, bits, where_ref, base_ref, *refs):
    begin, owners, held, origin, height = plan["groups"][group]
    count = len(held)
    grads, (low_ref, high_ref, send_ref, flat, pair_ref) = refs[:count], refs[count:]
    span = plan["span"]
    core, mine = where_ref[0], where_ref[1]
    first, last = None, 0
    for label, shape in held:
        row = plan["places"][label][0] - origin
        first = row if first is None else first
        last = row + -(-math.prod(shape) // LANES)
    if first:
        flat[0:first, :] = jnp.zeros((first, LANES), f32)
    flat[last // 8 * 8 :, :] = jnp.zeros((height - last // 8 * 8, LANES), f32)
    window = (plan["bases"][begin] - origin, plan["bases"][begin + owners - 1] + span - origin)
    for (label, shape), ref in zip(held, grads):
        write_param(flat, plan["places"][label][0] - origin, shape, ref, pair_ref, window)

    def rows_of(entry, part):
        owner = (decode(entry, part, bits) ^ mine) & (owners - 1)
        base = base_ref[begin + owner] - origin + part * (span // 2)
        return flat[pl.ds(pl.multiple_of(base, 16), span // 2), :].astype(bf16)

    def place(entry, carry):
        low_ref[entry] = rows_of(entry, core)
        high_ref[entry] = rows_of(entry + owners // 2, core)
        send_ref[entry] = rows_of(entry, 1 - core)
        send_ref[entry + owners // 2] = rows_of(entry + owners // 2, 1 - core)
        return carry

    lax.fori_loop(0, owners // 2, place, 0)


def flatten(where, grads, plan, group):
    vmem = pl.BlockSpec(memory_space=pltpu.VMEM)
    smem = pl.BlockSpec(memory_space=pltpu.SMEM)
    begin, owners, held, origin, height = plan["groups"][group]
    rows = plan["span"] // 2
    values = [grads[label] for label, shape in held]
    return pl.pallas_call(
        functools.partial(flatten_kernel, plan, group, owners.bit_length() - 1),
        out_shape=(
            jax.ShapeDtypeStruct((owners // 2, rows, LANES), bf16),
            jax.ShapeDtypeStruct((owners // 2, rows, LANES), bf16),
            jax.ShapeDtypeStruct((owners, rows, LANES), bf16),
        ),
        in_specs=[smem, smem] + [vmem] * len(values),
        out_specs=(vmem, vmem, vmem),
        scratch_shapes=[
            pltpu.VMEM((height, LANES), f32),
            pltpu.VMEM((5, MS, LANES), f32),
        ],
        cost_estimate=estimate(1_000_000, 10_000_000),
        name="flatten" + str(group),
    )(where, jnp.asarray(plan["bases"], jnp.int32), *values)


def ln_parts(value):
    mean = jnp.mean(value, -1, keepdims=True)
    centred = value - mean
    variance = jnp.mean(centred * centred, -1, keepdims=True)
    inverse = lax.rsqrt(variance + norm_eps)
    return centred * inverse, inverse


def ln_back(grad, hat, inverse, gain):
    scaled = grad * gain
    first = jnp.mean(scaled, -1, keepdims=True)
    second = jnp.mean(scaled * hat, -1, keepdims=True)
    return inverse * (scaled - first - hat * second)


def gelu_parts(value):
    cdf = 0.5 + 0.5 * lax.erf(value * (2.0**-0.5))
    density = jnp.exp(value * value * -0.5) * (1.0 / math.sqrt(2.0 * math.pi))
    return value * cdf, cdf + value * density


def col_sum(value):
    return jnp.sum(value, 0, keepdims=True)


def groups(width):
    size = width // HEADS
    found = []
    for start in range(0, width, LANES):
        stop = min(start + LANES, width)
        found.append((start, stop, (stop - start) // size))
    return found, size


def stack_heads(value, count, size):
    lane = lax.broadcasted_iota(jnp.int32, value.shape, 1)
    zero = jnp.zeros_like(value)
    return jnp.concatenate(
        [
            jnp.where((lane >= head * size) & (lane < (head + 1) * size), value, zero)
            for head in range(count)
        ],
        0,
    )


def merge_heads(value, count, size):
    rows = value.shape[0] // count
    lane = lax.broadcasted_iota(jnp.int32, (rows, value.shape[1]), 1)
    merged = value[0:rows]
    for head in range(1, count):
        merged = jnp.where(lane >= head * size, value[head * rows : (head + 1) * rows], merged)
    return merged


def attention_forward(pair, length, tall, tokens, weights, keeps):
    ln1_ref, qkv_w, qkv_b, proj_w, proj_b, ln2_ref = weights
    a1_ref, qkv_ref, probs_ref, att_ref, mid_ref, n2_ref = keeps
    width = tokens.shape[-1]
    found, size = groups(width)
    scale = size ** (-0.5)
    hat, _ = ln_parts(tokens)
    a1 = (hat * ln1_ref[0:1, :] + ln1_ref[1:2, :]).astype(bf16)
    a1_ref[...] = a1
    qkv_ref[...] = (mm(a1, qkv_w[...]) + qkv_b[...]).astype(bf16)
    key_lane = lax.broadcasted_iota(jnp.int32, (1, tall), 1)
    bias = jnp.where(key_lane < length, 0.0, -1e30).astype(f32)
    for crop in range(pair):
        here = slice(crop * tall, (crop + 1) * tall)
        for start, stop, count in found:
            query = stack_heads(qkv_ref[here, start:stop], count, size)
            key = qkv_ref[here, width + start : width + stop]
            value = qkv_ref[here, 2 * width + start : 2 * width + stop]
            scores = mm_t(query, key) * scale + bias
            summit = jnp.max(scores, -1, keepdims=True)
            weights = jnp.exp(scores - summit)
            probs = (weights / jnp.sum(weights, -1, keepdims=True)).astype(bf16)
            first = start // size
            for head in range(count):
                probs_ref[crop, first + head] = probs[head * tall : (head + 1) * tall]
            att_ref[here, start:stop] = merge_heads(mm(probs, value), count, size).astype(bf16)
    mid = tokens + mm(att_ref[...], proj_w[...]) + proj_b[...]
    mid_ref[...] = mid
    hat, _ = ln_parts(mid)
    n2_ref[...] = (hat * ln2_ref[0:1, :] + ln2_ref[1:2, :]).astype(bf16)


def mlp_forward(chunk, mid_ref, n2_ref, weights, keeps):
    fc1_w, fc1_b, fc2_w, fc2_b = weights
    z_ref, slope_ref, y_ref = keeps
    y_ref[...] = mid_ref[...] + fc2_b[...]
    for number in range(fc1_w.shape[1] // chunk):
        cols = slice(number * chunk, (number + 1) * chunk)
        inner = mm(n2_ref[...], fc1_w[:, cols]) + fc1_b[:, cols]
        active, slope = gelu_parts(inner)
        z_ref[:, cols] = active.astype(bf16)
        slope_ref[:, cols] = slope.astype(bf16)
        y_ref[...] += mm(z_ref[:, cols], fc2_w[cols, :])


def keep_heads(pair, tall, y_ref, head_ref):
    for crop in range(pair):
        slot = pl.program_id(0) * pair + crop
        head_ref[pl.ds(slot, 1), :] = y_ref[crop * tall : crop * tall + 1, :]


def carry(value, norm, weight, bias):
    hat, _ = ln_parts(value)
    active, _ = gelu_parts(hat * norm[0:1, :] + norm[1:2, :])
    return (mm(active.astype(bf16), weight[...]) + bias[...]).astype(bf16)


def attention_kernel(pair, length, tall, tok_ref, *refs):
    tokens = tok_ref[...].reshape(pair * tall, tok_ref.shape[-1]).astype(f32)
    attention_forward(pair, length, tall, tokens, refs[:6], refs[6:])


def block_kernel(pair, length, tall, chunk, tok_ref, *refs):
    tokens = tok_ref[...].reshape(pair * tall, tok_ref.shape[-1]).astype(f32)
    attention_forward(pair, length, tall, tokens, refs[:6], refs[10:16])
    mlp_forward(chunk, refs[14], refs[15], refs[6:10], refs[16:19])
    keep_heads(pair, tall, refs[18], refs[19])


def mlp_kernel(pair, tall, chunk, mid_ref, n2_ref, *refs):
    weights, heads, (far_head, *far), near = refs[:4], None, refs[4:8], refs[8:11]
    z_ref, slope_ref, y_ref, head_ref, near_ref, far_ref = refs[11:]
    mlp_forward(chunk, mid_ref, n2_ref, weights, (z_ref, slope_ref, y_ref))
    keep_heads(pair, tall, y_ref, head_ref)

    @pl.when(pl.program_id(0) == pl.num_programs(0) - 1)
    def _():
        near_ref[...] = carry(head_ref[...], *near)
        far_ref[...] = carry(far_head[...], *far)


ATTENTION = ("ln1", "qkv_w", "qkv_b", "proj_w", "proj_b", "ln2")
MLP = ("fc1_w", "fc1_b", "fc2_w", "fc2_b")
TO = ("to_ln", "to_w", "to_b")


def pick(params, label, names):
    return [params[label + "_" + name] for name in names]


def row_spec(rows, cols):
    return pl.BlockSpec((rows, cols), lambda i: (i, 0))


def fixed_spec(shape):
    rank = len(shape)
    return pl.BlockSpec(shape, lambda i: (0,) * rank)


def kept_outs(crops, tall, width, hidden, pair):
    rows, flat = pair * tall, crops * tall

    def entry(cols, dtype):
        return row_spec(rows, cols), jax.ShapeDtypeStruct((flat, cols), dtype)

    attention = [
        entry(width, bf16),
        entry(3 * width, bf16),
        (
            pl.BlockSpec((pair, HEADS, tall, tall), lambda i: (i, 0, 0, 0)),
            jax.ShapeDtypeStruct((crops, HEADS, tall, tall), bf16),
        ),
        entry(width, bf16),
        entry(width, f32),
        entry(width, bf16),
    ]
    mlp = [
        entry(hidden, bf16),
        entry(hidden, bf16),
        entry(width, f32),
        (fixed_spec((crops, width)), jax.ShapeDtypeStruct((crops, width), f32)),
    ]
    return attention, mlp


def block_forward(tokens, params, label, length, pair):
    crops, tall, width = tokens.shape
    hidden = params[label + "_fc1_w"].shape[1]
    weights = pick(params, label, ATTENTION + MLP)
    attention, mlp = kept_outs(crops, tall, width, hidden, pair)
    outs = attention + mlp
    flops = 2 * crops * tall * (4 * width * width + 2 * width * hidden)
    return pl.pallas_call(
        functools.partial(block_kernel, pair, length, tall, 384),
        grid=(crops // pair,),
        out_shape=[shape for spec, shape in outs],
        in_specs=[pl.BlockSpec((pair, tall, width), lambda i: (i, 0, 0))]
        + [whole(value.shape) for value in weights],
        out_specs=[spec for spec, shape in outs],
        cost_estimate=estimate(8 * flops, 10_000_000),
        name="block_" + label,
    )(tokens, *weights)


def attention_only(tokens, params, label, length, pair):
    crops, tall, width = tokens.shape
    weights = pick(params, label, ATTENTION)
    outs, _ = kept_outs(crops, tall, width, width, pair)
    flops = 2 * crops * tall * 4 * width * width
    return pl.pallas_call(
        functools.partial(attention_kernel, pair, length, tall),
        grid=(crops // pair,),
        out_shape=[shape for spec, shape in outs],
        in_specs=[pl.BlockSpec((pair, tall, width), lambda i: (i, 0, 0))]
        + [whole(value.shape) for value in weights],
        out_specs=[spec for spec, shape in outs],
        cost_estimate=estimate(8 * flops, 20_000_000),
        name="attention_" + label,
    )(tokens, *weights)


def mlp_only(mid, n2, far_head, params, label, far, crops, pair):
    flat, width = mid.shape
    tall = flat // crops
    rows = pair * tall
    hidden = params[label + "_fc1_w"].shape[1]
    weights = pick(params, label, MLP)
    extra = [far_head] + pick(params, far, TO) + pick(params, label, TO)
    _, outs = kept_outs(crops, tall, width, hidden, pair)
    for name in (label, far):
        shape = (crops, params[name + "_to_w"].shape[1])
        outs.append((fixed_spec(shape), jax.ShapeDtypeStruct(shape, bf16)))
    flops = 2 * flat * 2 * width * hidden
    return pl.pallas_call(
        functools.partial(mlp_kernel, pair, tall, 384),
        grid=(crops // pair,),
        out_shape=[shape for spec, shape in outs],
        in_specs=[row_spec(rows, width), row_spec(rows, width)]
        + [whole(value.shape) for value in weights + extra],
        out_specs=[spec for spec, shape in outs],
        cost_estimate=estimate(8 * flops, 20_000_000),
        name="mlp_" + label,
    )(mid, n2, *weights, *extra)


def cross_kernel(
    length,
    tall,
    crops,
    sent_ref,
    y_ref,
    gret_ref,
    ca_ln,
    q_w,
    q_b,
    k_w,
    v_w,
    v_b,
    o_w,
    o_b,
    back_ln,
    back_w,
    back_b,
    returned_ref,
    gsent_ref,
    gj_ref,
    d_ca_ln,
    d_q_w,
    d_q_b,
    d_k_w,
    d_v_w,
    d_v_b,
    d_o_w,
    d_o_b,
    d_back_ln,
    d_back_w,
    d_back_b,
    sent_f,
    n_all,
    score_all,
    mates_all,
    pairs_all,
    gn_head,
    gj_head,
):
    width = y_ref.shape[1]
    size = width // HEADS
    scale = size ** (-0.5)
    stacked = crops * 8
    lane = lax.broadcasted_iota(jnp.int32, (8, width), 1)
    head = lax.broadcasted_iota(jnp.int32, (8, width), 0)
    own_head = (lane >= head * size) & (lane < (head + 1) * size)
    row = lax.broadcasted_iota(jnp.int32, (tall, 1), 0)
    key_lane = lax.broadcasted_iota(jnp.int32, (1, tall), 1)
    bias = jnp.where(key_lane < length, 0.0, -1e30).astype(f32)
    gain, shift = ca_ln[0:1, :], ca_ln[1:2, :]
    sent_f[...] = sent_ref[...].astype(f32)
    hat, _ = ln_parts(sent_f[...])
    n_head = (hat * gain + shift).astype(bf16)

    def spread(value):
        return jnp.concatenate(
            [jnp.where(own_head, value[crop : crop + 1], 0.0) for crop in range(crops)], 0
        )

    def gathered(value):
        return jnp.concatenate(
            [
                col_sum(jnp.where(own_head, value[crop * 8 : crop * 8 + 8], 0.0))
                for crop in range(crops)
            ],
            0,
        )

    def normed_of(crop):
        return n_all[crop * tall : (crop + 1) * tall, :]

    def against(value):
        return jnp.concatenate(
            [
                mm_t(value[crop * 8 : crop * 8 + 8].astype(bf16), normed_of(crop))
                for crop in range(crops)
            ],
            0,
        )

    def mixed(value):
        return jnp.concatenate(
            [
                mm(value[crop * 8 : crop * 8 + 8].astype(bf16), normed_of(crop))
                for crop in range(crops)
            ],
            0,
        )

    query = spread((mm(n_head, q_w[...]) + q_b[...]).astype(bf16).astype(f32)).astype(bf16)
    keyed = mm_t(query, k_w[...]) * scale
    blank = jnp.zeros((8, width), f32)
    for crop in range(crops):
        mates_all[crop] = jnp.concatenate([keyed[crop * 8 : crop * 8 + 8], blank], 0).astype(bf16)

    def joined(crop):
        here = pl.ds(pl.multiple_of(crop * tall, 16), tall)
        return here, jnp.where(row == 0, sent_f[pl.ds(crop, 1), :], y_ref[here, :])

    def ahead(crop, carry):
        here, value = joined(crop)
        hat, _ = ln_parts(value)
        normed = (hat * gain + shift).astype(bf16)
        n_all[here, :] = normed
        score_all[pl.ds(crop, 1)] = mm_t(mates_all[crop], normed)[None, 0:8]
        return carry

    lax.fori_loop(0, crops, ahead, 0)
    scores = score_all[...].reshape(stacked, tall) + bias
    summit = jnp.max(scores, -1, keepdims=True)
    weights = jnp.exp(scores - summit)
    probs = weights / jnp.sum(weights, -1, keepdims=True)
    rounded = probs.astype(bf16).astype(f32)
    total = jnp.sum(rounded, -1, keepdims=True)
    mean_n = mixed(rounded).astype(bf16)
    attended = gathered(mm(mean_n, v_w[...]) + total * v_b[...]).astype(bf16)
    merged = sent_f[...] + mm(attended, o_w[...]) + o_b[...]
    hat, inverse = ln_parts(merged)
    active, slope = gelu_parts(hat * back_ln[0:1, :] + back_ln[1:2, :])
    active = active.astype(bf16)
    returned_ref[...] = (mm(active, back_w[...]) + back_b[...]).astype(bf16)
    gret = gret_ref[...]
    d_back_w[...] = t_mm(active, gret)
    d_back_b[...] = col_sum(gret.astype(f32))
    gact = mm_t(gret, back_w[...]) * slope
    d_back_ln[0:1, :] = col_sum(gact * hat)
    d_back_ln[1:2, :] = col_sum(gact)
    gfused = ln_back(gact, hat, inverse, back_ln[0:1, :])
    gfo = gfused.astype(bf16)
    d_o_w[...] = t_mm(attended, gfo)
    d_o_b[...] = col_sum(gfo.astype(f32))
    gatt = spread(mm_t(gfo, o_w[...]).astype(bf16).astype(f32))
    d_v_b[...] = col_sum(total * gatt)
    gbias = jnp.sum(gatt * v_b[...], -1, keepdims=True)
    gatt = gatt.astype(bf16)
    d_v_w[...] = t_mm(mean_n, gatt)
    valued = mm_t(gatt, v_w[...])
    gprobs = against(valued) + gbias
    inner = gprobs - jnp.sum(gprobs * probs, -1, keepdims=True)
    gscores = (probs * inner).astype(bf16).astype(f32)
    for crop in range(crops):
        part = slice(crop * 8, crop * 8 + 8)
        mates_all[crop] = jnp.concatenate([keyed[part], valued[part]], 0).astype(bf16)
        pairs_all[crop] = jnp.concatenate([gscores[part], rounded[part]], 0).astype(bf16)
    slid = (mixed(gscores) * scale).astype(bf16)
    d_k_w[...] = t_mm(slid, query)
    gq = gathered(mm(slid, k_w[...])).astype(bf16)
    d_q_w[...] = t_mm(n_head, gq)
    d_q_b[...] = col_sum(gq.astype(f32))
    gn_head[...] = mm_t(gq, q_w[...])
    d_ca_ln[...] = jnp.zeros_like(d_ca_ln)

    def finish(crop, carry):
        here, value = joined(crop)
        hat, inverse = ln_parts(value)
        gn = t_mm(pairs_all[crop], mates_all[crop])
        gn = gn + jnp.where(row == 0, gn_head[pl.ds(crop, 1), :], 0.0)
        d_ca_ln[0:1, :] += col_sum(gn * hat)
        d_ca_ln[1:2, :] += col_sum(gn)
        gj = ln_back(gn, hat, inverse, gain)
        gj_ref[here, :] = gj
        gj_head[pl.ds(crop, 1), :] = gj[0:1, :]
        return carry

    lax.fori_loop(0, crops, finish, 0)
    gsent_ref[...] = (gj_head[...] + gfused).astype(bf16)


def cross(sent, hosted, gret, params, label, length, tall):
    crops, width = sent.shape
    own = gret.shape[1]
    flat = crops * tall
    names = ("ca_ln", "ca_q_w", "ca_q_b", "ca_k_w", "ca_v_w", "ca_v_b", "ca_o_w", "ca_o_b")
    names = names + ("back_ln", "back_w", "back_b")
    weights = [params[label + "_" + name] for name in names]
    outs = [
        jax.ShapeDtypeStruct((crops, own), bf16),
        jax.ShapeDtypeStruct((crops, width), bf16),
        jax.ShapeDtypeStruct((flat, width), f32),
    ] + [jax.ShapeDtypeStruct(value.shape, f32) for value in weights]
    vmem = pl.BlockSpec(memory_space=pltpu.VMEM)
    small = pltpu.VMEM((crops, width), f32)
    values = pl.pallas_call(
        functools.partial(cross_kernel, length, tall, crops),
        out_shape=outs,
        in_specs=[vmem] * (3 + len(weights)),
        out_specs=[vmem] * len(outs),
        scratch_shapes=[
            small,
            pltpu.VMEM((flat, width), bf16),
            pltpu.VMEM((crops, 8, tall), f32),
            pltpu.VMEM((crops, 16, width), bf16),
            pltpu.VMEM((crops, 16, tall), bf16),
            small,
            small,
        ],
        cost_estimate=estimate(2 * flat * width * width * 2, 8_000_000),
        name="cross_" + label,
    )(sent, hosted, gret, *weights)
    grads = {label + "_" + name: value for name, value in zip(names, values[3:])}
    return values[0], values[1], values[2], grads


def head_backward(headrow_ref, gsent_ref, to_ln, to_w, d_to_ln, d_to_w, d_to_b, ghead_ref):
    hat, inverse = ln_parts(headrow_ref[...])
    active, slope = gelu_parts(hat * to_ln[0:1, :] + to_ln[1:2, :])
    gsent = gsent_ref[...]
    d_to_w[...] = t_mm(active.astype(bf16), gsent)
    d_to_b[...] = col_sum(gsent.astype(f32))
    gact = mm_t(gsent, to_w[...]) * slope
    d_to_ln[0:1, :] = col_sum(gact * hat)
    d_to_ln[1:2, :] = col_sum(gact)
    ghead_ref[...] = ln_back(gact, hat, inverse, to_ln[0:1, :])


def clear_all(refs):
    for ref in refs:
        ref[...] = jnp.zeros_like(ref)


def mlp_backward(pair, tall, chunk, live_ref, acts, weights, grads, out_ref, gy, gnormed):
    cot_ref, y_ref, gj_ref, mid_ref, n2_ref, z_ref, slope_ref, ghead, returned_ref = acts
    ln2_ref, fc1_w, fc2_w = weights
    d_ln2, d_fc1_w, d_fc1_b, d_fc2_w, d_fc2_b = grads
    length = out_ref.shape[2]
    row = lax.broadcasted_iota(jnp.int32, (tall, 1), 0)
    for crop in range(pair):
        here = slice(crop * tall, (crop + 1) * tall)
        slot = pl.program_id(0) * pair + crop
        live = jnp.where(slot < live_ref[0], 1.0, 0.0).astype(f32)
        seed = cot_ref[crop].astype(f32) * live + gj_ref[here, :]
        gy[here, :] = jnp.where(row == 0, ghead[pl.ds(slot, 1), :], seed)
        home = returned_ref[pl.ds(slot, 1), :]
        final = jnp.where(row == 0, home, y_ref[here, :])
        out_ref[0, crop] = final[0:length].astype(bf16)
    gm = gy[...].astype(bf16)
    d_fc2_b[...] += col_sum(gm.astype(f32))
    for number in range(fc1_w.shape[1] // chunk):
        cols = slice(number * chunk, (number + 1) * chunk)
        d_fc2_w[cols, :] += t_mm(z_ref[:, cols], gm)
        gu = slope_ref[:, cols].astype(f32) * mm_t(gm, fc2_w[cols, :])
        gu = gu.astype(bf16)
        d_fc1_w[:, cols] += t_mm(n2_ref[...], gu)
        d_fc1_b[:, cols] += col_sum(gu.astype(f32))
        part = mm_t(gu, fc1_w[:, cols])
        gnormed[...] = part if number == 0 else gnormed[...] + part
    hat, inverse = ln_parts(mid_ref[...])
    gn = gnormed[...]
    d_ln2[0:1, :] += col_sum(gn * hat)
    d_ln2[1:2, :] += col_sum(gn)
    gy[...] += ln_back(gn, hat, inverse, ln2_ref[0:1, :])


def attention_backward(pair, tall, acts, weights, grads, gtok_ref, gmid_ref, gqkv, gatt_ref):
    tok_ref, a1_ref, qkv_ref, probs_ref, att_ref = acts
    ln1_ref, qkv_w, proj_w = weights
    d_ln1, d_qkv_w, d_qkv_b, d_proj_w, d_proj_b = grads
    width = tok_ref.shape[-1]
    length = gtok_ref.shape[2]
    found, size = groups(width)
    scale = size ** (-0.5)
    gp = gmid_ref[...].astype(bf16)
    d_proj_w[...] += t_mm(att_ref[...], gp)
    d_proj_b[...] += col_sum(gp.astype(f32))
    gatt_ref[...] = mm_t(gp, proj_w[...]).astype(bf16)

    def one(crop, carry):
        here = pl.ds(crop * tall, tall)
        if not isinstance(crop, int):
            here = pl.ds(pl.multiple_of(crop * tall, 16), tall)
        for start, stop, count in found:
            first = start // size
            query = stack_heads(qkv_ref[here, start:stop], count, size)
            key = qkv_ref[here, width + start : width + stop]
            value = qkv_ref[here, 2 * width + start : 2 * width + stop]
            gatt = stack_heads(gatt_ref[here, start:stop], count, size)
            probs_low = jnp.concatenate([probs_ref[crop, first + head] for head in range(count)], 0)
            probs = probs_low.astype(f32)
            gprobs = mm_t(gatt, value)
            inner = gprobs - jnp.sum(gprobs * probs, -1, keepdims=True)
            gscores = (probs * inner).astype(bf16)
            gq = merge_heads(mm(gscores, key), count, size) * scale
            gk = t_mm(gscores, query) * scale
            gv = t_mm(probs_low, gatt)
            gqkv[here, start:stop] = gq.astype(bf16)
            gqkv[here, width + start : width + stop] = gk.astype(bf16)
            gqkv[here, 2 * width + start : 2 * width + stop] = gv.astype(bf16)
        return carry

    if len(found) > 2:
        lax.fori_loop(0, pair, one, 0)
    else:
        for crop in range(pair):
            one(crop, 0)
    grad = gqkv[...]
    d_qkv_w[...] += t_mm(a1_ref[...], grad)
    d_qkv_b[...] += col_sum(grad.astype(f32))
    gn = mm_t(grad, qkv_w[...])
    hat, inverse = ln_parts(tok_ref[...].reshape(pair * tall, width).astype(f32))
    d_ln1[0:1, :] += col_sum(gn * hat)
    d_ln1[1:2, :] += col_sum(gn)
    gtok = gmid_ref[...] + ln_back(gn, hat, inverse, ln1_ref[0:1, :])
    for crop in range(pair):
        gtok_ref[0, crop] = gtok[crop * tall : crop * tall + length].astype(bf16)


GRAD_MLP = ("ln2", "fc1_w", "fc1_b", "fc2_w", "fc2_b")
GRAD_ATTENTION = ("ln1", "qkv_w", "qkv_b", "proj_w", "proj_b")


def mlp_back_kernel(pair, tall, chunk, live_ref, *refs):
    cot_ref, y_ref, gj_ref, mid_ref, n2_ref, z_ref, slope_ref, returned_ref = refs[:8]
    weights = refs[8:11]
    near, far = refs[11:15], refs[15:19]
    out_ref, gmid_ref, ghead_far = refs[19:22]
    grads, near_grads, far_grads = refs[22:27], refs[27:30], refs[30:33]
    ghead, gnormed, home = refs[33:]

    @pl.when(pl.program_id(0) == 0)
    def _():
        head_backward(*near, *near_grads, ghead)
        head_backward(*far, *far_grads, ghead_far)
        clear_all(grads)
        home[...] = returned_ref[...].astype(f32)

    acts = (cot_ref, y_ref, gj_ref, mid_ref, n2_ref, z_ref, slope_ref, ghead, home)
    mlp_backward(pair, tall, chunk, live_ref, acts, weights, grads, out_ref, gmid_ref, gnormed)


def attention_back_kernel(pair, tall, gmid_ref, *refs):
    acts, weights, gtok_ref, grads = refs[:5], refs[5:8], refs[8], refs[9:14]

    @pl.when(pl.program_id(0) == 0)
    def _():
        clear_all(grads)

    attention_backward(pair, tall, acts, weights, grads, gtok_ref, gmid_ref, *refs[14:])


def block_back_kernel(pair, tall, chunk, live_ref, *refs):
    mlp_acts, acts = refs[:9], refs[9:14]
    weights, mlp_weights = refs[14:17], refs[17:20]
    out_ref, gtok_ref = refs[20:22]
    mlp_grads, grads = refs[22:27], refs[27:32]
    gy, gnormed, gqkv, gatt_ref, home = refs[32:]

    @pl.when(pl.program_id(0) == 0)
    def _():
        clear_all(mlp_grads + grads)
        home[...] = mlp_acts[8][...].astype(f32)

    mlp_backward(
        pair, tall, chunk, live_ref, (*mlp_acts[:8], home), mlp_weights, mlp_grads, out_ref, gy, gnormed
    )
    attention_backward(pair, tall, acts, weights, grads, gtok_ref, gy, gqkv, gatt_ref)


def named(label, names, values):
    return {label + "_" + name: value for name, value in zip(names, values)}


def grad_outs(params, label, names):
    return [
        (fixed_spec(value.shape), jax.ShapeDtypeStruct(value.shape, f32))
        for value in pick(params, label, names)
    ]


def token_out(crops, length, width, pair):
    return (
        pl.BlockSpec((1, pair, length, width), lambda i: (0, i, 0, 0)),
        jax.ShapeDtypeStruct((1, crops, length, width), bf16),
    )


def mlp_back(cot, live, kept, gj, near, far, returned, params, label, other, length, pair):
    crops, tall, width = cot.shape
    mid, n2, z, slope, y = kept
    hidden = z.shape[1]
    rows, flat = pair * tall, crops * tall
    weights = pick(params, label, ("ln2", "fc1_w", "fc2_w"))
    near = list(near) + pick(params, label, ("to_ln", "to_w"))
    far = list(far) + pick(params, other, ("to_ln", "to_w"))
    smem = pl.BlockSpec(memory_space=pltpu.SMEM)
    outs = [
        token_out(crops, length, width, pair),
        (row_spec(rows, width), jax.ShapeDtypeStruct((flat, width), f32)),
        (fixed_spec(far[0].shape), jax.ShapeDtypeStruct(far[0].shape, f32)),
    ]
    outs += grad_outs(params, label, GRAD_MLP)
    outs += grad_outs(params, label, TO) + grad_outs(params, other, TO)
    values = pl.pallas_call(
        functools.partial(mlp_back_kernel, pair, tall, 384),
        grid=(crops // pair,),
        out_shape=[shape for spec, shape in outs],
        in_specs=[smem, pl.BlockSpec((pair, tall, width), lambda i: (i, 0, 0))]
        + [row_spec(rows, width)] * 4
        + [row_spec(rows, hidden)] * 2
        + [whole(value.shape) for value in [returned] + weights + near + far],
        out_specs=[spec for spec, shape in outs],
        scratch_shapes=[
            pltpu.VMEM((crops, width), f32),
            pltpu.VMEM((rows, width), f32),
            pltpu.VMEM((crops, width), f32),
        ],
        cost_estimate=estimate(8 * 8 * flat * width * hidden, 20_000_000),
        name="mlp_back_" + label,
    )(live, cot, y, gj, mid, n2, z, slope, returned, *weights, *near, *far)
    grads = named(label, GRAD_MLP, values[3:8])
    grads.update(named(label, TO, values[8:11]))
    grads.update(named(other, TO, values[11:14]))
    return values[0], values[1], values[2], grads


def attention_back(tokens, gmid, kept, params, label, length, pair):
    crops, tall, width = tokens.shape
    a1, qkv, probs, att = kept
    rows, flat = pair * tall, crops * tall
    weights = pick(params, label, ("ln1", "qkv_w", "proj_w"))
    outs = [token_out(crops, length, width, pair)] + grad_outs(params, label, GRAD_ATTENTION)
    values = pl.pallas_call(
        functools.partial(attention_back_kernel, pair, tall),
        grid=(crops // pair,),
        out_shape=[shape for spec, shape in outs],
        in_specs=[
            row_spec(rows, width),
            pl.BlockSpec((pair, tall, width), lambda i: (i, 0, 0)),
            row_spec(rows, width),
            row_spec(rows, 3 * width),
            pl.BlockSpec((pair, HEADS, tall, tall), lambda i: (i, 0, 0, 0)),
            row_spec(rows, width),
        ]
        + [whole(value.shape) for value in weights],
        out_specs=[spec for spec, shape in outs],
        scratch_shapes=[pltpu.VMEM((rows, 3 * width), bf16), pltpu.VMEM((rows, width), bf16)],
        cost_estimate=estimate(8 * 16 * flat * width * width, 20_000_000),
        name="attention_back_" + label,
    )(gmid, tokens, a1, qkv, probs, att, *weights)
    return values[0], named(label, GRAD_ATTENTION, values[1:])


def block_back(tokens, cot, live, kept, gj, ghead, returned, params, label, length, pair):
    crops, tall, width = tokens.shape
    a1, qkv, probs, att, mid, n2, z, slope, y = kept
    hidden = z.shape[1]
    rows, flat = pair * tall, crops * tall
    weights = pick(params, label, ("ln1", "qkv_w", "proj_w", "ln2", "fc1_w", "fc2_w"))
    smem = pl.BlockSpec(memory_space=pltpu.SMEM)
    token_spec = pl.BlockSpec((pair, tall, width), lambda i: (i, 0, 0))
    outs = [token_out(crops, length, width, pair)] * 2
    outs += grad_outs(params, label, GRAD_MLP) + grad_outs(params, label, GRAD_ATTENTION)
    values = pl.pallas_call(
        functools.partial(block_back_kernel, pair, tall, 384),
        grid=(crops // pair,),
        out_shape=[shape for spec, shape in outs],
        in_specs=[smem, token_spec]
        + [row_spec(rows, width)] * 4
        + [row_spec(rows, hidden)] * 2
        + [whole(ghead.shape), whole(returned.shape)]
        + [
            token_spec,
            row_spec(rows, width),
            row_spec(rows, 3 * width),
            pl.BlockSpec((pair, HEADS, tall, tall), lambda i: (i, 0, 0, 0)),
            row_spec(rows, width),
        ]
        + [whole(value.shape) for value in weights],
        out_specs=[spec for spec, shape in outs],
        scratch_shapes=[
            pltpu.VMEM((rows, width), f32),
            pltpu.VMEM((rows, width), f32),
            pltpu.VMEM((rows, 3 * width), bf16),
            pltpu.VMEM((rows, width), bf16),
            pltpu.VMEM((crops, width), f32),
        ],
        cost_estimate=estimate(8 * 4 * flat * (4 * width * width + 2 * width * hidden), 20_000_000),
        name="block_back_" + label,
    )(live, cot, y, gj, mid, n2, z, slope, ghead, returned, tokens, a1, qkv, probs, att, *weights)
    grads = named(label, GRAD_MLP, values[2:7])
    grads.update(named(label, GRAD_ATTENTION, values[7:12]))
    return values[0], values[1], grads


def swap(value):
    return lax.ppermute(value, "branch", [(0, 1), (1, 0)])


def partner(value, bit):
    count = lax.axis_size("dp")
    return lax.ppermute(value, "dp", [(i, i ^ bit) for i in range(count)])


def side_partner(value, place):
    count = lax.axis_size("dp")
    pairs = []
    for core in range(2):
        bit = 1 << (place ^ core)
        pairs += [(core * count + i, core * count + (i ^ bit)) for i in range(count)]
    return lax.ppermute(value, ("branch", "dp"), pairs)


def tie(value, *others):
    return lax.optimization_barrier((value, *others))[0] if others else value


def gather_lines(held, first, last, jobs=()):
    for number, place in enumerate(range(first, last, -1)):
        got = partner(held, 1 << place)
        if number < len(jobs):
            got = tie(got, *jobs[number](held))
        held = jnp.concatenate([held, got], 0)
    return held


def gather_middle(held):
    return jnp.concatenate([held, side_partner(held, 1)], 0)


def add_low(*values):
    total = values[0].astype(f32)
    for value in values[1:]:
        total = total + value.astype(f32)
    return total.astype(bf16)


def reduce_start(low, high, got):
    half = low.shape[0]
    sent = add_low(high, got[half:])
    return sent, [low, got[:half], side_partner(sent, 0)]


def reduce_middle(parts):
    quarter = parts[0].shape[0] // 2
    sent = add_low(*[part[quarter:] for part in parts])
    return sent, [part[:quarter] for part in parts] + [side_partner(sent, 1)]


def reduce_line(parts, place):
    count = parts[0].shape[0] // 2
    sent = add_low(*[part[count:] for part in parts])
    return [part[:count] for part in parts] + [partner(sent, 1 << place)]


def reduce_lines(parts, first, last):
    for place in range(first, last):
        parts = reduce_line(parts, place)
    return parts


def add_up(parts):
    total = parts[0][0].astype(f32)
    for part in parts[1:]:
        total = total + part[0].astype(f32)
    return total


def shards(
    small_tokens,
    large_tokens,
    small_cot,
    large_cot,
    live_counts,
    master,
    first_moment,
    second_moment,
):
    count = lax.axis_size("branch") * lax.axis_size("dp")
    bits = lax.axis_size("dp").bit_length() - 1
    plan = grid_plan(count)
    core, mine = lax.axis_index("branch"), lax.axis_index("dp")
    where = jnp.stack([core, mine]).astype(jnp.int32)
    index = lax.axis_index(("branch", "dp"))
    size = master.shape[0]
    rows = plan["shard_rows"]
    table = lax.dynamic_index_in_dim(jnp.asarray(plan["table"]), index, 0, False)
    padded = jnp.pad(master, (0, rows * LANES - size)).reshape(rows, LANES)
    keep, send = align(where, table, padded, plan)
    got = swap(send)
    counts = live_counts[:, 0]
    own_count = lax.dynamic_slice_in_dim(counts, core, 1)
    far_count = lax.dynamic_slice_in_dim(counts, 1 - core, 1)
    crops, length_s = small_tokens.shape[1], small_tokens.shape[2]
    length_l = large_tokens.shape[2]
    tall_s, tall_l = round_up(length_s, 16), round_up(length_l, 16)
    pair = 2

    def inward(value):
        return jnp.transpose(value[0], (1, 0, 2))

    def settled(value):
        return with_layout_constraint(inward(value), Layout(major_to_minor=(0, 1, 2)))

    def outward(value):
        return jnp.transpose(value, (1, 0, 2))[None]

    def taller(value, length, tall):
        return jnp.pad(value[0], ((0, 0), (0, tall - length), (0, 0)))

    early = []

    def pad_tokens(held):
        early.append(taller(tie(small_tokens, held), length_s, tall_s))
        early.append(taller(tie(large_tokens, held), length_l, tall_l))
        return early[0:2]

    def pad_seeds(held):
        slots = jnp.arange(crops, dtype=jnp.int32)[:, None]
        small_held, large_held = tie(small_cot, held), tie(large_cot, held)
        early.append(taller(small_held, length_s, tall_s))
        early.append(taller(large_held, length_l, tall_l))
        early.append(jnp.where(slots < own_count, small_held[0, :, 0], 0))
        early.append(jnp.where(slots < far_count, large_held[0, :, 0], 0))
        return early[2:6]

    held = jnp.where(core == 0, keep, got)[None]
    near = gather_lines(held, bits - 1, 1, (pad_tokens, pad_seeds))
    small, large, small_seed, large_seed, ret_small, ret_large = early
    far = tie(jnp.where(core == 0, got, keep)[None], near)
    middle = (bits + 1) // 2
    far = gather_lines(far, bits - 1, middle)
    near = tie(gather_middle(near), far)
    near_end = side_partner(near, 0)
    far = gather_lines(far, middle, 1)
    near_end = tie(near_end, far)
    near_pieces = (near, near_end, swap(near), swap(near_end))
    ret_small, ret_large = swap(ret_small), swap(ret_large)

    params = unflatten(where, near_pieces, plan, 0, bits)
    straddling = params.pop(plan["sides"][1][0][0])
    far = tie(far, near_end)
    far = jnp.concatenate([far, tie(side_partner(far, 1), params["s_ln1"])], 0)
    *kept_s, head_s = block_forward(tie(small, far), params, "s", length_s, pair)
    far_end = side_partner(far, 0)
    kept_l = attention_only(tie(large, far_end), params, "l", length_l, 1)
    far_pieces = (far, far_end, swap(far), swap(far_end))
    params.update(unflatten(where, far_pieces, plan, 1, bits, (straddling,)))
    z_l, slope_l, y_l, head_l, sent_l, sent_s = mlp_only(
        kept_l[4], kept_l[5], head_s, params, "l", "s", crops, pair
    )
    got_s, got_l = swap(sent_s), swap(sent_l)
    grads = {}
    back_s, gsent_s, gj_l, part = cross(got_s, y_l, ret_small, params, "s", length_l, tall_l)
    grads.update(part)
    home_s, own_s = swap(back_s), swap(gsent_s)
    back_l, gsent_l, gj_s, part = cross(got_l, kept_s[8], ret_large, params, "l", length_s, tall_s)
    grads.update(part)
    home_l, own_l = swap(back_l), swap(gsent_l)
    large_out, gmid, ghead_s, part = mlp_back(
        large_seed,
        far_count,
        (kept_l[4], kept_l[5], z_l, slope_l, y_l),
        gj_l,
        (head_l, own_l),
        (head_s, own_s),
        home_l,
        params,
        "l",
        "s",
        length_l,
        pair,
    )
    grads.update(part)
    far_parts = flatten(where, grads, plan, 2)
    far_got = swap(far_parts[2])
    large_grad, part = attention_back(large, gmid, kept_l[:4], params, "l", length_l, pair)
    grads.update(part)
    grads["l_ln1"], far_got = lax.optimization_barrier((grads["l_ln1"], far_got))
    upper_parts = flatten(where, grads, plan, 1)
    upper_got = swap(upper_parts[2])
    sent_far, far_side = reduce_start(*far_parts[:2], far_got)
    sent_upper, upper = reduce_start(*upper_parts[:2], tie(upper_got, sent_far))
    ghead_s = tie(ghead_s, sent_far, sent_upper, gmid)
    small_out, small_grad, part = block_back(
        small, small_seed, own_count, kept_s, gj_s, ghead_s, home_s, params, "s", length_s, pair
    )
    grads.update(part)
    grads["s_ln1"] = tie(grads["s_ln1"], far_side[-1], upper[-1])
    lower_parts = flatten(where, grads, plan, 0)
    lower_got = swap(lower_parts[2])
    sent, far_side = reduce_middle(far_side)
    sent, upper = reduce_middle(upper)
    sent, lower = reduce_start(*lower_parts[:2], lower_got)
    lower[-1], large_out, large_grad = lax.optimization_barrier(
        (lower[-1], settled(tie(large_out, sent)), settled(tie(large_grad, sent)))
    )
    far_side[-1], upper[-1] = tie(far_side[-1], sent), tie(upper[-1], sent)
    far_side = reduce_line(far_side, 2)
    upper = reduce_lines(upper, 2, bits - 1)
    sent, lower = reduce_middle(lower)
    lower[-1], small_out, small_grad = lax.optimization_barrier(
        (lower[-1], settled(tie(small_out, sent)), settled(tie(small_grad, sent)))
    )
    lower = add_up(reduce_lines(lower, 2, bits - 1))
    far_total = add_up(reduce_lines(far_side, 3, bits))
    upper = add_up(upper)
    top = (mine >> (bits - 1)) & 1
    last_sent = jnp.where(top == 1, lower, upper).astype(bf16)
    near_total = jnp.where(top == 1, upper, lower)
    near_total = near_total + partner(last_sent, 1 << (bits - 1)).astype(f32)
    own = jnp.where(core == 0, near_total, far_total)
    got = swap(jnp.where(core == 0, far_total, near_total))
    summed, square = unalign(where, table, own, got, plan)
    square = square + swap(square)
    for place in range(bits):
        square = square + partner(square, 1 << place)
    grad_norm = jnp.sqrt(square[0, 0])
    own_grad = summed.reshape(-1)[:size]
    clipped = own_grad * jnp.minimum(1.0, clip_norm / grad_norm)
    new_first = beta_one * first_moment + (1.0 - beta_one) * clipped
    new_second = beta_two * second_moment + (1.0 - beta_two) * clipped * clipped
    new_master = master - rate * (
        new_first / bias_one / (jnp.sqrt(new_second / bias_two) + adam_eps) + decay * master
    )
    return (
        outward(small_out),
        outward(large_out),
        outward(small_grad),
        outward(large_grad),
        grad_norm,
        new_first,
        new_second,
        new_master,
        new_master.astype(bf16),
    )


def solution(mesh):
    return jax.shard_map(
        shards,
        mesh=mesh,
        in_specs=(
            P("branch", "dp", None, None),
            P("branch", "dp", None, None),
            P("branch", "dp", None, None),
            P("branch", "dp", None, None),
            P(None, "dp"),
            P(("branch", "dp")),
            P(("branch", "dp")),
            P(("branch", "dp")),
        ),
        out_specs=(
            P("branch", "dp", None, None),
            P("branch", "dp", None, None),
            P("branch", "dp", None, None),
            P("branch", "dp", None, None),
            P(),
            P(("branch", "dp")),
            P(("branch", "dp")),
            P(("branch", "dp")),
            P(("branch", "dp")),
        ),
        check_vma=False,
    )
```

```python
import functools
import math

import jax
import jax.numpy as jnp
import numpy as np
from jax import lax
from jax.experimental import pallas as pl
from jax.experimental.pallas import tpu as pltpu
from jax.experimental.layout import Layout, with_layout_constraint
from jax.sharding import PartitionSpec as P

DS = 192
DL = 384
MS = 768
ML = 1536
HEADS = 6

norm_eps = 1e-06
clip_norm = 1.0
beta_one = 0.5
beta_two = 0.5
adam_eps = 1e-08
rate = 0.05
decay = 0.05
bias_one = 1.0 - 0.5**5
bias_two = 1.0 - 0.5**5

f32 = jnp.float32
bf16 = jnp.bfloat16
LANES = 128


def layout():
    shapes = []
    for label, width, hidden in (("s", DS, MS), ("l", DL, ML)):
        shapes += [
            (label + "_ln1", (2, width)),
            (label + "_qkv_w", (width, 3 * width)),
            (label + "_qkv_b", (3 * width,)),
            (label + "_proj_w", (width, width)),
            (label + "_proj_b", (width,)),
            (label + "_ln2", (2, width)),
            (label + "_fc1_w", (width, hidden)),
            (label + "_fc1_b", (hidden,)),
            (label + "_fc2_w", (hidden, width)),
            (label + "_fc2_b", (width,)),
        ]
    for label, owner, other in (("s", DS, DL), ("l", DL, DS)):
        shapes += [
            (label + "_to_ln", (2, owner)),
            (label + "_to_w", (owner, other)),
            (label + "_to_b", (other,)),
            (label + "_ca_ln", (2, other)),
            (label + "_ca_q_w", (other, other)),
            (label + "_ca_q_b", (other,)),
            (label + "_ca_k_w", (other, other)),
            (label + "_ca_v_w", (other, other)),
            (label + "_ca_v_b", (other,)),
            (label + "_ca_o_w", (other, other)),
            (label + "_ca_o_b", (other,)),
            (label + "_back_ln", (2, other)),
            (label + "_back_w", (other, owner)),
            (label + "_back_b", (owner,)),
        ]
    return shapes


def round_up(value, unit):
    return -(-value // unit) * unit


def grid_plan(shards):
    names = []
    regions = []
    offset = 0
    for label, shape in layout():
        count = math.prod(shape)
        phase = offset % LANES
        if not regions or regions[-1][2] != phase:
            regions.append([offset, offset, phase])
        names.append((label, shape, offset, len(regions) - 1))
        offset += count
        regions[-1][1] = offset
    total = offset
    starts = []
    row = 0
    for first, last, phase in regions:
        starts.append(row)
        row += -(-(last - first) // LANES)
    rows = row
    places = {}
    for label, shape, place, region in names:
        places[label] = (starts[region] + (place - regions[region][0]) // LANES, shape)
    size = total // shards
    bases = []
    pieces = []
    for device in range(shards):
        low, high = device * size, (device + 1) * size
        own = []
        base = None
        for (first, last, phase), start in zip(regions, starts):
            left, right = max(low, first), min(high, last)
            if left >= right:
                continue
            if base is None:
                base = (start + (left - first) // LANES) // 16 * 16
            delta = start * LANES - first + low - base * LANES
            own.append((left - low, right - low, delta))
        bases.append(base)
        pieces.append(own)
    most = max(len(own) for own in pieces)
    table = np.zeros((shards, most * 3), np.int32)
    need = 0
    for device, own in enumerate(pieces):
        for number, (left, right, delta) in enumerate(own):
            table[device, 3 * number : 3 * number + 3] = (left, right, delta)
            need = max(need, right + delta)
    span = round_up(-(-need // LANES), 32)
    overlap = 16
    for device in range(1, shards):
        overlap = max(overlap, bases[device - 1] + span - bases[device])
    half = shards // 2
    edge = half * size
    sides = [[], []]
    for label, shape, place, region in names:
        if place < edge:
            sides[0].append((label, shape))
        if place + math.prod(shape) > edge:
            sides[1].append((label, shape))
    origins = [0, min(bases[half], places[sides[1][0][0]][0]) // 16 * 16]
    heights = []
    for side in range(2):
        last = bases[half * (side + 1) - 1] + span
        for label, shape in sides[side]:
            last = max(last, places[label][0] + -(-math.prod(shape) // LANES))
        heights.append(round_up(last - origins[side] + overlap, 16))
    groups = []
    for first, last in ((0, half // 2), (half // 2, half), (half, shards)):
        held = [
            (label, shape)
            for label, shape, place, region in names
            if place < last * size and place + math.prod(shape) > first * size
        ]
        origin = min([bases[first]] + [places[label][0] for label, shape in held]) // 16 * 16
        stop = max(
            [bases[last - 1] + span]
            + [places[label][0] + -(-math.prod(shape) // LANES) for label, shape in held]
        )
        groups.append((first, last - first, held, origin, round_up(stop - origin + overlap, 16)))
    return dict(
        places=places,
        groups=groups,
        rows=rows,
        half=half,
        sides=sides,
        origins=origins,
        heights=heights,
        size=size,
        bases=bases,
        table=table,
        most=most,
        span=span,
        overlap=overlap,
        shard_rows=round_up(-(-size // LANES), 16),
    )


def mm(left, right):
    return lax.dot_general(left, right, (((1,), (0,)), ((), ())), preferred_element_type=f32)


def mm_t(left, right):
    return lax.dot_general(left, right, (((1,), (1,)), ((), ())), preferred_element_type=f32)


def t_mm(left, right):
    return lax.dot_general(left, right, (((0,), (0,)), ((), ())), preferred_element_type=f32)


def vmem_spec(shape, index):
    return pl.BlockSpec(shape, index)


def whole(shape):
    rank = len(shape)
    return pl.BlockSpec(shape, lambda *_: (0,) * rank, pipeline_mode=pl.Buffered(1))


def estimate(flops, moved):
    return pl.CostEstimate(flops=int(flops), bytes_accessed=int(moved), transcendentals=0)


def shift_rows(ref, amount, rows, margin):
    down = amount // LANES
    across = amount - down * LANES
    here = ref[pl.ds(margin - down, rows), :]
    above = ref[pl.ds(margin - down - 1, rows), :]
    here = pltpu.roll(here, across, 1)
    above = pltpu.roll(above, across, 1)
    lane = lax.broadcasted_iota(jnp.int32, here.shape, 1)
    return jnp.where(lane < across, above, here)


def align_kernel(most, rows, span, margin, core_ref, table_ref, shard_ref, keep_ref, send_ref, padded):
    padded[...] = jnp.zeros_like(padded)
    padded[margin : margin + rows, :] = shard_ref[...]
    place = lax.broadcasted_iota(jnp.int32, (span, LANES), 0) * LANES
    place = place + lax.broadcasted_iota(jnp.int32, (span, LANES), 1)
    total = jnp.zeros((span, LANES), f32)
    for number in range(most):
        left = table_ref[3 * number]
        right = table_ref[3 * number + 1]
        delta = table_ref[3 * number + 2]
        moved = shift_rows(padded, delta, span, margin)
        total = jnp.where((place >= left + delta) & (place < right + delta), moved, total)
    total = total.astype(bf16)
    first = core_ref[0] == 0
    upper, lower = total[: span // 2], total[span // 2 :]
    keep_ref[...] = jnp.where(first, upper, lower)
    send_ref[...] = jnp.where(first, lower, upper)


def unalign_kernel(
    most, rows, span, margin, core_ref, table_ref, own_ref, got_ref, out_ref, padded
):
    first = core_ref[0] == 0
    padded[span:, :] = jnp.zeros((padded.shape[0] - span, LANES), f32)
    padded[0 : span // 2, :] = jnp.where(first, own_ref[...], got_ref[...])
    padded[span // 2 : span, :] = jnp.where(first, got_ref[...], own_ref[...])
    place = lax.broadcasted_iota(jnp.int32, (rows, LANES), 0) * LANES
    place = place + lax.broadcasted_iota(jnp.int32, (rows, LANES), 1)
    total = jnp.zeros((rows, LANES), f32)
    lane = lax.broadcasted_iota(jnp.int32, (rows, LANES), 1)
    for number in range(most):
        left = table_ref[3 * number]
        right = table_ref[3 * number + 1]
        delta = table_ref[3 * number + 2]
        down = delta // LANES
        across = delta - down * LANES
        back = lax.rem(LANES - across, LANES)
        here = pltpu.roll(padded[pl.ds(down, rows), :], back, 1)
        below = pltpu.roll(padded[pl.ds(down + 1, rows), :], back, 1)
        moved = jnp.where(lane < LANES - across, here, below)
        total = jnp.where((place >= left) & (place < right), moved, total)
    out_ref[...] = total


def settle_kernel(most, where_ref, table_ref, keep_ref, last_ref, *refs):
    *far_refs, own_ref, send_ref, norm_ref = refs
    core = where_ref[0]
    near = keep_ref[...] + last_ref[...].astype(f32)
    far = far_refs[0][0].astype(f32)
    for ref in far_refs[1:]:
        far = far + ref[0].astype(f32)
    rows = near.shape[0]
    place = (lax.broadcasted_iota(jnp.int32, near.shape, 0) + core * rows) * LANES
    place = place + lax.broadcasted_iota(jnp.int32, near.shape, 1)

    def squares(total, entry):
        found = jnp.zeros_like(total)
        for number in range(most):
            at = 3 * (entry * most + number)
            left, right, delta = table_ref[at], table_ref[at + 1], table_ref[at + 2]
            inside = (place >= left + delta) & (place < right + delta)
            found = jnp.where(inside, total * total, found)
        return found

    both = squares(near, 0) + squares(far, 1)
    norm_ref[...] = jnp.broadcast_to(jnp.sum(both).reshape(1, 1), (8, LANES))
    own_ref[...] = jnp.where(core == 0, near, far)
    send_ref[...] = jnp.where(core == 0, far, near)


def settle(where, tables, keep, last, far_parts, plan):
    smem = pl.BlockSpec(memory_space=pltpu.SMEM)
    part = jax.ShapeDtypeStruct(keep.shape, f32)
    return pl.pallas_call(
        functools.partial(settle_kernel, plan["most"]),
        grid=(1,),
        out_shape=(part, part, jax.ShapeDtypeStruct((8, LANES), f32)),
        in_specs=[smem, smem, fixed_spec(keep.shape), fixed_spec(keep.shape)]
        + [pl.BlockSpec((1, *keep.shape), lambda i: (0, 0, 0))] * len(far_parts),
        out_specs=(fixed_spec(keep.shape), fixed_spec(keep.shape), fixed_spec((8, LANES))),
        cost_estimate=estimate(1_000_000, 2_000_000),
        name="settle",
    )(where, tables, keep, last, *far_parts)


def align(core, table, shard, plan):
    rows, span, most = plan["shard_rows"], plan["span"], plan["most"]
    margin = 8 + round_up(int(plan["table"].max(initial=0, where=pick_delta(plan))) // LANES + 1, 8)
    tall = margin + max(rows, span) + 8
    vmem = pl.BlockSpec(memory_space=pltpu.VMEM)
    smem = pl.BlockSpec(memory_space=pltpu.SMEM)
    part = jax.ShapeDtypeStruct((span // 2, LANES), bf16)
    return pl.pallas_call(
        functools.partial(align_kernel, most, rows, span, margin),
        out_shape=(part, part),
        in_specs=[smem, smem, vmem],
        out_specs=(vmem, vmem),
        scratch_shapes=[pltpu.VMEM((tall, LANES), f32)],
        cost_estimate=estimate(1_000_000, 1_000_000),
        name="align",
    )(core, table, shard)


def unalign(core, table, own, got, plan):
    rows, span, most = plan["shard_rows"], plan["span"], plan["most"]
    margin = 16 + round_up(int(plan["table"].max(initial=0, where=pick_delta(plan))) // LANES + 1, 8)
    tall = max(rows, span) + margin
    vmem = pl.BlockSpec(memory_space=pltpu.VMEM)
    smem = pl.BlockSpec(memory_space=pltpu.SMEM)
    return pl.pallas_call(
        functools.partial(unalign_kernel, most, rows, span, margin),
        out_shape=jax.ShapeDtypeStruct((rows, LANES), f32),
        in_specs=[smem, smem, vmem, vmem],
        out_specs=vmem,
        scratch_shapes=[pltpu.VMEM((tall, LANES), f32)],
        cost_estimate=estimate(1_000_000, 1_000_000),
        name="unalign",
    )(core, table, own, got)


def pick_delta(plan):
    mask = np.zeros(plan["table"].shape, bool)
    mask[:, 2::3] = True
    return mask


def two_dim(shape):
    return shape if len(shape) == 2 else (1, shape[0])


def is_matrix(label):
    return label[-2:] == "_w"


def strided(start, count, step):
    return pl.ds(start, count) if step == 1 or count == 1 else pl.ds(start, count, stride=step)


def half_swap(value):
    return pltpu.roll(value, LANES // 2, 1)


def read_param(flat, row, shape, out_ref, pair_ref):
    depth, width = two_dim(shape)
    dtype = out_ref.dtype
    if width % LANES == 0:
        step = width // LANES
        for col in range(step):
            out_ref[:, col * LANES : (col + 1) * LANES] = flat[
                strided(row + col, depth, step), :
            ].astype(dtype)
        return
    half = LANES // 2
    lead = width // LANES
    if depth == 1:
        for col in range(lead):
            out_ref[:, col * LANES : (col + 1) * LANES] = flat[row + col : row + col + 1, :].astype(
                dtype
            )
        out_ref[:, lead * LANES :] = flat[row + lead : row + lead + 1, 0:half].astype(dtype)
        return
    step = 2 * width // LANES
    pairs = depth // 2
    lane = lax.broadcasted_iota(jnp.int32, (pairs, LANES), 1)
    blocks = [flat[strided(row + col, pairs, step), :] for col in range(step)]
    turned = [half_swap(block) for block in blocks[lead:]]
    for col in range(lead):
        pair_ref[col, strided(0, pairs, 2), :] = blocks[col]
        pair_ref[col, strided(1, pairs, 2), :] = jnp.where(lane < half, turned[col], turned[col + 1])
    pair_ref[lead, strided(0, pairs, 2), :] = blocks[lead]
    pair_ref[lead, strided(1, pairs, 2), :] = turned[lead]
    for col in range(lead):
        out_ref[:, col * LANES : (col + 1) * LANES] = pair_ref[col, 0:depth, :].astype(dtype)
    out_ref[:, lead * LANES :] = pair_ref[lead, 0:depth, 0:half].astype(dtype)


def write_param(flat, row, shape, in_ref, pair_ref, window):
    depth, width = two_dim(shape)
    if width % LANES == 0:
        step = width // LANES
        first = max(0, (window[0] - row) // step) // 8 * 8
        last = min(depth, round_up(max(0, -(-(window[1] - row) // step)), 8))
        for col in range(step):
            flat[strided(row + first * step + col, last - first, step), :] = in_ref[
                first:last, col * LANES : (col + 1) * LANES
            ]
        return
    half = LANES // 2
    lead = width // LANES
    if depth == 1:
        for col in range(lead):
            flat[row + col : row + col + 1, :] = in_ref[:, col * LANES : (col + 1) * LANES]
        tail = jnp.concatenate([in_ref[:, lead * LANES :], jnp.zeros((1, half), f32)], 1)
        flat[row + lead : row + lead + 1, :] = tail
        return
    step = 2 * width // LANES
    pairs = depth // 2
    lane = lax.broadcasted_iota(jnp.int32, (pairs, LANES), 1)
    for col in range(lead):
        pair_ref[col, 0:depth, :] = in_ref[:, col * LANES : (col + 1) * LANES]
    pair_ref[lead, 0:depth, 0:half] = in_ref[:, lead * LANES :]
    even = [pair_ref[col, strided(0, pairs, 2), :] for col in range(lead + 1)]
    odd = [half_swap(pair_ref[col, strided(1, pairs, 2), :]) for col in range(lead + 1)]
    for col in range(lead):
        flat[strided(row + col, pairs, step), :] = even[col]
    flat[strided(row + lead, pairs, step), :] = jnp.where(lane < half, even[lead], odd[0])
    for col in range(lead):
        flat[strided(row + lead + 1 + col, pairs, step), :] = jnp.where(
            lane < half, odd[col], odd[col + 1]
        )


def decode(number, core, bits):
    first = (number >> (bits - 1)) & 1
    second = (number >> (bits - 2)) & 1
    found = (first << core) | (second << (1 - core))
    for place in range(2, bits):
        found = found | (((number >> (bits - 1 - place)) & 1) << place)
    return found


def unflatten_kernel(plan, side, bits, where_ref, base_ref, *refs):
    pieces, refs = refs[:4], refs[4:]
    carried, refs = (refs[:1], refs[1:]) if side else ((), refs)
    outs, (flat, pair_ref) = refs[:-2], refs[-2:]
    span, overlap, half = plan["span"], plan["overlap"], plan["half"]
    origin = plan["origins"][side]
    core, mine = where_ref[0], where_ref[1]
    lead = plan["bases"][side * half] - origin
    if lead:
        flat[0:lead, :] = jnp.zeros((lead, LANES), f32)
    last = plan["bases"][side * half + half - 1] - origin + span
    if flat.shape[0] > last:
        flat[last:, :] = jnp.zeros((flat.shape[0] - last, LANES), f32)

    def base_of(owner):
        return pl.multiple_of(base_ref[side * half + owner] - origin, 16)

    def clear(owner, carry):
        base = base_of(owner)
        flat[pl.ds(base, overlap), :] = jnp.zeros((overlap, LANES), f32)
        flat[pl.ds(base + span - overlap, overlap), :] = jnp.zeros((overlap, LANES), f32)
        return carry

    lax.fori_loop(0, half, clear, 0)
    middle = span // 2
    for number, piece in enumerate(pieces):
        theirs = number // 2
        owner_core = core if theirs == 0 else 1 - core
        upper = number % 2 * (half // 2)
        for part in range(2):

            @pl.when(owner_core == part)
            def _(part=part, piece=piece, upper=upper):
                def place(entry, carry):
                    base = base_of(decode(entry + upper, part, bits) ^ mine)
                    value = piece[entry].astype(f32)
                    if part == 0:
                        flat[pl.ds(base, overlap), :] += value[:overlap]
                        flat[pl.ds(base + overlap, middle - overlap), :] = value[overlap:]
                    else:
                        flat[pl.ds(base + middle, middle - overlap), :] = value[: middle - overlap]
                        flat[pl.ds(base + span - overlap, overlap), :] += value[middle - overlap :]
                    return carry

                lax.fori_loop(0, half // 2, place, 0)

    for number, ((label, shape), out_ref) in enumerate(zip(plan["sides"][side], outs)):
        read_param(flat, plan["places"][label][0] - origin, shape, out_ref, pair_ref)
        if side and number == 0:
            out_ref[...] += carried[0][...]


def unflatten(where, pieces, plan, side, bits, carried=()):
    outs = []
    for label, shape in plan["sides"][side]:
        outs.append(jax.ShapeDtypeStruct(two_dim(shape), bf16 if is_matrix(label) else f32))
    vmem = pl.BlockSpec(memory_space=pltpu.VMEM)
    smem = pl.BlockSpec(memory_space=pltpu.SMEM)
    values = pl.pallas_call(
        functools.partial(unflatten_kernel, plan, side, bits),
        out_shape=outs,
        in_specs=[smem, smem] + [vmem] * (len(pieces) + len(carried)),
        out_specs=[vmem] * len(outs),
        scratch_shapes=[
            pltpu.VMEM((plan["heights"][side], LANES), f32),
            pltpu.VMEM((5, MS, LANES), f32),
        ],
        cost_estimate=estimate(1_000_000, 8_000_000),
        name="unflatten" + str(side),
    )(where, jnp.asarray(plan["bases"], jnp.int32), *pieces, *carried)
    return {label: value for (label, shape), value in zip(plan["sides"][side], values)}


def flatten_kernel(plan, group, bits, where_ref, base_ref, *refs):
    begin, owners, held, origin, height = plan["groups"][group]
    count = len(held)
    grads, (low_ref, high_ref, send_ref, flat, pair_ref) = refs[:count], refs[count:]
    span = plan["span"]
    core, mine = where_ref[0], where_ref[1]
    first, last = None, 0
    for label, shape in held:
        row = plan["places"][label][0] - origin
        first = row if first is None else first
        last = row + -(-math.prod(shape) // LANES)
    if first:
        flat[0:first, :] = jnp.zeros((first, LANES), f32)
    flat[last // 8 * 8 :, :] = jnp.zeros((height - last // 8 * 8, LANES), f32)
    window = (plan["bases"][begin] - origin, plan["bases"][begin + owners - 1] + span - origin)
    for (label, shape), ref in zip(held, grads):
        write_param(flat, plan["places"][label][0] - origin, shape, ref, pair_ref, window)

    def rows_of(entry, part):
        owner = (decode(entry, part, bits) ^ mine) & (owners - 1)
        base = base_ref[begin + owner] - origin + part * (span // 2)
        return flat[pl.ds(pl.multiple_of(base, 16), span // 2), :].astype(bf16)

    def place(entry, carry):
        low_ref[entry] = rows_of(entry, core)
        high_ref[entry] = rows_of(entry + owners // 2, core)
        send_ref[entry] = rows_of(entry, 1 - core)
        send_ref[entry + owners // 2] = rows_of(entry + owners // 2, 1 - core)
        return carry

    lax.fori_loop(0, owners // 2, place, 0)


def flatten(where, grads, plan, group):
    vmem = pl.BlockSpec(memory_space=pltpu.VMEM)
    smem = pl.BlockSpec(memory_space=pltpu.SMEM)
    begin, owners, held, origin, height = plan["groups"][group]
    rows = plan["span"] // 2
    values = [grads[label] for label, shape in held]
    return pl.pallas_call(
        functools.partial(flatten_kernel, plan, group, owners.bit_length() - 1),
        out_shape=(
            jax.ShapeDtypeStruct((owners // 2, rows, LANES), bf16),
            jax.ShapeDtypeStruct((owners // 2, rows, LANES), bf16),
            jax.ShapeDtypeStruct((owners, rows, LANES), bf16),
        ),
        in_specs=[smem, smem] + [vmem] * len(values),
        out_specs=(vmem, vmem, vmem),
        scratch_shapes=[
            pltpu.VMEM((height, LANES), f32),
            pltpu.VMEM((5, MS, LANES), f32),
        ],
        cost_estimate=estimate(1_000_000, 10_000_000),
        name="flatten" + str(group),
    )(where, jnp.asarray(plan["bases"], jnp.int32), *values)


def ln_parts(value):
    mean = jnp.mean(value, -1, keepdims=True)
    centred = value - mean
    variance = jnp.mean(centred * centred, -1, keepdims=True)
    inverse = lax.rsqrt(variance + norm_eps)
    return centred * inverse, inverse


def ln_back(grad, hat, inverse, gain):
    scaled = grad * gain
    first = jnp.mean(scaled, -1, keepdims=True)
    second = jnp.mean(scaled * hat, -1, keepdims=True)
    return inverse * (scaled - first - hat * second)


def gelu_parts(value):
    cdf = 0.5 + 0.5 * lax.erf(value * (2.0**-0.5))
    density = jnp.exp(value * value * -0.5) * (1.0 / math.sqrt(2.0 * math.pi))
    return value * cdf, cdf + value * density


def col_sum(value):
    return jnp.sum(value, 0, keepdims=True)


def groups(width):
    size = width // HEADS
    found = []
    for start in range(0, width, LANES):
        stop = min(start + LANES, width)
        found.append((start, stop, (stop - start) // size))
    return found, size


def stack_heads(value, count, size):
    lane = lax.broadcasted_iota(jnp.int32, value.shape, 1)
    zero = jnp.zeros_like(value)
    return jnp.concatenate(
        [
            jnp.where((lane >= head * size) & (lane < (head + 1) * size), value, zero)
            for head in range(count)
        ],
        0,
    )


def merge_heads(value, count, size):
    rows = value.shape[0] // count
    lane = lax.broadcasted_iota(jnp.int32, (rows, value.shape[1]), 1)
    merged = value[0:rows]
    for head in range(1, count):
        merged = jnp.where(lane >= head * size, value[head * rows : (head + 1) * rows], merged)
    return merged


def attention_forward(pair, length, tall, tokens, weights, keeps):
    ln1_ref, qkv_w, qkv_b, proj_w, proj_b, ln2_ref = weights
    a1_ref, qkv_ref, probs_ref, att_ref, mid_ref, n2_ref = keeps
    width = tokens.shape[-1]
    found, size = groups(width)
    scale = size ** (-0.5)
    hat, _ = ln_parts(tokens)
    a1 = (hat * ln1_ref[0:1, :] + ln1_ref[1:2, :]).astype(bf16)
    a1_ref[...] = a1
    qkv_ref[...] = (mm(a1, qkv_w[...]) + qkv_b[...]).astype(bf16)
    key_lane = lax.broadcasted_iota(jnp.int32, (1, tall), 1)
    bias = jnp.where(key_lane < length, 0.0, -1e30).astype(f32)
    for crop in range(pair):
        here = slice(crop * tall, (crop + 1) * tall)
        for start, stop, count in found:
            query = stack_heads(qkv_ref[here, start:stop], count, size)
            key = qkv_ref[here, width + start : width + stop]
            value = qkv_ref[here, 2 * width + start : 2 * width + stop]
            scores = mm_t(query, key) * scale + bias
            summit = jnp.max(scores, -1, keepdims=True)
            weights = jnp.exp(scores - summit)
            probs = (weights / jnp.sum(weights, -1, keepdims=True)).astype(bf16)
            first = start // size
            for head in range(count):
                probs_ref[crop, first + head] = probs[head * tall : (head + 1) * tall]
            att_ref[here, start:stop] = merge_heads(mm(probs, value), count, size).astype(bf16)
    mid = tokens + mm(att_ref[...], proj_w[...]) + proj_b[...]
    mid_ref[...] = mid
    hat, _ = ln_parts(mid)
    n2_ref[...] = (hat * ln2_ref[0:1, :] + ln2_ref[1:2, :]).astype(bf16)


def mlp_forward(chunk, mid_ref, n2_ref, weights, keeps):
    fc1_w, fc1_b, fc2_w, fc2_b = weights
    z_ref, slope_ref, y_ref = keeps
    y_ref[...] = mid_ref[...] + fc2_b[...]
    for number in range(fc1_w.shape[1] // chunk):
        cols = slice(number * chunk, (number + 1) * chunk)
        inner = mm(n2_ref[...], fc1_w[:, cols]) + fc1_b[:, cols]
        active, slope = gelu_parts(inner)
        z_ref[:, cols] = active.astype(bf16)
        slope_ref[:, cols] = slope.astype(bf16)
        y_ref[...] += mm(z_ref[:, cols], fc2_w[cols, :])


def keep_heads(pair, tall, y_ref, head_ref):
    for crop in range(pair):
        slot = pl.program_id(0) * pair + crop
        head_ref[pl.ds(slot, 1), :] = y_ref[crop * tall : crop * tall + 1, :]


def carry(value, norm, weight, bias):
    hat, _ = ln_parts(value)
    active, _ = gelu_parts(hat * norm[0:1, :] + norm[1:2, :])
    return (mm(active.astype(bf16), weight[...]) + bias[...]).astype(bf16)


def attention_kernel(pair, length, tall, tok_ref, *refs):
    tokens = tok_ref[...].reshape(pair * tall, tok_ref.shape[-1]).astype(f32)
    attention_forward(pair, length, tall, tokens, refs[:6], refs[6:])


def block_kernel(pair, length, tall, chunk, tok_ref, *refs):
    tokens = tok_ref[...].reshape(pair * tall, tok_ref.shape[-1]).astype(f32)
    attention_forward(pair, length, tall, tokens, refs[:6], refs[10:16])
    mlp_forward(chunk, refs[14], refs[15], refs[6:10], refs[16:19])
    keep_heads(pair, tall, refs[18], refs[19])


def mlp_kernel(pair, tall, chunk, mid_ref, n2_ref, *refs):
    weights, heads, (far_head, *far), near = refs[:4], None, refs[4:8], refs[8:11]
    z_ref, slope_ref, y_ref, head_ref, near_ref, far_ref = refs[11:]
    mlp_forward(chunk, mid_ref, n2_ref, weights, (z_ref, slope_ref, y_ref))
    keep_heads(pair, tall, y_ref, head_ref)

    @pl.when(pl.program_id(0) == pl.num_programs(0) - 1)
    def _():
        near_ref[...] = carry(head_ref[...], *near)
        far_ref[...] = carry(far_head[...], *far)


ATTENTION = ("ln1", "qkv_w", "qkv_b", "proj_w", "proj_b", "ln2")
MLP = ("fc1_w", "fc1_b", "fc2_w", "fc2_b")
TO = ("to_ln", "to_w", "to_b")


def pick(params, label, names):
    return [params[label + "_" + name] for name in names]


def row_spec(rows, cols):
    return pl.BlockSpec((rows, cols), lambda i: (i, 0))


def fixed_spec(shape):
    rank = len(shape)
    return pl.BlockSpec(shape, lambda i: (0,) * rank)


def kept_outs(crops, tall, width, hidden, pair):
    rows, flat = pair * tall, crops * tall

    def entry(cols, dtype):
        return row_spec(rows, cols), jax.ShapeDtypeStruct((flat, cols), dtype)

    attention = [
        entry(width, bf16),
        entry(3 * width, bf16),
        (
            pl.BlockSpec((pair, HEADS, tall, tall), lambda i: (i, 0, 0, 0)),
            jax.ShapeDtypeStruct((crops, HEADS, tall, tall), bf16),
        ),
        entry(width, bf16),
        entry(width, f32),
        entry(width, bf16),
    ]
    mlp = [
        entry(hidden, bf16),
        entry(hidden, bf16),
        entry(width, f32),
        (fixed_spec((crops, width)), jax.ShapeDtypeStruct((crops, width), f32)),
    ]
    return attention, mlp


def block_forward(tokens, params, label, length, pair):
    crops, tall, width = tokens.shape
    hidden = params[label + "_fc1_w"].shape[1]
    weights = pick(params, label, ATTENTION + MLP)
    attention, mlp = kept_outs(crops, tall, width, hidden, pair)
    outs = attention + mlp
    flops = 2 * crops * tall * (4 * width * width + 2 * width * hidden)
    return pl.pallas_call(
        functools.partial(block_kernel, pair, length, tall, 384),
        grid=(crops // pair,),
        out_shape=[shape for spec, shape in outs],
        in_specs=[pl.BlockSpec((pair, tall, width), lambda i: (i, 0, 0))]
        + [whole(value.shape) for value in weights],
        out_specs=[spec for spec, shape in outs],
        cost_estimate=estimate(8 * flops, 10_000_000),
        name="block_" + label,
    )(tokens, *weights)


def attention_only(tokens, params, label, length, pair):
    crops, tall, width = tokens.shape
    weights = pick(params, label, ATTENTION)
    outs, _ = kept_outs(crops, tall, width, width, pair)
    flops = 2 * crops * tall * 4 * width * width
    return pl.pallas_call(
        functools.partial(attention_kernel, pair, length, tall),
        grid=(crops // pair,),
        out_shape=[shape for spec, shape in outs],
        in_specs=[pl.BlockSpec((pair, tall, width), lambda i: (i, 0, 0))]
        + [whole(value.shape) for value in weights],
        out_specs=[spec for spec, shape in outs],
        cost_estimate=estimate(8 * flops, 20_000_000),
        name="attention_" + label,
    )(tokens, *weights)


def mlp_only(mid, n2, far_head, params, label, far, crops, pair):
    flat, width = mid.shape
    tall = flat // crops
    rows = pair * tall
    hidden = params[label + "_fc1_w"].shape[1]
    weights = pick(params, label, MLP)
    extra = [far_head] + pick(params, far, TO) + pick(params, label, TO)
    _, outs = kept_outs(crops, tall, width, hidden, pair)
    for name in (label, far):
        shape = (crops, params[name + "_to_w"].shape[1])
        outs.append((fixed_spec(shape), jax.ShapeDtypeStruct(shape, bf16)))
    flops = 2 * flat * 2 * width * hidden
    return pl.pallas_call(
        functools.partial(mlp_kernel, pair, tall, 384),
        grid=(crops // pair,),
        out_shape=[shape for spec, shape in outs],
        in_specs=[row_spec(rows, width), row_spec(rows, width)]
        + [whole(value.shape) for value in weights + extra],
        out_specs=[spec for spec, shape in outs],
        cost_estimate=estimate(8 * flops, 20_000_000),
        name="mlp_" + label,
    )(mid, n2, *weights, *extra)


def cross_kernel(
    length,
    tall,
    crops,
    sent_ref,
    y_ref,
    gret_ref,
    ca_ln,
    q_w,
    q_b,
    k_w,
    v_w,
    v_b,
    o_w,
    o_b,
    back_ln,
    back_w,
    back_b,
    returned_ref,
    gsent_ref,
    gj_ref,
    d_ca_ln,
    d_q_w,
    d_q_b,
    d_k_w,
    d_v_w,
    d_v_b,
    d_o_w,
    d_o_b,
    d_back_ln,
    d_back_w,
    d_back_b,
    sent_f,
    n_all,
    score_all,
    mates_all,
    pairs_all,
    gn_head,
    gj_head,
):
    width = y_ref.shape[1]
    size = width // HEADS
    scale = size ** (-0.5)
    stacked = crops * 8
    lane = lax.broadcasted_iota(jnp.int32, (8, width), 1)
    head = lax.broadcasted_iota(jnp.int32, (8, width), 0)
    own_head = (lane >= head * size) & (lane < (head + 1) * size)
    row = lax.broadcasted_iota(jnp.int32, (tall, 1), 0)
    key_lane = lax.broadcasted_iota(jnp.int32, (1, tall), 1)
    bias = jnp.where(key_lane < length, 0.0, -1e30).astype(f32)
    gain, shift = ca_ln[0:1, :], ca_ln[1:2, :]
    sent_f[...] = sent_ref[...].astype(f32)
    hat, _ = ln_parts(sent_f[...])
    n_head = (hat * gain + shift).astype(bf16)

    def spread(value):
        return jnp.concatenate(
            [jnp.where(own_head, value[crop : crop + 1], 0.0) for crop in range(crops)], 0
        )

    def gathered(value):
        return jnp.concatenate(
            [
                col_sum(jnp.where(own_head, value[crop * 8 : crop * 8 + 8], 0.0))
                for crop in range(crops)
            ],
            0,
        )

    def normed_of(crop):
        return n_all[crop * tall : (crop + 1) * tall, :]

    def against(value):
        return jnp.concatenate(
            [
                mm_t(value[crop * 8 : crop * 8 + 8].astype(bf16), normed_of(crop))
                for crop in range(crops)
            ],
            0,
        )

    def mixed(value):
        return jnp.concatenate(
            [
                mm(value[crop * 8 : crop * 8 + 8].astype(bf16), normed_of(crop))
                for crop in range(crops)
            ],
            0,
        )

    query = spread((mm(n_head, q_w[...]) + q_b[...]).astype(bf16).astype(f32)).astype(bf16)
    keyed = mm_t(query, k_w[...]) * scale
    blank = jnp.zeros((8, width), f32)
    for crop in range(crops):
        mates_all[crop] = jnp.concatenate([keyed[crop * 8 : crop * 8 + 8], blank], 0).astype(bf16)

    def joined(crop):
        here = pl.ds(pl.multiple_of(crop * tall, 16), tall)
        return here, jnp.where(row == 0, sent_f[pl.ds(crop, 1), :], y_ref[here, :])

    def ahead(crop, carry):
        here, value = joined(crop)
        hat, _ = ln_parts(value)
        normed = (hat * gain + shift).astype(bf16)
        n_all[here, :] = normed
        score_all[pl.ds(crop, 1)] = mm_t(mates_all[crop], normed)[None, 0:8]
        return carry

    lax.fori_loop(0, crops, ahead, 0)
    scores = score_all[...].reshape(stacked, tall) + bias
    summit = jnp.max(scores, -1, keepdims=True)
    weights = jnp.exp(scores - summit)
    probs = weights / jnp.sum(weights, -1, keepdims=True)
    rounded = probs.astype(bf16).astype(f32)
    total = jnp.sum(rounded, -1, keepdims=True)
    mean_n = mixed(rounded).astype(bf16)
    attended = gathered(mm(mean_n, v_w[...]) + total * v_b[...]).astype(bf16)
    merged = sent_f[...] + mm(attended, o_w[...]) + o_b[...]
    hat, inverse = ln_parts(merged)
    active, slope = gelu_parts(hat * back_ln[0:1, :] + back_ln[1:2, :])
    active = active.astype(bf16)
    returned_ref[...] = (mm(active, back_w[...]) + back_b[...]).astype(bf16)
    gret = gret_ref[...]
    d_back_w[...] = t_mm(active, gret)
    d_back_b[...] = col_sum(gret.astype(f32))
    gact = mm_t(gret, back_w[...]) * slope
    d_back_ln[0:1, :] = col_sum(gact * hat)
    d_back_ln[1:2, :] = col_sum(gact)
    gfused = ln_back(gact, hat, inverse, back_ln[0:1, :])
    gfo = gfused.astype(bf16)
    d_o_w[...] = t_mm(attended, gfo)
    d_o_b[...] = col_sum(gfo.astype(f32))
    gatt = spread(mm_t(gfo, o_w[...]).astype(bf16).astype(f32))
    d_v_b[...] = col_sum(total * gatt)
    gbias = jnp.sum(gatt * v_b[...], -1, keepdims=True)
    gatt = gatt.astype(bf16)
    d_v_w[...] = t_mm(mean_n, gatt)
    valued = mm_t(gatt, v_w[...])
    gprobs = against(valued) + gbias
    inner = gprobs - jnp.sum(gprobs * probs, -1, keepdims=True)
    gscores = (probs * inner).astype(bf16).astype(f32)
    for crop in range(crops):
        part = slice(crop * 8, crop * 8 + 8)
        mates_all[crop] = jnp.concatenate([keyed[part], valued[part]], 0).astype(bf16)
        pairs_all[crop] = jnp.concatenate([gscores[part], rounded[part]], 0).astype(bf16)
    slid = (mixed(gscores) * scale).astype(bf16)
    d_k_w[...] = t_mm(slid, query)
    gq = gathered(mm(slid, k_w[...])).astype(bf16)
    d_q_w[...] = t_mm(n_head, gq)
    d_q_b[...] = col_sum(gq.astype(f32))
    gn_head[...] = mm_t(gq, q_w[...])
    d_ca_ln[...] = jnp.zeros_like(d_ca_ln)

    def finish(crop, carry):
        here, value = joined(crop)
        hat, inverse = ln_parts(value)
        gn = t_mm(pairs_all[crop], mates_all[crop])
        gn = gn + jnp.where(row == 0, gn_head[pl.ds(crop, 1), :], 0.0)
        d_ca_ln[0:1, :] += col_sum(gn * hat)
        d_ca_ln[1:2, :] += col_sum(gn)
        gj = ln_back(gn, hat, inverse, gain)
        gj_ref[here, :] = gj
        gj_head[pl.ds(crop, 1), :] = gj[0:1, :]
        return carry

    lax.fori_loop(0, crops, finish, 0)
    gsent_ref[...] = (gj_head[...] + gfused).astype(bf16)


def cross(sent, hosted, gret, params, label, length, tall):
    crops, width = sent.shape
    own = gret.shape[1]
    flat = crops * tall
    names = ("ca_ln", "ca_q_w", "ca_q_b", "ca_k_w", "ca_v_w", "ca_v_b", "ca_o_w", "ca_o_b")
    names = names + ("back_ln", "back_w", "back_b")
    weights = [params[label + "_" + name] for name in names]
    outs = [
        jax.ShapeDtypeStruct((crops, own), bf16),
        jax.ShapeDtypeStruct((crops, width), bf16),
        jax.ShapeDtypeStruct((flat, width), f32),
    ] + [jax.ShapeDtypeStruct(value.shape, f32) for value in weights]
    vmem = pl.BlockSpec(memory_space=pltpu.VMEM)
    small = pltpu.VMEM((crops, width), f32)
    values = pl.pallas_call(
        functools.partial(cross_kernel, length, tall, crops),
        out_shape=outs,
        in_specs=[vmem] * (3 + len(weights)),
        out_specs=[vmem] * len(outs),
        scratch_shapes=[
            small,
            pltpu.VMEM((flat, width), bf16),
            pltpu.VMEM((crops, 8, tall), f32),
            pltpu.VMEM((crops, 16, width), bf16),
            pltpu.VMEM((crops, 16, tall), bf16),
            small,
            small,
        ],
        cost_estimate=estimate(2 * flat * width * width * 2, 8_000_000),
        name="cross_" + label,
    )(sent, hosted, gret, *weights)
    grads = {label + "_" + name: value for name, value in zip(names, values[3:])}
    return values[0], values[1], values[2], grads


def head_backward(headrow_ref, gsent_ref, to_ln, to_w, d_to_ln, d_to_w, d_to_b, ghead_ref):
    hat, inverse = ln_parts(headrow_ref[...])
    active, slope = gelu_parts(hat * to_ln[0:1, :] + to_ln[1:2, :])
    gsent = gsent_ref[...]
    d_to_w[...] = t_mm(active.astype(bf16), gsent)
    d_to_b[...] = col_sum(gsent.astype(f32))
    gact = mm_t(gsent, to_w[...]) * slope
    d_to_ln[0:1, :] = col_sum(gact * hat)
    d_to_ln[1:2, :] = col_sum(gact)
    ghead_ref[...] = ln_back(gact, hat, inverse, to_ln[0:1, :])


def clear_all(refs):
    for ref in refs:
        ref[...] = jnp.zeros_like(ref)


def mlp_backward(pair, tall, chunk, live_ref, acts, weights, grads, out_ref, gy, gnormed):
    cot_ref, y_ref, gj_ref, mid_ref, n2_ref, z_ref, slope_ref, ghead, returned_ref = acts
    ln2_ref, fc1_w, fc2_w = weights
    d_ln2, d_fc1_w, d_fc1_b, d_fc2_w, d_fc2_b = grads
    length = out_ref.shape[2]
    row = lax.broadcasted_iota(jnp.int32, (tall, 1), 0)
    for crop in range(pair):
        here = slice(crop * tall, (crop + 1) * tall)
        slot = pl.program_id(0) * pair + crop
        live = jnp.where(slot < live_ref[0], 1.0, 0.0).astype(f32)
        seed = cot_ref[crop].astype(f32) * live + gj_ref[here, :]
        gy[here, :] = jnp.where(row == 0, ghead[pl.ds(slot, 1), :], seed)
        home = returned_ref[pl.ds(slot, 1), :]
        final = jnp.where(row == 0, home, y_ref[here, :])
        out_ref[0, crop] = final[0:length].astype(bf16)
    gm = gy[...].astype(bf16)
    d_fc2_b[...] += col_sum(gm.astype(f32))

    def one(number, first):
        start = number * chunk
        if not isinstance(number, int):
            start = pl.multiple_of(start, LANES)
        cols = pl.ds(start, chunk)
        d_fc2_w[cols, :] += t_mm(z_ref[:, cols], gm)
        gu = slope_ref[:, cols].astype(f32) * mm_t(gm, fc2_w[cols, :])
        gu = gu.astype(bf16)
        d_fc1_w[:, cols] += t_mm(n2_ref[...], gu)
        d_fc1_b[:, cols] += col_sum(gu.astype(f32))
        part = mm_t(gu, fc1_w[:, cols])
        gnormed[...] = part if first else gnormed[...] + part

    def two(number, carry):
        one(2 * number, False)
        one(2 * number + 1, False)
        return carry

    chunks = fc1_w.shape[1] // chunk
    if chunks > 2:
        gnormed[...] = jnp.zeros_like(gnormed)
        lax.fori_loop(0, chunks // 2, two, 0)
        for number in range(chunks // 2 * 2, chunks):
            one(number, False)
    else:
        for number in range(chunks):
            one(number, number == 0)
    hat, inverse = ln_parts(mid_ref[...])
    gn = gnormed[...]
    d_ln2[0:1, :] += col_sum(gn * hat)
    d_ln2[1:2, :] += col_sum(gn)
    gy[...] += ln_back(gn, hat, inverse, ln2_ref[0:1, :])


def attention_backward(pair, tall, acts, weights, grads, gtok_ref, gmid_ref, gqkv, gatt_ref):
    tok_ref, a1_ref, qkv_ref, probs_ref, att_ref = acts
    ln1_ref, qkv_w, proj_w = weights
    d_ln1, d_qkv_w, d_qkv_b, d_proj_w, d_proj_b = grads
    width = tok_ref.shape[-1]
    length = gtok_ref.shape[2]
    found, size = groups(width)
    scale = size ** (-0.5)
    gp = gmid_ref[...].astype(bf16)
    d_proj_w[...] += t_mm(att_ref[...], gp)
    d_proj_b[...] += col_sum(gp.astype(f32))
    gatt_ref[...] = mm_t(gp, proj_w[...]).astype(bf16)

    def one(crop, carry):
        here = pl.ds(crop * tall, tall)
        if not isinstance(crop, int):
            here = pl.ds(pl.multiple_of(crop * tall, 16), tall)
        for start, stop, count in found:
            first = start // size
            query = stack_heads(qkv_ref[here, start:stop], count, size)
            key = qkv_ref[here, width + start : width + stop]
            value = qkv_ref[here, 2 * width + start : 2 * width + stop]
            gatt = stack_heads(gatt_ref[here, start:stop], count, size)
            probs_low = jnp.concatenate([probs_ref[crop, first + head] for head in range(count)], 0)
            probs = probs_low.astype(f32)
            gprobs = mm_t(gatt, value)
            inner = gprobs - jnp.sum(gprobs * probs, -1, keepdims=True)
            gscores = (probs * inner).astype(bf16)
            gq = merge_heads(mm(gscores, key), count, size) * scale
            gk = t_mm(gscores, query) * scale
            gv = t_mm(probs_low, gatt)
            gqkv[here, start:stop] = gq.astype(bf16)
            gqkv[here, width + start : width + stop] = gk.astype(bf16)
            gqkv[here, 2 * width + start : 2 * width + stop] = gv.astype(bf16)
        return carry

    if len(found) > 2:
        lax.fori_loop(0, pair, one, 0)
    else:
        for crop in range(pair):
            one(crop, 0)
    grad = gqkv[...]
    d_qkv_w[...] += t_mm(a1_ref[...], grad)
    d_qkv_b[...] += col_sum(grad.astype(f32))
    gn = mm_t(grad, qkv_w[...])
    hat, inverse = ln_parts(tok_ref[...].reshape(pair * tall, width).astype(f32))
    d_ln1[0:1, :] += col_sum(gn * hat)
    d_ln1[1:2, :] += col_sum(gn)
    gtok = gmid_ref[...] + ln_back(gn, hat, inverse, ln1_ref[0:1, :])
    for crop in range(pair):
        gtok_ref[0, crop] = gtok[crop * tall : crop * tall + length].astype(bf16)


GRAD_MLP = ("ln2", "fc1_w", "fc1_b", "fc2_w", "fc2_b")
GRAD_ATTENTION = ("ln1", "qkv_w", "qkv_b", "proj_w", "proj_b")


def mlp_back_kernel(pair, tall, chunk, live_ref, *refs):
    cot_ref, y_ref, gj_ref, mid_ref, n2_ref, z_ref, slope_ref, returned_ref = refs[:8]
    weights = refs[8:11]
    near, far = refs[11:15], refs[15:19]
    out_ref, gmid_ref, ghead_far = refs[19:22]
    grads, near_grads, far_grads = refs[22:27], refs[27:30], refs[30:33]
    ghead, gnormed, home = refs[33:]

    @pl.when(pl.program_id(0) == 0)
    def _():
        head_backward(*near, *near_grads, ghead)
        head_backward(*far, *far_grads, ghead_far)
        clear_all(grads)
        home[...] = returned_ref[...].astype(f32)

    acts = (cot_ref, y_ref, gj_ref, mid_ref, n2_ref, z_ref, slope_ref, ghead, home)
    mlp_backward(pair, tall, chunk, live_ref, acts, weights, grads, out_ref, gmid_ref, gnormed)


def attention_back_kernel(pair, tall, gmid_ref, *refs):
    acts, weights, gtok_ref, grads = refs[:5], refs[5:8], refs[8], refs[9:14]

    @pl.when(pl.program_id(0) == 0)
    def _():
        clear_all(grads)

    attention_backward(pair, tall, acts, weights, grads, gtok_ref, gmid_ref, *refs[14:])


def block_back_kernel(pair, tall, chunk, live_ref, *refs):
    mlp_acts, acts = refs[:9], refs[9:14]
    weights, mlp_weights = refs[14:17], refs[17:20]
    out_ref, gtok_ref = refs[20:22]
    mlp_grads, grads = refs[22:27], refs[27:32]
    gy, gnormed, gqkv, gatt_ref, home = refs[32:]

    @pl.when(pl.program_id(0) == 0)
    def _():
        clear_all(mlp_grads + grads)
        home[...] = mlp_acts[8][...].astype(f32)

    mlp_backward(
        pair, tall, chunk, live_ref, (*mlp_acts[:8], home), mlp_weights, mlp_grads, out_ref, gy, gnormed
    )
    attention_backward(pair, tall, acts, weights, grads, gtok_ref, gy, gqkv, gatt_ref)


def named(label, names, values):
    return {label + "_" + name: value for name, value in zip(names, values)}


def grad_outs(params, label, names):
    return [
        (fixed_spec(value.shape), jax.ShapeDtypeStruct(value.shape, f32))
        for value in pick(params, label, names)
    ]


def token_out(crops, length, width, pair):
    return (
        pl.BlockSpec((1, pair, length, width), lambda i: (0, i, 0, 0)),
        jax.ShapeDtypeStruct((1, crops, length, width), bf16),
    )


def mlp_back(cot, live, kept, gj, near, far, returned, params, label, other, length, pair):
    crops, tall, width = cot.shape
    mid, n2, z, slope, y = kept
    hidden = z.shape[1]
    rows, flat = pair * tall, crops * tall
    weights = pick(params, label, ("ln2", "fc1_w", "fc2_w"))
    near = list(near) + pick(params, label, ("to_ln", "to_w"))
    far = list(far) + pick(params, other, ("to_ln", "to_w"))
    smem = pl.BlockSpec(memory_space=pltpu.SMEM)
    outs = [
        token_out(crops, length, width, pair),
        (row_spec(rows, width), jax.ShapeDtypeStruct((flat, width), f32)),
        (fixed_spec(far[0].shape), jax.ShapeDtypeStruct(far[0].shape, f32)),
    ]
    outs += grad_outs(params, label, GRAD_MLP)
    outs += grad_outs(params, label, TO) + grad_outs(params, other, TO)
    values = pl.pallas_call(
        functools.partial(mlp_back_kernel, pair, tall, 384),
        grid=(crops // pair,),
        out_shape=[shape for spec, shape in outs],
        in_specs=[smem, pl.BlockSpec((pair, tall, width), lambda i: (i, 0, 0))]
        + [row_spec(rows, width)] * 4
        + [row_spec(rows, hidden)] * 2
        + [whole(value.shape) for value in [returned] + weights + near + far],
        out_specs=[spec for spec, shape in outs],
        scratch_shapes=[
            pltpu.VMEM((crops, width), f32),
            pltpu.VMEM((rows, width), f32),
            pltpu.VMEM((crops, width), f32),
        ],
        cost_estimate=estimate(8 * 8 * flat * width * hidden, 20_000_000),
        name="mlp_back_" + label,
    )(live, cot, y, gj, mid, n2, z, slope, returned, *weights, *near, *far)
    grads = named(label, GRAD_MLP, values[3:8])
    grads.update(named(label, TO, values[8:11]))
    grads.update(named(other, TO, values[11:14]))
    return values[0], values[1], values[2], grads


def attention_back(tokens, gmid, kept, params, label, length, pair):
    crops, tall, width = tokens.shape
    a1, qkv, probs, att = kept
    rows, flat = pair * tall, crops * tall
    weights = pick(params, label, ("ln1", "qkv_w", "proj_w"))
    outs = [token_out(crops, length, width, pair)] + grad_outs(params, label, GRAD_ATTENTION)
    values = pl.pallas_call(
        functools.partial(attention_back_kernel, pair, tall),
        grid=(crops // pair,),
        out_shape=[shape for spec, shape in outs],
        in_specs=[
            row_spec(rows, width),
            pl.BlockSpec((pair, tall, width), lambda i: (i, 0, 0)),
            row_spec(rows, width),
            row_spec(rows, 3 * width),
            pl.BlockSpec((pair, HEADS, tall, tall), lambda i: (i, 0, 0, 0)),
            row_spec(rows, width),
        ]
        + [whole(value.shape) for value in weights],
        out_specs=[spec for spec, shape in outs],
        scratch_shapes=[pltpu.VMEM((rows, 3 * width), bf16), pltpu.VMEM((rows, width), bf16)],
        cost_estimate=estimate(8 * 16 * flat * width * width, 20_000_000),
        name="attention_back_" + label,
    )(gmid, tokens, a1, qkv, probs, att, *weights)
    return values[0], named(label, GRAD_ATTENTION, values[1:])


def block_back(tokens, cot, live, kept, gj, ghead, returned, params, label, length, pair):
    crops, tall, width = tokens.shape
    a1, qkv, probs, att, mid, n2, z, slope, y = kept
    hidden = z.shape[1]
    rows, flat = pair * tall, crops * tall
    weights = pick(params, label, ("ln1", "qkv_w", "proj_w", "ln2", "fc1_w", "fc2_w"))
    smem = pl.BlockSpec(memory_space=pltpu.SMEM)
    token_spec = pl.BlockSpec((pair, tall, width), lambda i: (i, 0, 0))
    outs = [token_out(crops, length, width, pair)] * 2
    outs += grad_outs(params, label, GRAD_MLP) + grad_outs(params, label, GRAD_ATTENTION)
    values = pl.pallas_call(
        functools.partial(block_back_kernel, pair, tall, 384),
        grid=(crops // pair,),
        out_shape=[shape for spec, shape in outs],
        in_specs=[smem, token_spec]
        + [row_spec(rows, width)] * 4
        + [row_spec(rows, hidden)] * 2
        + [whole(ghead.shape), whole(returned.shape)]
        + [
            token_spec,
            row_spec(rows, width),
            row_spec(rows, 3 * width),
            pl.BlockSpec((pair, HEADS, tall, tall), lambda i: (i, 0, 0, 0)),
            row_spec(rows, width),
        ]
        + [whole(value.shape) for value in weights],
        out_specs=[spec for spec, shape in outs],
        scratch_shapes=[
            pltpu.VMEM((rows, width), f32),
            pltpu.VMEM((rows, width), f32),
            pltpu.VMEM((rows, 3 * width), bf16),
            pltpu.VMEM((rows, width), bf16),
            pltpu.VMEM((crops, width), f32),
        ],
        cost_estimate=estimate(8 * 4 * flat * (4 * width * width + 2 * width * hidden), 20_000_000),
        name="block_back_" + label,
    )(live, cot, y, gj, mid, n2, z, slope, ghead, returned, tokens, a1, qkv, probs, att, *weights)
    grads = named(label, GRAD_MLP, values[2:7])
    grads.update(named(label, GRAD_ATTENTION, values[7:12]))
    return values[0], values[1], grads


def swap(value):
    return lax.ppermute(value, "branch", [(0, 1), (1, 0)])


def partner(value, bit):
    count = lax.axis_size("dp")
    return lax.ppermute(value, "dp", [(i, i ^ bit) for i in range(count)])


def side_partner(value, place):
    count = lax.axis_size("dp")
    pairs = []
    for core in range(2):
        bit = 1 << (place ^ core)
        pairs += [(core * count + i, core * count + (i ^ bit)) for i in range(count)]
    return lax.ppermute(value, ("branch", "dp"), pairs)


def tie(value, *others):
    return lax.optimization_barrier((value, *others))[0] if others else value


def gather_lines(held, first, last, jobs=()):
    for number, place in enumerate(range(first, last, -1)):
        got = partner(held, 1 << place)
        if number < len(jobs):
            got = tie(got, *jobs[number](held))
        held = jnp.concatenate([held, got], 0)
    return held


def gather_middle(held):
    return jnp.concatenate([held, side_partner(held, 1)], 0)


def add_low(*values):
    total = values[0].astype(f32)
    for value in values[1:]:
        total = total + value.astype(f32)
    return total.astype(bf16)


def reduce_step(parts, count, send):
    count = count // 2
    sent = add_low(*[part[count : 2 * count] for part in parts])
    return sent, parts + [send(sent)], count


def reduce_start(low, high, got):
    half = low.shape[0]
    sent = add_low(high, got[half:])
    return sent, [low, got, side_partner(sent, 0)], half


def reduce_middle(parts, count):
    return reduce_step(parts, count, lambda sent: side_partner(sent, 1))


def reduce_lines(parts, count, first, last):
    for place in range(first, last):
        _, parts, count = reduce_step(parts, count, lambda sent: partner(sent, 1 << place))
    return parts, count


def add_up(parts):
    total = parts[0][0].astype(f32)
    for part in parts[1:]:
        total = total + part[0].astype(f32)
    return total


def shards(
    small_tokens,
    large_tokens,
    small_cot,
    large_cot,
    live_counts,
    master,
    first_moment,
    second_moment,
):
    count = lax.axis_size("branch") * lax.axis_size("dp")
    bits = lax.axis_size("dp").bit_length() - 1
    plan = grid_plan(count)
    core, mine = lax.axis_index("branch"), lax.axis_index("dp")
    where = jnp.stack([core, mine]).astype(jnp.int32)
    index = lax.axis_index(("branch", "dp"))
    size = master.shape[0]
    rows = plan["shard_rows"]
    table = lax.dynamic_index_in_dim(jnp.asarray(plan["table"]), index, 0, False)
    padded = jnp.pad(master, (0, rows * LANES - size)).reshape(rows, LANES)
    keep, send = align(where, table, padded, plan)
    got = swap(send)
    counts = live_counts[:, 0]
    own_count = lax.dynamic_slice_in_dim(counts, core, 1)
    far_count = lax.dynamic_slice_in_dim(counts, 1 - core, 1)
    crops, length_s = small_tokens.shape[1], small_tokens.shape[2]
    length_l = large_tokens.shape[2]
    tall_s, tall_l = round_up(length_s, 16), round_up(length_l, 16)
    pair = 2

    def inward(value):
        return jnp.transpose(value[0], (1, 0, 2))

    def settled(value):
        return with_layout_constraint(inward(value), Layout(major_to_minor=(0, 1, 2)))

    def outward(value):
        return jnp.transpose(value, (1, 0, 2))[None]

    def taller(value, length, tall):
        return jnp.pad(value[0], ((0, 0), (0, tall - length), (0, 0)))

    early = []

    def pad_tokens(held):
        early.append(taller(tie(small_tokens, held), length_s, tall_s))
        early.append(taller(tie(large_tokens, held), length_l, tall_l))
        return early[0:2]

    def pad_seeds(held):
        slots = jnp.arange(crops, dtype=jnp.int32)[:, None]
        small_held, large_held = tie(small_cot, held), tie(large_cot, held)
        early.append(taller(small_held, length_s, tall_s))
        early.append(taller(large_held, length_l, tall_l))
        early.append(jnp.where(slots < own_count, small_held[0, :, 0], 0))
        early.append(jnp.where(slots < far_count, large_held[0, :, 0], 0))
        return early[2:6]

    held = jnp.where(core == 0, keep, got)[None]
    near = gather_lines(held, bits - 1, 1, (pad_tokens, pad_seeds))
    small, large, small_seed, large_seed, ret_small, ret_large = early
    far = tie(jnp.where(core == 0, got, keep)[None], near)
    middle = (bits + 1) // 2
    far = gather_lines(far, bits - 1, middle)
    near = tie(gather_middle(near), far)
    near_end = side_partner(near, 0)
    far = gather_lines(far, middle, 1)
    near_end = tie(near_end, far)
    near_pieces = (near, near_end, swap(near), swap(near_end))
    ret_small, ret_large = swap(ret_small), swap(ret_large)

    params = unflatten(where, near_pieces, plan, 0, bits)
    straddling = params.pop(plan["sides"][1][0][0])
    far = tie(far, near_end)
    far = jnp.concatenate([far, tie(side_partner(far, 1), params["s_ln1"])], 0)
    *kept_s, head_s = block_forward(tie(small, far), params, "s", length_s, pair)
    far_end = side_partner(far, 0)
    kept_l = attention_only(tie(large, far_end), params, "l", length_l, pair)
    far_pieces = (far, far_end, swap(far), swap(far_end))
    params.update(unflatten(where, far_pieces, plan, 1, bits, (straddling,)))
    z_l, slope_l, y_l, head_l, sent_l, sent_s = mlp_only(
        kept_l[4], kept_l[5], head_s, params, "l", "s", crops, pair
    )
    got_s, got_l = swap(sent_s), swap(sent_l)
    grads = {}
    back_s, gsent_s, gj_l, part = cross(got_s, y_l, ret_small, params, "s", length_l, tall_l)
    grads.update(part)
    home_s, own_s = swap(back_s), swap(gsent_s)
    back_l, gsent_l, gj_s, part = cross(got_l, kept_s[8], ret_large, params, "l", length_s, tall_s)
    grads.update(part)
    home_l, own_l = swap(back_l), swap(gsent_l)
    large_out, gmid, ghead_s, part = mlp_back(
        large_seed,
        far_count,
        (kept_l[4], kept_l[5], z_l, slope_l, y_l),
        gj_l,
        (head_l, own_l),
        (head_s, own_s),
        home_l,
        params,
        "l",
        "s",
        length_l,
        pair,
    )
    grads.update(part)
    far_parts = flatten(where, grads, plan, 2)
    far_got = swap(far_parts[2])
    large_grad, part = attention_back(large, gmid, kept_l[:4], params, "l", length_l, pair)
    grads.update(part)
    grads["l_ln1"], far_got = lax.optimization_barrier((grads["l_ln1"], far_got))
    upper_parts = flatten(where, grads, plan, 1)
    upper_got = swap(upper_parts[2])
    sent_far, far_side, far_left = reduce_start(*far_parts[:2], far_got)
    sent_upper, upper, upper_left = reduce_start(*upper_parts[:2], tie(upper_got, sent_far))
    ghead_s = tie(ghead_s, sent_far, sent_upper, gmid)
    small_out, small_grad, part = block_back(
        small, small_seed, own_count, kept_s, gj_s, ghead_s, home_s, params, "s", length_s, pair
    )
    grads.update(part)
    grads["s_ln1"] = tie(grads["s_ln1"], far_side[-1], upper[-1])
    lower_parts = flatten(where, grads, plan, 0)
    lower_got = swap(lower_parts[2])
    _, far_side, far_left = reduce_middle(far_side, far_left)
    _, upper, upper_left = reduce_middle(upper, upper_left)
    sent, lower, lower_left = reduce_start(*lower_parts[:2], lower_got)
    lower[-1], large_out, large_grad = lax.optimization_barrier(
        (lower[-1], settled(tie(large_out, sent)), settled(tie(large_grad, sent)))
    )
    far_side[-1], upper[-1] = tie(far_side[-1], sent), tie(upper[-1], sent)
    far_side, far_left = reduce_lines(far_side, far_left, 2, 3)
    upper, _ = reduce_lines(upper, upper_left, 2, bits - 1)
    sent, lower, lower_left = reduce_middle(lower, lower_left)
    lower[-1], small_out, small_grad = lax.optimization_barrier(
        (lower[-1], settled(tie(small_out, sent)), settled(tie(small_grad, sent)))
    )
    lower = add_up(reduce_lines(lower, lower_left, 2, bits - 1)[0])
    far_side, _ = reduce_lines(far_side, far_left, 3, bits)
    upper = add_up(upper)
    top = (mine >> (bits - 1)) & 1
    last_sent = jnp.where(top == 1, lower, upper).astype(bf16)
    near_total = jnp.where(top == 1, upper, lower)
    last_got = partner(last_sent, 1 << (bits - 1))
    everyone = jnp.asarray(plan["table"])
    tables = [
        lax.dynamic_index_in_dim(everyone, mine + begin, 0, False) for begin in (0, plan["half"])
    ]
    own, send, square = settle(
        where, jnp.concatenate(tables), near_total, last_got, far_side, plan
    )
    got = swap(send)
    square = square + swap(square)
    summed = unalign(where, table, own, tie(got, square), plan)
    for place in range(bits):
        there = partner(square, 1 << place)
        square = square + (tie(there, summed) if place == 0 else there)
    grad_norm = jnp.sqrt(square[0, 0])
    own_grad = summed.reshape(-1)[:size]
    clipped = own_grad * jnp.minimum(1.0, clip_norm / grad_norm)
    new_first = beta_one * first_moment + (1.0 - beta_one) * clipped
    new_second = beta_two * second_moment + (1.0 - beta_two) * clipped * clipped
    new_master = master - rate * (
        new_first / bias_one / (jnp.sqrt(new_second / bias_two) + adam_eps) + decay * master
    )
    return (
        outward(small_out),
        outward(large_out),
        outward(small_grad),
        outward(large_grad),
        grad_norm,
        new_first,
        new_second,
        new_master,
        new_master.astype(bf16),
    )


def solution(mesh):
    return jax.shard_map(
        shards,
        mesh=mesh,
        in_specs=(
            P("branch", "dp", None, None),
            P("branch", "dp", None, None),
            P("branch", "dp", None, None),
            P("branch", "dp", None, None),
            P(None, "dp"),
            P(("branch", "dp")),
            P(("branch", "dp")),
            P(("branch", "dp")),
        ),
        out_specs=(
            P("branch", "dp", None, None),
            P("branch", "dp", None, None),
            P("branch", "dp", None, None),
            P("branch", "dp", None, None),
            P(),
            P(("branch", "dp")),
            P(("branch", "dp")),
            P(("branch", "dp")),
            P(("branch", "dp")),
        ),
        check_vma=False,
    )
```

```python
import functools
import math

import jax
import jax.numpy as jnp
import numpy as np
from jax import lax
from jax.experimental import pallas as pl
from jax.experimental.pallas import tpu as pltpu
from jax.experimental.layout import Layout, with_layout_constraint
from jax.sharding import PartitionSpec as P

DS = 192
DL = 384
MS = 768
ML = 1536
HEADS = 6

norm_eps = 1e-06
clip_norm = 1.0
beta_one = 0.5
beta_two = 0.5
adam_eps = 1e-08
rate = 0.05
decay = 0.05
bias_one = 1.0 - 0.5**5
bias_two = 1.0 - 0.5**5

f32 = jnp.float32
bf16 = jnp.bfloat16
LANES = 128


def layout():
    shapes = []
    for label, width, hidden in (("s", DS, MS), ("l", DL, ML)):
        shapes += [
            (label + "_ln1", (2, width)),
            (label + "_qkv_w", (width, 3 * width)),
            (label + "_qkv_b", (3 * width,)),
            (label + "_proj_w", (width, width)),
            (label + "_proj_b", (width,)),
            (label + "_ln2", (2, width)),
            (label + "_fc1_w", (width, hidden)),
            (label + "_fc1_b", (hidden,)),
            (label + "_fc2_w", (hidden, width)),
            (label + "_fc2_b", (width,)),
        ]
    for label, owner, other in (("s", DS, DL), ("l", DL, DS)):
        shapes += [
            (label + "_to_ln", (2, owner)),
            (label + "_to_w", (owner, other)),
            (label + "_to_b", (other,)),
            (label + "_ca_ln", (2, other)),
            (label + "_ca_q_w", (other, other)),
            (label + "_ca_q_b", (other,)),
            (label + "_ca_k_w", (other, other)),
            (label + "_ca_v_w", (other, other)),
            (label + "_ca_v_b", (other,)),
            (label + "_ca_o_w", (other, other)),
            (label + "_ca_o_b", (other,)),
            (label + "_back_ln", (2, other)),
            (label + "_back_w", (other, owner)),
            (label + "_back_b", (owner,)),
        ]
    return shapes


def round_up(value, unit):
    return -(-value // unit) * unit


def grid_plan(shards):
    names = []
    regions = []
    offset = 0
    for label, shape in layout():
        count = math.prod(shape)
        phase = offset % LANES
        if not regions or regions[-1][2] != phase:
            regions.append([offset, offset, phase])
        names.append((label, shape, offset, len(regions) - 1))
        offset += count
        regions[-1][1] = offset
    total = offset
    starts = []
    row = 0
    for first, last, phase in regions:
        starts.append(row)
        row += -(-(last - first) // LANES)
    rows = row
    places = {}
    for label, shape, place, region in names:
        places[label] = (starts[region] + (place - regions[region][0]) // LANES, shape)
    size = total // shards
    bases = []
    pieces = []
    for device in range(shards):
        low, high = device * size, (device + 1) * size
        own = []
        base = None
        for (first, last, phase), start in zip(regions, starts):
            left, right = max(low, first), min(high, last)
            if left >= right:
                continue
            if base is None:
                base = (start + (left - first) // LANES) // 16 * 16
            delta = start * LANES - first + low - base * LANES
            own.append((left - low, right - low, delta))
        bases.append(base)
        pieces.append(own)
    most = max(len(own) for own in pieces)
    table = np.zeros((shards, most * 3), np.int32)
    need = 0
    for device, own in enumerate(pieces):
        for number, (left, right, delta) in enumerate(own):
            table[device, 3 * number : 3 * number + 3] = (left, right, delta)
            need = max(need, right + delta)
    span = round_up(-(-need // LANES), 32)
    overlap = 16
    for device in range(1, shards):
        overlap = max(overlap, bases[device - 1] + span - bases[device])
    half = shards // 2
    edge = half * size
    sides = [[], []]
    for label, shape, place, region in names:
        if place < edge:
            sides[0].append((label, shape))
        if place + math.prod(shape) > edge:
            sides[1].append((label, shape))
    origins = [0, min(bases[half], places[sides[1][0][0]][0]) // 16 * 16]
    heights = []
    for side in range(2):
        last = bases[half * (side + 1) - 1] + span
        for label, shape in sides[side]:
            last = max(last, places[label][0] + -(-math.prod(shape) // LANES))
        heights.append(round_up(last - origins[side] + overlap, 16))
    groups = []
    for first, last in ((0, half // 2), (half // 2, half), (half, shards)):
        held = [
            (label, shape)
            for label, shape, place, region in names
            if place < last * size and place + math.prod(shape) > first * size
        ]
        origin = min([bases[first]] + [places[label][0] for label, shape in held]) // 16 * 16
        stop = max(
            [bases[last - 1] + span]
            + [places[label][0] + -(-math.prod(shape) // LANES) for label, shape in held]
        )
        groups.append((first, last - first, held, origin, round_up(stop - origin + overlap, 16)))
    return dict(
        places=places,
        groups=groups,
        rows=rows,
        half=half,
        sides=sides,
        origins=origins,
        heights=heights,
        size=size,
        bases=bases,
        table=table,
        most=most,
        span=span,
        overlap=overlap,
        shard_rows=round_up(-(-size // LANES), 16),
    )


def mm(left, right):
    return lax.dot_general(left, right, (((1,), (0,)), ((), ())), preferred_element_type=f32)


def mm_t(left, right):
    return lax.dot_general(left, right, (((1,), (1,)), ((), ())), preferred_element_type=f32)


def t_mm(left, right):
    return lax.dot_general(left, right, (((0,), (0,)), ((), ())), preferred_element_type=f32)


def vmem_spec(shape, index):
    return pl.BlockSpec(shape, index)


def whole(shape):
    rank = len(shape)
    return pl.BlockSpec(shape, lambda *_: (0,) * rank, pipeline_mode=pl.Buffered(1))


def estimate(flops, moved):
    return pl.CostEstimate(flops=int(flops), bytes_accessed=int(moved), transcendentals=0)


def shift_rows(ref, amount, rows, margin):
    down = amount // LANES
    across = amount - down * LANES
    here = ref[pl.ds(margin - down, rows), :]
    above = ref[pl.ds(margin - down - 1, rows), :]
    here = pltpu.roll(here, across, 1)
    above = pltpu.roll(above, across, 1)
    lane = lax.broadcasted_iota(jnp.int32, here.shape, 1)
    return jnp.where(lane < across, above, here)


def align_kernel(most, rows, span, margin, core_ref, table_ref, shard_ref, keep_ref, send_ref, padded):
    padded[...] = jnp.zeros_like(padded)
    padded[margin : margin + rows, :] = shard_ref[...]
    place = lax.broadcasted_iota(jnp.int32, (span, LANES), 0) * LANES
    place = place + lax.broadcasted_iota(jnp.int32, (span, LANES), 1)
    total = jnp.zeros((span, LANES), f32)
    for number in range(most):
        left = table_ref[3 * number]
        right = table_ref[3 * number + 1]
        delta = table_ref[3 * number + 2]
        moved = shift_rows(padded, delta, span, margin)
        total = jnp.where((place >= left + delta) & (place < right + delta), moved, total)
    total = total.astype(bf16)
    first = core_ref[0] == 0
    upper, lower = total[: span // 2], total[span // 2 :]
    keep_ref[...] = jnp.where(first, upper, lower)
    send_ref[...] = jnp.where(first, lower, upper)


def unalign_kernel(
    most, rows, span, margin, core_ref, table_ref, own_ref, got_ref, out_ref, padded
):
    first = core_ref[0] == 0
    padded[span:, :] = jnp.zeros((padded.shape[0] - span, LANES), f32)
    padded[0 : span // 2, :] = jnp.where(first, own_ref[...], got_ref[...])
    padded[span // 2 : span, :] = jnp.where(first, got_ref[...], own_ref[...])
    place = lax.broadcasted_iota(jnp.int32, (rows, LANES), 0) * LANES
    place = place + lax.broadcasted_iota(jnp.int32, (rows, LANES), 1)
    total = jnp.zeros((rows, LANES), f32)
    lane = lax.broadcasted_iota(jnp.int32, (rows, LANES), 1)
    for number in range(most):
        left = table_ref[3 * number]
        right = table_ref[3 * number + 1]
        delta = table_ref[3 * number + 2]
        down = delta // LANES
        across = delta - down * LANES
        back = lax.rem(LANES - across, LANES)
        here = pltpu.roll(padded[pl.ds(down, rows), :], back, 1)
        below = pltpu.roll(padded[pl.ds(down + 1, rows), :], back, 1)
        moved = jnp.where(lane < LANES - across, here, below)
        total = jnp.where((place >= left) & (place < right), moved, total)
    out_ref[...] = total


def settle_kernel(most, where_ref, table_ref, keep_ref, last_ref, *refs):
    *far_refs, own_ref, send_ref, norm_ref = refs
    core = where_ref[0]
    near = keep_ref[...] + last_ref[...].astype(f32)
    far = far_refs[0][0].astype(f32)
    for ref in far_refs[1:]:
        far = far + ref[0].astype(f32)
    rows = near.shape[0]
    place = (lax.broadcasted_iota(jnp.int32, near.shape, 0) + core * rows) * LANES
    place = place + lax.broadcasted_iota(jnp.int32, near.shape, 1)

    def squares(total, entry):
        found = jnp.zeros_like(total)
        for number in range(most):
            at = 3 * (entry * most + number)
            left, right, delta = table_ref[at], table_ref[at + 1], table_ref[at + 2]
            inside = (place >= left + delta) & (place < right + delta)
            found = jnp.where(inside, total * total, found)
        return found

    both = squares(near, 0) + squares(far, 1)
    norm_ref[...] = jnp.broadcast_to(jnp.sum(both).reshape(1, 1), (8, LANES))
    own_ref[...] = jnp.where(core == 0, near, far)
    send_ref[...] = jnp.where(core == 0, far, near)


def settle(where, tables, keep, last, far_parts, plan):
    smem = pl.BlockSpec(memory_space=pltpu.SMEM)
    part = jax.ShapeDtypeStruct(keep.shape, f32)
    return pl.pallas_call(
        functools.partial(settle_kernel, plan["most"]),
        grid=(1,),
        out_shape=(part, part, jax.ShapeDtypeStruct((8, LANES), f32)),
        in_specs=[smem, smem, fixed_spec(keep.shape), fixed_spec(keep.shape)]
        + [pl.BlockSpec((1, *keep.shape), lambda i: (0, 0, 0))] * len(far_parts),
        out_specs=(fixed_spec(keep.shape), fixed_spec(keep.shape), fixed_spec((8, LANES))),
        cost_estimate=estimate(1_000_000, 2_000_000),
        name="settle",
    )(where, tables, keep, last, *far_parts)


def align(core, table, shard, plan):
    rows, span, most = plan["shard_rows"], plan["span"], plan["most"]
    margin = 8 + round_up(int(plan["table"].max(initial=0, where=pick_delta(plan))) // LANES + 1, 8)
    tall = margin + max(rows, span) + 8
    vmem = pl.BlockSpec(memory_space=pltpu.VMEM)
    smem = pl.BlockSpec(memory_space=pltpu.SMEM)
    part = jax.ShapeDtypeStruct((span // 2, LANES), bf16)
    return pl.pallas_call(
        functools.partial(align_kernel, most, rows, span, margin),
        out_shape=(part, part),
        in_specs=[smem, smem, vmem],
        out_specs=(vmem, vmem),
        scratch_shapes=[pltpu.VMEM((tall, LANES), f32)],
        cost_estimate=estimate(1_000_000, 1_000_000),
        name="align",
    )(core, table, shard)


def unalign(core, table, own, got, plan):
    rows, span, most = plan["shard_rows"], plan["span"], plan["most"]
    margin = 16 + round_up(int(plan["table"].max(initial=0, where=pick_delta(plan))) // LANES + 1, 8)
    tall = max(rows, span) + margin
    vmem = pl.BlockSpec(memory_space=pltpu.VMEM)
    smem = pl.BlockSpec(memory_space=pltpu.SMEM)
    return pl.pallas_call(
        functools.partial(unalign_kernel, most, rows, span, margin),
        out_shape=jax.ShapeDtypeStruct((rows, LANES), f32),
        in_specs=[smem, smem, vmem, vmem],
        out_specs=vmem,
        scratch_shapes=[pltpu.VMEM((tall, LANES), f32)],
        cost_estimate=estimate(1_000_000, 1_000_000),
        name="unalign",
    )(core, table, own, got)


def pick_delta(plan):
    mask = np.zeros(plan["table"].shape, bool)
    mask[:, 2::3] = True
    return mask


def two_dim(shape):
    return shape if len(shape) == 2 else (1, shape[0])


def is_matrix(label):
    return label[-2:] == "_w"


def strided(start, count, step):
    return pl.ds(start, count) if step == 1 or count == 1 else pl.ds(start, count, stride=step)


def half_swap(value):
    return pltpu.roll(value, LANES // 2, 1)


def read_param(flat, row, shape, out_ref, pair_ref):
    depth, width = two_dim(shape)
    dtype = out_ref.dtype
    if width % LANES == 0:
        step = width // LANES
        for col in range(step):
            out_ref[:, col * LANES : (col + 1) * LANES] = flat[
                strided(row + col, depth, step), :
            ].astype(dtype)
        return
    half = LANES // 2
    lead = width // LANES
    if depth == 1:
        for col in range(lead):
            out_ref[:, col * LANES : (col + 1) * LANES] = flat[row + col : row + col + 1, :].astype(
                dtype
            )
        out_ref[:, lead * LANES :] = flat[row + lead : row + lead + 1, 0:half].astype(dtype)
        return
    step = 2 * width // LANES
    pairs = depth // 2
    lane = lax.broadcasted_iota(jnp.int32, (pairs, LANES), 1)
    blocks = [flat[strided(row + col, pairs, step), :] for col in range(step)]
    turned = [half_swap(block) for block in blocks[lead:]]
    for col in range(lead):
        pair_ref[col, strided(0, pairs, 2), :] = blocks[col]
        pair_ref[col, strided(1, pairs, 2), :] = jnp.where(lane < half, turned[col], turned[col + 1])
    pair_ref[lead, strided(0, pairs, 2), :] = blocks[lead]
    pair_ref[lead, strided(1, pairs, 2), :] = turned[lead]
    for col in range(lead):
        out_ref[:, col * LANES : (col + 1) * LANES] = pair_ref[col, 0:depth, :].astype(dtype)
    out_ref[:, lead * LANES :] = pair_ref[lead, 0:depth, 0:half].astype(dtype)


def write_param(flat, row, shape, in_ref, pair_ref, window):
    depth, width = two_dim(shape)
    if width % LANES == 0:
        step = width // LANES
        first = max(0, (window[0] - row) // step) // 8 * 8
        last = min(depth, round_up(max(0, -(-(window[1] - row) // step)), 8))
        for col in range(step):
            flat[strided(row + first * step + col, last - first, step), :] = in_ref[
                first:last, col * LANES : (col + 1) * LANES
            ]
        return
    half = LANES // 2
    lead = width // LANES
    if depth == 1:
        for col in range(lead):
            flat[row + col : row + col + 1, :] = in_ref[:, col * LANES : (col + 1) * LANES]
        tail = jnp.concatenate([in_ref[:, lead * LANES :], jnp.zeros((1, half), f32)], 1)
        flat[row + lead : row + lead + 1, :] = tail
        return
    step = 2 * width // LANES
    pairs = depth // 2
    lane = lax.broadcasted_iota(jnp.int32, (pairs, LANES), 1)
    for col in range(lead):
        pair_ref[col, 0:depth, :] = in_ref[:, col * LANES : (col + 1) * LANES]
    pair_ref[lead, 0:depth, 0:half] = in_ref[:, lead * LANES :]
    even = [pair_ref[col, strided(0, pairs, 2), :] for col in range(lead + 1)]
    odd = [half_swap(pair_ref[col, strided(1, pairs, 2), :]) for col in range(lead + 1)]
    for col in range(lead):
        flat[strided(row + col, pairs, step), :] = even[col]
    flat[strided(row + lead, pairs, step), :] = jnp.where(lane < half, even[lead], odd[0])
    for col in range(lead):
        flat[strided(row + lead + 1 + col, pairs, step), :] = jnp.where(
            lane < half, odd[col], odd[col + 1]
        )


def decode(number, core, bits):
    first = (number >> (bits - 1)) & 1
    second = (number >> (bits - 2)) & 1
    found = (first << core) | (second << (1 - core))
    for place in range(2, bits):
        found = found | (((number >> (bits - 1 - place)) & 1) << place)
    return found


def unflatten_kernel(plan, side, bits, where_ref, base_ref, *refs):
    pieces, refs = refs[:4], refs[4:]
    carried, refs = (refs[:1], refs[1:]) if side else ((), refs)
    outs, (flat, pair_ref) = refs[:-2], refs[-2:]
    span, overlap, half = plan["span"], plan["overlap"], plan["half"]
    origin = plan["origins"][side]
    core, mine = where_ref[0], where_ref[1]
    lead = plan["bases"][side * half] - origin
    if lead:
        flat[0:lead, :] = jnp.zeros((lead, LANES), f32)
    last = plan["bases"][side * half + half - 1] - origin + span
    if flat.shape[0] > last:
        flat[last:, :] = jnp.zeros((flat.shape[0] - last, LANES), f32)

    def base_of(owner):
        return pl.multiple_of(base_ref[side * half + owner] - origin, 16)

    def clear(owner, carry):
        base = base_of(owner)
        flat[pl.ds(base, overlap), :] = jnp.zeros((overlap, LANES), f32)
        flat[pl.ds(base + span - overlap, overlap), :] = jnp.zeros((overlap, LANES), f32)
        return carry

    lax.fori_loop(0, half, clear, 0)
    middle = span // 2
    for number, piece in enumerate(pieces):
        theirs = number // 2
        owner_core = core if theirs == 0 else 1 - core
        upper = number % 2 * (half // 2)
        for part in range(2):

            @pl.when(owner_core == part)
            def _(part=part, piece=piece, upper=upper):
                def place(entry, carry):
                    base = base_of(decode(entry + upper, part, bits) ^ mine)
                    value = piece[entry].astype(f32)
                    if part == 0:
                        flat[pl.ds(base, overlap), :] += value[:overlap]
                        flat[pl.ds(base + overlap, middle - overlap), :] = value[overlap:]
                    else:
                        flat[pl.ds(base + middle, middle - overlap), :] = value[: middle - overlap]
                        flat[pl.ds(base + span - overlap, overlap), :] += value[middle - overlap :]
                    return carry

                lax.fori_loop(0, half // 2, place, 0)

    for number, ((label, shape), out_ref) in enumerate(zip(plan["sides"][side], outs)):
        read_param(flat, plan["places"][label][0] - origin, shape, out_ref, pair_ref)
        if side and number == 0:
            out_ref[...] += carried[0][...]


def unflatten(where, pieces, plan, side, bits, carried=()):
    outs = []
    for label, shape in plan["sides"][side]:
        outs.append(jax.ShapeDtypeStruct(two_dim(shape), bf16 if is_matrix(label) else f32))
    vmem = pl.BlockSpec(memory_space=pltpu.VMEM)
    smem = pl.BlockSpec(memory_space=pltpu.SMEM)
    values = pl.pallas_call(
        functools.partial(unflatten_kernel, plan, side, bits),
        out_shape=outs,
        in_specs=[smem, smem] + [vmem] * (len(pieces) + len(carried)),
        out_specs=[vmem] * len(outs),
        scratch_shapes=[
            pltpu.VMEM((plan["heights"][side], LANES), f32),
            pltpu.VMEM((5, MS, LANES), f32),
        ],
        cost_estimate=estimate(1_000_000, 8_000_000),
        name="unflatten" + str(side),
    )(where, jnp.asarray(plan["bases"], jnp.int32), *pieces, *carried)
    return {label: value for (label, shape), value in zip(plan["sides"][side], values)}


def flatten_kernel(plan, group, bits, where_ref, base_ref, *refs):
    begin, owners, held, origin, height = plan["groups"][group]
    count = len(held)
    grads, (low_ref, high_ref, send_ref, flat, pair_ref) = refs[:count], refs[count:]
    span = plan["span"]
    core, mine = where_ref[0], where_ref[1]
    first, last = None, 0
    for label, shape in held:
        row = plan["places"][label][0] - origin
        first = row if first is None else first
        last = row + -(-math.prod(shape) // LANES)
    if first:
        flat[0:first, :] = jnp.zeros((first, LANES), f32)
    flat[last // 8 * 8 :, :] = jnp.zeros((height - last // 8 * 8, LANES), f32)
    window = (plan["bases"][begin] - origin, plan["bases"][begin + owners - 1] + span - origin)
    for (label, shape), ref in zip(held, grads):
        write_param(flat, plan["places"][label][0] - origin, shape, ref, pair_ref, window)

    def rows_of(entry, part):
        owner = (decode(entry, part, bits) ^ mine) & (owners - 1)
        base = base_ref[begin + owner] - origin + part * (span // 2)
        return flat[pl.ds(pl.multiple_of(base, 16), span // 2), :].astype(bf16)

    def place(entry, carry):
        low_ref[entry] = rows_of(entry, core)
        high_ref[entry] = rows_of(entry + owners // 2, core)
        send_ref[entry] = rows_of(entry, 1 - core)
        send_ref[entry + owners // 2] = rows_of(entry + owners // 2, 1 - core)
        return carry

    lax.fori_loop(0, owners // 2, place, 0)


def flatten(where, grads, plan, group):
    vmem = pl.BlockSpec(memory_space=pltpu.VMEM)
    smem = pl.BlockSpec(memory_space=pltpu.SMEM)
    begin, owners, held, origin, height = plan["groups"][group]
    rows = plan["span"] // 2
    values = [grads[label] for label, shape in held]
    return pl.pallas_call(
        functools.partial(flatten_kernel, plan, group, owners.bit_length() - 1),
        out_shape=(
            jax.ShapeDtypeStruct((owners // 2, rows, LANES), bf16),
            jax.ShapeDtypeStruct((owners // 2, rows, LANES), bf16),
            jax.ShapeDtypeStruct((owners, rows, LANES), bf16),
        ),
        in_specs=[smem, smem] + [vmem] * len(values),
        out_specs=(vmem, vmem, vmem),
        scratch_shapes=[
            pltpu.VMEM((height, LANES), f32),
            pltpu.VMEM((5, MS, LANES), f32),
        ],
        cost_estimate=estimate(1_000_000, 10_000_000),
        name="flatten" + str(group),
    )(where, jnp.asarray(plan["bases"], jnp.int32), *values)


def ln_parts(value):
    mean = jnp.mean(value, -1, keepdims=True)
    centred = value - mean
    variance = jnp.mean(centred * centred, -1, keepdims=True)
    inverse = lax.rsqrt(variance + norm_eps)
    return centred * inverse, inverse


def ln_back(grad, hat, inverse, gain):
    scaled = grad * gain
    first = jnp.mean(scaled, -1, keepdims=True)
    second = jnp.mean(scaled * hat, -1, keepdims=True)
    return inverse * (scaled - first - hat * second)


def gelu_parts(value):
    cdf = 0.5 + 0.5 * lax.erf(value * (2.0**-0.5))
    density = jnp.exp(value * value * -0.5) * (1.0 / math.sqrt(2.0 * math.pi))
    return value * cdf, cdf + value * density


def col_sum(value):
    return jnp.sum(value, 0, keepdims=True)


def groups(width):
    size = width // HEADS
    found = []
    for start in range(0, width, LANES):
        stop = min(start + LANES, width)
        found.append((start, stop, (stop - start) // size))
    return found, size


def stack_heads(value, count, size):
    lane = lax.broadcasted_iota(jnp.int32, value.shape, 1)
    zero = jnp.zeros_like(value)
    return jnp.concatenate(
        [
            jnp.where((lane >= head * size) & (lane < (head + 1) * size), value, zero)
            for head in range(count)
        ],
        0,
    )


def merge_heads(value, count, size):
    rows = value.shape[0] // count
    lane = lax.broadcasted_iota(jnp.int32, (rows, value.shape[1]), 1)
    merged = value[0:rows]
    for head in range(1, count):
        merged = jnp.where(lane >= head * size, value[head * rows : (head + 1) * rows], merged)
    return merged


def attention_forward(pair, length, tall, tokens, weights, keeps):
    ln1_ref, qkv_w, qkv_b, proj_w, proj_b, ln2_ref = weights
    a1_ref, qkv_ref, probs_ref, att_ref, mid_ref, n2_ref = keeps
    width = tokens.shape[-1]
    found, size = groups(width)
    scale = size ** (-0.5)
    hat, _ = ln_parts(tokens)
    a1 = (hat * ln1_ref[0:1, :] + ln1_ref[1:2, :]).astype(bf16)
    a1_ref[...] = a1
    qkv_ref[...] = (mm(a1, qkv_w[...]) + qkv_b[...]).astype(bf16)
    key_lane = lax.broadcasted_iota(jnp.int32, (1, tall), 1)
    bias = jnp.where(key_lane < length, 0.0, -1e30).astype(f32)
    for crop in range(pair):
        here = slice(crop * tall, (crop + 1) * tall)
        for start, stop, count in found:
            query = stack_heads(qkv_ref[here, start:stop], count, size)
            key = qkv_ref[here, width + start : width + stop]
            value = qkv_ref[here, 2 * width + start : 2 * width + stop]
            scores = mm_t(query, key) * scale + bias
            summit = jnp.max(scores, -1, keepdims=True)
            weights = jnp.exp(scores - summit)
            probs = (weights / jnp.sum(weights, -1, keepdims=True)).astype(bf16)
            first = start // size
            for head in range(count):
                probs_ref[crop, first + head] = probs[head * tall : (head + 1) * tall]
            att_ref[here, start:stop] = merge_heads(mm(probs, value), count, size).astype(bf16)
    mid = tokens + mm(att_ref[...], proj_w[...]) + proj_b[...]
    mid_ref[...] = mid
    hat, _ = ln_parts(mid)
    n2_ref[...] = (hat * ln2_ref[0:1, :] + ln2_ref[1:2, :]).astype(bf16)


def mlp_forward(chunk, mid_ref, n2_ref, weights, keeps):
    fc1_w, fc1_b, fc2_w, fc2_b = weights
    z_ref, slope_ref, y_ref = keeps
    y_ref[...] = mid_ref[...] + fc2_b[...]
    for number in range(fc1_w.shape[1] // chunk):
        cols = slice(number * chunk, (number + 1) * chunk)
        inner = mm(n2_ref[...], fc1_w[:, cols]) + fc1_b[:, cols]
        active, slope = gelu_parts(inner)
        z_ref[:, cols] = active.astype(bf16)
        slope_ref[:, cols] = slope.astype(bf16)
        y_ref[...] += mm(z_ref[:, cols], fc2_w[cols, :])


def keep_heads(pair, tall, y_ref, head_ref):
    for crop in range(pair):
        slot = pl.program_id(0) * pair + crop
        head_ref[pl.ds(slot, 1), :] = y_ref[crop * tall : crop * tall + 1, :]


def carry(value, norm, weight, bias):
    hat, _ = ln_parts(value)
    active, _ = gelu_parts(hat * norm[0:1, :] + norm[1:2, :])
    return (mm(active.astype(bf16), weight[...]) + bias[...]).astype(bf16)


def attention_kernel(pair, length, tall, tok_ref, *refs):
    tokens = tok_ref[...].reshape(pair * tall, tok_ref.shape[-1]).astype(f32)
    attention_forward(pair, length, tall, tokens, refs[:6], refs[6:])


def block_kernel(pair, length, tall, chunk, tok_ref, *refs):
    tokens = tok_ref[...].reshape(pair * tall, tok_ref.shape[-1]).astype(f32)
    attention_forward(pair, length, tall, tokens, refs[:6], refs[10:16])
    mlp_forward(chunk, refs[14], refs[15], refs[6:10], refs[16:19])
    keep_heads(pair, tall, refs[18], refs[19])


def mlp_kernel(pair, tall, chunk, mid_ref, n2_ref, *refs):
    weights, heads, (far_head, *far), near = refs[:4], None, refs[4:8], refs[8:11]
    z_ref, slope_ref, y_ref, head_ref, near_ref, far_ref = refs[11:]
    mlp_forward(chunk, mid_ref, n2_ref, weights, (z_ref, slope_ref, y_ref))
    keep_heads(pair, tall, y_ref, head_ref)

    @pl.when(pl.program_id(0) == pl.num_programs(0) - 1)
    def _():
        near_ref[...] = carry(head_ref[...], *near)
        far_ref[...] = carry(far_head[...], *far)


ATTENTION = ("ln1", "qkv_w", "qkv_b", "proj_w", "proj_b", "ln2")
MLP = ("fc1_w", "fc1_b", "fc2_w", "fc2_b")
TO = ("to_ln", "to_w", "to_b")


def pick(params, label, names):
    return [params[label + "_" + name] for name in names]


def row_spec(rows, cols):
    return pl.BlockSpec((rows, cols), lambda i: (i, 0))


def fixed_spec(shape):
    rank = len(shape)
    return pl.BlockSpec(shape, lambda i: (0,) * rank)


def kept_outs(crops, tall, width, hidden, pair):
    rows, flat = pair * tall, crops * tall

    def entry(cols, dtype):
        return row_spec(rows, cols), jax.ShapeDtypeStruct((flat, cols), dtype)

    attention = [
        entry(width, bf16),
        entry(3 * width, bf16),
        (
            pl.BlockSpec((pair, HEADS, tall, tall), lambda i: (i, 0, 0, 0)),
            jax.ShapeDtypeStruct((crops, HEADS, tall, tall), bf16),
        ),
        entry(width, bf16),
        entry(width, f32),
        entry(width, bf16),
    ]
    mlp = [
        entry(hidden, bf16),
        entry(hidden, bf16),
        entry(width, f32),
        (fixed_spec((crops, width)), jax.ShapeDtypeStruct((crops, width), f32)),
    ]
    return attention, mlp


def block_forward(tokens, params, label, length, pair):
    crops, tall, width = tokens.shape
    hidden = params[label + "_fc1_w"].shape[1]
    weights = pick(params, label, ATTENTION + MLP)
    attention, mlp = kept_outs(crops, tall, width, hidden, pair)
    outs = attention + mlp
    flops = 2 * crops * tall * (4 * width * width + 2 * width * hidden)
    return pl.pallas_call(
        functools.partial(block_kernel, pair, length, tall, 384),
        grid=(crops // pair,),
        out_shape=[shape for spec, shape in outs],
        in_specs=[pl.BlockSpec((pair, tall, width), lambda i: (i, 0, 0))]
        + [whole(value.shape) for value in weights],
        out_specs=[spec for spec, shape in outs],
        cost_estimate=estimate(8 * flops, 10_000_000),
        name="block_" + label,
    )(tokens, *weights)


def attention_only(tokens, params, label, length, pair):
    crops, tall, width = tokens.shape
    weights = pick(params, label, ATTENTION)
    outs, _ = kept_outs(crops, tall, width, width, pair)
    flops = 2 * crops * tall * 4 * width * width
    return pl.pallas_call(
        functools.partial(attention_kernel, pair, length, tall),
        grid=(crops // pair,),
        out_shape=[shape for spec, shape in outs],
        in_specs=[pl.BlockSpec((pair, tall, width), lambda i: (i, 0, 0))]
        + [whole(value.shape) for value in weights],
        out_specs=[spec for spec, shape in outs],
        cost_estimate=estimate(8 * flops, 20_000_000),
        name="attention_" + label,
    )(tokens, *weights)


def mlp_only(mid, n2, far_head, params, label, far, crops, pair):
    flat, width = mid.shape
    tall = flat // crops
    rows = pair * tall
    hidden = params[label + "_fc1_w"].shape[1]
    weights = pick(params, label, MLP)
    extra = [far_head] + pick(params, far, TO) + pick(params, label, TO)
    _, outs = kept_outs(crops, tall, width, hidden, pair)
    for name in (label, far):
        shape = (crops, params[name + "_to_w"].shape[1])
        outs.append((fixed_spec(shape), jax.ShapeDtypeStruct(shape, bf16)))
    flops = 2 * flat * 2 * width * hidden
    return pl.pallas_call(
        functools.partial(mlp_kernel, pair, tall, 384),
        grid=(crops // pair,),
        out_shape=[shape for spec, shape in outs],
        in_specs=[row_spec(rows, width), row_spec(rows, width)]
        + [whole(value.shape) for value in weights + extra],
        out_specs=[spec for spec, shape in outs],
        cost_estimate=estimate(8 * flops, 20_000_000),
        name="mlp_" + label,
    )(mid, n2, *weights, *extra)


def cross_kernel(
    length,
    tall,
    crops,
    sent_ref,
    y_ref,
    gret_ref,
    ca_ln,
    q_w,
    q_b,
    k_w,
    v_w,
    v_b,
    o_w,
    o_b,
    back_ln,
    back_w,
    back_b,
    returned_ref,
    gsent_ref,
    gj_ref,
    d_ca_ln,
    d_q_w,
    d_q_b,
    d_k_w,
    d_v_w,
    d_v_b,
    d_o_w,
    d_o_b,
    d_back_ln,
    d_back_w,
    d_back_b,
    sent_f,
    n_all,
    score_all,
    mates_all,
    pairs_all,
    gn_head,
    gj_head,
):
    width = y_ref.shape[1]
    size = width // HEADS
    scale = size ** (-0.5)
    stacked = crops * 8
    lane = lax.broadcasted_iota(jnp.int32, (8, width), 1)
    head = lax.broadcasted_iota(jnp.int32, (8, width), 0)
    own_head = (lane >= head * size) & (lane < (head + 1) * size)
    row = lax.broadcasted_iota(jnp.int32, (tall, 1), 0)
    key_lane = lax.broadcasted_iota(jnp.int32, (1, tall), 1)
    bias = jnp.where(key_lane < length, 0.0, -1e30).astype(f32)
    gain, shift = ca_ln[0:1, :], ca_ln[1:2, :]
    sent_f[...] = sent_ref[...].astype(f32)
    hat, _ = ln_parts(sent_f[...])
    n_head = (hat * gain + shift).astype(bf16)

    def spread(value):
        return jnp.concatenate(
            [jnp.where(own_head, value[crop : crop + 1], 0.0) for crop in range(crops)], 0
        )

    def gathered(value):
        return jnp.concatenate(
            [
                col_sum(jnp.where(own_head, value[crop * 8 : crop * 8 + 8], 0.0))
                for crop in range(crops)
            ],
            0,
        )

    def normed_of(crop):
        return n_all[crop * tall : (crop + 1) * tall, :]

    def against(value):
        return jnp.concatenate(
            [
                mm_t(value[crop * 8 : crop * 8 + 8].astype(bf16), normed_of(crop))
                for crop in range(crops)
            ],
            0,
        )

    def mixed(value):
        return jnp.concatenate(
            [
                mm(value[crop * 8 : crop * 8 + 8].astype(bf16), normed_of(crop))
                for crop in range(crops)
            ],
            0,
        )

    query = spread((mm(n_head, q_w[...]) + q_b[...]).astype(bf16).astype(f32)).astype(bf16)
    keyed = mm_t(query, k_w[...]) * scale
    blank = jnp.zeros((8, width), f32)
    for crop in range(crops):
        mates_all[crop] = jnp.concatenate([keyed[crop * 8 : crop * 8 + 8], blank], 0).astype(bf16)

    def joined(crop):
        here = pl.ds(pl.multiple_of(crop * tall, 16), tall)
        return here, jnp.where(row == 0, sent_f[pl.ds(crop, 1), :], y_ref[here, :])

    def ahead(crop, carry):
        here, value = joined(crop)
        hat, _ = ln_parts(value)
        normed = (hat * gain + shift).astype(bf16)
        n_all[here, :] = normed
        score_all[pl.ds(crop, 1)] = mm_t(mates_all[crop], normed)[None, 0:8]
        return carry

    lax.fori_loop(0, crops, ahead, 0)
    scores = score_all[...].reshape(stacked, tall) + bias
    summit = jnp.max(scores, -1, keepdims=True)
    weights = jnp.exp(scores - summit)
    probs = weights / jnp.sum(weights, -1, keepdims=True)
    rounded = probs.astype(bf16).astype(f32)
    total = jnp.sum(rounded, -1, keepdims=True)
    mean_n = mixed(rounded).astype(bf16)
    attended = gathered(mm(mean_n, v_w[...]) + total * v_b[...]).astype(bf16)
    merged = sent_f[...] + mm(attended, o_w[...]) + o_b[...]
    hat, inverse = ln_parts(merged)
    active, slope = gelu_parts(hat * back_ln[0:1, :] + back_ln[1:2, :])
    active = active.astype(bf16)
    returned_ref[...] = (mm(active, back_w[...]) + back_b[...]).astype(bf16)
    gret = gret_ref[...]
    d_back_w[...] = t_mm(active, gret)
    d_back_b[...] = col_sum(gret.astype(f32))
    gact = mm_t(gret, back_w[...]) * slope
    d_back_ln[0:1, :] = col_sum(gact * hat)
    d_back_ln[1:2, :] = col_sum(gact)
    gfused = ln_back(gact, hat, inverse, back_ln[0:1, :])
    gfo = gfused.astype(bf16)
    d_o_w[...] = t_mm(attended, gfo)
    d_o_b[...] = col_sum(gfo.astype(f32))
    gatt = spread(mm_t(gfo, o_w[...]).astype(bf16).astype(f32))
    d_v_b[...] = col_sum(total * gatt)
    gbias = jnp.sum(gatt * v_b[...], -1, keepdims=True)
    gatt = gatt.astype(bf16)
    d_v_w[...] = t_mm(mean_n, gatt)
    valued = mm_t(gatt, v_w[...])
    gprobs = against(valued) + gbias
    inner = gprobs - jnp.sum(gprobs * probs, -1, keepdims=True)
    gscores = (probs * inner).astype(bf16).astype(f32)
    for crop in range(crops):
        part = slice(crop * 8, crop * 8 + 8)
        mates_all[crop] = jnp.concatenate([keyed[part], valued[part]], 0).astype(bf16)
        pairs_all[crop] = jnp.concatenate([gscores[part], rounded[part]], 0).astype(bf16)
    slid = (mixed(gscores) * scale).astype(bf16)
    d_k_w[...] = t_mm(slid, query)
    gq = gathered(mm(slid, k_w[...])).astype(bf16)
    d_q_w[...] = t_mm(n_head, gq)
    d_q_b[...] = col_sum(gq.astype(f32))
    gn_head[...] = mm_t(gq, q_w[...])
    d_ca_ln[...] = jnp.zeros_like(d_ca_ln)

    def finish(crop, carry):
        here, value = joined(crop)
        hat, inverse = ln_parts(value)
        gn = t_mm(pairs_all[crop], mates_all[crop])
        gn = gn + jnp.where(row == 0, gn_head[pl.ds(crop, 1), :], 0.0)
        d_ca_ln[0:1, :] += col_sum(gn * hat)
        d_ca_ln[1:2, :] += col_sum(gn)
        gj = ln_back(gn, hat, inverse, gain)
        gj_ref[here, :] = gj
        gj_head[pl.ds(crop, 1), :] = gj[0:1, :]
        return carry

    lax.fori_loop(0, crops, finish, 0)
    gsent_ref[...] = (gj_head[...] + gfused).astype(bf16)


def cross(sent, hosted, gret, params, label, length, tall):
    crops, width = sent.shape
    own = gret.shape[1]
    flat = crops * tall
    names = ("ca_ln", "ca_q_w", "ca_q_b", "ca_k_w", "ca_v_w", "ca_v_b", "ca_o_w", "ca_o_b")
    names = names + ("back_ln", "back_w", "back_b")
    weights = [params[label + "_" + name] for name in names]
    outs = [
        jax.ShapeDtypeStruct((crops, own), bf16),
        jax.ShapeDtypeStruct((crops, width), bf16),
        jax.ShapeDtypeStruct((flat, width), f32),
    ] + [jax.ShapeDtypeStruct(value.shape, f32) for value in weights]
    vmem = pl.BlockSpec(memory_space=pltpu.VMEM)
    small = pltpu.VMEM((crops, width), f32)
    values = pl.pallas_call(
        functools.partial(cross_kernel, length, tall, crops),
        out_shape=outs,
        in_specs=[vmem] * (3 + len(weights)),
        out_specs=[vmem] * len(outs),
        scratch_shapes=[
            small,
            pltpu.VMEM((flat, width), bf16),
            pltpu.VMEM((crops, 8, tall), f32),
            pltpu.VMEM((crops, 16, width), bf16),
            pltpu.VMEM((crops, 16, tall), bf16),
            small,
            small,
        ],
        cost_estimate=estimate(2 * flat * width * width * 2, 8_000_000),
        name="cross_" + label,
    )(sent, hosted, gret, *weights)
    grads = {label + "_" + name: value for name, value in zip(names, values[3:])}
    return values[0], values[1], values[2], grads


def head_backward(headrow_ref, gsent_ref, to_ln, to_w, d_to_ln, d_to_w, d_to_b, ghead_ref):
    hat, inverse = ln_parts(headrow_ref[...])
    active, slope = gelu_parts(hat * to_ln[0:1, :] + to_ln[1:2, :])
    gsent = gsent_ref[...]
    d_to_w[...] = t_mm(active.astype(bf16), gsent)
    d_to_b[...] = col_sum(gsent.astype(f32))
    gact = mm_t(gsent, to_w[...]) * slope
    d_to_ln[0:1, :] = col_sum(gact * hat)
    d_to_ln[1:2, :] = col_sum(gact)
    ghead_ref[...] = ln_back(gact, hat, inverse, to_ln[0:1, :])


def clear_all(refs):
    for ref in refs:
        ref[...] = jnp.zeros_like(ref)


def mlp_backward(pair, tall, chunk, live_ref, acts, weights, grads, out_ref, gy, gnormed):
    cot_ref, y_ref, gj_ref, mid_ref, n2_ref, z_ref, slope_ref, ghead, returned_ref = acts
    ln2_ref, fc1_w, fc2_w = weights
    d_ln2, d_fc1_w, d_fc1_b, d_fc2_w, d_fc2_b = grads
    length = out_ref.shape[2]
    row = lax.broadcasted_iota(jnp.int32, (tall, 1), 0)
    for crop in range(pair):
        here = slice(crop * tall, (crop + 1) * tall)
        slot = pl.program_id(0) * pair + crop
        live = jnp.where(slot < live_ref[0], 1.0, 0.0).astype(f32)
        seed = cot_ref[crop].astype(f32) * live + gj_ref[here, :]
        gy[here, :] = jnp.where(row == 0, ghead[pl.ds(slot, 1), :], seed)
        home = returned_ref[pl.ds(slot, 1), :]
        final = jnp.where(row == 0, home, y_ref[here, :])
        out_ref[0, crop] = final[0:length].astype(bf16)
    gm = gy[...].astype(bf16)
    d_fc2_b[...] += col_sum(gm.astype(f32))

    def one(number, first):
        start = number * chunk
        if not isinstance(number, int):
            start = pl.multiple_of(start, LANES)
        cols = pl.ds(start, chunk)
        d_fc2_w[cols, :] += t_mm(z_ref[:, cols], gm)
        gu = slope_ref[:, cols].astype(f32) * mm_t(gm, fc2_w[cols, :])
        gu = gu.astype(bf16)
        d_fc1_w[:, cols] += t_mm(n2_ref[...], gu)
        d_fc1_b[:, cols] += col_sum(gu.astype(f32))
        part = mm_t(gu, fc1_w[:, cols])
        gnormed[...] = part if first else gnormed[...] + part

    def looped(number, carry):
        one(number, False)
        return carry

    chunks = fc1_w.shape[1] // chunk
    if fc1_w.shape[1] > 1024:
        gnormed[...] = jnp.zeros_like(gnormed)
        lax.fori_loop(0, chunks, looped, 0)
    else:
        for number in range(chunks):
            one(number, number == 0)
    hat, inverse = ln_parts(mid_ref[...])
    gn = gnormed[...]
    d_ln2[0:1, :] += col_sum(gn * hat)
    d_ln2[1:2, :] += col_sum(gn)
    gy[...] += ln_back(gn, hat, inverse, ln2_ref[0:1, :])


def attention_backward(pair, tall, acts, weights, grads, gtok_ref, gmid_ref, gqkv, gatt_ref):
    tok_ref, a1_ref, qkv_ref, probs_ref, att_ref = acts
    ln1_ref, qkv_w, proj_w = weights
    d_ln1, d_qkv_w, d_qkv_b, d_proj_w, d_proj_b = grads
    width = tok_ref.shape[-1]
    length = gtok_ref.shape[2]
    found, size = groups(width)
    scale = size ** (-0.5)
    gp = gmid_ref[...].astype(bf16)
    d_proj_w[...] += t_mm(att_ref[...], gp)
    d_proj_b[...] += col_sum(gp.astype(f32))
    gatt_ref[...] = mm_t(gp, proj_w[...]).astype(bf16)

    def one(crop, carry):
        here = pl.ds(crop * tall, tall)
        if not isinstance(crop, int):
            here = pl.ds(pl.multiple_of(crop * tall, 16), tall)
        for start, stop, count in found:
            first = start // size
            query = stack_heads(qkv_ref[here, start:stop], count, size)
            key = qkv_ref[here, width + start : width + stop]
            value = qkv_ref[here, 2 * width + start : 2 * width + stop]
            gatt = stack_heads(gatt_ref[here, start:stop], count, size)
            probs_low = jnp.concatenate([probs_ref[crop, first + head] for head in range(count)], 0)
            probs = probs_low.astype(f32)
            gprobs = mm_t(gatt, value)
            inner = gprobs - jnp.sum(gprobs * probs, -1, keepdims=True)
            gscores = (probs * inner).astype(bf16)
            gq = merge_heads(mm(gscores, key), count, size) * scale
            gk = t_mm(gscores, query) * scale
            gv = t_mm(probs_low, gatt)
            gqkv[here, start:stop] = gq.astype(bf16)
            gqkv[here, width + start : width + stop] = gk.astype(bf16)
            gqkv[here, 2 * width + start : 2 * width + stop] = gv.astype(bf16)
        return carry

    if len(found) > 2:
        lax.fori_loop(0, pair, one, 0)
    else:
        for crop in range(pair):
            one(crop, 0)
    grad = gqkv[...]
    d_qkv_w[...] += t_mm(a1_ref[...], grad)
    d_qkv_b[...] += col_sum(grad.astype(f32))
    gn = mm_t(grad, qkv_w[...])
    hat, inverse = ln_parts(tok_ref[...].reshape(pair * tall, width).astype(f32))
    d_ln1[0:1, :] += col_sum(gn * hat)
    d_ln1[1:2, :] += col_sum(gn)
    gtok = gmid_ref[...] + ln_back(gn, hat, inverse, ln1_ref[0:1, :])
    for crop in range(pair):
        gtok_ref[0, crop] = gtok[crop * tall : crop * tall + length].astype(bf16)


GRAD_MLP = ("ln2", "fc1_w", "fc1_b", "fc2_w", "fc2_b")
GRAD_ATTENTION = ("ln1", "qkv_w", "qkv_b", "proj_w", "proj_b")


def mlp_back_kernel(pair, tall, chunk, live_ref, *refs):
    cot_ref, y_ref, gj_ref, mid_ref, n2_ref, z_ref, slope_ref, returned_ref = refs[:8]
    weights = refs[8:11]
    near, far = refs[11:15], refs[15:19]
    out_ref, gmid_ref, ghead_far = refs[19:22]
    grads, near_grads, far_grads = refs[22:27], refs[27:30], refs[30:33]
    ghead, gnormed, home = refs[33:]

    @pl.when(pl.program_id(0) == 0)
    def _():
        head_backward(*near, *near_grads, ghead)
        head_backward(*far, *far_grads, ghead_far)
        clear_all(grads)
        home[...] = returned_ref[...].astype(f32)

    acts = (cot_ref, y_ref, gj_ref, mid_ref, n2_ref, z_ref, slope_ref, ghead, home)
    mlp_backward(pair, tall, chunk, live_ref, acts, weights, grads, out_ref, gmid_ref, gnormed)


def attention_back_kernel(pair, tall, gmid_ref, *refs):
    acts, weights, gtok_ref, grads = refs[:5], refs[5:8], refs[8], refs[9:14]

    @pl.when(pl.program_id(0) == 0)
    def _():
        clear_all(grads)

    attention_backward(pair, tall, acts, weights, grads, gtok_ref, gmid_ref, *refs[14:])


def block_back_kernel(pair, tall, chunk, live_ref, *refs):
    mlp_acts, acts = refs[:9], refs[9:14]
    weights, mlp_weights = refs[14:17], refs[17:20]
    out_ref, gtok_ref = refs[20:22]
    mlp_grads, grads = refs[22:27], refs[27:32]
    gy, gnormed, gqkv, gatt_ref, home = refs[32:]

    @pl.when(pl.program_id(0) == 0)
    def _():
        clear_all(mlp_grads + grads)
        home[...] = mlp_acts[8][...].astype(f32)

    mlp_backward(
        pair, tall, chunk, live_ref, (*mlp_acts[:8], home), mlp_weights, mlp_grads, out_ref, gy, gnormed
    )
    attention_backward(pair, tall, acts, weights, grads, gtok_ref, gy, gqkv, gatt_ref)


def named(label, names, values):
    return {label + "_" + name: value for name, value in zip(names, values)}


def grad_outs(params, label, names):
    return [
        (fixed_spec(value.shape), jax.ShapeDtypeStruct(value.shape, f32))
        for value in pick(params, label, names)
    ]


def token_out(crops, length, width, pair):
    return (
        pl.BlockSpec((1, pair, length, width), lambda i: (0, i, 0, 0)),
        jax.ShapeDtypeStruct((1, crops, length, width), bf16),
    )


def mlp_back(cot, live, kept, gj, near, far, returned, params, label, other, length, pair):
    crops, tall, width = cot.shape
    mid, n2, z, slope, y = kept
    hidden = z.shape[1]
    rows, flat = pair * tall, crops * tall
    weights = pick(params, label, ("ln2", "fc1_w", "fc2_w"))
    near = list(near) + pick(params, label, ("to_ln", "to_w"))
    far = list(far) + pick(params, other, ("to_ln", "to_w"))
    smem = pl.BlockSpec(memory_space=pltpu.SMEM)
    outs = [
        token_out(crops, length, width, pair),
        (row_spec(rows, width), jax.ShapeDtypeStruct((flat, width), f32)),
        (fixed_spec(far[0].shape), jax.ShapeDtypeStruct(far[0].shape, f32)),
    ]
    outs += grad_outs(params, label, GRAD_MLP)
    outs += grad_outs(params, label, TO) + grad_outs(params, other, TO)
    values = pl.pallas_call(
        functools.partial(mlp_back_kernel, pair, tall, 768),
        grid=(crops // pair,),
        out_shape=[shape for spec, shape in outs],
        in_specs=[smem, pl.BlockSpec((pair, tall, width), lambda i: (i, 0, 0))]
        + [row_spec(rows, width)] * 4
        + [row_spec(rows, hidden)] * 2
        + [whole(value.shape) for value in [returned] + weights + near + far],
        out_specs=[spec for spec, shape in outs],
        scratch_shapes=[
            pltpu.VMEM((crops, width), f32),
            pltpu.VMEM((rows, width), f32),
            pltpu.VMEM((crops, width), f32),
        ],
        cost_estimate=estimate(8 * 8 * flat * width * hidden, 20_000_000),
        name="mlp_back_" + label,
    )(live, cot, y, gj, mid, n2, z, slope, returned, *weights, *near, *far)
    grads = named(label, GRAD_MLP, values[3:8])
    grads.update(named(label, TO, values[8:11]))
    grads.update(named(other, TO, values[11:14]))
    return values[0], values[1], values[2], grads


def attention_back(tokens, gmid, kept, params, label, length, pair):
    crops, tall, width = tokens.shape
    a1, qkv, probs, att = kept
    rows, flat = pair * tall, crops * tall
    weights = pick(params, label, ("ln1", "qkv_w", "proj_w"))
    outs = [token_out(crops, length, width, pair)] + grad_outs(params, label, GRAD_ATTENTION)
    values = pl.pallas_call(
        functools.partial(attention_back_kernel, pair, tall),
        grid=(crops // pair,),
        out_shape=[shape for spec, shape in outs],
        in_specs=[
            row_spec(rows, width),
            pl.BlockSpec((pair, tall, width), lambda i: (i, 0, 0)),
            row_spec(rows, width),
            row_spec(rows, 3 * width),
            pl.BlockSpec((pair, HEADS, tall, tall), lambda i: (i, 0, 0, 0)),
            row_spec(rows, width),
        ]
        + [whole(value.shape) for value in weights],
        out_specs=[spec for spec, shape in outs],
        scratch_shapes=[pltpu.VMEM((rows, 3 * width), bf16), pltpu.VMEM((rows, width), bf16)],
        cost_estimate=estimate(8 * 16 * flat * width * width, 20_000_000),
        name="attention_back_" + label,
    )(gmid, tokens, a1, qkv, probs, att, *weights)
    return values[0], named(label, GRAD_ATTENTION, values[1:])


def block_back(tokens, cot, live, kept, gj, ghead, returned, params, label, length, pair):
    crops, tall, width = tokens.shape
    a1, qkv, probs, att, mid, n2, z, slope, y = kept
    hidden = z.shape[1]
    rows, flat = pair * tall, crops * tall
    weights = pick(params, label, ("ln1", "qkv_w", "proj_w", "ln2", "fc1_w", "fc2_w"))
    smem = pl.BlockSpec(memory_space=pltpu.SMEM)
    token_spec = pl.BlockSpec((pair, tall, width), lambda i: (i, 0, 0))
    outs = [token_out(crops, length, width, pair)] * 2
    outs += grad_outs(params, label, GRAD_MLP) + grad_outs(params, label, GRAD_ATTENTION)
    values = pl.pallas_call(
        functools.partial(block_back_kernel, pair, tall, 384),
        grid=(crops // pair,),
        out_shape=[shape for spec, shape in outs],
        in_specs=[smem, token_spec]
        + [row_spec(rows, width)] * 4
        + [row_spec(rows, hidden)] * 2
        + [whole(ghead.shape), whole(returned.shape)]
        + [
            token_spec,
            row_spec(rows, width),
            row_spec(rows, 3 * width),
            pl.BlockSpec((pair, HEADS, tall, tall), lambda i: (i, 0, 0, 0)),
            row_spec(rows, width),
        ]
        + [whole(value.shape) for value in weights],
        out_specs=[spec for spec, shape in outs],
        scratch_shapes=[
            pltpu.VMEM((rows, width), f32),
            pltpu.VMEM((rows, width), f32),
            pltpu.VMEM((rows, 3 * width), bf16),
            pltpu.VMEM((rows, width), bf16),
            pltpu.VMEM((crops, width), f32),
        ],
        cost_estimate=estimate(8 * 4 * flat * (4 * width * width + 2 * width * hidden), 20_000_000),
        name="block_back_" + label,
    )(live, cot, y, gj, mid, n2, z, slope, ghead, returned, tokens, a1, qkv, probs, att, *weights)
    grads = named(label, GRAD_MLP, values[2:7])
    grads.update(named(label, GRAD_ATTENTION, values[7:12]))
    return values[0], values[1], grads


def swap(value):
    return lax.ppermute(value, "branch", [(0, 1), (1, 0)])


def partner(value, bit):
    count = lax.axis_size("dp")
    return lax.ppermute(value, "dp", [(i, i ^ bit) for i in range(count)])


def side_partner(value, place):
    count = lax.axis_size("dp")
    pairs = []
    for core in range(2):
        bit = 1 << (place ^ core)
        pairs += [(core * count + i, core * count + (i ^ bit)) for i in range(count)]
    return lax.ppermute(value, ("branch", "dp"), pairs)


def tie(value, *others):
    return lax.optimization_barrier((value, *others))[0] if others else value


def gather_lines(held, first, last, jobs=()):
    for number, place in enumerate(range(first, last, -1)):
        got = partner(held, 1 << place)
        if number < len(jobs):
            got = tie(got, *jobs[number](held))
        held = jnp.concatenate([held, got], 0)
    return held


def gather_middle(held):
    return jnp.concatenate([held, side_partner(held, 1)], 0)


def add_low(*values):
    total = values[0].astype(f32)
    for value in values[1:]:
        total = total + value.astype(f32)
    return total.astype(bf16)


def reduce_step(parts, count, send):
    count = count // 2
    sent = add_low(*[part[count : 2 * count] for part in parts])
    return sent, parts + [send(sent)], count


def reduce_start(low, high, got):
    half = low.shape[0]
    sent = add_low(high, got[half:])
    return sent, [low, got, side_partner(sent, 0)], half


def reduce_middle(parts, count):
    return reduce_step(parts, count, lambda sent: side_partner(sent, 1))


def reduce_lines(parts, count, first, last):
    for place in range(first, last):
        _, parts, count = reduce_step(parts, count, lambda sent: partner(sent, 1 << place))
    return parts, count


def add_up(parts):
    total = parts[0][0].astype(f32)
    for part in parts[1:]:
        total = total + part[0].astype(f32)
    return total


def shards(
    small_tokens,
    large_tokens,
    small_cot,
    large_cot,
    live_counts,
    master,
    first_moment,
    second_moment,
):
    count = lax.axis_size("branch") * lax.axis_size("dp")
    bits = lax.axis_size("dp").bit_length() - 1
    plan = grid_plan(count)
    core, mine = lax.axis_index("branch"), lax.axis_index("dp")
    where = jnp.stack([core, mine]).astype(jnp.int32)
    index = lax.axis_index(("branch", "dp"))
    size = master.shape[0]
    rows = plan["shard_rows"]
    table = lax.dynamic_index_in_dim(jnp.asarray(plan["table"]), index, 0, False)
    padded = jnp.pad(master, (0, rows * LANES - size)).reshape(rows, LANES)
    keep, send = align(where, table, padded, plan)
    got = swap(send)
    counts = live_counts[:, 0]
    own_count = lax.dynamic_slice_in_dim(counts, core, 1)
    far_count = lax.dynamic_slice_in_dim(counts, 1 - core, 1)
    crops, length_s = small_tokens.shape[1], small_tokens.shape[2]
    length_l = large_tokens.shape[2]
    tall_s, tall_l = round_up(length_s, 16), round_up(length_l, 16)
    pair = 2

    def inward(value):
        return jnp.transpose(value[0], (1, 0, 2))

    def settled(value):
        return with_layout_constraint(inward(value), Layout(major_to_minor=(0, 1, 2)))

    def outward(value):
        return jnp.transpose(value, (1, 0, 2))[None]

    def taller(value, length, tall):
        return jnp.pad(value[0], ((0, 0), (0, tall - length), (0, 0)))

    early = []

    def pad_tokens(held):
        early.append(taller(tie(small_tokens, held), length_s, tall_s))
        early.append(taller(tie(large_tokens, held), length_l, tall_l))
        return early[0:2]

    def pad_seeds(held):
        slots = jnp.arange(crops, dtype=jnp.int32)[:, None]
        small_held, large_held = tie(small_cot, held), tie(large_cot, held)
        early.append(taller(small_held, length_s, tall_s))
        early.append(taller(large_held, length_l, tall_l))
        early.append(jnp.where(slots < own_count, small_held[0, :, 0], 0))
        early.append(jnp.where(slots < far_count, large_held[0, :, 0], 0))
        return early[2:6]

    held = jnp.where(core == 0, keep, got)[None]
    near = gather_lines(held, bits - 1, 1, (pad_tokens, pad_seeds))
    small, large, small_seed, large_seed, ret_small, ret_large = early
    far = tie(jnp.where(core == 0, got, keep)[None], near)
    middle = (bits + 1) // 2
    far = gather_lines(far, bits - 1, middle)
    near = tie(gather_middle(near), far)
    near_end = side_partner(near, 0)
    far = gather_lines(far, middle, 1)
    near_end = tie(near_end, far)
    near_pieces = (near, near_end, swap(near), swap(near_end))
    ret_small, ret_large = swap(ret_small), swap(ret_large)

    params = unflatten(where, near_pieces, plan, 0, bits)
    straddling = params.pop(plan["sides"][1][0][0])
    far = tie(far, near_end)
    far = jnp.concatenate([far, tie(side_partner(far, 1), params["s_ln1"])], 0)
    *kept_s, head_s = block_forward(tie(small, far), params, "s", length_s, pair)
    far_end = side_partner(far, 0)
    kept_l = attention_only(tie(large, far_end), params, "l", length_l, pair)
    far_pieces = (far, far_end, swap(far), swap(far_end))
    params.update(unflatten(where, far_pieces, plan, 1, bits, (straddling,)))
    z_l, slope_l, y_l, head_l, sent_l, sent_s = mlp_only(
        kept_l[4], kept_l[5], head_s, params, "l", "s", crops, pair
    )
    got_s, got_l = swap(sent_s), swap(sent_l)
    grads = {}
    back_s, gsent_s, gj_l, part = cross(got_s, y_l, ret_small, params, "s", length_l, tall_l)
    grads.update(part)
    home_s, own_s = swap(back_s), swap(gsent_s)
    back_l, gsent_l, gj_s, part = cross(got_l, kept_s[8], ret_large, params, "l", length_s, tall_s)
    grads.update(part)
    home_l, own_l = swap(back_l), swap(gsent_l)
    large_out, gmid, ghead_s, part = mlp_back(
        large_seed,
        far_count,
        (kept_l[4], kept_l[5], z_l, slope_l, y_l),
        gj_l,
        (head_l, own_l),
        (head_s, own_s),
        home_l,
        params,
        "l",
        "s",
        length_l,
        pair,
    )
    grads.update(part)
    far_parts = flatten(where, grads, plan, 2)
    far_got = swap(far_parts[2])
    large_grad, part = attention_back(large, gmid, kept_l[:4], params, "l", length_l, pair)
    grads.update(part)
    grads["l_ln1"], far_got = lax.optimization_barrier((grads["l_ln1"], far_got))
    upper_parts = flatten(where, grads, plan, 1)
    upper_got = swap(upper_parts[2])
    sent_far, far_side, far_left = reduce_start(*far_parts[:2], far_got)
    sent_upper, upper, upper_left = reduce_start(*upper_parts[:2], tie(upper_got, sent_far))
    ghead_s = tie(ghead_s, sent_far, sent_upper, gmid)
    small_out, small_grad, part = block_back(
        small, small_seed, own_count, kept_s, gj_s, ghead_s, home_s, params, "s", length_s, pair
    )
    grads.update(part)
    grads["s_ln1"] = tie(grads["s_ln1"], far_side[-1], upper[-1])
    lower_parts = flatten(where, grads, plan, 0)
    lower_got = swap(lower_parts[2])
    _, far_side, far_left = reduce_middle(far_side, far_left)
    _, upper, upper_left = reduce_middle(upper, upper_left)
    sent, lower, lower_left = reduce_start(*lower_parts[:2], lower_got)
    lower[-1], large_out, large_grad = lax.optimization_barrier(
        (lower[-1], settled(tie(large_out, sent)), settled(tie(large_grad, sent)))
    )
    far_side[-1], upper[-1] = tie(far_side[-1], sent), tie(upper[-1], sent)
    far_side, far_left = reduce_lines(far_side, far_left, 2, 3)
    upper, _ = reduce_lines(upper, upper_left, 2, bits - 1)
    sent, lower, lower_left = reduce_middle(lower, lower_left)
    lower[-1], small_out, small_grad = lax.optimization_barrier(
        (lower[-1], settled(tie(small_out, sent)), settled(tie(small_grad, sent)))
    )
    lower = add_up(reduce_lines(lower, lower_left, 2, bits - 1)[0])
    far_side, _ = reduce_lines(far_side, far_left, 3, bits)
    upper = add_up(upper)
    top = (mine >> (bits - 1)) & 1
    last_sent = jnp.where(top == 1, lower, upper).astype(bf16)
    near_total = jnp.where(top == 1, upper, lower)
    last_got = partner(last_sent, 1 << (bits - 1))
    everyone = jnp.asarray(plan["table"])
    tables = [
        lax.dynamic_index_in_dim(everyone, mine + begin, 0, False) for begin in (0, plan["half"])
    ]
    own, send, square = settle(
        where, jnp.concatenate(tables), near_total, last_got, far_side, plan
    )
    got = swap(send)
    square = square + swap(square)
    summed = unalign(where, table, own, tie(got, square), plan)
    for place in range(bits):
        there = partner(square, 1 << place)
        square = square + (tie(there, summed) if place == 0 else there)
    grad_norm = jnp.sqrt(square[0, 0])
    own_grad = summed.reshape(-1)[:size]
    clipped = own_grad * jnp.minimum(1.0, clip_norm / grad_norm)
    new_first = beta_one * first_moment + (1.0 - beta_one) * clipped
    new_second = beta_two * second_moment + (1.0 - beta_two) * clipped * clipped
    new_master = master - rate * (
        new_first / bias_one / (jnp.sqrt(new_second / bias_two) + adam_eps) + decay * master
    )
    return (
        outward(small_out),
        outward(large_out),
        outward(small_grad),
        outward(large_grad),
        grad_norm,
        new_first,
        new_second,
        new_master,
        new_master.astype(bf16),
    )


def solution(mesh):
    return jax.shard_map(
        shards,
        mesh=mesh,
        in_specs=(
            P("branch", "dp", None, None),
            P("branch", "dp", None, None),
            P("branch", "dp", None, None),
            P("branch", "dp", None, None),
            P(None, "dp"),
            P(("branch", "dp")),
            P(("branch", "dp")),
            P(("branch", "dp")),
        ),
        out_specs=(
            P("branch", "dp", None, None),
            P("branch", "dp", None, None),
            P("branch", "dp", None, None),
            P("branch", "dp", None, None),
            P(),
            P(("branch", "dp")),
            P(("branch", "dp")),
            P(("branch", "dp")),
            P(("branch", "dp")),
        ),
        check_vma=False,
    )
```

```python
import functools
import math

import jax
import jax.numpy as jnp
import numpy as np
from jax import lax
from jax.experimental import pallas as pl
from jax.experimental.pallas import tpu as pltpu
from jax.experimental.layout import Layout, with_layout_constraint
from jax.sharding import PartitionSpec as P

DS = 192
DL = 384
MS = 768
ML = 1536
HEADS = 6

norm_eps = 1e-06
clip_norm = 1.0
beta_one = 0.5
beta_two = 0.5
adam_eps = 1e-08
rate = 0.05
decay = 0.05
bias_one = 1.0 - 0.5**5
bias_two = 1.0 - 0.5**5

f32 = jnp.float32
bf16 = jnp.bfloat16
LANES = 128


def layout():
    shapes = []
    for label, width, hidden in (("s", DS, MS), ("l", DL, ML)):
        shapes += [
            (label + "_ln1", (2, width)),
            (label + "_qkv_w", (width, 3 * width)),
            (label + "_qkv_b", (3 * width,)),
            (label + "_proj_w", (width, width)),
            (label + "_proj_b", (width,)),
            (label + "_ln2", (2, width)),
            (label + "_fc1_w", (width, hidden)),
            (label + "_fc1_b", (hidden,)),
            (label + "_fc2_w", (hidden, width)),
            (label + "_fc2_b", (width,)),
        ]
    for label, owner, other in (("s", DS, DL), ("l", DL, DS)):
        shapes += [
            (label + "_to_ln", (2, owner)),
            (label + "_to_w", (owner, other)),
            (label + "_to_b", (other,)),
            (label + "_ca_ln", (2, other)),
            (label + "_ca_q_w", (other, other)),
            (label + "_ca_q_b", (other,)),
            (label + "_ca_k_w", (other, other)),
            (label + "_ca_v_w", (other, other)),
            (label + "_ca_v_b", (other,)),
            (label + "_ca_o_w", (other, other)),
            (label + "_ca_o_b", (other,)),
            (label + "_back_ln", (2, other)),
            (label + "_back_w", (other, owner)),
            (label + "_back_b", (owner,)),
        ]
    return shapes


def round_up(value, unit):
    return -(-value // unit) * unit


def grid_plan(shards):
    names = []
    regions = []
    offset = 0
    for label, shape in layout():
        count = math.prod(shape)
        phase = offset % LANES
        if not regions or regions[-1][2] != phase:
            regions.append([offset, offset, phase])
        names.append((label, shape, offset, len(regions) - 1))
        offset += count
        regions[-1][1] = offset
    total = offset
    starts = []
    row = 0
    for first, last, phase in regions:
        starts.append(row)
        row += -(-(last - first) // LANES)
    rows = row
    places = {}
    for label, shape, place, region in names:
        places[label] = (starts[region] + (place - regions[region][0]) // LANES, shape)
    size = total // shards
    bases = []
    pieces = []
    for device in range(shards):
        low, high = device * size, (device + 1) * size
        own = []
        base = None
        for (first, last, phase), start in zip(regions, starts):
            left, right = max(low, first), min(high, last)
            if left >= right:
                continue
            if base is None:
                base = (start + (left - first) // LANES) // 16 * 16
            delta = start * LANES - first + low - base * LANES
            own.append((left - low, right - low, delta))
        bases.append(base)
        pieces.append(own)
    most = max(len(own) for own in pieces)
    table = np.zeros((shards, most * 3), np.int32)
    need = 0
    for device, own in enumerate(pieces):
        for number, (left, right, delta) in enumerate(own):
            table[device, 3 * number : 3 * number + 3] = (left, right, delta)
            need = max(need, right + delta)
    span = round_up(-(-need // LANES), 32)
    overlap = 16
    for device in range(1, shards):
        overlap = max(overlap, bases[device - 1] + span - bases[device])
    half = shards // 2
    edge = half * size
    sides = [[], []]
    for label, shape, place, region in names:
        if place < edge:
            sides[0].append((label, shape))
        if place + math.prod(shape) > edge:
            sides[1].append((label, shape))
    origins = [0, min(bases[half], places[sides[1][0][0]][0]) // 16 * 16]
    heights = []
    for side in range(2):
        last = bases[half * (side + 1) - 1] + span
        for label, shape in sides[side]:
            last = max(last, places[label][0] + -(-math.prod(shape) // LANES))
        heights.append(round_up(last - origins[side] + overlap, 16))
    groups = []
    for first, last in ((0, half // 2), (half // 2, half), (half, shards)):
        held = [
            (label, shape)
            for label, shape, place, region in names
            if place < last * size and place + math.prod(shape) > first * size
        ]
        origin = min([bases[first]] + [places[label][0] for label, shape in held]) // 16 * 16
        stop = max(
            [bases[last - 1] + span]
            + [places[label][0] + -(-math.prod(shape) // LANES) for label, shape in held]
        )
        groups.append((first, last - first, held, origin, round_up(stop - origin + overlap, 16)))
    return dict(
        places=places,
        groups=groups,
        rows=rows,
        half=half,
        sides=sides,
        origins=origins,
        heights=heights,
        size=size,
        bases=bases,
        table=table,
        most=most,
        span=span,
        overlap=overlap,
        shard_rows=round_up(-(-size // LANES), 16),
    )


def mm(left, right):
    return lax.dot_general(left, right, (((1,), (0,)), ((), ())), preferred_element_type=f32)


def mm_t(left, right):
    return lax.dot_general(left, right, (((1,), (1,)), ((), ())), preferred_element_type=f32)


def t_mm(left, right):
    return lax.dot_general(left, right, (((0,), (0,)), ((), ())), preferred_element_type=f32)


def vmem_spec(shape, index):
    return pl.BlockSpec(shape, index)


def whole(shape):
    rank = len(shape)
    return pl.BlockSpec(shape, lambda *_: (0,) * rank, pipeline_mode=pl.Buffered(1))


def estimate(flops, moved):
    return pl.CostEstimate(flops=int(flops), bytes_accessed=int(moved), transcendentals=0)


def shift_rows(ref, amount, rows, margin):
    down = amount // LANES
    across = amount - down * LANES
    here = ref[pl.ds(margin - down, rows), :]
    above = ref[pl.ds(margin - down - 1, rows), :]
    here = pltpu.roll(here, across, 1)
    above = pltpu.roll(above, across, 1)
    lane = lax.broadcasted_iota(jnp.int32, here.shape, 1)
    return jnp.where(lane < across, above, here)


def align_kernel(most, rows, span, margin, core_ref, table_ref, shard_ref, keep_ref, send_ref, padded):
    padded[...] = jnp.zeros_like(padded)
    padded[margin : margin + rows, :] = shard_ref[...]
    place = lax.broadcasted_iota(jnp.int32, (span, LANES), 0) * LANES
    place = place + lax.broadcasted_iota(jnp.int32, (span, LANES), 1)
    total = jnp.zeros((span, LANES), f32)
    for number in range(most):
        left = table_ref[3 * number]
        right = table_ref[3 * number + 1]
        delta = table_ref[3 * number + 2]
        moved = shift_rows(padded, delta, span, margin)
        total = jnp.where((place >= left + delta) & (place < right + delta), moved, total)
    total = total.astype(bf16)
    first = core_ref[0] == 0
    upper, lower = total[: span // 2], total[span // 2 :]
    keep_ref[...] = jnp.where(first, upper, lower)
    send_ref[...] = jnp.where(first, lower, upper)


def unalign_kernel(
    most, rows, span, margin, core_ref, table_ref, own_ref, got_ref, out_ref, padded
):
    first = core_ref[0] == 0
    padded[span:, :] = jnp.zeros((padded.shape[0] - span, LANES), f32)
    padded[0 : span // 2, :] = jnp.where(first, own_ref[...], got_ref[...])
    padded[span // 2 : span, :] = jnp.where(first, got_ref[...], own_ref[...])
    place = lax.broadcasted_iota(jnp.int32, (rows, LANES), 0) * LANES
    place = place + lax.broadcasted_iota(jnp.int32, (rows, LANES), 1)
    total = jnp.zeros((rows, LANES), f32)
    lane = lax.broadcasted_iota(jnp.int32, (rows, LANES), 1)
    for number in range(most):
        left = table_ref[3 * number]
        right = table_ref[3 * number + 1]
        delta = table_ref[3 * number + 2]
        down = delta // LANES
        across = delta - down * LANES
        back = lax.rem(LANES - across, LANES)
        here = pltpu.roll(padded[pl.ds(down, rows), :], back, 1)
        below = pltpu.roll(padded[pl.ds(down + 1, rows), :], back, 1)
        moved = jnp.where(lane < LANES - across, here, below)
        total = jnp.where((place >= left) & (place < right), moved, total)
    out_ref[...] = total


def settle_kernel(most, where_ref, table_ref, keep_ref, last_ref, *refs):
    *far_refs, own_ref, send_ref, norm_ref = refs
    core = where_ref[0]
    near = keep_ref[...] + last_ref[...].astype(f32)
    far = far_refs[0][0].astype(f32)
    for ref in far_refs[1:]:
        far = far + ref[0].astype(f32)
    rows = near.shape[0]
    place = (lax.broadcasted_iota(jnp.int32, near.shape, 0) + core * rows) * LANES
    place = place + lax.broadcasted_iota(jnp.int32, near.shape, 1)

    def squares(total, entry):
        found = jnp.zeros_like(total)
        for number in range(most):
            at = 3 * (entry * most + number)
            left, right, delta = table_ref[at], table_ref[at + 1], table_ref[at + 2]
            inside = (place >= left + delta) & (place < right + delta)
            found = jnp.where(inside, total * total, found)
        return found

    both = squares(near, 0) + squares(far, 1)
    norm_ref[...] = jnp.broadcast_to(jnp.sum(both).reshape(1, 1), (8, LANES))
    own_ref[...] = jnp.where(core == 0, near, far)
    send_ref[...] = jnp.where(core == 0, far, near)


def settle(where, tables, keep, last, far_parts, plan):
    smem = pl.BlockSpec(memory_space=pltpu.SMEM)
    part = jax.ShapeDtypeStruct(keep.shape, f32)
    return pl.pallas_call(
        functools.partial(settle_kernel, plan["most"]),
        grid=(1,),
        out_shape=(part, part, jax.ShapeDtypeStruct((8, LANES), f32)),
        in_specs=[smem, smem, fixed_spec(keep.shape), fixed_spec(keep.shape)]
        + [pl.BlockSpec((1, *keep.shape), lambda i: (0, 0, 0))] * len(far_parts),
        out_specs=(fixed_spec(keep.shape), fixed_spec(keep.shape), fixed_spec((8, LANES))),
        cost_estimate=estimate(1_000_000, 2_000_000),
        name="settle",
    )(where, tables, keep, last, *far_parts)


def align(core, table, shard, plan):
    rows, span, most = plan["shard_rows"], plan["span"], plan["most"]
    margin = 8 + round_up(int(plan["table"].max(initial=0, where=pick_delta(plan))) // LANES + 1, 8)
    tall = margin + max(rows, span) + 8
    vmem = pl.BlockSpec(memory_space=pltpu.VMEM)
    smem = pl.BlockSpec(memory_space=pltpu.SMEM)
    part = jax.ShapeDtypeStruct((span // 2, LANES), bf16)
    return pl.pallas_call(
        functools.partial(align_kernel, most, rows, span, margin),
        out_shape=(part, part),
        in_specs=[smem, smem, vmem],
        out_specs=(vmem, vmem),
        scratch_shapes=[pltpu.VMEM((tall, LANES), f32)],
        cost_estimate=estimate(1_000_000, 1_000_000),
        name="align",
    )(core, table, shard)


def unalign(core, table, own, got, plan):
    rows, span, most = plan["shard_rows"], plan["span"], plan["most"]
    margin = 16 + round_up(int(plan["table"].max(initial=0, where=pick_delta(plan))) // LANES + 1, 8)
    tall = max(rows, span) + margin
    vmem = pl.BlockSpec(memory_space=pltpu.VMEM)
    smem = pl.BlockSpec(memory_space=pltpu.SMEM)
    return pl.pallas_call(
        functools.partial(unalign_kernel, most, rows, span, margin),
        out_shape=jax.ShapeDtypeStruct((rows, LANES), f32),
        in_specs=[smem, smem, vmem, vmem],
        out_specs=vmem,
        scratch_shapes=[pltpu.VMEM((tall, LANES), f32)],
        cost_estimate=estimate(1_000_000, 1_000_000),
        name="unalign",
    )(core, table, own, got)


def pick_delta(plan):
    mask = np.zeros(plan["table"].shape, bool)
    mask[:, 2::3] = True
    return mask


def two_dim(shape):
    return shape if len(shape) == 2 else (1, shape[0])


def is_matrix(label):
    return label[-2:] == "_w"


def strided(start, count, step):
    return pl.ds(start, count) if step == 1 or count == 1 else pl.ds(start, count, stride=step)


def half_swap(value):
    return pltpu.roll(value, LANES // 2, 1)


def read_param(flat, row, shape, out_ref, pair_ref):
    depth, width = two_dim(shape)
    dtype = out_ref.dtype
    if width % LANES == 0:
        step = width // LANES
        for col in range(step):
            out_ref[:, col * LANES : (col + 1) * LANES] = flat[
                strided(row + col, depth, step), :
            ].astype(dtype)
        return
    half = LANES // 2
    lead = width // LANES
    if depth == 1:
        for col in range(lead):
            out_ref[:, col * LANES : (col + 1) * LANES] = flat[row + col : row + col + 1, :].astype(
                dtype
            )
        out_ref[:, lead * LANES :] = flat[row + lead : row + lead + 1, 0:half].astype(dtype)
        return
    step = 2 * width // LANES
    pairs = depth // 2
    lane = lax.broadcasted_iota(jnp.int32, (pairs, LANES), 1)
    blocks = [flat[strided(row + col, pairs, step), :] for col in range(step)]
    turned = [half_swap(block) for block in blocks[lead:]]
    for col in range(lead):
        pair_ref[col, strided(0, pairs, 2), :] = blocks[col]
        pair_ref[col, strided(1, pairs, 2), :] = jnp.where(lane < half, turned[col], turned[col + 1])
    pair_ref[lead, strided(0, pairs, 2), :] = blocks[lead]
    pair_ref[lead, strided(1, pairs, 2), :] = turned[lead]
    for col in range(lead):
        out_ref[:, col * LANES : (col + 1) * LANES] = pair_ref[col, 0:depth, :].astype(dtype)
    out_ref[:, lead * LANES :] = pair_ref[lead, 0:depth, 0:half].astype(dtype)


def write_param(flat, row, shape, in_ref, pair_ref, window):
    depth, width = two_dim(shape)
    if width % LANES == 0:
        step = width // LANES
        first = max(0, (window[0] - row) // step) // 8 * 8
        last = min(depth, round_up(max(0, -(-(window[1] - row) // step)), 8))
        for col in range(step):
            flat[strided(row + first * step + col, last - first, step), :] = in_ref[
                first:last, col * LANES : (col + 1) * LANES
            ]
        return
    half = LANES // 2
    lead = width // LANES
    if depth == 1:
        for col in range(lead):
            flat[row + col : row + col + 1, :] = in_ref[:, col * LANES : (col + 1) * LANES]
        tail = jnp.concatenate([in_ref[:, lead * LANES :], jnp.zeros((1, half), f32)], 1)
        flat[row + lead : row + lead + 1, :] = tail
        return
    step = 2 * width // LANES
    pairs = depth // 2
    lane = lax.broadcasted_iota(jnp.int32, (pairs, LANES), 1)
    for col in range(lead):
        pair_ref[col, 0:depth, :] = in_ref[:, col * LANES : (col + 1) * LANES]
    pair_ref[lead, 0:depth, 0:half] = in_ref[:, lead * LANES :]
    even = [pair_ref[col, strided(0, pairs, 2), :] for col in range(lead + 1)]
    odd = [half_swap(pair_ref[col, strided(1, pairs, 2), :]) for col in range(lead + 1)]
    for col in range(lead):
        flat[strided(row + col, pairs, step), :] = even[col]
    flat[strided(row + lead, pairs, step), :] = jnp.where(lane < half, even[lead], odd[0])
    for col in range(lead):
        flat[strided(row + lead + 1 + col, pairs, step), :] = jnp.where(
            lane < half, odd[col], odd[col + 1]
        )


def decode(number, core, bits):
    first = (number >> (bits - 1)) & 1
    second = (number >> (bits - 2)) & 1
    found = (first << core) | (second << (1 - core))
    for place in range(2, bits):
        found = found | (((number >> (bits - 1 - place)) & 1) << place)
    return found


def unflatten_kernel(plan, side, bits, where_ref, base_ref, *refs):
    pieces, refs = refs[:4], refs[4:]
    carried, refs = (refs[:1], refs[1:]) if side else ((), refs)
    outs, (flat, pair_ref) = refs[:-2], refs[-2:]
    span, overlap, half = plan["span"], plan["overlap"], plan["half"]
    origin = plan["origins"][side]
    core, mine = where_ref[0], where_ref[1]
    lead = plan["bases"][side * half] - origin
    if lead:
        flat[0:lead, :] = jnp.zeros((lead, LANES), f32)
    last = plan["bases"][side * half + half - 1] - origin + span
    if flat.shape[0] > last:
        flat[last:, :] = jnp.zeros((flat.shape[0] - last, LANES), f32)

    def base_of(owner):
        return pl.multiple_of(base_ref[side * half + owner] - origin, 16)

    def clear(owner, carry):
        base = base_of(owner)
        flat[pl.ds(base, overlap), :] = jnp.zeros((overlap, LANES), f32)
        flat[pl.ds(base + span - overlap, overlap), :] = jnp.zeros((overlap, LANES), f32)
        return carry

    lax.fori_loop(0, half, clear, 0)
    middle = span // 2
    for number, piece in enumerate(pieces):
        theirs = number // 2
        owner_core = core if theirs == 0 else 1 - core
        upper = number % 2 * (half // 2)
        for part in range(2):

            @pl.when(owner_core == part)
            def _(part=part, piece=piece, upper=upper):
                def place(entry, carry):
                    base = base_of(decode(entry + upper, part, bits) ^ mine)
                    value = piece[entry].astype(f32)
                    if part == 0:
                        flat[pl.ds(base, overlap), :] += value[:overlap]
                        flat[pl.ds(base + overlap, middle - overlap), :] = value[overlap:]
                    else:
                        flat[pl.ds(base + middle, middle - overlap), :] = value[: middle - overlap]
                        flat[pl.ds(base + span - overlap, overlap), :] += value[middle - overlap :]
                    return carry

                lax.fori_loop(0, half // 2, place, 0)

    for number, ((label, shape), out_ref) in enumerate(zip(plan["sides"][side], outs)):
        read_param(flat, plan["places"][label][0] - origin, shape, out_ref, pair_ref)
        if side and number == 0:
            out_ref[...] += carried[0][...]


def unflatten(where, pieces, plan, side, bits, carried=()):
    outs = []
    for label, shape in plan["sides"][side]:
        outs.append(jax.ShapeDtypeStruct(two_dim(shape), bf16 if is_matrix(label) else f32))
    vmem = pl.BlockSpec(memory_space=pltpu.VMEM)
    smem = pl.BlockSpec(memory_space=pltpu.SMEM)
    values = pl.pallas_call(
        functools.partial(unflatten_kernel, plan, side, bits),
        out_shape=outs,
        in_specs=[smem, smem] + [vmem] * (len(pieces) + len(carried)),
        out_specs=[vmem] * len(outs),
        scratch_shapes=[
            pltpu.VMEM((plan["heights"][side], LANES), f32),
            pltpu.VMEM((5, MS, LANES), f32),
        ],
        cost_estimate=estimate(1_000_000, 8_000_000),
        name="unflatten" + str(side),
    )(where, jnp.asarray(plan["bases"], jnp.int32), *pieces, *carried)
    return {label: value for (label, shape), value in zip(plan["sides"][side], values)}


def flatten_kernel(plan, group, bits, where_ref, base_ref, *refs):
    begin, owners, held, origin, height = plan["groups"][group]
    count = len(held)
    grads, (low_ref, high_ref, send_ref, flat, pair_ref) = refs[:count], refs[count:]
    span = plan["span"]
    core, mine = where_ref[0], where_ref[1]
    first, last = None, 0
    for label, shape in held:
        row = plan["places"][label][0] - origin
        first = row if first is None else first
        last = row + -(-math.prod(shape) // LANES)
    if first:
        flat[0:first, :] = jnp.zeros((first, LANES), f32)
    flat[last // 8 * 8 :, :] = jnp.zeros((height - last // 8 * 8, LANES), f32)
    window = (plan["bases"][begin] - origin, plan["bases"][begin + owners - 1] + span - origin)
    for (label, shape), ref in zip(held, grads):
        write_param(flat, plan["places"][label][0] - origin, shape, ref, pair_ref, window)

    def rows_of(entry, part):
        owner = (decode(entry, part, bits) ^ mine) & (owners - 1)
        base = base_ref[begin + owner] - origin + part * (span // 2)
        return flat[pl.ds(pl.multiple_of(base, 16), span // 2), :].astype(bf16)

    def place(entry, carry):
        low_ref[entry] = rows_of(entry, core)
        high_ref[entry] = rows_of(entry + owners // 2, core)
        send_ref[entry] = rows_of(entry, 1 - core)
        send_ref[entry + owners // 2] = rows_of(entry + owners // 2, 1 - core)
        return carry

    lax.fori_loop(0, owners // 2, place, 0)


def flatten(where, grads, plan, group):
    vmem = pl.BlockSpec(memory_space=pltpu.VMEM)
    smem = pl.BlockSpec(memory_space=pltpu.SMEM)
    begin, owners, held, origin, height = plan["groups"][group]
    rows = plan["span"] // 2
    values = [grads[label] for label, shape in held]
    return pl.pallas_call(
        functools.partial(flatten_kernel, plan, group, owners.bit_length() - 1),
        out_shape=(
            jax.ShapeDtypeStruct((owners // 2, rows, LANES), bf16),
            jax.ShapeDtypeStruct((owners // 2, rows, LANES), bf16),
            jax.ShapeDtypeStruct((owners, rows, LANES), bf16),
        ),
        in_specs=[smem, smem] + [vmem] * len(values),
        out_specs=(vmem, vmem, vmem),
        scratch_shapes=[
            pltpu.VMEM((height, LANES), f32),
            pltpu.VMEM((5, MS, LANES), f32),
        ],
        cost_estimate=estimate(1_000_000, 10_000_000),
        name="flatten" + str(group),
    )(where, jnp.asarray(plan["bases"], jnp.int32), *values)


def ln_parts(value):
    mean = jnp.mean(value, -1, keepdims=True)
    centred = value - mean
    variance = jnp.mean(centred * centred, -1, keepdims=True)
    inverse = lax.rsqrt(variance + norm_eps)
    return centred * inverse, inverse


def ln_back(grad, hat, inverse, gain):
    scaled = grad * gain
    first = jnp.mean(scaled, -1, keepdims=True)
    second = jnp.mean(scaled * hat, -1, keepdims=True)
    return inverse * (scaled - first - hat * second)


def gelu_parts(value):
    cdf = 0.5 + 0.5 * lax.erf(value * (2.0**-0.5))
    density = jnp.exp(value * value * -0.5) * (1.0 / math.sqrt(2.0 * math.pi))
    return value * cdf, cdf + value * density


def col_sum(value):
    return jnp.sum(value, 0, keepdims=True)


def groups(width):
    size = width // HEADS
    found = []
    for start in range(0, width, LANES):
        stop = min(start + LANES, width)
        found.append((start, stop, (stop - start) // size))
    return found, size


def stack_heads(value, count, size):
    lane = lax.broadcasted_iota(jnp.int32, value.shape, 1)
    zero = jnp.zeros_like(value)
    return jnp.concatenate(
        [
            jnp.where((lane >= head * size) & (lane < (head + 1) * size), value, zero)
            for head in range(count)
        ],
        0,
    )


def merge_heads(value, count, size):
    rows = value.shape[0] // count
    lane = lax.broadcasted_iota(jnp.int32, (rows, value.shape[1]), 1)
    merged = value[0:rows]
    for head in range(1, count):
        merged = jnp.where(lane >= head * size, value[head * rows : (head + 1) * rows], merged)
    return merged


def attention_forward(pair, length, tall, tokens, weights, keeps):
    ln1_ref, qkv_w, qkv_b, proj_w, proj_b, ln2_ref = weights
    a1_ref, qkv_ref, probs_ref, att_ref, mid_ref, n2_ref = keeps
    width = tokens.shape[-1]
    found, size = groups(width)
    scale = size ** (-0.5)
    hat, _ = ln_parts(tokens)
    a1 = (hat * ln1_ref[0:1, :] + ln1_ref[1:2, :]).astype(bf16)
    a1_ref[...] = a1
    qkv_ref[...] = (mm(a1, qkv_w[...]) + qkv_b[...]).astype(bf16)
    key_lane = lax.broadcasted_iota(jnp.int32, (1, tall), 1)
    bias = jnp.where(key_lane < length, 0.0, -1e30).astype(f32)
    for crop in range(pair):
        here = slice(crop * tall, (crop + 1) * tall)
        for start, stop, count in found:
            query = stack_heads(qkv_ref[here, start:stop], count, size)
            key = qkv_ref[here, width + start : width + stop]
            value = qkv_ref[here, 2 * width + start : 2 * width + stop]
            scores = mm_t(query, key) * scale + bias
            summit = jnp.max(scores, -1, keepdims=True)
            weights = jnp.exp(scores - summit)
            probs = (weights / jnp.sum(weights, -1, keepdims=True)).astype(bf16)
            first = start // size
            for head in range(count):
                probs_ref[crop, first + head] = probs[head * tall : (head + 1) * tall]
            att_ref[here, start:stop] = merge_heads(mm(probs, value), count, size).astype(bf16)
    mid = tokens + mm(att_ref[...], proj_w[...]) + proj_b[...]
    mid_ref[...] = mid
    hat, _ = ln_parts(mid)
    n2_ref[...] = (hat * ln2_ref[0:1, :] + ln2_ref[1:2, :]).astype(bf16)


def mlp_forward(chunk, mid_ref, n2_ref, weights, keeps):
    fc1_w, fc1_b, fc2_w, fc2_b = weights
    z_ref, slope_ref, y_ref = keeps
    y_ref[...] = mid_ref[...] + fc2_b[...]
    for number in range(fc1_w.shape[1] // chunk):
        cols = slice(number * chunk, (number + 1) * chunk)
        inner = mm(n2_ref[...], fc1_w[:, cols]) + fc1_b[:, cols]
        active, slope = gelu_parts(inner)
        z_ref[:, cols] = active.astype(bf16)
        slope_ref[:, cols] = slope.astype(bf16)
        y_ref[...] += mm(z_ref[:, cols], fc2_w[cols, :])


def keep_heads(pair, tall, y_ref, head_ref):
    for crop in range(pair):
        slot = pl.program_id(0) * pair + crop
        head_ref[pl.ds(slot, 1), :] = y_ref[crop * tall : crop * tall + 1, :]


def carry(value, norm, weight, bias):
    hat, _ = ln_parts(value)
    active, _ = gelu_parts(hat * norm[0:1, :] + norm[1:2, :])
    return (mm(active.astype(bf16), weight[...]) + bias[...]).astype(bf16)


def attention_kernel(pair, length, tall, tok_ref, *refs):
    tokens = tok_ref[...].reshape(pair * tall, tok_ref.shape[-1]).astype(f32)
    attention_forward(pair, length, tall, tokens, refs[:6], refs[6:])


def block_kernel(pair, length, tall, chunk, tok_ref, *refs):
    tokens = tok_ref[...].reshape(pair * tall, tok_ref.shape[-1]).astype(f32)
    attention_forward(pair, length, tall, tokens, refs[:6], refs[10:16])
    mlp_forward(chunk, refs[14], refs[15], refs[6:10], refs[16:19])
    keep_heads(pair, tall, refs[18], refs[19])


def mlp_kernel(pair, tall, chunk, mid_ref, n2_ref, *refs):
    weights, heads, (far_head, *far), near = refs[:4], None, refs[4:8], refs[8:11]
    z_ref, slope_ref, y_ref, head_ref, near_ref, far_ref = refs[11:]
    mlp_forward(chunk, mid_ref, n2_ref, weights, (z_ref, slope_ref, y_ref))
    keep_heads(pair, tall, y_ref, head_ref)

    @pl.when(pl.program_id(0) == pl.num_programs(0) - 1)
    def _():
        near_ref[...] = carry(head_ref[...], *near)
        far_ref[...] = carry(far_head[...], *far)


ATTENTION = ("ln1", "qkv_w", "qkv_b", "proj_w", "proj_b", "ln2")
MLP = ("fc1_w", "fc1_b", "fc2_w", "fc2_b")
TO = ("to_ln", "to_w", "to_b")


def pick(params, label, names):
    return [params[label + "_" + name] for name in names]


def row_spec(rows, cols):
    return pl.BlockSpec((rows, cols), lambda i: (i, 0))


def fixed_spec(shape):
    rank = len(shape)
    return pl.BlockSpec(shape, lambda i: (0,) * rank)


def kept_outs(crops, tall, width, hidden, pair):
    rows, flat = pair * tall, crops * tall

    def entry(cols, dtype):
        return row_spec(rows, cols), jax.ShapeDtypeStruct((flat, cols), dtype)

    attention = [
        entry(width, bf16),
        entry(3 * width, bf16),
        (
            pl.BlockSpec((pair, HEADS, tall, tall), lambda i: (i, 0, 0, 0)),
            jax.ShapeDtypeStruct((crops, HEADS, tall, tall), bf16),
        ),
        entry(width, bf16),
        entry(width, f32),
        entry(width, bf16),
    ]
    mlp = [
        entry(hidden, bf16),
        entry(hidden, bf16),
        entry(width, f32),
        (fixed_spec((crops, width)), jax.ShapeDtypeStruct((crops, width), f32)),
    ]
    return attention, mlp


def block_forward(tokens, params, label, length, pair):
    crops, tall, width = tokens.shape
    hidden = params[label + "_fc1_w"].shape[1]
    weights = pick(params, label, ATTENTION + MLP)
    attention, mlp = kept_outs(crops, tall, width, hidden, pair)
    outs = attention + mlp
    flops = 2 * crops * tall * (4 * width * width + 2 * width * hidden)
    return pl.pallas_call(
        functools.partial(block_kernel, pair, length, tall, 768),
        grid=(crops // pair,),
        out_shape=[shape for spec, shape in outs],
        in_specs=[pl.BlockSpec((pair, tall, width), lambda i: (i, 0, 0))]
        + [whole(value.shape) for value in weights],
        out_specs=[spec for spec, shape in outs],
        cost_estimate=estimate(8 * flops, 10_000_000),
        name="block_" + label,
    )(tokens, *weights)


def attention_only(tokens, params, label, length, pair):
    crops, tall, width = tokens.shape
    weights = pick(params, label, ATTENTION)
    outs, _ = kept_outs(crops, tall, width, width, pair)
    flops = 2 * crops * tall * 4 * width * width
    return pl.pallas_call(
        functools.partial(attention_kernel, pair, length, tall),
        grid=(crops // pair,),
        out_shape=[shape for spec, shape in outs],
        in_specs=[pl.BlockSpec((pair, tall, width), lambda i: (i, 0, 0))]
        + [whole(value.shape) for value in weights],
        out_specs=[spec for spec, shape in outs],
        cost_estimate=estimate(8 * flops, 20_000_000),
        name="attention_" + label,
    )(tokens, *weights)


def mlp_only(mid, n2, far_head, params, label, far, crops, pair):
    flat, width = mid.shape
    tall = flat // crops
    rows = pair * tall
    hidden = params[label + "_fc1_w"].shape[1]
    weights = pick(params, label, MLP)
    extra = [far_head] + pick(params, far, TO) + pick(params, label, TO)
    _, outs = kept_outs(crops, tall, width, hidden, pair)
    for name in (label, far):
        shape = (crops, params[name + "_to_w"].shape[1])
        outs.append((fixed_spec(shape), jax.ShapeDtypeStruct(shape, bf16)))
    flops = 2 * flat * 2 * width * hidden
    return pl.pallas_call(
        functools.partial(mlp_kernel, pair, tall, 768),
        grid=(crops // pair,),
        out_shape=[shape for spec, shape in outs],
        in_specs=[row_spec(rows, width), row_spec(rows, width)]
        + [whole(value.shape) for value in weights + extra],
        out_specs=[spec for spec, shape in outs],
        cost_estimate=estimate(8 * flops, 20_000_000),
        name="mlp_" + label,
    )(mid, n2, *weights, *extra)


def cross_kernel(
    length,
    tall,
    crops,
    sent_ref,
    y_ref,
    gret_ref,
    ca_ln,
    q_w,
    q_b,
    k_w,
    v_w,
    v_b,
    o_w,
    o_b,
    back_ln,
    back_w,
    back_b,
    returned_ref,
    gsent_ref,
    gj_ref,
    d_ca_ln,
    d_q_w,
    d_q_b,
    d_k_w,
    d_v_w,
    d_v_b,
    d_o_w,
    d_o_b,
    d_back_ln,
    d_back_w,
    d_back_b,
    sent_f,
    n_all,
    score_all,
    mates_all,
    pairs_all,
    gn_head,
    gj_head,
):
    width = y_ref.shape[1]
    size = width // HEADS
    scale = size ** (-0.5)
    stacked = crops * 8
    lane = lax.broadcasted_iota(jnp.int32, (8, width), 1)
    head = lax.broadcasted_iota(jnp.int32, (8, width), 0)
    own_head = (lane >= head * size) & (lane < (head + 1) * size)
    row = lax.broadcasted_iota(jnp.int32, (tall, 1), 0)
    key_lane = lax.broadcasted_iota(jnp.int32, (1, tall), 1)
    bias = jnp.where(key_lane < length, 0.0, -1e30).astype(f32)
    gain, shift = ca_ln[0:1, :], ca_ln[1:2, :]
    sent_f[...] = sent_ref[...].astype(f32)
    hat, _ = ln_parts(sent_f[...])
    n_head = (hat * gain + shift).astype(bf16)

    def spread(value):
        return jnp.concatenate(
            [jnp.where(own_head, value[crop : crop + 1], 0.0) for crop in range(crops)], 0
        )

    def gathered(value):
        return jnp.concatenate(
            [
                col_sum(jnp.where(own_head, value[crop * 8 : crop * 8 + 8], 0.0))
                for crop in range(crops)
            ],
            0,
        )

    def normed_of(crop):
        return n_all[crop * tall : (crop + 1) * tall, :]

    def against(value):
        return jnp.concatenate(
            [
                mm_t(value[crop * 8 : crop * 8 + 8].astype(bf16), normed_of(crop))
                for crop in range(crops)
            ],
            0,
        )

    def mixed(value):
        return jnp.concatenate(
            [
                mm(value[crop * 8 : crop * 8 + 8].astype(bf16), normed_of(crop))
                for crop in range(crops)
            ],
            0,
        )

    query = spread((mm(n_head, q_w[...]) + q_b[...]).astype(bf16).astype(f32)).astype(bf16)
    keyed = mm_t(query, k_w[...]) * scale
    blank = jnp.zeros((8, width), f32)
    for crop in range(crops):
        mates_all[crop] = jnp.concatenate([keyed[crop * 8 : crop * 8 + 8], blank], 0).astype(bf16)

    def joined(crop):
        here = pl.ds(pl.multiple_of(crop * tall, 16), tall)
        return here, jnp.where(row == 0, sent_f[pl.ds(crop, 1), :], y_ref[here, :])

    def ahead(crop, carry):
        here, value = joined(crop)
        hat, _ = ln_parts(value)
        normed = (hat * gain + shift).astype(bf16)
        n_all[here, :] = normed
        score_all[pl.ds(crop, 1)] = mm_t(mates_all[crop], normed)[None, 0:8]
        return carry

    lax.fori_loop(0, crops, ahead, 0)
    scores = score_all[...].reshape(stacked, tall) + bias
    summit = jnp.max(scores, -1, keepdims=True)
    weights = jnp.exp(scores - summit)
    probs = weights / jnp.sum(weights, -1, keepdims=True)
    rounded = probs.astype(bf16).astype(f32)
    total = jnp.sum(rounded, -1, keepdims=True)
    mean_n = mixed(rounded).astype(bf16)
    attended = gathered(mm(mean_n, v_w[...]) + total * v_b[...]).astype(bf16)
    merged = sent_f[...] + mm(attended, o_w[...]) + o_b[...]
    hat, inverse = ln_parts(merged)
    active, slope = gelu_parts(hat * back_ln[0:1, :] + back_ln[1:2, :])
    active = active.astype(bf16)
    returned_ref[...] = (mm(active, back_w[...]) + back_b[...]).astype(bf16)
    gret = gret_ref[...]
    d_back_w[...] = t_mm(active, gret)
    d_back_b[...] = col_sum(gret.astype(f32))
    gact = mm_t(gret, back_w[...]) * slope
    d_back_ln[0:1, :] = col_sum(gact * hat)
    d_back_ln[1:2, :] = col_sum(gact)
    gfused = ln_back(gact, hat, inverse, back_ln[0:1, :])
    gfo = gfused.astype(bf16)
    d_o_w[...] = t_mm(attended, gfo)
    d_o_b[...] = col_sum(gfo.astype(f32))
    gatt = spread(mm_t(gfo, o_w[...]).astype(bf16).astype(f32))
    d_v_b[...] = col_sum(total * gatt)
    gbias = jnp.sum(gatt * v_b[...], -1, keepdims=True)
    gatt = gatt.astype(bf16)
    d_v_w[...] = t_mm(mean_n, gatt)
    valued = mm_t(gatt, v_w[...])
    gprobs = against(valued) + gbias
    inner = gprobs - jnp.sum(gprobs * probs, -1, keepdims=True)
    gscores = (probs * inner).astype(bf16).astype(f32)
    for crop in range(crops):
        part = slice(crop * 8, crop * 8 + 8)
        mates_all[crop] = jnp.concatenate([keyed[part], valued[part]], 0).astype(bf16)
        pairs_all[crop] = jnp.concatenate([gscores[part], rounded[part]], 0).astype(bf16)
    slid = (mixed(gscores) * scale).astype(bf16)
    d_k_w[...] = t_mm(slid, query)
    gq = gathered(mm(slid, k_w[...])).astype(bf16)
    d_q_w[...] = t_mm(n_head, gq)
    d_q_b[...] = col_sum(gq.astype(f32))
    gn_head[...] = mm_t(gq, q_w[...])
    d_ca_ln[...] = jnp.zeros_like(d_ca_ln)

    def finish(crop, carry):
        here, value = joined(crop)
        hat, inverse = ln_parts(value)
        gn = t_mm(pairs_all[crop], mates_all[crop])
        gn = gn + jnp.where(row == 0, gn_head[pl.ds(crop, 1), :], 0.0)
        d_ca_ln[0:1, :] += col_sum(gn * hat)
        d_ca_ln[1:2, :] += col_sum(gn)
        gj = ln_back(gn, hat, inverse, gain)
        gj_ref[here, :] = gj
        gj_head[pl.ds(crop, 1), :] = gj[0:1, :]
        return carry

    lax.fori_loop(0, crops, finish, 0)
    gsent_ref[...] = (gj_head[...] + gfused).astype(bf16)


def cross(sent, hosted, gret, params, label, length, tall):
    crops, width = sent.shape
    own = gret.shape[1]
    flat = crops * tall
    names = ("ca_ln", "ca_q_w", "ca_q_b", "ca_k_w", "ca_v_w", "ca_v_b", "ca_o_w", "ca_o_b")
    names = names + ("back_ln", "back_w", "back_b")
    weights = [params[label + "_" + name] for name in names]
    outs = [
        jax.ShapeDtypeStruct((crops, own), bf16),
        jax.ShapeDtypeStruct((crops, width), bf16),
        jax.ShapeDtypeStruct((flat, width), f32),
    ] + [jax.ShapeDtypeStruct(value.shape, f32) for value in weights]
    vmem = pl.BlockSpec(memory_space=pltpu.VMEM)
    small = pltpu.VMEM((crops, width), f32)
    values = pl.pallas_call(
        functools.partial(cross_kernel, length, tall, crops),
        out_shape=outs,
        in_specs=[vmem] * (3 + len(weights)),
        out_specs=[vmem] * len(outs),
        scratch_shapes=[
            small,
            pltpu.VMEM((flat, width), bf16),
            pltpu.VMEM((crops, 8, tall), f32),
            pltpu.VMEM((crops, 16, width), bf16),
            pltpu.VMEM((crops, 16, tall), bf16),
            small,
            small,
        ],
        cost_estimate=estimate(2 * flat * width * width * 2, 8_000_000),
        name="cross_" + label,
    )(sent, hosted, gret, *weights)
    grads = {label + "_" + name: value for name, value in zip(names, values[3:])}
    return values[0], values[1], values[2], grads


def head_backward(headrow_ref, gsent_ref, to_ln, to_w, d_to_ln, d_to_w, d_to_b, ghead_ref):
    hat, inverse = ln_parts(headrow_ref[...])
    active, slope = gelu_parts(hat * to_ln[0:1, :] + to_ln[1:2, :])
    gsent = gsent_ref[...]
    d_to_w[...] = t_mm(active.astype(bf16), gsent)
    d_to_b[...] = col_sum(gsent.astype(f32))
    gact = mm_t(gsent, to_w[...]) * slope
    d_to_ln[0:1, :] = col_sum(gact * hat)
    d_to_ln[1:2, :] = col_sum(gact)
    ghead_ref[...] = ln_back(gact, hat, inverse, to_ln[0:1, :])


def clear_all(refs):
    for ref in refs:
        ref[...] = jnp.zeros_like(ref)


def mlp_backward(pair, tall, chunk, live_ref, acts, weights, grads, out_ref, gy, gnormed):
    cot_ref, y_ref, gj_ref, mid_ref, n2_ref, z_ref, slope_ref, ghead, returned_ref = acts
    ln2_ref, fc1_w, fc2_w = weights
    d_ln2, d_fc1_w, d_fc1_b, d_fc2_w, d_fc2_b = grads
    length = out_ref.shape[2]
    row = lax.broadcasted_iota(jnp.int32, (tall, 1), 0)
    for crop in range(pair):
        here = slice(crop * tall, (crop + 1) * tall)
        slot = pl.program_id(0) * pair + crop
        live = jnp.where(slot < live_ref[0], 1.0, 0.0).astype(f32)
        seed = cot_ref[crop].astype(f32) * live + gj_ref[here, :]
        gy[here, :] = jnp.where(row == 0, ghead[pl.ds(slot, 1), :], seed)
        home = returned_ref[pl.ds(slot, 1), :]
        final = jnp.where(row == 0, home, y_ref[here, :])
        out_ref[0, crop] = final[0:length].astype(bf16)
    gm = gy[...].astype(bf16)
    d_fc2_b[...] += col_sum(gm.astype(f32))

    def one(number, first):
        start = number * chunk
        if not isinstance(number, int):
            start = pl.multiple_of(start, LANES)
        cols = pl.ds(start, chunk)
        d_fc2_w[cols, :] += t_mm(z_ref[:, cols], gm)
        gu = slope_ref[:, cols].astype(f32) * mm_t(gm, fc2_w[cols, :])
        gu = gu.astype(bf16)
        d_fc1_w[:, cols] += t_mm(n2_ref[...], gu)
        d_fc1_b[:, cols] += col_sum(gu.astype(f32))
        part = mm_t(gu, fc1_w[:, cols])
        gnormed[...] = part if first else gnormed[...] + part

    def looped(number, carry):
        one(number, False)
        return carry

    chunks = fc1_w.shape[1] // chunk
    if fc1_w.shape[1] > 1024:
        gnormed[...] = jnp.zeros_like(gnormed)
        lax.fori_loop(0, chunks, looped, 0)
    else:
        for number in range(chunks):
            one(number, number == 0)
    hat, inverse = ln_parts(mid_ref[...])
    gn = gnormed[...]
    d_ln2[0:1, :] += col_sum(gn * hat)
    d_ln2[1:2, :] += col_sum(gn)
    gy[...] += ln_back(gn, hat, inverse, ln2_ref[0:1, :])


def attention_backward(pair, tall, acts, weights, grads, gtok_ref, gmid_ref, gqkv, gatt_ref):
    tok_ref, a1_ref, qkv_ref, probs_ref, att_ref = acts
    ln1_ref, qkv_w, proj_w = weights
    d_ln1, d_qkv_w, d_qkv_b, d_proj_w, d_proj_b = grads
    width = tok_ref.shape[-1]
    length = gtok_ref.shape[2]
    found, size = groups(width)
    scale = size ** (-0.5)
    gp = gmid_ref[...].astype(bf16)
    d_proj_w[...] += t_mm(att_ref[...], gp)
    d_proj_b[...] += col_sum(gp.astype(f32))
    gatt_ref[...] = mm_t(gp, proj_w[...]).astype(bf16)

    def one(crop, carry):
        here = pl.ds(crop * tall, tall)
        if not isinstance(crop, int):
            here = pl.ds(pl.multiple_of(crop * tall, 16), tall)
        for start, stop, count in found:
            first = start // size
            query = stack_heads(qkv_ref[here, start:stop], count, size)
            key = qkv_ref[here, width + start : width + stop]
            value = qkv_ref[here, 2 * width + start : 2 * width + stop]
            gatt = stack_heads(gatt_ref[here, start:stop], count, size)
            probs_low = jnp.concatenate([probs_ref[crop, first + head] for head in range(count)], 0)
            probs = probs_low.astype(f32)
            gprobs = mm_t(gatt, value)
            inner = gprobs - jnp.sum(gprobs * probs, -1, keepdims=True)
            gscores = (probs * inner).astype(bf16)
            gq = merge_heads(mm(gscores, key), count, size) * scale
            gk = t_mm(gscores, query) * scale
            gv = t_mm(probs_low, gatt)
            gqkv[here, start:stop] = gq.astype(bf16)
            gqkv[here, width + start : width + stop] = gk.astype(bf16)
            gqkv[here, 2 * width + start : 2 * width + stop] = gv.astype(bf16)
        return carry

    if len(found) > 2:
        lax.fori_loop(0, pair, one, 0)
    else:
        for crop in range(pair):
            one(crop, 0)
    grad = gqkv[...]
    d_qkv_w[...] += t_mm(a1_ref[...], grad)
    d_qkv_b[...] += col_sum(grad.astype(f32))
    gn = mm_t(grad, qkv_w[...])
    hat, inverse = ln_parts(tok_ref[...].reshape(pair * tall, width).astype(f32))
    d_ln1[0:1, :] += col_sum(gn * hat)
    d_ln1[1:2, :] += col_sum(gn)
    gtok = gmid_ref[...] + ln_back(gn, hat, inverse, ln1_ref[0:1, :])
    for crop in range(pair):
        gtok_ref[0, crop] = gtok[crop * tall : crop * tall + length].astype(bf16)


GRAD_MLP = ("ln2", "fc1_w", "fc1_b", "fc2_w", "fc2_b")
GRAD_ATTENTION = ("ln1", "qkv_w", "qkv_b", "proj_w", "proj_b")


def mlp_back_kernel(pair, tall, chunk, live_ref, *refs):
    cot_ref, y_ref, gj_ref, mid_ref, n2_ref, z_ref, slope_ref, returned_ref = refs[:8]
    weights = refs[8:11]
    near, far = refs[11:15], refs[15:19]
    out_ref, gmid_ref, ghead_far = refs[19:22]
    grads, near_grads, far_grads = refs[22:27], refs[27:30], refs[30:33]
    ghead, gnormed, home = refs[33:]

    @pl.when(pl.program_id(0) == 0)
    def _():
        head_backward(*near, *near_grads, ghead)
        head_backward(*far, *far_grads, ghead_far)
        clear_all(grads)
        home[...] = returned_ref[...].astype(f32)

    acts = (cot_ref, y_ref, gj_ref, mid_ref, n2_ref, z_ref, slope_ref, ghead, home)
    mlp_backward(pair, tall, chunk, live_ref, acts, weights, grads, out_ref, gmid_ref, gnormed)


def attention_back_kernel(pair, tall, gmid_ref, *refs):
    acts, weights, gtok_ref, grads = refs[:5], refs[5:8], refs[8], refs[9:14]

    @pl.when(pl.program_id(0) == 0)
    def _():
        clear_all(grads)

    attention_backward(pair, tall, acts, weights, grads, gtok_ref, gmid_ref, *refs[14:])


def block_back_kernel(pair, tall, chunk, live_ref, *refs):
    mlp_acts, acts = refs[:9], refs[9:14]
    weights, mlp_weights = refs[14:17], refs[17:20]
    out_ref, gtok_ref = refs[20:22]
    mlp_grads, grads = refs[22:27], refs[27:32]
    gy, gnormed, gqkv, gatt_ref, home = refs[32:]

    @pl.when(pl.program_id(0) == 0)
    def _():
        clear_all(mlp_grads + grads)
        home[...] = mlp_acts[8][...].astype(f32)

    mlp_backward(
        pair, tall, chunk, live_ref, (*mlp_acts[:8], home), mlp_weights, mlp_grads, out_ref, gy, gnormed
    )
    attention_backward(pair, tall, acts, weights, grads, gtok_ref, gy, gqkv, gatt_ref)


def named(label, names, values):
    return {label + "_" + name: value for name, value in zip(names, values)}


def grad_outs(params, label, names):
    return [
        (fixed_spec(value.shape), jax.ShapeDtypeStruct(value.shape, f32))
        for value in pick(params, label, names)
    ]


def token_out(crops, length, width, pair):
    return (
        pl.BlockSpec((1, pair, length, width), lambda i: (0, i, 0, 0)),
        jax.ShapeDtypeStruct((1, crops, length, width), bf16),
    )


def mlp_back(cot, live, kept, gj, near, far, returned, params, label, other, length, pair):
    crops, tall, width = cot.shape
    mid, n2, z, slope, y = kept
    hidden = z.shape[1]
    rows, flat = pair * tall, crops * tall
    weights = pick(params, label, ("ln2", "fc1_w", "fc2_w"))
    near = list(near) + pick(params, label, ("to_ln", "to_w"))
    far = list(far) + pick(params, other, ("to_ln", "to_w"))
    smem = pl.BlockSpec(memory_space=pltpu.SMEM)
    outs = [
        token_out(crops, length, width, pair),
        (row_spec(rows, width), jax.ShapeDtypeStruct((flat, width), f32)),
        (fixed_spec(far[0].shape), jax.ShapeDtypeStruct(far[0].shape, f32)),
    ]
    outs += grad_outs(params, label, GRAD_MLP)
    outs += grad_outs(params, label, TO) + grad_outs(params, other, TO)
    values = pl.pallas_call(
        functools.partial(mlp_back_kernel, pair, tall, 768),
        grid=(crops // pair,),
        out_shape=[shape for spec, shape in outs],
        in_specs=[smem, pl.BlockSpec((pair, tall, width), lambda i: (i, 0, 0))]
        + [row_spec(rows, width)] * 4
        + [row_spec(rows, hidden)] * 2
        + [whole(value.shape) for value in [returned] + weights + near + far],
        out_specs=[spec for spec, shape in outs],
        scratch_shapes=[
            pltpu.VMEM((crops, width), f32),
            pltpu.VMEM((rows, width), f32),
            pltpu.VMEM((crops, width), f32),
        ],
        cost_estimate=estimate(8 * 8 * flat * width * hidden, 20_000_000),
        name="mlp_back_" + label,
    )(live, cot, y, gj, mid, n2, z, slope, returned, *weights, *near, *far)
    grads = named(label, GRAD_MLP, values[3:8])
    grads.update(named(label, TO, values[8:11]))
    grads.update(named(other, TO, values[11:14]))
    return values[0], values[1], values[2], grads


def attention_back(tokens, gmid, kept, params, label, length, pair):
    crops, tall, width = tokens.shape
    a1, qkv, probs, att = kept
    rows, flat = pair * tall, crops * tall
    weights = pick(params, label, ("ln1", "qkv_w", "proj_w"))
    outs = [token_out(crops, length, width, pair)] + grad_outs(params, label, GRAD_ATTENTION)
    values = pl.pallas_call(
        functools.partial(attention_back_kernel, pair, tall),
        grid=(crops // pair,),
        out_shape=[shape for spec, shape in outs],
        in_specs=[
            row_spec(rows, width),
            pl.BlockSpec((pair, tall, width), lambda i: (i, 0, 0)),
            row_spec(rows, width),
            row_spec(rows, 3 * width),
            pl.BlockSpec((pair, HEADS, tall, tall), lambda i: (i, 0, 0, 0)),
            row_spec(rows, width),
        ]
        + [whole(value.shape) for value in weights],
        out_specs=[spec for spec, shape in outs],
        scratch_shapes=[pltpu.VMEM((rows, 3 * width), bf16), pltpu.VMEM((rows, width), bf16)],
        cost_estimate=estimate(8 * 16 * flat * width * width, 20_000_000),
        name="attention_back_" + label,
    )(gmid, tokens, a1, qkv, probs, att, *weights)
    return values[0], named(label, GRAD_ATTENTION, values[1:])


def block_back(tokens, cot, live, kept, gj, ghead, returned, params, label, length, pair):
    crops, tall, width = tokens.shape
    a1, qkv, probs, att, mid, n2, z, slope, y = kept
    hidden = z.shape[1]
    rows, flat = pair * tall, crops * tall
    weights = pick(params, label, ("ln1", "qkv_w", "proj_w", "ln2", "fc1_w", "fc2_w"))
    smem = pl.BlockSpec(memory_space=pltpu.SMEM)
    token_spec = pl.BlockSpec((pair, tall, width), lambda i: (i, 0, 0))
    outs = [token_out(crops, length, width, pair)] * 2
    outs += grad_outs(params, label, GRAD_MLP) + grad_outs(params, label, GRAD_ATTENTION)
    values = pl.pallas_call(
        functools.partial(block_back_kernel, pair, tall, 768),
        grid=(crops // pair,),
        out_shape=[shape for spec, shape in outs],
        in_specs=[smem, token_spec]
        + [row_spec(rows, width)] * 4
        + [row_spec(rows, hidden)] * 2
        + [whole(ghead.shape), whole(returned.shape)]
        + [
            token_spec,
            row_spec(rows, width),
            row_spec(rows, 3 * width),
            pl.BlockSpec((pair, HEADS, tall, tall), lambda i: (i, 0, 0, 0)),
            row_spec(rows, width),
        ]
        + [whole(value.shape) for value in weights],
        out_specs=[spec for spec, shape in outs],
        scratch_shapes=[
            pltpu.VMEM((rows, width), f32),
            pltpu.VMEM((rows, width), f32),
            pltpu.VMEM((rows, 3 * width), bf16),
            pltpu.VMEM((rows, width), bf16),
            pltpu.VMEM((crops, width), f32),
        ],
        cost_estimate=estimate(8 * 4 * flat * (4 * width * width + 2 * width * hidden), 20_000_000),
        name="block_back_" + label,
    )(live, cot, y, gj, mid, n2, z, slope, ghead, returned, tokens, a1, qkv, probs, att, *weights)
    grads = named(label, GRAD_MLP, values[2:7])
    grads.update(named(label, GRAD_ATTENTION, values[7:12]))
    return values[0], values[1], grads


def swap(value):
    return lax.ppermute(value, "branch", [(0, 1), (1, 0)])


def partner(value, bit):
    count = lax.axis_size("dp")
    return lax.ppermute(value, "dp", [(i, i ^ bit) for i in range(count)])


def side_partner(value, place):
    count = lax.axis_size("dp")
    pairs = []
    for core in range(2):
        bit = 1 << (place ^ core)
        pairs += [(core * count + i, core * count + (i ^ bit)) for i in range(count)]
    return lax.ppermute(value, ("branch", "dp"), pairs)


def tie(value, *others):
    return lax.optimization_barrier((value, *others))[0] if others else value


def gather_lines(held, first, last, jobs=()):
    for number, place in enumerate(range(first, last, -1)):
        got = partner(held, 1 << place)
        if number < len(jobs):
            got = tie(got, *jobs[number](held))
        held = jnp.concatenate([held, got], 0)
    return held


def gather_middle(held):
    return jnp.concatenate([held, side_partner(held, 1)], 0)


def add_low(*values):
    total = values[0].astype(f32)
    for value in values[1:]:
        total = total + value.astype(f32)
    return total.astype(bf16)


def reduce_step(parts, count, send):
    count = count // 2
    sent = add_low(*[part[count : 2 * count] for part in parts])
    return sent, parts + [send(sent)], count


def reduce_start(low, high, got):
    half = low.shape[0]
    sent = add_low(high, got[half:])
    return sent, [low, got, side_partner(sent, 0)], half


def reduce_middle(parts, count):
    return reduce_step(parts, count, lambda sent: side_partner(sent, 1))


def reduce_lines(parts, count, first, last):
    for place in range(first, last):
        _, parts, count = reduce_step(parts, count, lambda sent: partner(sent, 1 << place))
    return parts, count


def add_up(parts):
    total = parts[0][0].astype(f32)
    for part in parts[1:]:
        total = total + part[0].astype(f32)
    return total


def shards(
    small_tokens,
    large_tokens,
    small_cot,
    large_cot,
    live_counts,
    master,
    first_moment,
    second_moment,
):
    count = lax.axis_size("branch") * lax.axis_size("dp")
    bits = lax.axis_size("dp").bit_length() - 1
    plan = grid_plan(count)
    core, mine = lax.axis_index("branch"), lax.axis_index("dp")
    where = jnp.stack([core, mine]).astype(jnp.int32)
    index = lax.axis_index(("branch", "dp"))
    size = master.shape[0]
    rows = plan["shard_rows"]
    table = lax.dynamic_index_in_dim(jnp.asarray(plan["table"]), index, 0, False)
    padded = jnp.pad(master, (0, rows * LANES - size)).reshape(rows, LANES)
    keep, send = align(where, table, padded, plan)
    got = swap(send)
    counts = live_counts[:, 0]
    own_count = lax.dynamic_slice_in_dim(counts, core, 1)
    far_count = lax.dynamic_slice_in_dim(counts, 1 - core, 1)
    crops, length_s = small_tokens.shape[1], small_tokens.shape[2]
    length_l = large_tokens.shape[2]
    tall_s, tall_l = round_up(length_s, 16), round_up(length_l, 16)
    pair = 2

    def inward(value):
        return jnp.transpose(value[0], (1, 0, 2))

    def settled(value):
        return with_layout_constraint(inward(value), Layout(major_to_minor=(0, 1, 2)))

    def outward(value):
        return jnp.transpose(value, (1, 0, 2))[None]

    def taller(value, length, tall):
        return jnp.pad(value[0], ((0, 0), (0, tall - length), (0, 0)))

    early = []

    def pad_tokens(held):
        early.append(taller(tie(small_tokens, held), length_s, tall_s))
        early.append(taller(tie(large_tokens, held), length_l, tall_l))
        return early[0:2]

    def pad_seeds(held):
        slots = jnp.arange(crops, dtype=jnp.int32)[:, None]
        small_held, large_held = tie(small_cot, held), tie(large_cot, held)
        early.append(taller(small_held, length_s, tall_s))
        early.append(taller(large_held, length_l, tall_l))
        early.append(jnp.where(slots < own_count, small_held[0, :, 0], 0))
        early.append(jnp.where(slots < far_count, large_held[0, :, 0], 0))
        return early[2:6]

    held = jnp.where(core == 0, keep, got)[None]
    near = gather_lines(held, bits - 1, 1, (pad_tokens, pad_seeds))
    small, large, small_seed, large_seed, ret_small, ret_large = early
    far = tie(jnp.where(core == 0, got, keep)[None], near)
    middle = (bits + 1) // 2
    far = gather_lines(far, bits - 1, middle)
    near = tie(gather_middle(near), far)
    near_end = side_partner(near, 0)
    far = gather_lines(far, middle, 1)
    near_end = tie(near_end, far)
    near_pieces = (near, near_end, swap(near), swap(near_end))
    ret_small, ret_large = swap(ret_small), swap(ret_large)

    params = unflatten(where, near_pieces, plan, 0, bits)
    straddling = params.pop(plan["sides"][1][0][0])
    far = tie(far, near_end)
    far = jnp.concatenate([far, tie(side_partner(far, 1), params["s_ln1"])], 0)
    *kept_s, head_s = block_forward(tie(small, far), params, "s", length_s, pair)
    far_end = side_partner(far, 0)
    kept_l = attention_only(tie(large, far_end), params, "l", length_l, pair)
    far_pieces = (far, far_end, swap(far), swap(far_end))
    params.update(unflatten(where, far_pieces, plan, 1, bits, (straddling,)))
    z_l, slope_l, y_l, head_l, sent_l, sent_s = mlp_only(
        kept_l[4], kept_l[5], head_s, params, "l", "s", crops, pair
    )
    got_s, got_l = swap(sent_s), swap(sent_l)
    grads = {}
    back_s, gsent_s, gj_l, part = cross(got_s, y_l, ret_small, params, "s", length_l, tall_l)
    grads.update(part)
    home_s, own_s = swap(back_s), swap(gsent_s)
    back_l, gsent_l, gj_s, part = cross(got_l, kept_s[8], ret_large, params, "l", length_s, tall_s)
    grads.update(part)
    home_l, own_l = swap(back_l), swap(gsent_l)
    large_out, gmid, ghead_s, part = mlp_back(
        large_seed,
        far_count,
        (kept_l[4], kept_l[5], z_l, slope_l, y_l),
        gj_l,
        (head_l, own_l),
        (head_s, own_s),
        home_l,
        params,
        "l",
        "s",
        length_l,
        pair,
    )
    grads.update(part)
    far_parts = flatten(where, grads, plan, 2)
    far_got = swap(far_parts[2])
    large_grad, part = attention_back(large, gmid, kept_l[:4], params, "l", length_l, pair)
    grads.update(part)
    grads["l_ln1"], far_got = lax.optimization_barrier((grads["l_ln1"], far_got))
    upper_parts = flatten(where, grads, plan, 1)
    upper_got = swap(upper_parts[2])
    sent_far, far_side, far_left = reduce_start(*far_parts[:2], far_got)
    sent_upper, upper, upper_left = reduce_start(*upper_parts[:2], tie(upper_got, sent_far))
    ghead_s = tie(ghead_s, sent_far, sent_upper, gmid)
    small_out, small_grad, part = block_back(
        small, small_seed, own_count, kept_s, gj_s, ghead_s, home_s, params, "s", length_s, pair
    )
    grads.update(part)
    grads["s_ln1"] = tie(grads["s_ln1"], far_side[-1], upper[-1])
    lower_parts = flatten(where, grads, plan, 0)
    lower_got = swap(lower_parts[2])
    _, far_side, far_left = reduce_middle(far_side, far_left)
    _, upper, upper_left = reduce_middle(upper, upper_left)
    sent, lower, lower_left = reduce_start(*lower_parts[:2], lower_got)
    lower[-1], large_out, large_grad = lax.optimization_barrier(
        (lower[-1], settled(tie(large_out, sent)), settled(tie(large_grad, sent)))
    )
    far_side[-1], upper[-1] = tie(far_side[-1], sent), tie(upper[-1], sent)
    far_side, far_left = reduce_lines(far_side, far_left, 2, 3)
    upper, _ = reduce_lines(upper, upper_left, 2, bits - 1)
    sent, lower, lower_left = reduce_middle(lower, lower_left)
    lower[-1], small_out, small_grad = lax.optimization_barrier(
        (lower[-1], settled(tie(small_out, sent)), settled(tie(small_grad, sent)))
    )
    lower = add_up(reduce_lines(lower, lower_left, 2, bits - 1)[0])
    far_side, _ = reduce_lines(far_side, far_left, 3, bits)
    upper = add_up(upper)
    top = (mine >> (bits - 1)) & 1
    last_sent = jnp.where(top == 1, lower, upper).astype(bf16)
    near_total = jnp.where(top == 1, upper, lower)
    last_got = partner(last_sent, 1 << (bits - 1))
    everyone = jnp.asarray(plan["table"])
    tables = [
        lax.dynamic_index_in_dim(everyone, mine + begin, 0, False) for begin in (0, plan["half"])
    ]
    own, send, square = settle(
        where, jnp.concatenate(tables), near_total, last_got, far_side, plan
    )
    got = swap(send)
    square = square + swap(square)
    summed = unalign(where, table, own, tie(got, square), plan)
    for place in range(bits):
        there = partner(square, 1 << place)
        square = square + (tie(there, summed) if place == 0 else there)
    grad_norm = jnp.sqrt(square[0, 0])
    own_grad = summed.reshape(-1)[:size]
    clipped = own_grad * jnp.minimum(1.0, clip_norm / grad_norm)
    new_first = beta_one * first_moment + (1.0 - beta_one) * clipped
    new_second = beta_two * second_moment + (1.0 - beta_two) * clipped * clipped
    new_master = master - rate * (
        new_first / bias_one / (jnp.sqrt(new_second / bias_two) + adam_eps) + decay * master
    )
    return (
        outward(small_out),
        outward(large_out),
        outward(small_grad),
        outward(large_grad),
        grad_norm,
        new_first,
        new_second,
        new_master,
        new_master.astype(bf16),
    )


def solution(mesh):
    return jax.shard_map(
        shards,
        mesh=mesh,
        in_specs=(
            P("branch", "dp", None, None),
            P("branch", "dp", None, None),
            P("branch", "dp", None, None),
            P("branch", "dp", None, None),
            P(None, "dp"),
            P(("branch", "dp")),
            P(("branch", "dp")),
            P(("branch", "dp")),
        ),
        out_specs=(
            P("branch", "dp", None, None),
            P("branch", "dp", None, None),
            P("branch", "dp", None, None),
            P("branch", "dp", None, None),
            P(),
            P(("branch", "dp")),
            P(("branch", "dp")),
            P(("branch", "dp")),
            P(("branch", "dp")),
        ),
        check_vma=False,
    )
```
